32 devices in a mesh: groups: 2 (over y), tile: 4 (over z), batch: 2 (over x), chan: 2 (over core).
Axes of the slice: x: 2, y: 2, z: 4, core: 2. Of those that a mesh axis runs over, the one named last changes fastest.
Arguments:
- features: bfloat16 [4, 48, 256, 256], P(('groups', 'batch'), 'tile'), parts along dimension 0, may hold values from -6 to 6
- labels: int32 [4, 48, 2304], P(('groups', 'batch'), 'tile'), parts along dimension 0, may hold values from -1 to 11, as said below
- w_shared: bfloat16 [3, 3, 256, 256], P(None, None, None, 'chan'), may hold values from -0.125 to 0.125
- b_shared: float32 [256], P('chan'), may hold values from -3 to 3
- w_cls: bfloat16 [3, 3, 256, 99], P(None, None, 'chan'), may hold values from -0.125 to 0.125
- b_cls: float32 [99], replicated, may hold values from -3 to -1
Outputs:
- grad_shared: float32 [6, 3, 256, 256], P('groups', None, None, 'chan'), parts along dimension 0
- grad_shared_bias: float32 [512], P(('groups', 'chan')), parts along dimension 0
- grad_cls: float32 [6, 3, 256, 99], P('groups', None, 'chan'), parts along dimension 0
- grad_cls_bias: float32 [198], P('groups'), parts along dimension 0
- loss: float32 [2], P('groups'), parts along dimension 0
The draws below stay inside these ranges and needn't reach their ends.
There are 2 independent parts, one for each index of `groups`. The reference program is written for one: setup_inputs(seed, part) draws one part's arguments, and reference() takes and returns one part's arrays. A program takes and returns all parts, laid end to end along the dimension named above; an argument that names none is the same for every part. Nothing has to cross between parts.
Inputs may be any that keep to these rules, and one draw needn't show every extreme that they name: `labels`: each anchor is a background anchor (0), ignored (-1) or names a class of 1 to 11.
All inputs are finite; a program needn't handle non-finite values.
Results may differ from the reference program's by a relative error of at most 0.0027.
Values may be sent and summed in bfloat16 or wider, within the bound.
No kernel may reach another device: no remote copies, remote signals or barrier semaphores. Data moves between devices by JAX's collectives and lax.ppermute only.
A program may use at most 128 MiB of HBM per device.

```python
import jax
import jax.numpy as jnp
from jax import lax

C = 256
ANCH = 9
CLASSES = 11
W = 256
LOGITS = 99
PAGE_ROWS = 48
PAGES = 2


def draw_labels(key, part):
    shape = (PAGES, PAGE_ROWS, W * ANCH)
    first, second = jax.random.split(jax.random.fold_in(key, 7))
    level = jax.random.randint(first, shape, 0, 10000)
    row_index = lax.broadcasted_iota(jnp.int32, shape, 1)
    bound = 300 + 600 * row_index // PAGE_ROWS
    classes = jax.random.randint(second, shape, 1, CLASSES + 1)
    return jnp.where(level < bound, classes, jnp.where(level < bound + 500, -1, 0)).astype(jnp.int32)


def level_of(key, dims, shards, low, largest):
    def one(position, parts):
        draws = jax.random.uniform(jax.random.fold_in(jax.random.fold_in(key, 6), position), (parts,), jnp.float32, low / len(shards), largest / len(shards))
        return jnp.repeat(jnp.exp(draws), dims[position] // parts).reshape((-1,) + (1,) * (len(dims) - position - 1))

    factor_of = one(*shards[0])
    for cut in shards[1:]:
        factor_of = factor_of * one(*cut)
    return factor_of


def normal_values(own_key, shape, width, most, cuts=(), kind=jnp.bfloat16):
    result = width * jax.random.normal(own_key, shape, jnp.float32)
    if cuts:
        result = result * level_of(own_key, shape, cuts, -0.22, 0.18)
    return jnp.clip(result, -most, most).astype(kind)


def setup_inputs(seed: int = 0, part: int = 0) -> dict:
    keys = jax.random.split(jax.random.key(seed), 7)
    own_keys = jax.random.split(jax.random.fold_in(keys[6], part), 7)
    features = normal_values(own_keys[0], (PAGES, PAGE_ROWS, W, C), 1.0, 6.0, ((0, 2), (1, 4)))
    labels = draw_labels(jax.random.fold_in(jax.random.fold_in(keys[6], part), 71), part)
    w_shared = normal_values(keys[2], (3, 3, C, C), (9 * C) ** -0.5, 0.125, ((3, 2),))
    b_shared = normal_values(keys[3], (C,), 0.5, 3.0, ((0, 2),), jnp.float32)
    w_cls = normal_values(keys[4], (3, 3, C, LOGITS), (9 * C) ** -0.5, 0.125, ((2, 2),))
    b_cls = jnp.clip(jax.random.uniform(keys[5], (LOGITS,), jnp.float32, -3.0, -1.0), -3.0, -1.0)
    return {"features": features, "labels": labels, "w_shared": w_shared, "b_shared": b_shared, "w_cls": w_cls, "b_cls": b_cls}


def focal_sum(z, lab):
    classes = jnp.arange(1, CLASSES + 1, dtype=jnp.int32)
    target = (lab[..., None] == classes).astype(jnp.float32)
    keep = (lab >= 0).astype(jnp.float32)[..., None]
    prob = jax.nn.sigmoid(z)
    cross = jax.nn.softplus(z) - target * z
    p_true = prob * target + (1.0 - prob) * (1.0 - target)
    weight = 0.25 * target + 0.75 * (1.0 - target)
    return jnp.sum(keep * weight * jnp.square(1.0 - p_true) * cross)

def conv_rows(padded, weight, rows, cols):
    total = jnp.zeros((rows, cols, weight.shape[3]), jnp.float32)
    for i in range(3):
        for j in range(3):
            total = total + jnp.einsum('rcx,xo->rco', padded[i:i + rows, j:j + cols].astype(jnp.float32), weight[i, j].astype(jnp.float32))
    return total

def reference(features, labels, w_shared, b_shared, w_cls, b_cls):
    rows = PAGE_ROWS
    cols = W
    count = jnp.sum((labels > 0).astype(jnp.float32))
    loss_sum = jnp.zeros((), jnp.float32)
    grad_sb = jnp.zeros((C,), jnp.float32)
    grad_cb = jnp.zeros((LOGITS,), jnp.float32)
    grad_s = [jnp.zeros((C, C), jnp.float32) for _ in range(9)]
    grad_c = [jnp.zeros((C, LOGITS), jnp.float32) for _ in range(9)]
    for page in range(PAGES):
        xpad = jnp.pad(features[page], ((1, 1), (1, 1), (0, 0)))
        pre = conv_rows(xpad, w_shared, rows, cols) + b_shared
        hidden = jnp.maximum(pre, 0.0).astype(jnp.bfloat16)
        hpad = jnp.pad(hidden, ((1, 1), (1, 1), (0, 0)))
        logits = conv_rows(hpad, w_cls, rows, cols) + b_cls
        z = logits.reshape(rows, cols, ANCH, CLASSES)
        lab = labels[page].reshape(rows, cols, ANCH)
        loss_sum = loss_sum + focal_sum(z, lab)
        dz = (jax.grad(focal_sum)(z, lab) / count).reshape(rows, cols, LOGITS)
        grad_cb = grad_cb + lax.optimization_barrier(jnp.sum(dz, axis=(0, 1)))
        dlog = dz.astype(jnp.bfloat16)
        dpad = jnp.pad(dlog, ((1, 1), (1, 1), (0, 0)))
        dhid = jnp.zeros((rows, cols, C), jnp.float32)
        for i in range(3):
            for j in range(3):
                grad_c[3 * i + j] = grad_c[3 * i + j] + jnp.einsum('rcx,rca->xa', hpad[i:i + rows, j:j + cols].astype(jnp.float32), dlog.astype(jnp.float32))
                dhid = dhid + jnp.einsum('rca,xa->rcx', dpad[2 - i:2 - i + rows, 2 - j:2 - j + cols].astype(jnp.float32), w_cls[i, j].astype(jnp.float32))
        dpre = jnp.where(pre > 0.0, dhid, 0.0)
        grad_sb = grad_sb + lax.optimization_barrier(jnp.sum(dpre, axis=(0, 1)))
        dp16 = dpre.astype(jnp.bfloat16)
        for i in range(3):
            for j in range(3):
                grad_s[3 * i + j] = grad_s[3 * i + j] + jnp.einsum('rcx,rco->xo', xpad[i:i + rows, j:j + cols].astype(jnp.float32), dp16.astype(jnp.float32))
    grad_shared = jnp.stack(grad_s).reshape(3, 3, C, C)
    grad_cls = jnp.stack(grad_c).reshape(3, 3, C, LOGITS)
    loss = (loss_sum / count).reshape(1)
    return (grad_shared, grad_sb, grad_cls, grad_cb, loss)
```

```python
import functools

import jax
import jax.numpy as jnp
from jax import lax
from jax.experimental import pallas as pl
from jax.experimental.pallas import tpu as pltpu
from jax.sharding import PartitionSpec as P

ANCH = 9
CLASSES = 11
LOGITS = 99
LANES = 128
CLS_ROWS = 112
BF16 = jnp.bfloat16
F32 = jnp.float32


def shift_cells(field, by):
    cells = field.shape[0]
    rolled = pltpu.roll(field, by % cells, axis=0)
    cell = lax.broadcasted_iota(jnp.int32, field.shape, 0)
    edge = 0 if by > 0 else cells - 1
    return jnp.where(cell == edge, 0.0, rolled)


def dot(left, right, dims=((1,), (0,))):
    return lax.dot_general(left, right, (dims, ((), ())), preferred_element_type=F32)


def head_kernel(
    where_ref, count_ref, f_ref, halo_ref, lab_ref, hlab_ref, w1a_ref, w1b_ref, b1_ref, w2_ref, b2_ref,
    gcls_ref, own_ref, other_ref, small_ref,
    xw_ref, hid_ref, dlog_ref, dt_ref,
):
    half = f_ref.shape[0] // 2
    cols = f_ref.shape[1]
    c = where_ref[0]
    first = where_ref[1]
    total = where_ref[2]
    near = half + 3
    xw_ref[pl.ds(3 - 3 * c, near)] = f_ref[pl.ds((half - 3) * c, near)]
    xw_ref[pl.ds(near * c, 3)] = halo_ref[...]
    w1 = [
        jnp.concatenate(
            [jnp.concatenate([w1a_ref[i, j], w1b_ref[i, j]], axis=1) for j in range(3)], axis=1
        )
        for i in range(3)
    ]
    w1 = jnp.concatenate(w1, axis=0)
    chans = w1.shape[1] // 3
    b1 = b1_ref[...]

    def conv1(h, carry):
        lhs = jnp.concatenate([xw_ref[h], xw_ref[h + 1], xw_ref[h + 2]], axis=1)
        y = dot(lhs, w1)
        pre = shift_cells(y[:, :chans], 1) + y[:, chans : 2 * chans] + shift_cells(y[:, 2 * chans :], -1) + b1
        row = first + h - 2
        inside = jnp.logical_and(row >= 0, row < total)
        hid_ref[h] = jnp.where(inside, jnp.maximum(pre, 0.0), 0.0).astype(BF16)
        return carry

    lax.fori_loop(0, half + 4, conv1, 0)

    lane = lax.broadcasted_iota(jnp.int32, (1, LANES), 1)
    kind = (lane % CLASSES + 1).astype(F32)
    real = lane < LOGITS
    anchor = lax.broadcasted_iota(jnp.int32, (ANCH, LANES), 0)
    column = lax.broadcasted_iota(jnp.int32, (ANCH, LANES), 1)
    spread = jnp.where(jnp.logical_and(column // CLASSES == anchor, column < LOGITS), 1.0, 0.0).astype(BF16)
    w2n = [jnp.concatenate([w2_ref[i, j] for j in range(3)], axis=1) for i in range(3)]
    w2n = jnp.concatenate(w2n, axis=0)
    b2 = b2_ref[...]
    inverse = 1.0 / jnp.full((1, LANES), count_ref[0], F32)

    def focal(l, carry):
        gcb, loss = carry
        lhs = jnp.concatenate([hid_ref[l], hid_ref[l + 1], hid_ref[l + 2]], axis=1)
        y = dot(lhs, w2n)
        z = shift_cells(y[:, :LANES], 1) + y[:, LANES : 2 * LANES] + shift_cells(y[:, 2 * LANES :], -1) + b2
        at_halo = jnp.where(c == 0, l == 0, l == half + 1)
        local = jnp.clip(l - 1 + half * c, 0, 2 * half - 1)
        mine = lab_ref[local]
        lab9 = jnp.where(at_halo, hlab_ref[...], mine)
        lab = dot(lab9, spread)
        hit = lab == kind
        keep = jnp.logical_and(lab >= 0.0, real)
        u = jnp.where(hit, -z, z)
        e = jnp.exp(-jnp.abs(u))
        r = 1.0 / (1.0 + e)
        er = e * r
        up = u >= 0.0
        s = jnp.where(up, r, er)
        comp = jnp.where(up, er, r)
        soft = jnp.maximum(u, 0.0) + jnp.log1p(e)
        ws = jnp.where(keep, jnp.where(hit, 0.25, 0.75), 0.0) * s * s
        slope = ws * (2.0 * comp * soft + s)
        dz = jnp.where(hit, -slope, slope) * inverse
        d16 = dz.astype(BF16)
        dlog_ref[l] = d16
        own = jnp.logical_and(l >= 1, l <= half)
        weight = jnp.where(own, 1.0, 0.0)
        gcb = gcb + weight * jnp.sum(dz, axis=0, keepdims=True)
        loss = loss + weight * jnp.sum(ws * soft, axis=0, keepdims=True)

        @pl.when(own)
        def _():
            turned = jnp.transpose(d16.astype(F32))[:CLS_ROWS]
            cell = lax.broadcasted_iota(jnp.int32, turned.shape, 1)
            left = jnp.where(cell == cols - 1, 0.0, pltpu.roll(turned, cols - 1, axis=1))
            right = jnp.where(cell == 0, 0.0, pltpu.roll(turned, 1, axis=1))
            dt_ref[l - 1] = jnp.concatenate([left, turned, right], axis=0).astype(BF16)

        return gcb, loss

    zero = jnp.zeros((1, LANES), F32)
    gcb, loss = lax.fori_loop(0, half + 2, focal, (zero, zero))

    dt = jnp.concatenate([dt_ref[d] for d in range(half)], axis=1)
    for i in range(3):
        rows = hid_ref[i + 1 : i + 1 + half].reshape(half * cols, chans)
        gcls_ref[i] = dot(dt, rows)

    w2t = [jnp.concatenate([w2_ref[i, j] for i in range(3)], axis=1) for j in range(3)]
    w2t = jnp.concatenate(w2t, axis=0)

    def dpre_row(d, gsb):
        lhs = jnp.concatenate([dlog_ref[d + 2], dlog_ref[d + 1], dlog_ref[d]], axis=1)
        q = dot(lhs, w2t, ((1,), (1,)))
        dhid = shift_cells(q[:, :chans], -1) + q[:, chans : 2 * chans] + shift_cells(q[:, 2 * chans :], 1)
        dpre = jnp.where(hid_ref[d + 2].astype(F32) > 0.0, dhid, 0.0)
        d16 = dpre.astype(BF16)
        own_ref[d] = d16[:, : chans // 2]
        other_ref[d] = d16[:, chans // 2 :]
        return gsb + jnp.sum(dpre, axis=0, keepdims=True)

    gsb = lax.fori_loop(0, half, dpre_row, jnp.zeros((1, chans), F32))
    small_ref[0:1] = gcb
    small_ref[1:2] = jnp.broadcast_to(jnp.sum(loss, axis=1, keepdims=True), (1, LANES)) * inverse
    small_ref[2:3] = jnp.zeros((1, LANES), F32)
    small_ref[3:4] = gsb[:, : chans // 2]
    small_ref[4:5] = gsb[:, chans // 2 :]
    small_ref[5:8] = jnp.zeros((3, LANES), F32)


def shared_kernel(where_ref, f_ref, before_ref, after_ref, own_ref, other_ref, out_ref, x_ref, d_ref):
    rows, cols, chans = f_ref.shape
    half = rows // 2
    c = where_ref[0]
    x_ref[0] = before_ref[...]
    x_ref[1 : rows + 1] = f_ref[...]
    x_ref[rows + 1] = after_ref[...]

    def place(ref, start):
        def body(d, carry):
            mid = ref[d].astype(F32)
            d_ref[start + d] = jnp.concatenate(
                [shift_cells(mid, -1).astype(BF16), ref[d], shift_cells(mid, 1).astype(BF16)], axis=1
            )
            return carry

        lax.fori_loop(0, half, body, 0)

    place(own_ref, half * c)
    place(other_ref, half * (1 - c))
    rhs = d_ref[...].reshape(rows * cols, d_ref.shape[2])
    outs = rhs.shape[1] // 3
    for i in range(3):
        lhs = x_ref[i : i + rows].reshape(rows * cols, chans)
        g = dot(lhs, rhs, ((0,), (0,)))
        for j in range(3):
            out_ref[i, j] = g[:, j * outs : (j + 1) * outs]


def swap(x, axis, bit):
    size = lax.axis_size(axis)
    return lax.ppermute(x, axis, [(i, i ^ bit) for i in range(size)])


def piece(x, index, size):
    return lax.dynamic_slice_in_dim(x, index * size, size, axis=0)


def scatter_sum(x, axis):
    size = lax.axis_size(axis)
    me = lax.axis_index(axis)
    rows = x.shape[0] // size
    total = piece(x, me, rows)
    for bit in range(1, size):
        total = total + swap(piece(x, me ^ bit, rows).astype(BF16), axis, bit).astype(F32)
    return total


def gather(x, axis):
    size = lax.axis_size(axis)
    me = lax.axis_index(axis)
    rows = x.shape[0]
    whole = jnp.zeros((rows * size,) + x.shape[1:], x.dtype)
    whole = lax.dynamic_update_slice_in_dim(whole, x, me * rows, axis=0)
    for bit in range(1, size):
        whole = lax.dynamic_update_slice_in_dim(whole, swap(x, axis, bit), (me ^ bit) * rows, axis=0)
    return whole


def sum_all(x, axis):
    size = lax.axis_size(axis)
    parts = [x] + [swap(x, axis, bit) for bit in range(1, size)]
    while len(parts) > 1:
        parts = [parts[k] + parts[k + 1] for k in range(0, len(parts), 2)]
    return parts[0]


def shards(features, labels, w_shared, b_shared, w_cls, b_cls):
    _, rows, cols, chans = features.shape
    half = rows // 2
    outs = w_shared.shape[3]
    tiles = lax.axis_size("tile")
    c = lax.axis_index("chan")
    t = lax.axis_index("tile")
    f = features[0]

    pairs = []
    for i in range(tiles - 1):
        pairs += [(2 * i + 1, 2 * i + 2), (2 * i + 2, 2 * i + 1)]
    line = ("tile", "chan")
    lab_edge = lax.dynamic_slice_in_dim(labels[0], (rows - 1) * c, 1, axis=0)
    halo = lax.ppermute(lax.dynamic_slice_in_dim(f, (rows - 3) * c, 3, axis=0), line, pairs)
    hlab = lax.ppermute(lab_edge, line, pairs)
    count = jnp.full((8, LANES), jnp.sum((labels > 0).astype(F32)), F32)
    count = sum_all(sum_all(count, "batch"), "tile")[0, :1]
    w1b = swap(w_shared, "chan", 1)
    w2b = swap(w_cls, "chan", 1)
    b1b = swap(b_shared, "chan", 1)

    at_edge = jnp.where(c == 0, t == 0, t == tiles - 1)
    hlab = jnp.where(at_edge, -1, hlab).astype(BF16).reshape(cols, ANCH)
    lab = labels[0].astype(BF16).reshape(rows, cols, ANCH)
    b1 = jnp.concatenate([b_shared, b1b]).reshape(1, 2 * outs)
    w2 = jnp.pad(jnp.concatenate([w_cls, w2b], axis=2), ((0, 0), (0, 0), (0, 0), (0, LANES - LOGITS)))
    b2 = jnp.pad(b_cls, (0, LANES - LOGITS)).reshape(1, LANES)
    where = jnp.stack([c, t * rows + half * c, tiles * rows]).astype(jnp.int32)

    vmem = pl.BlockSpec(memory_space=pltpu.VMEM)
    smem = pl.BlockSpec(memory_space=pltpu.SMEM)
    gcls, own, other, small = pl.pallas_call(
        head_kernel,
        in_specs=[smem, smem] + [vmem] * 9,
        out_specs=[vmem] * 4,
        out_shape=[
            jax.ShapeDtypeStruct((3, 3 * CLS_ROWS, chans), F32),
            jax.ShapeDtypeStruct((half, cols, outs), BF16),
            jax.ShapeDtypeStruct((half, cols, outs), BF16),
            jax.ShapeDtypeStruct((8, LANES), F32),
        ],
        scratch_shapes=[
            pltpu.VMEM((half + 6, cols, chans), BF16),
            pltpu.VMEM((half + 4, cols, chans), BF16),
            pltpu.VMEM((half + 2, cols, LANES), BF16),
            pltpu.VMEM((half, 3 * CLS_ROWS, cols), BF16),
        ],
        compiler_params=pltpu.CompilerParams(vmem_limit_bytes=50 * 1024 * 1024),
        name="head",
    )(where, count, f, halo, lab, hlab, w_shared, w1b, b1, w2, b2)

    theirs = swap(other, "chan", 1)
    near = lax.dynamic_index_in_dim(halo, 2 - 2 * c, axis=0, keepdims=False)
    far = swap(near, "chan", 1)
    before = jnp.where(c == 0, near, far)
    after = jnp.where(c == 0, far, near)
    gsh = pl.pallas_call(
        shared_kernel,
        in_specs=[smem] + [vmem] * 5,
        out_specs=vmem,
        out_shape=jax.ShapeDtypeStruct((3, 3, chans, outs), F32),
        scratch_shapes=[
            pltpu.VMEM((rows + 2, cols, chans), BF16),
            pltpu.VMEM((rows, cols, 3 * outs), BF16),
        ],
        compiler_params=pltpu.CompilerParams(vmem_limit_bytes=50 * 1024 * 1024),
        name="shared",
    )(where, f, before, after, own, theirs)

    gcls = gcls.reshape(9 * CLS_ROWS, chans)
    gcls = gcls[:, :outs] + swap(gcls[:, outs:], "chan", 1)
    gcls = jnp.pad(gcls, ((0, 1024 - 9 * CLS_ROWS), (0, 0)))
    far_small = swap(jnp.concatenate([small[0:3], small[4:5], small[3:4], small[5:8]]), "chan", 1)
    small = small + far_small
    small = sum_all(sum_all(small, "batch"), "tile")

    def reduced(x):
        share = scatter_sum(scatter_sum(x, "batch"), "tile").astype(BF16)
        return gather(gather(share, "tile"), "batch").astype(F32)

    gcls = reduced(gcls)[: 9 * CLS_ROWS].reshape(9, CLS_ROWS, outs)
    grad_cls = jnp.swapaxes(gcls, 1, 2)[:, :, :LOGITS].reshape(3, 3, outs, LOGITS)
    grad_shared = reduced(gsh.reshape(9 * chans, outs)).reshape(3, 3, chans, outs)
    return (
        grad_shared,
        small[3],
        grad_cls,
        small[0, :LOGITS],
        small[1, :1],
    )


def solution(mesh):
    placed = (
        P(("groups", "batch"), "tile", None, None),
        P(("groups", "batch"), "tile", None),
        P(None, None, None, "chan"),
        P("chan"),
        P(None, None, "chan", None),
        P(),
    )
    return jax.shard_map(
        shards,
        mesh=mesh,
        in_specs=placed,
        out_specs=(
            P("groups", None, None, "chan"),
            P(("groups", "chan")),
            P("groups", None, "chan", None),
            P("groups"),
            P("groups"),
        ),
        check_vma=False,
    )
```

```python
import functools

import jax
import jax.numpy as jnp
from jax import lax
from jax.experimental import pallas as pl
from jax.experimental.pallas import tpu as pltpu
from jax.sharding import PartitionSpec as P

ANCH = 9
CLASSES = 11
LOGITS = 99
LANES = 128
ANCH_ROWS = 16
CLS_ROWS = 112
CLS_TOTAL = 1024
TRIO = 32
BF16 = jnp.bfloat16
F32 = jnp.float32
VMEM = pl.BlockSpec(memory_space=pltpu.VMEM)
SMEM = pl.BlockSpec(memory_space=pltpu.SMEM)


def call(kernel, name, outs, inputs, scratch=()):
    return pl.pallas_call(
        kernel,
        in_specs=[SMEM] + [VMEM] * (len(inputs) - 1),
        out_specs=[VMEM] * len(outs),
        out_shape=[jax.ShapeDtypeStruct(shape, kind) for shape, kind in outs],
        scratch_shapes=[pltpu.VMEM(shape, kind) for shape, kind in scratch],
        compiler_params=pltpu.CompilerParams(vmem_limit_bytes=48 * 1024 * 1024),
        name=name,
    )(*inputs)


def shift_cells(field, by):
    cells = field.shape[0]
    rolled = pltpu.roll(field, by % cells, axis=0)
    cell = lax.broadcasted_iota(jnp.int32, field.shape, 0)
    edge = 0 if by > 0 else cells - 1
    return jnp.where(cell == edge, 0.0, rolled)


def dot(left, right, dims=((1,), (0,))):
    return lax.dot_general(left, right, (dims, ((), ())), preferred_element_type=F32)


def three(x):
    high = x.astype(BF16)
    rest = x - high.astype(F32)
    middle = rest.astype(BF16)
    low = (rest - middle.astype(F32)).astype(BF16)
    return high, middle, low


def put_trio(ref, start, x):
    high, middle, low = three(x)
    ref[start : start + TRIO] = jnp.concatenate([high, middle, low, jnp.zeros_like(low)], axis=0)


def get_trio(ref, start):
    part = ref[start : start + TRIO].astype(F32)
    return part[0:8] + part[8:16] + part[16:24]


def prep_kernel(where_ref, f_ref, lab_ref, w2_ref, b1_ref, msg_ref, labt_ref, pack_ref, count_ref):
    rows, cols, chans = f_ref.shape
    c = where_ref[0]
    for k in range(3):
        msg_ref[cols * k : cols * (k + 1)] = f_ref[(rows - 3) * c + k]
    lab = lab_ref[...]
    count_ref[...] = jnp.full(count_ref.shape, jnp.sum(jnp.where(lab > 0, 1.0, 0.0)), F32)
    size = lab.shape[1]
    place = lax.broadcasted_iota(jnp.int32, (ANCH_ROWS, size), 1) % ANCH
    anchor = lax.broadcasted_iota(jnp.int32, (ANCH_ROWS, size), 0)
    mine = jnp.where(place == anchor, 1.0, 0.0)
    left = jnp.concatenate([mine * lab[r : r + 1].astype(F32) for r in range(rows)], axis=0).astype(BF16)
    offset = lax.broadcasted_iota(jnp.int32, (size, cols), 0) - ANCH * lax.broadcasted_iota(jnp.int32, (size, cols), 1)
    pick = jnp.where(jnp.logical_and(offset >= 0, offset < ANCH), 1.0, 0.0).astype(BF16)
    turned = dot(left, pick).astype(BF16)
    for r in range(rows):
        labt_ref[r] = turned[ANCH_ROWS * r : ANCH_ROWS * (r + 1)]
    msg_ref[3 * cols : 3 * cols + ANCH_ROWS] = jnp.where(
        c == 0, turned[:ANCH_ROWS].astype(F32), turned[ANCH_ROWS * (rows - 1) :].astype(F32)
    ).astype(BF16)
    deep = w2_ref.shape[2]
    for tap in range(9):
        pack_ref[deep * tap : deep * (tap + 1)] = jnp.zeros((deep, LANES), BF16)
        pack_ref[deep * tap : deep * (tap + 1), :LOGITS] = w2_ref[tap // 3, tap % 3]
    bias = jnp.broadcast_to(b1_ref[...], (8, deep))
    put_trio(pack_ref, 9 * deep, bias)


def head_kernel(
    where_ref, f_ref, halo_ref, labt_ref, w1a_ref, w1b_ref, packa_ref, packb_ref, b2_ref, *rest,
):
    *count_refs, hid_ref, dt_ref, own_ref, other_ref, small_ref, xw_ref, dlog_ref = rest

    half = f_ref.shape[0] // 2
    cols = f_ref.shape[1]
    c = where_ref[0]
    first = where_ref[1]
    total = where_ref[2]
    near = half + 3
    xw_ref[pl.ds(3 - 3 * c, near)] = f_ref[pl.ds((half - 3) * c, near)]
    for k in range(3):
        xw_ref[near * c + k] = halo_ref[cols * k : cols * (k + 1)]
    w1 = [
        jnp.concatenate(
            [jnp.concatenate([w1a_ref[i, j], w1b_ref[i, j]], axis=1) for j in range(3)], axis=1
        )
        for i in range(3)
    ]
    w1 = jnp.concatenate(w1, axis=0)
    chans = w1.shape[1] // 3
    deep = chans // 2
    b1 = jnp.concatenate([get_trio(packa_ref, 9 * deep)[:1], get_trio(packb_ref, 9 * deep)[:1]], axis=1)
    counts = [ref[...] for ref in count_refs]
    while len(counts) > 1:
        counts = [counts[k] + counts[k + 1] for k in range(0, len(counts), 2)]

    def conv1(h, carry):
        lhs = jnp.concatenate([xw_ref[h], xw_ref[h + 1], xw_ref[h + 2]], axis=1)
        y = dot(lhs, w1)
        pre = shift_cells(y[:, :chans], 1) + y[:, chans : 2 * chans] + shift_cells(y[:, 2 * chans :], -1) + b1
        row = first + h - 2
        inside = jnp.logical_and(row >= 0, row < total)
        hid_ref[h] = jnp.where(inside, jnp.maximum(pre, 0.0), 0.0).astype(BF16)
        return carry

    lax.fori_loop(0, half + 4, conv1, 0)

    lane = lax.broadcasted_iota(jnp.int32, (1, LANES), 1)
    kind = (lane % CLASSES + 1).astype(F32)
    real = lane < LOGITS
    anchor = lax.broadcasted_iota(jnp.int32, (ANCH_ROWS, LANES), 0)
    column = lax.broadcasted_iota(jnp.int32, (ANCH_ROWS, LANES), 1)
    spread = jnp.where(jnp.logical_and(column // CLASSES == anchor, column < LOGITS), 1.0, 0.0).astype(BF16)


    def tap(ref, i, j):
        return ref[deep * (3 * i + j) : deep * (3 * i + j + 1)]

    w2 = [[jnp.concatenate([tap(packa_ref, i, j), tap(packb_ref, i, j)], axis=0) for j in range(3)] for i in range(3)]
    w2n = [jnp.concatenate(w2[i], axis=1) for i in range(3)]
    w2n = jnp.concatenate(w2n, axis=0)
    b2 = jnp.concatenate([b2_ref[...], jnp.zeros((1, LANES - LOGITS), F32)], axis=1)
    inverse = 1.0 / counts[0][:1]

    def focal(l, carry):
        gcb, loss = carry
        lhs = jnp.concatenate([hid_ref[l], hid_ref[l + 1], hid_ref[l + 2]], axis=1)
        y = dot(lhs, w2n)
        z = shift_cells(y[:, :LANES], 1) + y[:, LANES : 2 * LANES] + shift_cells(y[:, 2 * LANES :], -1) + b2
        at_halo = jnp.where(c == 0, l == 0, l == half + 1)
        local = jnp.clip(l - 1 + half * c, 0, 2 * half - 1)
        mine = labt_ref[local].astype(F32)
        far = halo_ref[3 * cols : 3 * cols + ANCH_ROWS].astype(F32)
        lab = dot(jnp.where(at_halo, far, mine).astype(BF16), spread, ((0,), (0,)))
        row = first + l - 1
        inside = jnp.logical_and(row >= 0, row < total)
        hit = lab == kind
        keep = jnp.logical_and(jnp.logical_and(lab >= 0.0, real), inside)
        u = jnp.where(hit, -z, z)
        e = jnp.exp(-jnp.abs(u))
        r = 1.0 / (1.0 + e)
        er = e * r
        up = u >= 0.0
        s = jnp.where(up, r, er)
        comp = jnp.where(up, er, r)
        soft = jnp.maximum(u, 0.0) + jnp.log1p(e)
        ws = jnp.where(keep, jnp.where(hit, 0.25, 0.75), 0.0) * s * s
        slope = ws * (2.0 * comp * soft + s)
        dz = jnp.where(hit, -slope, slope) * inverse
        d16 = dz.astype(BF16)
        dlog_ref[l] = d16
        own = jnp.logical_and(l >= 1, l <= half)
        weight = jnp.where(own, 1.0, 0.0)
        gcb = gcb + weight * jnp.sum(dz, axis=0, keepdims=True)
        loss = loss + weight * jnp.sum(ws * soft, axis=0, keepdims=True)

        @pl.when(own)
        def _():
            turned = jnp.transpose(d16.astype(F32))[:CLS_ROWS]
            cell = lax.broadcasted_iota(jnp.int32, turned.shape, 1)
            left = jnp.where(cell == cols - 1, 0.0, pltpu.roll(turned, cols - 1, axis=1))
            right = jnp.where(cell == 0, 0.0, pltpu.roll(turned, 1, axis=1))
            dt_ref[l - 1] = jnp.concatenate([left, turned, right], axis=0).astype(BF16)

        return gcb, loss

    zero = jnp.zeros((1, LANES), F32)
    gcb, loss = lax.fori_loop(0, half + 2, focal, (zero, zero))

    w2t = [jnp.concatenate([w2[i][j] for i in range(3)], axis=1) for j in range(3)]
    w2t = jnp.concatenate(w2t, axis=0)

    def dpre_row(d, gsb):
        lhs = jnp.concatenate([dlog_ref[d + 2], dlog_ref[d + 1], dlog_ref[d]], axis=1)
        q = dot(lhs, w2t, ((1,), (1,)))
        dhid = shift_cells(q[:, :chans], -1) + q[:, chans : 2 * chans] + shift_cells(q[:, 2 * chans :], 1)
        dpre = jnp.where(hid_ref[d + 2].astype(F32) > 0.0, dhid, 0.0)
        d16 = dpre.astype(BF16)
        own_ref[d] = d16[:, : chans // 2]
        other_ref[d] = d16[:, chans // 2 :]
        return gsb + jnp.sum(dpre, axis=0, keepdims=True)

    gsb = lax.fori_loop(0, half, dpre_row, jnp.zeros((1, chans), F32))
    small_ref[0:1] = gcb
    small_ref[1:2] = jnp.broadcast_to(jnp.sum(loss, axis=1, keepdims=True), (1, LANES)) * inverse
    small_ref[2:3] = jnp.zeros((1, LANES), F32)
    small_ref[3:4] = gsb[:, : chans // 2]
    small_ref[4:5] = gsb[:, chans // 2 :]
    small_ref[5:8] = jnp.zeros((3, LANES), F32)


def cls_kernel(where_ref, hid_ref, dt_ref, own_ref, other_ref):
    half, _, cols = dt_ref.shape
    chans = hid_ref.shape[2]
    deep = chans // 2
    dt = jnp.concatenate([dt_ref[d] for d in range(half)], axis=1)
    size = 3 * CLS_ROWS
    for i in range(3):
        g = dot(dt, hid_ref[i + 1 : i + 1 + half].reshape(half * cols, chans))
        own_ref[size * i : size * (i + 1)] = g[:, :deep]
        other_ref[size * i : size * (i + 1)] = g[:, deep:]
    blank = jnp.zeros((CLS_TOTAL - 3 * size, deep), F32)
    own_ref[3 * size :] = blank
    other_ref[3 * size :] = blank


def split(total, me, keep_ref, send_refs):
    rows = keep_ref.shape[0]
    keep_ref[...] = total[pl.ds(pl.multiple_of(me * rows, 8), rows)]
    for k, ref in enumerate(send_refs):
        ref[0:rows] = total[pl.ds(pl.multiple_of((me ^ (k + 1)) * rows, 8), rows)].astype(BF16)


def shared_kernel(slot, where_ref, f_ref, halo_ref, far_ref, own_ref, other_ref, small_ref, theirs_ref, *rest):
    keep_ref, sum_ref, *send_refs, x_ref, d_ref, g_ref = rest
    rows, cols, chans = f_ref.shape
    half = rows // 2
    c = where_ref[0]
    near = halo_ref[pl.ds(pl.multiple_of(2 * cols * (1 - c), 16), cols)]
    far = far_ref[pl.ds(pl.multiple_of(2 * cols * c, 16), cols)]
    x_ref[pl.ds((rows + 1) * c, 1)] = near.reshape(1, cols, chans)
    x_ref[pl.ds((rows + 1) * (1 - c), 1)] = far.reshape(1, cols, chans)
    x_ref[1 : rows + 1] = f_ref[...]

    def place(ref, start):
        def body(d, carry):
            mid = ref[d].astype(F32)
            d_ref[start + d] = jnp.concatenate(
                [shift_cells(mid, -1).astype(BF16), ref[d], shift_cells(mid, 1).astype(BF16)], axis=1
            )
            return carry

        lax.fori_loop(0, half, body, 0)

    place(own_ref, half * c)
    place(other_ref, half * (1 - c))
    rhs = d_ref[...].reshape(rows * cols, d_ref.shape[2])
    outs = rhs.shape[1] // 3
    for i in range(3):
        lhs = x_ref[i : i + rows].reshape(rows * cols, chans)
        g = dot(lhs, rhs, ((0,), (0,)))
        for j in range(3):
            start = (3 * i + j) * chans
            g_ref[start : start + chans] = g[:, j * outs : (j + 1) * outs]
    split(g_ref, where_ref[slot], keep_ref, send_refs)
    mine, theirs = small_ref[...], theirs_ref[...]
    sums = jnp.concatenate([mine[0:3] + theirs[0:3], mine[3:4] + theirs[4:5], mine[4:8]], axis=0)
    sum_ref[...] = sums
    for ref in send_refs:
        put_trio(ref, keep_ref.shape[0], sums)


def pair_sum(parts):
    while len(parts) > 1:
        parts = [parts[k] + parts[k + 1] for k in range(0, len(parts), 2)]
    return parts[0]


def step_kernel(slot, n_in, trio, where_ref, *refs):
    base_ref, refs = refs[0], refs[1:]
    if trio:
        small_ref, refs = refs[0], refs[1:]
    in_refs, refs = refs[:n_in], refs[n_in:]
    rows = base_ref.shape[0]
    total = base_ref[...]
    for ref in in_refs:
        total = total + ref[0:rows].astype(F32)
    if trio:
        sums = pair_sum([small_ref[...]] + [get_trio(ref, rows) for ref in in_refs])
    if slot is None:
        refs[0][...] = total.astype(BF16)
        if trio:
            refs[1][...] = sums
        return
    keep_ref, refs = refs[0], refs[1:]
    if trio:
        sum_ref, refs = refs[0], refs[1:]
        sum_ref[...] = sums
    *send_refs, total_ref = refs
    total_ref[...] = total
    split(total_ref, where_ref[slot], keep_ref, send_refs)
    if trio:
        for ref in send_refs:
            put_trio(ref, keep_ref.shape[0], sums)


def step(where, slot, size, base, small, arrived, name):
    trio = TRIO if small is not None else 0
    rows, width = base.shape
    inputs = [where, base] + ([small] if trio else []) + list(arrived)
    smalls = [((8, LANES), F32)] if trio else []
    kernel = functools.partial(step_kernel, slot, len(arrived), trio)
    if slot is None:
        return call(kernel, name, [((rows, width), BF16)] + smalls, inputs)
    share = rows // size
    outs = [((share, width), F32)] + smalls + [((share + trio, width), BF16)] * (size - 1)
    return call(kernel, name, outs, inputs, [((rows, width), F32)])


def join_kernel(slot, where_ref, *refs):
    *in_refs, out_ref = refs
    rows = in_refs[0].shape[0]
    me = where_ref[slot]
    for k, ref in enumerate(in_refs):
        out_ref[pl.ds(pl.multiple_of((me ^ k) * rows, 8), rows)] = ref[...].astype(out_ref.dtype)


def join(where, slot, parts, kind, name):
    rows, width = parts[0].shape
    return call(
        functools.partial(join_kernel, slot), name, [((rows * len(parts), width), kind)], [where] + parts
    )[0]


def join_cls_kernel(slot, where_ref, *refs):
    *in_refs, out_ref, whole_ref = refs
    join_kernel(slot, where_ref, *in_refs, whole_ref)
    for tap in range(9):
        turned = jnp.transpose(whole_ref[CLS_ROWS * tap : CLS_ROWS * tap + LANES])
        out_ref[tap // 3, tap % 3] = turned[:, :LOGITS]


def swap(x, axis, bit=1):
    size = lax.axis_size(axis)
    return lax.ppermute(x, axis, [(i, i ^ bit) for i in range(size)])


def others(x, axis):
    return [swap(x, axis, bit) for bit in range(1, lax.axis_size(axis))]


def exchange(sends, axis):
    return [swap(x, axis, k + 1) for k, x in enumerate(sends)]


def shards(features, labels, w_shared, b_shared, w_cls, b_cls):
    _, rows, cols, chans = features.shape
    half = rows // 2
    outs = w_shared.shape[3]
    tiles = lax.axis_size("tile")
    pages = lax.axis_size("batch")
    c = lax.axis_index("chan")
    t = lax.axis_index("tile")
    f = features[0]
    where = jnp.stack([c, t * rows + half * c, jnp.int32(tiles * rows), t, lax.axis_index("batch")]).astype(jnp.int32)
    TILE, BATCH = 3, 4

    msg, labt, pack, count = call(
        prep_kernel, "prep",
        [
            ((3 * cols + ANCH_ROWS, chans), BF16),
            ((rows, ANCH_ROWS, cols), BF16),
            ((9 * outs + TRIO, LANES), BF16),
            ((8, LANES), F32),
        ],
        [where, f, labels[0], w_cls, b_shared.reshape(1, outs)],
    )
    pairs = []
    for i in range(tiles - 1):
        pairs += [(2 * i + 1, 2 * i + 2), (2 * i + 2, 2 * i + 1)]
    halo = lax.ppermute(msg, ("tile", "chan"), pairs)
    w1b = swap(w_shared, "chan")
    packb = swap(pack, "chan")
    count = pair_sum([count] + others(count, "batch"))
    counts = [count] + others(count, "tile")

    hid, dt, own, other, small = call(
        head_kernel, "head",
        [
            ((half + 4, cols, chans), BF16),
            ((half, 3 * CLS_ROWS, cols), BF16),
            ((half, cols, outs), BF16),
            ((half, cols, outs), BF16),
            ((8, LANES), F32),
        ],
        [where, f, halo, labt, w_shared, w1b, pack, packb, b_cls.reshape(1, LOGITS)] + counts,
        [((half + 6, cols, chans), BF16), ((half + 2, cols, LANES), BF16)],
    )
    theirs = swap(other, "chan")
    far = swap(halo, "chan")
    small_theirs = swap(small, "chan")
    gcls, gcls_other = call(
        cls_kernel, "cls", [((CLS_TOTAL, outs), F32)] * 2, [where, hid, dt]
    )
    gcls_theirs = swap(gcls_other, "chan")

    share = 9 * chans // pages
    keep, small, *sends = call(
        functools.partial(shared_kernel, BATCH), "shared",
        [((share, outs), F32), ((8, LANES), F32)] + [((share + TRIO, outs), BF16)] * (pages - 1),
        [where, f, halo, far, own, theirs, small, small_theirs],
        [((rows + 2, cols, chans), BF16), ((rows, cols, 3 * outs), BF16), ((9 * chans, outs), F32)],
    )
    ckeep, *csends = step(where, TILE, tiles, gcls, None, [gcls_theirs], "cls_tile")

    arrived = exchange(sends, "batch")
    carrived = exchange(csends, "tile")
    keep, small, *sends = step(where, TILE, tiles, keep, small, arrived, "shared_tile")
    ckeep, *csends = step(where, BATCH, pages, ckeep, None, carrived, "cls_batch")
    arrived = exchange(sends, "tile")
    carrived = exchange(csends, "batch")
    done, small = step(where, None, 1, keep, small, arrived, "shared_round")
    (cdone,) = step(where, None, 1, ckeep, None, carrived, "cls_round")
    block = join(where, TILE, [done] + others(done, "tile"), BF16, "shared_join")
    cblock = join(where, BATCH, [cdone] + others(cdone, "batch"), BF16, "cls_join")
    grad_shared = join(where, BATCH, [block] + others(block, "batch"), F32, "shared_out")
    (grad_cls,) = call(
        functools.partial(join_cls_kernel, TILE), "cls_out",
        [((3, 3, outs, LOGITS), F32)],
        [where, cblock] + others(cblock, "tile"),
        [((CLS_TOTAL, outs), F32)],
    )
    return (
        grad_shared.reshape(3, 3, chans, outs),
        small[3],
        grad_cls,
        small[0, :LOGITS],
        small[1, :1],
    )


def solution(mesh):
    placed = (
        P(("groups", "batch"), "tile", None, None),
        P(("groups", "batch"), "tile", None),
        P(None, None, None, "chan"),
        P("chan"),
        P(None, None, "chan", None),
        P(),
    )
    return jax.shard_map(
        shards,
        mesh=mesh,
        in_specs=placed,
        out_specs=(
            P("groups", None, None, "chan"),
            P(("groups", "chan")),
            P("groups", None, "chan", None),
            P("groups"),
            P("groups"),
        ),
        check_vma=False,
    )
```

```python
import functools

import jax
import jax.numpy as jnp
from jax import lax
from jax.experimental import pallas as pl
from jax.experimental.pallas import tpu as pltpu
from jax.sharding import PartitionSpec as P

ANCH = 9
CLASSES = 11
LOGITS = 99
LANES = 128
ANCH_ROWS = 16
CLS_ROWS = 112
CLS_TOTAL = 1024
TRIO = 32
BF16 = jnp.bfloat16
F32 = jnp.float32
VMEM = pl.BlockSpec(memory_space=pltpu.VMEM)
ANY = pl.BlockSpec(memory_space=pl.ANY)
SMEM = pl.BlockSpec(memory_space=pltpu.SMEM)


def call(kernel, name, outs, inputs, scratch=(), after=()):
    n = len(inputs)
    inputs = list(inputs) + list(after)

    def body(*refs):
        kernel(*refs[:n], *refs[len(inputs) :])

    return pl.pallas_call(
        body,
        in_specs=[SMEM] + [VMEM] * (n - 1) + [ANY] * len(after),
        out_specs=[VMEM] * len(outs),
        out_shape=[jax.ShapeDtypeStruct(shape, kind) for shape, kind in outs],
        scratch_shapes=[pltpu.VMEM(shape, kind) for shape, kind in scratch],
        compiler_params=pltpu.CompilerParams(vmem_limit_bytes=48 * 1024 * 1024),
        name=name,
    )(*inputs)


def shift_cells(field, by):
    cells = field.shape[0]
    rolled = pltpu.roll(field, by % cells, axis=0)
    cell = lax.broadcasted_iota(jnp.int32, field.shape, 0)
    edge = 0 if by > 0 else cells - 1
    return jnp.where(cell == edge, 0.0, rolled)


def dot(left, right, dims=((1,), (0,))):
    return lax.dot_general(left, right, (dims, ((), ())), preferred_element_type=F32)


def three(x):
    high = x.astype(BF16)
    rest = x - high.astype(F32)
    middle = rest.astype(BF16)
    low = (rest - middle.astype(F32)).astype(BF16)
    return high, middle, low


def put_trio(ref, start, x):
    high, middle, low = three(x)
    ref[start : start + TRIO] = jnp.concatenate([high, middle, low, jnp.zeros_like(low)], axis=0)


def get_trio(ref, start):
    part = ref[start : start + TRIO].astype(F32)
    return part[0:8] + part[8:16] + part[16:24]


def count_kernel(lab_ref, count_ref):
    lab = lab_ref[...]
    count_ref[...] = jnp.full(count_ref.shape, jnp.sum(jnp.where(lab > 0, 1.0, 0.0)), F32)


def prep_kernel(where_ref, f_ref, lab_ref, w2_ref, b1_ref, msg_ref, labt_ref, pack_ref):
    rows = lab_ref.shape[0]
    cols = f_ref.shape[1]
    c = where_ref[0]
    for k in range(3):
        msg_ref[cols * k : cols * (k + 1)] = f_ref[k]
    size = lab_ref.shape[2]
    place = lax.broadcasted_iota(jnp.int32, (ANCH_ROWS, size), 1) % ANCH
    anchor = lax.broadcasted_iota(jnp.int32, (ANCH_ROWS, size), 0)
    mine = jnp.where(place == anchor, 1.0, 0.0)
    left = jnp.concatenate([mine * lab_ref[r].astype(F32) for r in range(rows)], axis=0).astype(BF16)
    offset = lax.broadcasted_iota(jnp.int32, (size, cols), 0) - ANCH * lax.broadcasted_iota(jnp.int32, (size, cols), 1)
    pick = jnp.where(jnp.logical_and(offset >= 0, offset < ANCH), 1.0, 0.0).astype(BF16)
    turned = dot(left, pick).astype(BF16)
    for r in range(rows):
        labt_ref[r] = turned[ANCH_ROWS * r : ANCH_ROWS * (r + 1)]
    msg_ref[3 * cols : 3 * cols + ANCH_ROWS] = jnp.where(
        c == 0, turned[:ANCH_ROWS].astype(F32), turned[ANCH_ROWS * (rows - 1) :].astype(F32)
    ).astype(BF16)
    deep = w2_ref.shape[3]
    for tap in range(9):
        pack_ref[LANES * tap : LANES * (tap + 1)] = jnp.zeros((LANES, deep), BF16)
        pack_ref[LANES * tap : LANES * tap + LOGITS] = w2_ref[tap // 3, tap % 3]
    put_trio(pack_ref, 9 * LANES, jnp.broadcast_to(b1_ref[...], (8, deep)))


def head_kernel(
    where_ref, f_ref, halo_ref, labt_ref, w1a_ref, w1b_ref, packa_ref, packb_ref, b2_ref,
    hid_ref, dz_ref, loss_ref, xw_ref,
):

    half = f_ref.shape[0] // 2
    cols = f_ref.shape[1]
    c = where_ref[0]
    first = where_ref[1]
    total = where_ref[2]
    near = half + 3
    xw_ref[pl.ds(3 - 3 * c, near)] = f_ref[pl.ds((half - 3) * c, near)]
    for k in range(3):
        xw_ref[near * c + k] = halo_ref[cols * k : cols * (k + 1)]
    w1 = [
        jnp.concatenate(
            [jnp.concatenate([w1a_ref[i, j], w1b_ref[i, j]], axis=1) for j in range(3)], axis=1
        )
        for i in range(3)
    ]
    w1 = jnp.concatenate(w1, axis=0)
    chans = w1.shape[1] // 3
    deep = chans // 2
    b1 = jnp.concatenate([get_trio(packa_ref, 9 * LANES)[:1], get_trio(packb_ref, 9 * LANES)[:1]], axis=1)

    def conv1(h, carry):
        lhs = jnp.concatenate([xw_ref[h], xw_ref[h + 1], xw_ref[h + 2]], axis=1)
        y = dot(lhs, w1)
        pre = shift_cells(y[:, :chans], 1) + y[:, chans : 2 * chans] + shift_cells(y[:, 2 * chans :], -1) + b1
        row = first + h - 2
        inside = jnp.logical_and(row >= 0, row < total)
        hid_ref[h] = jnp.where(inside, jnp.maximum(pre, 0.0), 0.0).astype(BF16)
        return carry

    lax.fori_loop(0, half + 4, conv1, 0)

    lane = lax.broadcasted_iota(jnp.int32, (1, LANES), 1)
    kind = (lane % CLASSES + 1).astype(F32)
    real = lane < LOGITS
    anchor = lax.broadcasted_iota(jnp.int32, (ANCH_ROWS, LANES), 0)
    column = lax.broadcasted_iota(jnp.int32, (ANCH_ROWS, LANES), 1)
    spread = jnp.where(jnp.logical_and(column // CLASSES == anchor, column < LOGITS), 1.0, 0.0).astype(BF16)
    w2 = [
        jnp.concatenate([jnp.concatenate([tap(packa_ref, i, j), tap(packb_ref, i, j)], axis=1) for j in range(3)], axis=0)
        for i in range(3)
    ]
    w2 = jnp.concatenate(w2, axis=1)
    b2 = jnp.concatenate([b2_ref[...], jnp.zeros((1, LANES - LOGITS), F32)], axis=1)

    def focal(l, loss):
        lhs = jnp.concatenate([hid_ref[l], hid_ref[l + 1], hid_ref[l + 2]], axis=1)
        y = dot(lhs, w2, ((1,), (1,)))
        z = shift_cells(y[:, :LANES], 1) + y[:, LANES : 2 * LANES] + shift_cells(y[:, 2 * LANES :], -1) + b2
        at_halo = jnp.where(c == 0, l == 0, l == half + 1)
        local = jnp.clip(l - 1 + half * c, 0, 2 * half - 1)
        mine = labt_ref[local].astype(F32)
        far = halo_ref[3 * cols : 3 * cols + ANCH_ROWS].astype(F32)
        lab = dot(jnp.where(at_halo, far, mine).astype(BF16), spread, ((0,), (0,)))
        row = first + l - 1
        inside = jnp.logical_and(row >= 0, row < total)
        hit = lab == kind
        keep = jnp.logical_and(jnp.logical_and(lab >= 0.0, real), inside)
        u = jnp.where(hit, -z, z)
        e = jnp.exp(-jnp.abs(u))
        r = 1.0 / (1.0 + e)
        er = e * r
        up = u >= 0.0
        s = jnp.where(up, r, er)
        comp = jnp.where(up, er, r)
        soft = jnp.maximum(u, 0.0) + jnp.log1p(e)
        ws = jnp.where(keep, jnp.where(hit, 0.25, 0.75), 0.0) * s * s
        slope = ws * (2.0 * comp * soft + s)
        dz_ref[l] = jnp.where(hit, -slope, slope)
        own = jnp.logical_and(l >= 1, l <= half)
        return loss + jnp.where(own, 1.0, 0.0) * jnp.sum(ws * soft, axis=0, keepdims=True)

    loss_ref[...] = lax.fori_loop(0, half + 2, focal, jnp.zeros((1, LANES), F32))


def tap(ref, i, j):
    return ref[LANES * (3 * i + j) : LANES * (3 * i + j + 1)]


def back_kernel(where_ref, hid_ref, dz_ref, loss_ref, packa_ref, packb_ref, *rest):
    *count_refs, dt_ref, own_ref, other_ref, small_ref, dlog_ref = rest
    half, _, cols = dt_ref.shape
    chans = hid_ref.shape[2]
    inverse = 1.0 / pair_sum([ref[...] for ref in count_refs])[:1]

    def scaled(l):
        dz = dz_ref[l] * inverse
        d16 = dz.astype(BF16)
        dlog_ref[l] = d16
        return dz, d16

    scaled(0)
    scaled(half + 1)

    def turn(d, gcb):
        dz, d16 = scaled(d + 1)
        turned = jnp.transpose(d16.astype(F32))[:CLS_ROWS]
        cell = lax.broadcasted_iota(jnp.int32, turned.shape, 1)
        left = jnp.where(cell == cols - 1, 0.0, pltpu.roll(turned, cols - 1, axis=1))
        right = jnp.where(cell == 0, 0.0, pltpu.roll(turned, 1, axis=1))
        dt_ref[d] = jnp.concatenate([left, turned, right], axis=0).astype(BF16)
        return gcb + jnp.sum(dz, axis=0, keepdims=True)

    gcb = lax.fori_loop(0, half, turn, jnp.zeros((1, LANES), F32))
    w2t = [
        jnp.concatenate([x for j in range(3) for x in (tap(packa_ref, i, j), tap(packb_ref, i, j))], axis=1)
        for i in range(3)
    ]
    w2t = jnp.concatenate(w2t, axis=0)

    def dpre_row(d, gsb):
        lhs = jnp.concatenate([dlog_ref[d + 2], dlog_ref[d + 1], dlog_ref[d]], axis=1)
        q = dot(lhs, w2t)
        dhid = shift_cells(q[:, :chans], -1) + q[:, chans : 2 * chans] + shift_cells(q[:, 2 * chans :], 1)
        dpre = jnp.where(hid_ref[d + 2].astype(F32) > 0.0, dhid, 0.0)
        d16 = dpre.astype(BF16)
        own_ref[d] = d16[:, : chans // 2]
        other_ref[d] = d16[:, chans // 2 :]
        return gsb + jnp.sum(dpre, axis=0, keepdims=True)

    gsb = lax.fori_loop(0, half, dpre_row, jnp.zeros((1, chans), F32))
    small_ref[0:1] = gcb
    small_ref[1:2] = jnp.broadcast_to(jnp.sum(loss_ref[...], axis=1, keepdims=True), (1, LANES)) * inverse
    small_ref[2:3] = jnp.zeros((1, LANES), F32)
    small_ref[3:4] = gsb[:, : chans // 2]
    small_ref[4:5] = gsb[:, chans // 2 :]
    small_ref[5:8] = jnp.zeros((3, LANES), F32)


def cls_kernel(where_ref, hid_ref, dt_ref, own_ref, other_ref):
    half, _, cols = dt_ref.shape
    chans = hid_ref.shape[2]
    deep = chans // 2
    dt = jnp.concatenate([dt_ref[d] for d in range(half)], axis=1)
    size = 3 * CLS_ROWS
    for i in range(3):
        g = dot(dt, hid_ref[i + 1 : i + 1 + half].reshape(half * cols, chans))
        own_ref[size * i : size * (i + 1)] = g[:, :deep]
        other_ref[size * i : size * (i + 1)] = g[:, deep:]
    blank = jnp.zeros((CLS_TOTAL - 3 * size, deep), F32)
    own_ref[3 * size :] = blank
    other_ref[3 * size :] = blank


def split(total, me, keep_ref, send_refs):
    rows = keep_ref.shape[0]
    keep_ref[...] = total[pl.ds(pl.multiple_of(me * rows, 8), rows)]
    for k, ref in enumerate(send_refs):
        ref[0:rows] = total[pl.ds(pl.multiple_of((me ^ (k + 1)) * rows, 8), rows)].astype(BF16)


def shared_kernel(slot, where_ref, f_ref, halo_ref, far_ref, own_ref, other_ref, small_ref, theirs_ref, *rest):
    keep_ref, sum_ref, *send_refs, x_ref, d_ref, g_ref = rest
    rows, cols, chans = f_ref.shape
    half = rows // 2
    c = where_ref[0]
    near = halo_ref[pl.ds(pl.multiple_of(2 * cols * (1 - c), 16), cols)]
    far = far_ref[pl.ds(pl.multiple_of(2 * cols * c, 16), cols)]
    x_ref[pl.ds((rows + 1) * c, 1)] = near.reshape(1, cols, chans)
    x_ref[pl.ds((rows + 1) * (1 - c), 1)] = far.reshape(1, cols, chans)
    x_ref[1 : rows + 1] = f_ref[...]

    def place(ref, start):
        def body(d, carry):
            mid = ref[d].astype(F32)
            d_ref[start + d] = jnp.concatenate(
                [shift_cells(mid, -1).astype(BF16), ref[d], shift_cells(mid, 1).astype(BF16)], axis=1
            )
            return carry

        lax.fori_loop(0, half, body, 0)

    place(own_ref, half * c)
    place(other_ref, half * (1 - c))
    rhs = d_ref[...].reshape(rows * cols, d_ref.shape[2])
    outs = rhs.shape[1] // 3
    for i in range(3):
        lhs = x_ref[i : i + rows].reshape(rows * cols, chans)
        g = dot(lhs, rhs, ((0,), (0,)))
        for j in range(3):
            start = (3 * i + j) * chans
            g_ref[start : start + chans] = g[:, j * outs : (j + 1) * outs]
    split(g_ref, where_ref[slot], keep_ref, send_refs)
    mine, theirs = small_ref[...], theirs_ref[...]
    sums = jnp.concatenate([mine[0:3] + theirs[0:3], mine[3:4] + theirs[4:5], mine[4:8]], axis=0)
    sum_ref[...] = sums
    for ref in send_refs:
        put_trio(ref, keep_ref.shape[0], sums)


def pair_sum(parts):
    while len(parts) > 1:
        parts = [parts[k] + parts[k + 1] for k in range(0, len(parts), 2)]
    return parts[0]


def step_kernel(slot, n_in, trio, where_ref, *refs):
    base_ref, refs = refs[0], refs[1:]
    if trio:
        small_ref, refs = refs[0], refs[1:]
    in_refs, refs = refs[:n_in], refs[n_in:]
    rows = base_ref.shape[0]
    total = base_ref[...]
    for ref in in_refs:
        total = total + ref[0:rows].astype(F32)
    if trio:
        sums = pair_sum([small_ref[...]] + [get_trio(ref, rows) for ref in in_refs])
    if slot is None:
        refs[0][...] = total.astype(BF16)
        if trio:
            refs[1][...] = sums
        return
    keep_ref, refs = refs[0], refs[1:]
    if trio:
        sum_ref, refs = refs[0], refs[1:]
        sum_ref[...] = sums
    *send_refs, total_ref = refs
    total_ref[...] = total
    split(total_ref, where_ref[slot], keep_ref, send_refs)
    if trio:
        for ref in send_refs:
            put_trio(ref, keep_ref.shape[0], sums)


def step(where, slot, size, base, small, arrived, name, after=()):
    trio = TRIO if small is not None else 0
    rows, width = base.shape
    inputs = [where, base] + ([small] if trio else []) + list(arrived)
    smalls = [((8, LANES), F32)] if trio else []
    kernel = functools.partial(step_kernel, slot, len(arrived), trio)
    if slot is None:
        return call(kernel, name, [((rows, width), BF16)] + smalls, inputs, after=after)
    share = rows // size
    outs = [((share, width), F32)] + smalls + [((share + trio, width), BF16)] * (size - 1)
    return call(kernel, name, outs, inputs, [((rows, width), F32)], after)


def join_kernel(slot, where_ref, *refs):
    *in_refs, out_ref = refs
    rows = in_refs[0].shape[0]
    me = where_ref[slot]
    for k, ref in enumerate(in_refs):
        out_ref[pl.ds(pl.multiple_of((me ^ k) * rows, 8), rows)] = ref[...].astype(out_ref.dtype)


def join(where, slot, parts, kind, name, after=()):
    rows, width = parts[0].shape
    return call(
        functools.partial(join_kernel, slot), name, [((rows * len(parts), width), kind)], [where] + parts, after=after
    )[0]


def join_cls_kernel(slot, where_ref, *refs):
    *in_refs, out_ref, whole_ref = refs
    join_kernel(slot, where_ref, *in_refs, whole_ref)
    for tap in range(9):
        out_ref[tap // 3, tap % 3] = whole_ref[CLS_ROWS * tap : CLS_ROWS * tap + LOGITS]


def swap(x, axis, bit=1):
    size = lax.axis_size(axis)
    return lax.ppermute(x, axis, [(i, i ^ bit) for i in range(size)])


def others(x, axis):
    return [swap(x, axis, bit) for bit in range(1, lax.axis_size(axis))]


def exchange(sends, axis):
    return [swap(x, axis, k + 1) for k, x in enumerate(sends)]


def shards(features, labels, w_shared, b_shared, w_cls, b_cls):
    _, rows, cols, chans = features.shape
    half = rows // 2
    outs = w_shared.shape[3]
    tiles = lax.axis_size("tile")
    pages = lax.axis_size("batch")
    c = lax.axis_index("chan")
    t = lax.axis_index("tile")
    f = features[0]
    where = jnp.stack([c, t * rows + half * c, jnp.int32(tiles * rows), t, lax.axis_index("batch")]).astype(jnp.int32)
    TILE, BATCH = 3, 4

    lab = labels.reshape(rows, 1, labels.shape[2])
    count = pl.pallas_call(
        count_kernel, in_specs=[VMEM], out_specs=VMEM, out_shape=jax.ShapeDtypeStruct((8, LANES), F32), name="count"
    )(lab)
    whole = lambda *shape: pl.BlockSpec(shape, lambda g, w: (0,) * len(shape))
    w2 = jnp.swapaxes(w_cls, 2, 3)
    msg, labt, pack = pl.pallas_call(
        prep_kernel,
        grid_spec=pltpu.PrefetchScalarGridSpec(
            num_scalar_prefetch=1,
            grid=(1,),
            in_specs=[
                pl.BlockSpec((3, cols, chans), lambda g, w: ((rows // 3 - 1) * w[0], 0, 0)),
                whole(*lab.shape),
                whole(*w2.shape),
                whole(1, outs),
            ],
            out_specs=[
                whole(3 * cols + ANCH_ROWS, chans),
                whole(rows, ANCH_ROWS, cols),
                whole(9 * LANES + TRIO, outs),
            ],
        ),
        out_shape=[
            jax.ShapeDtypeStruct((3 * cols + ANCH_ROWS, chans), BF16),
            jax.ShapeDtypeStruct((rows, ANCH_ROWS, cols), BF16),
            jax.ShapeDtypeStruct((9 * LANES + TRIO, outs), BF16),
        ],
        name="prep",
    )(where, f, lab, w2, b_shared.reshape(1, outs))
    pairs = []
    for i in range(tiles - 1):
        pairs += [(2 * i + 1, 2 * i + 2), (2 * i + 2, 2 * i + 1)]
    halo = lax.ppermute(msg, ("tile", "chan"), pairs)
    w1b = swap(w_shared, "chan")
    packb = swap(pack, "chan")
    count = pair_sum([count] + others(count, "batch"))
    counts = [count] + others(count, "tile")

    hid, dz, loss = call(
        head_kernel, "head",
        [((half + 4, cols, chans), BF16), ((half + 2, cols, LANES), F32), ((1, LANES), F32)],
        [where, f, halo, labt, w_shared, w1b, pack, packb, b_cls.reshape(1, LOGITS)],
        [((half + 6, cols, chans), BF16)],
    )
    dt, own, other, small = call(
        back_kernel, "back",
        [
            ((half, 3 * CLS_ROWS, cols), BF16),
            ((half, cols, outs), BF16),
            ((half, cols, outs), BF16),
            ((8, LANES), F32),
        ],
        [where, hid, dz, loss, pack, packb] + counts,
        [((half + 2, cols, LANES), BF16)],
    )
    theirs = swap(other, "chan")
    far = swap(halo, "chan")
    small_theirs = swap(small, "chan")
    gcls, gcls_other = call(
        cls_kernel, "cls", [((CLS_TOTAL, outs), F32)] * 2, [where, hid, dt]
    )
    gcls_theirs = swap(gcls_other, "chan")

    share = 9 * chans // pages
    keep, small, *sends = call(
        functools.partial(shared_kernel, BATCH), "shared",
        [((share, outs), F32), ((8, LANES), F32)] + [((share + TRIO, outs), BF16)] * (pages - 1),
        [where, f, halo, far, own, theirs, small, small_theirs],
        [((rows + 2, cols, chans), BF16), ((rows, cols, 3 * outs), BF16), ((9 * chans, outs), F32)],
    )
    ckeep, *csends = step(where, TILE, tiles, gcls, None, [gcls_theirs], "cls_tile")

    arrived = exchange(sends, "batch")
    carrived = exchange(csends, "tile")
    keep, small, *sends = step(where, TILE, tiles, keep, small, arrived, "shared_tile")
    ckeep, *csends = step(where, BATCH, pages, ckeep, None, carrived, "cls_batch", [small])
    arrived = exchange(sends, "tile")
    carrived = exchange(csends, "batch")
    done, small = step(where, None, 1, keep, small, arrived, "shared_round")
    (cdone,) = step(where, None, 1, ckeep, None, carrived, "cls_round", [small])
    block = join(where, TILE, [done] + others(done, "tile"), BF16, "shared_join")
    cblock = join(where, BATCH, [cdone] + others(cdone, "batch"), BF16, "cls_join", [block])
    grad_shared = join(where, BATCH, [block] + others(block, "batch"), F32, "shared_out")
    (grad_cls,) = call(
        functools.partial(join_cls_kernel, TILE), "cls_out",
        [((3, 3, LOGITS, outs), F32)],
        [where, cblock] + others(cblock, "tile"),
        [((CLS_TOTAL, outs), F32)],
    )
    return (
        grad_shared.reshape(3, 3, chans, outs),
        small[3],
        jnp.swapaxes(grad_cls, 2, 3),
        small[0, :LOGITS],
        small[1, :1],
    )


def solution(mesh):
    placed = (
        P(("groups", "batch"), "tile", None, None),
        P(("groups", "batch"), "tile", None),
        P(None, None, None, "chan"),
        P("chan"),
        P(None, None, "chan", None),
        P(),
    )
    return jax.shard_map(
        shards,
        mesh=mesh,
        in_specs=placed,
        out_specs=(
            P("groups", None, None, "chan"),
            P(("groups", "chan")),
            P("groups", None, "chan", None),
            P("groups"),
            P("groups"),
        ),
        check_vma=False,
    )
```

```python
import functools

import jax
import jax.numpy as jnp
from jax import lax
from jax.experimental import pallas as pl
from jax.experimental.pallas import tpu as pltpu
from jax.sharding import PartitionSpec as P

ANCH = 9
CLASSES = 11
LOGITS = 99
LANES = 128
ANCH_ROWS = 16
CLS_ROWS = 112
CLS_TOTAL = 1024
TILE, BATCH = 3, 4
TRIO = 32
BF16 = jnp.bfloat16
F32 = jnp.float32
VMEM = pl.BlockSpec(memory_space=pltpu.VMEM)
HBM = pl.BlockSpec(memory_space=pltpu.HBM)
SMEM = pl.BlockSpec(memory_space=pltpu.SMEM)


def call(kernel, name, micros, outs, inputs, scratch=(), specs=None):
    return pl.pallas_call(
        kernel,
        in_specs=specs or [SMEM] + [VMEM] * (len(inputs) - 1),
        out_specs=[VMEM] * len(outs),
        out_shape=[jax.ShapeDtypeStruct(shape, kind) for shape, kind in outs],
        scratch_shapes=[pltpu.VMEM(*shape) if isinstance(shape, tuple) else shape for shape in scratch],
        cost_estimate=pl.CostEstimate(flops=int(micros * 1e9), bytes_accessed=int(micros * 1e6), transcendentals=0),
        compiler_params=pltpu.CompilerParams(vmem_limit_bytes=48 * 1024 * 1024),
        name=name,
    )(*inputs)


def shift_cells(field, by):
    cells = field.shape[0]
    rolled = pltpu.roll(field, by % cells, axis=0)
    cell = lax.broadcasted_iota(jnp.int32, field.shape, 0)
    edge = 0 if by > 0 else cells - 1
    return jnp.where(cell == edge, 0.0, rolled)


def dot(left, right, dims=((1,), (0,))):
    return lax.dot_general(left, right, (dims, ((), ())), preferred_element_type=F32)


def three(x):
    high = x.astype(BF16)
    rest = x - high.astype(F32)
    middle = rest.astype(BF16)
    low = (rest - middle.astype(F32)).astype(BF16)
    return high, middle, low


def put_trio(ref, start, x):
    high, middle, low = three(x)
    ref[start : start + TRIO] = jnp.concatenate([high, middle, low, jnp.zeros_like(low)], axis=0)


def get_trio(ref, start):
    part = ref[start : start + TRIO].astype(F32)
    return part[0:8] + part[8:16] + part[16:24]


def edge_kernel(where_ref, f_ref, lab_ref, msg_ref, labt_ref, count_ref, sem):
    rows, cols, _ = f_ref.shape
    c = where_ref[0]
    copies = [
        pltpu.make_async_copy(f_ref.at[(rows - 3) * c + k], msg_ref.at[pl.ds(cols * k, cols)], sem.at[k])
        for k in range(3)
    ]
    for copy in copies:
        copy.start()
    size = lab_ref.shape[2]
    place = lax.broadcasted_iota(jnp.int32, (ANCH_ROWS, size), 1) % ANCH
    anchor = lax.broadcasted_iota(jnp.int32, (ANCH_ROWS, size), 0)
    mine = place == anchor
    labs = [lab_ref[r].astype(F32) for r in range(rows)]
    named = [jnp.where(lab > 0.0, 1.0, 0.0) for lab in labs]
    count_ref[...] = jnp.full(count_ref.shape, jnp.sum(sum(named[1:], named[0])), F32)
    left = jnp.concatenate([jnp.where(mine, lab, 0.0) for lab in labs], axis=0).astype(BF16)
    offset = lax.broadcasted_iota(jnp.int32, (size, cols), 0) - ANCH * lax.broadcasted_iota(jnp.int32, (size, cols), 1)
    pick = jnp.where(jnp.logical_and(offset >= 0, offset < ANCH), 1.0, 0.0).astype(BF16)
    turned = dot(left, pick).astype(BF16)
    for r in range(rows):
        labt_ref[r] = turned[ANCH_ROWS * r : ANCH_ROWS * (r + 1)]
    msg_ref[3 * cols : 3 * cols + ANCH_ROWS] = jnp.where(
        c == 0, turned[:ANCH_ROWS].astype(F32), turned[ANCH_ROWS * (rows - 1) :].astype(F32)
    ).astype(BF16)
    for copy in copies:
        copy.wait()


def pack_kernel(where_ref, w2_ref, b1_ref, pack_ref):
    deep = w2_ref.shape[3]
    for tap in range(9):
        pack_ref[LANES * tap : LANES * (tap + 1)] = jnp.zeros((LANES, deep), BF16)
        pack_ref[LANES * tap : LANES * tap + LOGITS] = w2_ref[tap // 3, tap % 3]
    put_trio(pack_ref, 9 * LANES, jnp.broadcast_to(b1_ref[...], (8, deep)))


def head_kernel(
    where_ref, f_ref, halo_ref, labt_ref, w1a_ref, w1b_ref, packa_ref, packb_ref, b2_ref,
    hid_ref, dz_ref, loss_ref, xw_ref,
):

    half = f_ref.shape[0] // 2
    cols = f_ref.shape[1]
    c = where_ref[0]
    first = where_ref[1]
    total = where_ref[2]
    near = half + 3
    xw_ref[pl.ds(3 - 3 * c, near)] = f_ref[pl.ds((half - 3) * c, near)]
    for k in range(3):
        xw_ref[near * c + k] = halo_ref[cols * k : cols * (k + 1)]
    w1 = [
        jnp.concatenate(
            [jnp.concatenate([w1a_ref[i, j], w1b_ref[i, j]], axis=1) for j in range(3)], axis=1
        )
        for i in range(3)
    ]
    w1 = jnp.concatenate(w1, axis=0)
    chans = w1.shape[1] // 3
    deep = chans // 2
    b1 = jnp.concatenate([get_trio(packa_ref, 9 * LANES)[:1], get_trio(packb_ref, 9 * LANES)[:1]], axis=1)

    def conv1(h, carry):
        lhs = jnp.concatenate([xw_ref[h], xw_ref[h + 1], xw_ref[h + 2]], axis=1)
        y = dot(lhs, w1)
        pre = shift_cells(y[:, :chans], 1) + y[:, chans : 2 * chans] + shift_cells(y[:, 2 * chans :], -1) + b1
        row = first + h - 2
        inside = jnp.logical_and(row >= 0, row < total)
        hid_ref[h] = jnp.where(inside, jnp.maximum(pre, 0.0), 0.0).astype(BF16)
        return carry

    lax.fori_loop(0, half + 4, conv1, 0)

    lane = lax.broadcasted_iota(jnp.int32, (1, LANES), 1)
    kind = (lane % CLASSES + 1).astype(F32)
    real = lane < LOGITS
    anchor = lax.broadcasted_iota(jnp.int32, (ANCH_ROWS, LANES), 0)
    column = lax.broadcasted_iota(jnp.int32, (ANCH_ROWS, LANES), 1)
    spread = jnp.where(jnp.logical_and(column // CLASSES == anchor, column < LOGITS), 1.0, 0.0).astype(BF16)
    w2 = [
        jnp.concatenate([jnp.concatenate([tap(packa_ref, i, j), tap(packb_ref, i, j)], axis=1) for j in range(3)], axis=0)
        for i in range(3)
    ]
    w2 = jnp.concatenate(w2, axis=1)
    b2 = jnp.concatenate([b2_ref[...], jnp.zeros((1, LANES - LOGITS), F32)], axis=1)

    def focal(l, loss):
        lhs = jnp.concatenate([hid_ref[l], hid_ref[l + 1], hid_ref[l + 2]], axis=1)
        y = dot(lhs, w2, ((1,), (1,)))
        z = shift_cells(y[:, :LANES], 1) + y[:, LANES : 2 * LANES] + shift_cells(y[:, 2 * LANES :], -1) + b2
        at_halo = jnp.where(c == 0, l == 0, l == half + 1)
        local = jnp.clip(l - 1 + half * c, 0, 2 * half - 1)
        mine = labt_ref[local].astype(F32)
        far = halo_ref[3 * cols : 3 * cols + ANCH_ROWS].astype(F32)
        lab = dot(jnp.where(at_halo, far, mine).astype(BF16), spread, ((0,), (0,)))
        row = first + l - 1
        inside = jnp.logical_and(row >= 0, row < total)
        hit = lab == kind
        keep = jnp.logical_and(jnp.logical_and(lab >= 0.0, real), inside)
        u = jnp.where(hit, -z, z)
        e = jnp.exp(-jnp.abs(u))
        r = 1.0 / (1.0 + e)
        er = e * r
        up = u >= 0.0
        s = jnp.where(up, r, er)
        comp = jnp.where(up, er, r)
        soft = jnp.maximum(u, 0.0) + jnp.log1p(e)
        ws = jnp.where(keep, jnp.where(hit, 0.25, 0.75), 0.0) * s * s
        slope = ws * (2.0 * comp * soft + s)
        dz_ref[l] = jnp.where(hit, -slope, slope)
        own = jnp.logical_and(l >= 1, l <= half)
        return loss + jnp.where(own, 1.0, 0.0) * jnp.sum(ws * soft, axis=0, keepdims=True)

    loss_ref[...] = lax.fori_loop(0, half + 2, focal, jnp.zeros((1, LANES), F32))


def tap(ref, i, j):
    return ref[LANES * (3 * i + j) : LANES * (3 * i + j + 1)]


def back_kernel(where_ref, hid_ref, dz_ref, loss_ref, packa_ref, packb_ref, *rest):
    *count_refs, dt_ref, own_ref, other_ref, small_ref, dlog_ref = rest
    half, _, cols = dt_ref.shape
    chans = hid_ref.shape[2]
    inverse = 1.0 / pair_sum([ref[...] for ref in count_refs])[:1]

    def scaled(l):
        dz = dz_ref[l] * inverse
        d16 = dz.astype(BF16)
        dlog_ref[l] = d16
        return dz, d16

    scaled(0)
    scaled(half + 1)

    def turn(d, gcb):
        dz, d16 = scaled(d + 1)
        turned = jnp.transpose(d16.astype(F32))[:CLS_ROWS]
        cell = lax.broadcasted_iota(jnp.int32, turned.shape, 1)
        left = jnp.where(cell == cols - 1, 0.0, pltpu.roll(turned, cols - 1, axis=1))
        right = jnp.where(cell == 0, 0.0, pltpu.roll(turned, 1, axis=1))
        dt_ref[d] = jnp.concatenate([left, turned, right], axis=0).astype(BF16)
        return gcb + jnp.sum(dz, axis=0, keepdims=True)

    gcb = lax.fori_loop(0, half, turn, jnp.zeros((1, LANES), F32))
    w2t = [
        jnp.concatenate([x for j in range(3) for x in (tap(packa_ref, i, j), tap(packb_ref, i, j))], axis=1)
        for i in range(3)
    ]
    w2t = jnp.concatenate(w2t, axis=0)

    def dpre_row(d, gsb):
        lhs = jnp.concatenate([dlog_ref[d + 2], dlog_ref[d + 1], dlog_ref[d]], axis=1)
        q = dot(lhs, w2t)
        dhid = shift_cells(q[:, :chans], -1) + q[:, chans : 2 * chans] + shift_cells(q[:, 2 * chans :], 1)
        dpre = jnp.where(hid_ref[d + 2].astype(F32) > 0.0, dhid, 0.0)
        d16 = dpre.astype(BF16)
        own_ref[d] = d16[:, : chans // 2]
        other_ref[d] = d16[:, chans // 2 :]
        return gsb + jnp.sum(dpre, axis=0, keepdims=True)

    gsb = lax.fori_loop(0, half, dpre_row, jnp.zeros((1, chans), F32))
    small_ref[0:1] = gcb
    small_ref[1:2] = jnp.broadcast_to(jnp.sum(loss_ref[...], axis=1, keepdims=True), (1, LANES)) * inverse
    small_ref[2:3] = jnp.zeros((1, LANES), F32)
    small_ref[3:4] = gsb[:, : chans // 2]
    small_ref[4:5] = gsb[:, chans // 2 :]
    small_ref[5:8] = jnp.zeros((3, LANES), F32)


def cls_kernel(where_ref, hid_ref, dt_ref, own_ref, other_ref):
    half, _, cols = dt_ref.shape
    chans = hid_ref.shape[2]
    deep = chans // 2
    dt = jnp.concatenate([dt_ref[d] for d in range(half)], axis=1)
    size = 3 * CLS_ROWS
    for i in range(3):
        g = dot(dt, hid_ref[i + 1 : i + 1 + half].reshape(half * cols, chans))
        own_ref[size * i : size * (i + 1)] = g[:, :deep]
        other_ref[size * i : size * (i + 1)] = g[:, deep:]
    blank = jnp.zeros((CLS_TOTAL - 3 * size, deep), F32)
    own_ref[3 * size :] = blank
    other_ref[3 * size :] = blank


def split(total, me, keep_ref, send_refs):
    rows = keep_ref.shape[0]
    keep_ref[...] = total[pl.ds(pl.multiple_of(me * rows, 8), rows)]
    for k, ref in enumerate(send_refs):
        ref[0:rows] = total[pl.ds(pl.multiple_of((me ^ (k + 1)) * rows, 8), rows)].astype(BF16)


def shared_kernel(
    n_send, where_ref, f_ref, halo_ref, far_ref, own_ref, other_ref, small_ref, theirs_ref, cls_ref, cls_theirs_ref, *rest
):
    keep_ref, sum_ref, *send_refs, x_ref, d_ref, g_ref, cls_total_ref = rest
    send_refs, cls_keep_ref, cls_send_refs = send_refs[:n_send], send_refs[n_send], send_refs[n_send + 1 :]
    rows, cols, chans = f_ref.shape
    half = rows // 2
    c = where_ref[0]
    near = halo_ref[pl.ds(pl.multiple_of(2 * cols * (1 - c), 16), cols)]
    far = far_ref[pl.ds(pl.multiple_of(2 * cols * c, 16), cols)]
    x_ref[pl.ds((rows + 1) * c, 1)] = near.reshape(1, cols, chans)
    x_ref[pl.ds((rows + 1) * (1 - c), 1)] = far.reshape(1, cols, chans)
    x_ref[1 : rows + 1] = f_ref[...]

    def place(ref, start):
        def body(d, carry):
            mid = ref[d].astype(F32)
            d_ref[start + d] = jnp.concatenate(
                [shift_cells(mid, -1).astype(BF16), ref[d], shift_cells(mid, 1).astype(BF16)], axis=1
            )
            return carry

        lax.fori_loop(0, half, body, 0)

    place(own_ref, half * c)
    place(other_ref, half * (1 - c))
    rhs = d_ref[...].reshape(rows * cols, d_ref.shape[2])
    outs = rhs.shape[1] // 3
    for i in range(3):
        lhs = x_ref[i : i + rows].reshape(rows * cols, chans)
        g = dot(lhs, rhs, ((0,), (0,)))
        for j in range(3):
            start = (3 * i + j) * chans
            g_ref[start : start + chans] = g[:, j * outs : (j + 1) * outs]
    split(g_ref, where_ref[BATCH], keep_ref, send_refs)
    cls_total_ref[...] = cls_ref[...] + cls_theirs_ref[...]
    split(cls_total_ref, where_ref[TILE], cls_keep_ref, cls_send_refs)
    mine, theirs = small_ref[...], theirs_ref[...]
    sums = jnp.concatenate([mine[0:3] + theirs[0:3], mine[3:4] + theirs[4:5], mine[4:8]], axis=0)
    sum_ref[...] = sums
    for ref in send_refs:
        put_trio(ref, keep_ref.shape[0], sums)


def pair_sum(parts):
    while len(parts) > 1:
        parts = [parts[k] + parts[k + 1] for k in range(0, len(parts), 2)]
    return parts[0]


def sum_kernel(n_in, n_cls, n_send, where_ref, base_ref, small_ref, cls_ref, *refs):
    in_refs, refs = refs[:n_in], refs[n_in:]
    cls_in_refs, refs = refs[:n_cls], refs[n_cls:]
    keep_ref, sum_ref, *refs, total_ref, cls_total_ref = refs
    send_refs, cls_keep_ref, cls_send_refs = refs[:n_send], refs[n_send], refs[n_send + 1 :]
    rows = base_ref.shape[0]
    total = base_ref[...]
    for ref in in_refs:
        total = total + ref[0:rows].astype(F32)
    total_ref[...] = total
    split(total_ref, where_ref[TILE], keep_ref, send_refs)
    sums = pair_sum([small_ref[...]] + [get_trio(ref, rows) for ref in in_refs])
    sum_ref[...] = sums
    for ref in send_refs:
        put_trio(ref, keep_ref.shape[0], sums)
    total = cls_ref[...]
    for ref in cls_in_refs:
        total = total + ref[...].astype(F32)
    cls_total_ref[...] = total
    split(cls_total_ref, where_ref[BATCH], cls_keep_ref, cls_send_refs)


def round_kernel(n_in, where_ref, base_ref, small_ref, cls_ref, *refs):
    in_refs, cls_in_refs = refs[:n_in], refs[n_in:-3]
    out_ref, sum_ref, cls_out_ref = refs[-3:]
    rows = base_ref.shape[0]
    total = base_ref[...]
    for ref in in_refs:
        total = total + ref[0:rows].astype(F32)
    out_ref[...] = total.astype(BF16)
    sum_ref[...] = pair_sum([small_ref[...]] + [get_trio(ref, rows) for ref in in_refs])
    total = cls_ref[...]
    for ref in cls_in_refs:
        total = total + ref[...].astype(F32)
    cls_out_ref[...] = total.astype(BF16)


def join(me, in_refs, out_ref):
    rows = in_refs[0].shape[0]
    for k, ref in enumerate(in_refs):
        out_ref[pl.ds(pl.multiple_of((me ^ k) * rows, 8), rows)] = ref[...].astype(out_ref.dtype)


def join_kernel(n_in, where_ref, *refs):
    join(where_ref[TILE], refs[:n_in], refs[-2])
    join(where_ref[BATCH], refs[n_in:-2], refs[-1])


def out_kernel(n_in, where_ref, *refs):
    out_ref, cls_out_ref, whole_ref = refs[-3:]
    join(where_ref[BATCH], refs[:n_in], out_ref)
    join(where_ref[TILE], refs[n_in:-3], whole_ref)
    for tap in range(9):
        cls_out_ref[tap // 3, tap % 3] = whole_ref[CLS_ROWS * tap : CLS_ROWS * tap + LOGITS]


def swap(x, axis, bit=1):
    size = lax.axis_size(axis)
    return lax.ppermute(x, axis, [(i, i ^ bit) for i in range(size)])


def others(x, axis):
    return [swap(x, axis, bit) for bit in range(1, lax.axis_size(axis))]


def exchange(sends, axis):
    return [swap(x, axis, k + 1) for k, x in enumerate(sends)]


def shards(features, labels, w_shared, b_shared, w_cls, b_cls):
    _, rows, cols, chans = features.shape
    half = rows // 2
    outs = w_shared.shape[3]
    tiles = lax.axis_size("tile")
    pages = lax.axis_size("batch")
    c = lax.axis_index("chan")
    t = lax.axis_index("tile")
    f = features[0]
    where = jnp.stack([c, t * rows + half * c, jnp.int32(tiles * rows), t, lax.axis_index("batch")]).astype(jnp.int32)
    lab = labels.reshape(rows, 1, labels.shape[2])
    msg, labt, count = call(
        edge_kernel, "edge", 1.5,
        [((3 * cols + ANCH_ROWS, chans), BF16), ((rows, ANCH_ROWS, cols), BF16), ((8, LANES), F32)],
        [where, f, lab],
        [pltpu.SemaphoreType.DMA((3,))],
        [SMEM, HBM, VMEM],
    )
    (pack,) = call(
        pack_kernel, "pack", 0.8, [((9 * LANES + TRIO, outs), BF16)],
        [where, jnp.swapaxes(w_cls, 2, 3), b_shared.reshape(1, outs)],
    )
    pairs = []
    for i in range(tiles - 1):
        pairs += [(2 * i + 1, 2 * i + 2), (2 * i + 2, 2 * i + 1)]
    halo = lax.ppermute(msg, ("tile", "chan"), pairs)
    w1b = swap(w_shared, "chan")
    packb = swap(pack, "chan")
    count = pair_sum([count] + others(count, "batch"))
    counts = [count] + others(count, "tile")

    hid, dz, loss = call(
        head_kernel, "head", 11,
        [((half + 4, cols, chans), BF16), ((half + 2, cols, LANES), F32), ((1, LANES), F32)],
        [where, f, halo, labt, w_shared, w1b, pack, packb, b_cls.reshape(1, LOGITS)],
        [((half + 6, cols, chans), BF16)],
    )
    dt, own, other, small = call(
        back_kernel, "back", 4,
        [
            ((half, 3 * CLS_ROWS, cols), BF16),
            ((half, cols, outs), BF16),
            ((half, cols, outs), BF16),
            ((8, LANES), F32),
        ],
        [where, hid, dz, loss, pack, packb] + counts,
        [((half + 2, cols, LANES), BF16)],
    )
    theirs = swap(other, "chan")
    far = swap(halo, "chan")
    small_theirs = swap(small, "chan")
    gcls, gcls_other = call(
        cls_kernel, "cls", 1.5, [((CLS_TOTAL, outs), F32)] * 2, [where, hid, dt]
    )
    gcls_theirs = swap(gcls_other, "chan")

    total = 9 * chans
    first, second = total // pages, total // (pages * tiles)
    cfirst, csecond = CLS_TOTAL // tiles, CLS_TOTAL // (pages * tiles)
    keep, small, *sends = call(
        functools.partial(shared_kernel, pages - 1), "shared", 4,
        [((first, outs), F32), ((8, LANES), F32)]
        + [((first + TRIO, outs), BF16)] * (pages - 1)
        + [((cfirst, outs), F32)]
        + [((cfirst, outs), BF16)] * (tiles - 1),
        [where, f, halo, far, own, theirs, small, small_theirs, gcls, gcls_theirs],
        [((rows + 2, cols, chans), BF16), ((rows, cols, 3 * outs), BF16), ((total, outs), F32), ((CLS_TOTAL, outs), F32)],
    )
    ckeep, csends = sends[pages - 1], sends[pages:]
    arrived = exchange(sends[: pages - 1], "batch")
    carrived = exchange(csends, "tile")
    keep, small, *sends = call(
        functools.partial(sum_kernel, pages - 1, tiles - 1, tiles - 1), "sum", 0.7,
        [((second, outs), F32), ((8, LANES), F32)]
        + [((second + TRIO, outs), BF16)] * (tiles - 1)
        + [((csecond, outs), F32)]
        + [((csecond, outs), BF16)] * (pages - 1),
        [where, keep, small, ckeep] + arrived + carrived,
        [((first, outs), F32), ((cfirst, outs), F32)],
    )
    ckeep, csends = sends[tiles - 1], sends[tiles:]
    arrived = exchange(sends[: tiles - 1], "tile")
    carrived = exchange(csends, "batch")
    done, small, cdone = call(
        functools.partial(round_kernel, tiles - 1), "round", 0.7,
        [((second, outs), BF16), ((8, LANES), F32), ((csecond, outs), BF16)],
        [where, keep, small, ckeep] + arrived + carrived,
    )
    block, cblock = call(
        functools.partial(join_kernel, tiles), "join", 0.7,
        [((first, outs), BF16), ((cfirst, outs), BF16)],
        [where, done] + others(done, "tile") + [cdone] + others(cdone, "batch"),
    )
    grad_shared, grad_cls = call(
        functools.partial(out_kernel, pages), "out", 1.5,
        [((total, outs), F32), ((3, 3, LOGITS, outs), F32)],
        [where, block] + others(block, "batch") + [cblock] + others(cblock, "tile"),
        [((CLS_TOTAL, outs), F32)],
    )
    return (
        grad_shared.reshape(3, 3, chans, outs),
        small[3],
        jnp.swapaxes(grad_cls, 2, 3),
        small[0, :LOGITS],
        small[1, :1],
    )


def solution(mesh):
    placed = (
        P(("groups", "batch"), "tile", None, None),
        P(("groups", "batch"), "tile", None),
        P(None, None, None, "chan"),
        P("chan"),
        P(None, None, "chan", None),
        P(),
    )
    return jax.shard_map(
        shards,
        mesh=mesh,
        in_specs=placed,
        out_specs=(
            P("groups", None, None, "chan"),
            P(("groups", "chan")),
            P("groups", None, "chan", None),
            P("groups"),
            P("groups"),
        ),
        check_vma=False,
    )
```

```python
import functools

import jax
import jax.numpy as jnp
from jax import lax
from jax.experimental import pallas as pl
from jax.experimental.pallas import tpu as pltpu
from jax.sharding import PartitionSpec as P

ANCH = 9
CLASSES = 11
LOGITS = 99
LANES = 128
ANCH_ROWS = 16
CLS_ROWS = 112
CLS_TOTAL = 1024
TILE, BATCH = 3, 4
TRIO = 32
BF16 = jnp.bfloat16
F32 = jnp.float32
VMEM = pl.BlockSpec(memory_space=pltpu.VMEM)
HBM = pl.BlockSpec(memory_space=pltpu.HBM)
SMEM = pl.BlockSpec(memory_space=pltpu.SMEM)


def call(kernel, name, micros, outs, inputs, scratch=(), specs=None, mib=48):
    return pl.pallas_call(
        kernel,
        in_specs=specs or [SMEM] + [VMEM] * (len(inputs) - 1),
        out_specs=[VMEM] * len(outs),
        out_shape=[jax.ShapeDtypeStruct(shape, kind) for shape, kind in outs],
        scratch_shapes=[pltpu.VMEM(*shape) if isinstance(shape, tuple) else shape for shape in scratch],
        cost_estimate=pl.CostEstimate(flops=int(micros * 1e9), bytes_accessed=int(micros * 1e6), transcendentals=0),
        compiler_params=pltpu.CompilerParams(vmem_limit_bytes=mib * 1024 * 1024),
        name=name,
    )(*inputs)


def shift_cells(field, by):
    cells = field.shape[0]
    rolled = pltpu.roll(field, by % cells, axis=0)
    cell = lax.broadcasted_iota(jnp.int32, field.shape, 0)
    edge = 0 if by > 0 else cells - 1
    return jnp.where(cell == edge, 0.0, rolled)


def dot(left, right, dims=((1,), (0,))):
    return lax.dot_general(left, right, (dims, ((), ())), preferred_element_type=F32)


def three(x):
    high = x.astype(BF16)
    rest = x - high.astype(F32)
    middle = rest.astype(BF16)
    low = (rest - middle.astype(F32)).astype(BF16)
    return high, middle, low


def put_trio(ref, start, x):
    high, middle, low = three(x)
    ref[start : start + TRIO] = jnp.concatenate([high, middle, low, jnp.zeros_like(low)], axis=0)


def get_trio(ref, start):
    part = ref[start : start + TRIO].astype(F32)
    return part[0:8] + part[8:16] + part[16:24]


def edge_kernel(where_ref, f_ref, lab_ref, w2_ref, b1_ref, msg_ref, labt_ref, count_ref, pack_ref, sem):
    rows, cols, _ = f_ref.shape
    c = where_ref[0]
    copies = [
        pltpu.make_async_copy(f_ref.at[(rows - 3) * c + k], msg_ref.at[pl.ds(cols * k, cols)], sem.at[k])
        for k in range(3)
    ]
    for copy in copies:
        copy.start()
    size = lab_ref.shape[2]
    place = lax.broadcasted_iota(jnp.int32, (ANCH_ROWS, size), 1) % ANCH
    anchor = lax.broadcasted_iota(jnp.int32, (ANCH_ROWS, size), 0)
    mine = place == anchor
    labs = [lab_ref[r].astype(F32) for r in range(rows)]
    named = [jnp.where(lab > 0.0, 1.0, 0.0) for lab in labs]
    count_ref[...] = jnp.full(count_ref.shape, jnp.sum(sum(named[1:], named[0])), F32)
    left = jnp.concatenate([jnp.where(mine, lab, 0.0) for lab in labs], axis=0).astype(BF16)
    offset = lax.broadcasted_iota(jnp.int32, (size, cols), 0) - ANCH * lax.broadcasted_iota(jnp.int32, (size, cols), 1)
    pick = jnp.where(jnp.logical_and(offset >= 0, offset < ANCH), 1.0, 0.0).astype(BF16)
    turned = dot(left, pick).astype(BF16)
    for r in range(rows):
        labt_ref[r] = turned[ANCH_ROWS * r : ANCH_ROWS * (r + 1)]
    msg_ref[3 * cols : 3 * cols + ANCH_ROWS] = jnp.where(
        c == 0, turned[:ANCH_ROWS].astype(F32), turned[ANCH_ROWS * (rows - 1) :].astype(F32)
    ).astype(BF16)
    deep = w2_ref.shape[3]
    for tap in range(9):
        pack_ref[LANES * tap : LANES * (tap + 1)] = jnp.zeros((LANES, deep), BF16)
        pack_ref[LANES * tap : LANES * tap + LOGITS] = w2_ref[tap // 3, tap % 3]
    put_trio(pack_ref, 9 * LANES, jnp.broadcast_to(b1_ref[...], (8, deep)))
    for copy in copies:
        copy.wait()


def head_kernel(
    where_ref, f_ref, halo_ref, labt_ref, w1a_ref, w1b_ref, packa_ref, packb_ref, b2_ref,
    hid_ref, dz_ref, loss_ref, xw_ref,
):

    half = f_ref.shape[0] // 2
    cols = f_ref.shape[1]
    c = where_ref[0]
    first = where_ref[1]
    total = where_ref[2]
    near = half + 3
    xw_ref[pl.ds(3 - 3 * c, near)] = f_ref[pl.ds((half - 3) * c, near)]
    for k in range(3):
        xw_ref[near * c + k] = halo_ref[cols * k : cols * (k + 1)]
    w1 = [
        jnp.concatenate(
            [jnp.concatenate([w1a_ref[i, j], w1b_ref[i, j]], axis=1) for j in range(3)], axis=1
        )
        for i in range(3)
    ]
    w1 = jnp.concatenate(w1, axis=0)
    chans = w1.shape[1] // 3
    deep = chans // 2
    b1 = jnp.concatenate([get_trio(packa_ref, 9 * LANES)[:1], get_trio(packb_ref, 9 * LANES)[:1]], axis=1)

    def conv1(h, carry):
        lhs = jnp.concatenate([xw_ref[h], xw_ref[h + 1], xw_ref[h + 2]], axis=1)
        y = dot(lhs, w1)
        pre = shift_cells(y[:, :chans], 1) + y[:, chans : 2 * chans] + shift_cells(y[:, 2 * chans :], -1) + b1
        row = first + h - 2
        inside = jnp.logical_and(row >= 0, row < total)
        hid_ref[h] = jnp.where(inside, jnp.maximum(pre, 0.0), 0.0).astype(BF16)
        return carry

    lax.fori_loop(0, half + 4, conv1, 0)

    lane = lax.broadcasted_iota(jnp.int32, (1, LANES), 1)
    kind = (lane % CLASSES + 1).astype(F32)
    real = lane < LOGITS
    anchor = lax.broadcasted_iota(jnp.int32, (ANCH_ROWS, LANES), 0)
    column = lax.broadcasted_iota(jnp.int32, (ANCH_ROWS, LANES), 1)
    spread = jnp.where(jnp.logical_and(column // CLASSES == anchor, column < LOGITS), 1.0, 0.0).astype(BF16)
    w2 = [
        jnp.concatenate([jnp.concatenate([tap(packa_ref, i, j), tap(packb_ref, i, j)], axis=1) for j in range(3)], axis=0)
        for i in range(3)
    ]
    w2 = jnp.concatenate(w2, axis=1)
    b2 = jnp.concatenate([b2_ref[...], jnp.zeros((1, LANES - LOGITS), F32)], axis=1)

    def focal(l, loss):
        lhs = jnp.concatenate([hid_ref[l], hid_ref[l + 1], hid_ref[l + 2]], axis=1)
        y = dot(lhs, w2, ((1,), (1,)))
        z = shift_cells(y[:, :LANES], 1) + y[:, LANES : 2 * LANES] + shift_cells(y[:, 2 * LANES :], -1) + b2
        at_halo = jnp.where(c == 0, l == 0, l == half + 1)
        local = jnp.clip(l - 1 + half * c, 0, 2 * half - 1)
        mine = labt_ref[local].astype(F32)
        far = halo_ref[3 * cols : 3 * cols + ANCH_ROWS].astype(F32)
        lab = dot(jnp.where(at_halo, far, mine).astype(BF16), spread, ((0,), (0,)))
        row = first + l - 1
        inside = jnp.logical_and(row >= 0, row < total)
        hit = lab == kind
        keep = jnp.logical_and(jnp.logical_and(lab >= 0.0, real), inside)
        u = jnp.where(hit, -z, z)
        e = jnp.exp(-jnp.abs(u))
        r = 1.0 / (1.0 + e)
        er = e * r
        up = u >= 0.0
        s = jnp.where(up, r, er)
        comp = jnp.where(up, er, r)
        soft = jnp.maximum(u, 0.0) + jnp.log1p(e)
        ws = jnp.where(keep, jnp.where(hit, 0.25, 0.75), 0.0) * s * s
        slope = ws * (2.0 * comp * soft + s)
        dz_ref[l] = jnp.where(hit, -slope, slope)
        own = jnp.logical_and(l >= 1, l <= half)
        return loss + jnp.where(own, 1.0, 0.0) * jnp.sum(ws * soft, axis=0, keepdims=True)

    loss_ref[...] = lax.fori_loop(0, half + 2, focal, jnp.zeros((1, LANES), F32))


def tap(ref, i, j):
    return ref[LANES * (3 * i + j) : LANES * (3 * i + j + 1)]


def back_kernel(where_ref, hid_ref, dz_ref, loss_ref, packa_ref, packb_ref, *rest):
    *count_refs, dt_ref, own_ref, other_ref, small_ref, dlog_ref = rest
    half, _, cols = dt_ref.shape
    chans = hid_ref.shape[2]
    inverse = 1.0 / pair_sum([ref[...] for ref in count_refs])[:1]

    def scaled(l):
        dz = dz_ref[l] * inverse
        d16 = dz.astype(BF16)
        dlog_ref[l] = d16
        return dz, d16

    scaled(0)
    scaled(half + 1)

    def turn(d, gcb):
        dz, d16 = scaled(d + 1)
        turned = jnp.transpose(d16.astype(F32))[:CLS_ROWS]
        cell = lax.broadcasted_iota(jnp.int32, turned.shape, 1)
        left = jnp.where(cell == cols - 1, 0.0, pltpu.roll(turned, cols - 1, axis=1))
        right = jnp.where(cell == 0, 0.0, pltpu.roll(turned, 1, axis=1))
        dt_ref[d] = jnp.concatenate([left, turned, right], axis=0).astype(BF16)
        return gcb + jnp.sum(dz, axis=0, keepdims=True)

    gcb = lax.fori_loop(0, half, turn, jnp.zeros((1, LANES), F32))
    w2t = [
        jnp.concatenate([x for j in range(3) for x in (tap(packa_ref, i, j), tap(packb_ref, i, j))], axis=1)
        for i in range(3)
    ]
    w2t = jnp.concatenate(w2t, axis=0)

    def dpre_row(d, gsb):
        lhs = jnp.concatenate([dlog_ref[d + 2], dlog_ref[d + 1], dlog_ref[d]], axis=1)
        q = dot(lhs, w2t)
        dhid = shift_cells(q[:, :chans], -1) + q[:, chans : 2 * chans] + shift_cells(q[:, 2 * chans :], 1)
        dpre = jnp.where(hid_ref[d + 2].astype(F32) > 0.0, dhid, 0.0)
        d16 = dpre.astype(BF16)
        own_ref[d] = d16[:, : chans // 2]
        other_ref[d] = d16[:, chans // 2 :]
        return gsb + jnp.sum(dpre, axis=0, keepdims=True)

    gsb = lax.fori_loop(0, half, dpre_row, jnp.zeros((1, chans), F32))
    small_ref[0:1] = gcb
    small_ref[1:2] = jnp.broadcast_to(jnp.sum(loss_ref[...], axis=1, keepdims=True), (1, LANES)) * inverse
    small_ref[2:3] = jnp.zeros((1, LANES), F32)
    small_ref[3:4] = gsb[:, : chans // 2]
    small_ref[4:5] = gsb[:, chans // 2 :]
    small_ref[5:8] = jnp.zeros((3, LANES), F32)


def cls_kernel(where_ref, hid_ref, dt_ref, own_ref, other_ref):
    half, _, cols = dt_ref.shape
    chans = hid_ref.shape[2]
    deep = chans // 2
    dt = jnp.concatenate([dt_ref[d] for d in range(half)], axis=1)
    size = 3 * CLS_ROWS
    for i in range(3):
        g = dot(dt, hid_ref[i + 1 : i + 1 + half].reshape(half * cols, chans))
        own_ref[size * i : size * (i + 1)] = g[:, :deep]
        other_ref[size * i : size * (i + 1)] = g[:, deep:]
    blank = jnp.zeros((CLS_TOTAL - 3 * size, deep), F32)
    own_ref[3 * size :] = blank
    other_ref[3 * size :] = blank


def split(total, me, keep_ref, send_refs):
    rows = keep_ref.shape[0]
    keep_ref[...] = total[pl.ds(pl.multiple_of(me * rows, 8), rows)]
    for k, ref in enumerate(send_refs):
        ref[0:rows] = total[pl.ds(pl.multiple_of((me ^ (k + 1)) * rows, 8), rows)].astype(BF16)


def shared_kernel(
    where_ref, f_ref, halo_ref, far_ref, own_ref, other_ref, small_ref, keep_ref, *rest
):
    *send_refs, x_ref, d_ref, g_ref = rest
    rows, cols, chans = f_ref.shape
    half = rows // 2
    c = where_ref[0]
    near = halo_ref[pl.ds(pl.multiple_of(2 * cols * (1 - c), 16), cols)]
    far = far_ref[pl.ds(pl.multiple_of(2 * cols * c, 16), cols)]
    x_ref[pl.ds((rows + 1) * c, 1)] = near.reshape(1, cols, chans)
    x_ref[pl.ds((rows + 1) * (1 - c), 1)] = far.reshape(1, cols, chans)
    x_ref[1 : rows + 1] = f_ref[...]

    def place(ref, start):
        def body(d, carry):
            mid = ref[d].astype(F32)
            d_ref[start + d] = jnp.concatenate(
                [shift_cells(mid, -1).astype(BF16), ref[d], shift_cells(mid, 1).astype(BF16)], axis=1
            )
            return carry

        lax.fori_loop(0, half, body, 0)

    place(own_ref, half * c)
    place(other_ref, half * (1 - c))
    rhs = d_ref[...].reshape(rows * cols, d_ref.shape[2])
    outs = rhs.shape[1] // 3
    for i in range(3):
        lhs = x_ref[i : i + rows].reshape(rows * cols, chans)
        g = dot(lhs, rhs, ((0,), (0,)))
        for j in range(3):
            start = (3 * i + j) * chans
            g_ref[start : start + chans] = g[:, j * outs : (j + 1) * outs]
    split(g_ref, where_ref[BATCH], keep_ref, send_refs)
    for ref in send_refs:
        put_trio(ref, keep_ref.shape[0], small_ref[...])


def cls_split_kernel(where_ref, cls_ref, theirs_ref, keep_ref, *rest):
    *send_refs, total_ref = rest
    total_ref[...] = cls_ref[...] + theirs_ref[...]
    split(total_ref, where_ref[TILE], keep_ref, send_refs)


def pair_sum(parts):
    while len(parts) > 1:
        parts = [parts[k] + parts[k + 1] for k in range(0, len(parts), 2)]
    return parts[0]


def sum_kernel(n_in, n_cls, n_send, where_ref, base_ref, small_ref, cls_ref, *refs):
    in_refs, refs = refs[:n_in], refs[n_in:]
    cls_in_refs, refs = refs[:n_cls], refs[n_cls:]
    keep_ref, sum_ref, *refs, total_ref, cls_total_ref = refs
    send_refs, cls_keep_ref, cls_send_refs = refs[:n_send], refs[n_send], refs[n_send + 1 :]
    rows = base_ref.shape[0]
    total = base_ref[...]
    for ref in in_refs:
        total = total + ref[0:rows].astype(F32)
    total_ref[...] = total
    split(total_ref, where_ref[TILE], keep_ref, send_refs)
    sums = pair_sum([small_ref[...]] + [get_trio(ref, rows) for ref in in_refs])
    sum_ref[...] = sums
    for ref in send_refs:
        put_trio(ref, keep_ref.shape[0], sums)
    total = cls_ref[...]
    for ref in cls_in_refs:
        total = total + ref[...].astype(F32)
    cls_total_ref[...] = total
    split(cls_total_ref, where_ref[BATCH], cls_keep_ref, cls_send_refs)


def round_kernel(n_in, where_ref, base_ref, small_ref, cls_ref, *refs):
    in_refs, cls_in_refs = refs[:n_in], refs[n_in:-3]
    out_ref, sum_ref, cls_out_ref = refs[-3:]
    rows = base_ref.shape[0]
    total = base_ref[...]
    for ref in in_refs:
        total = total + ref[0:rows].astype(F32)
    out_ref[...] = total.astype(BF16)
    sum_ref[...] = pair_sum([small_ref[...]] + [get_trio(ref, rows) for ref in in_refs])
    total = cls_ref[...]
    for ref in cls_in_refs:
        total = total + ref[...].astype(F32)
    cls_out_ref[...] = total.astype(BF16)


def join(me, in_refs, out_ref):
    rows = in_refs[0].shape[0]
    for k, ref in enumerate(in_refs):
        out_ref[pl.ds(pl.multiple_of((me ^ k) * rows, 8), rows)] = ref[...].astype(out_ref.dtype)


def join_kernel(n_in, where_ref, *refs):
    join(where_ref[TILE], refs[:n_in], refs[-2])
    join(where_ref[BATCH], refs[n_in:-2], refs[-1])


def out_kernel(n_in, where_ref, *refs):
    out_ref, cls_out_ref, whole_ref = refs[-3:]
    join(where_ref[BATCH], refs[:n_in], out_ref)
    join(where_ref[TILE], refs[n_in:-3], whole_ref)
    for tap in range(9):
        cls_out_ref[tap // 3, tap % 3] = whole_ref[CLS_ROWS * tap : CLS_ROWS * tap + LOGITS]


def swap(x, axis, bit=1):
    size = lax.axis_size(axis)
    return lax.ppermute(x, axis, [(i, i ^ bit) for i in range(size)])


def others(x, axis):
    return [swap(x, axis, bit) for bit in range(1, lax.axis_size(axis))]


def exchange(sends, axis):
    return [swap(x, axis, k + 1) for k, x in enumerate(sends)]


def shards(features, labels, w_shared, b_shared, w_cls, b_cls):
    _, rows, cols, chans = features.shape
    half = rows // 2
    outs = w_shared.shape[3]
    tiles = lax.axis_size("tile")
    pages = lax.axis_size("batch")
    c = lax.axis_index("chan")
    t = lax.axis_index("tile")
    f = features[0]
    where = jnp.stack([c, t * rows + half * c, jnp.int32(tiles * rows), t, lax.axis_index("batch")]).astype(jnp.int32)
    lab = labels.reshape(rows, 1, labels.shape[2])
    msg, labt, count, pack = call(
        edge_kernel, "edge", 2,
        [
            ((3 * cols + ANCH_ROWS, chans), BF16),
            ((rows, ANCH_ROWS, cols), BF16),
            ((8, LANES), F32),
            ((9 * LANES + TRIO, outs), BF16),
        ],
        [where, f, lab, jnp.swapaxes(w_cls, 2, 3), b_shared.reshape(1, outs)],
        [pltpu.SemaphoreType.DMA((3,))],
        [SMEM, HBM, VMEM, VMEM, VMEM],
        52,
    )
    pairs = []
    for i in range(tiles - 1):
        pairs += [(2 * i + 1, 2 * i + 2), (2 * i + 2, 2 * i + 1)]
    halo = lax.ppermute(msg, ("tile", "chan"), pairs)
    w1b = swap(w_shared, "chan")
    packb = swap(pack, "chan")
    count = pair_sum([count] + others(count, "batch"))
    counts = [count] + others(count, "tile")

    hid, dz, loss = call(
        head_kernel, "head", 11,
        [((half + 4, cols, chans), BF16), ((half + 2, cols, LANES), F32), ((1, LANES), F32)],
        [where, f, halo, labt, w_shared, w1b, pack, packb, b_cls.reshape(1, LOGITS)],
        [((half + 6, cols, chans), BF16)],
    )
    dt, own, other, small = call(
        back_kernel, "back", 4,
        [
            ((half, 3 * CLS_ROWS, cols), BF16),
            ((half, cols, outs), BF16),
            ((half, cols, outs), BF16),
            ((8, LANES), F32),
        ],
        [where, hid, dz, loss, pack, packb] + counts,
        [((half + 2, cols, LANES), BF16)],
    )
    theirs = swap(other, "chan")
    far = swap(halo, "chan")
    gcls, gcls_other = call(
        cls_kernel, "cls", 1.5, [((CLS_TOTAL, outs), F32)] * 2, [where, hid, dt]
    )
    gcls_theirs = swap(gcls_other, "chan")

    total = 9 * chans
    first, second = total // pages, total // (pages * tiles)
    cfirst, csecond = CLS_TOTAL // tiles, CLS_TOTAL // (pages * tiles)
    keep, *sends = call(
        shared_kernel, "shared", 4,
        [((first, outs), F32)] + [((first + TRIO, outs), BF16)] * (pages - 1),
        [where, f, halo, far, own, theirs, small],
        [((rows + 2, cols, chans), BF16), ((rows, cols, 3 * outs), BF16), ((total, outs), F32)],
    )
    ckeep, *csends = call(
        cls_split_kernel, "cls_split", 0.6,
        [((cfirst, outs), F32)] + [((cfirst, outs), BF16)] * (tiles - 1),
        [where, gcls, gcls_theirs],
        [((CLS_TOTAL, outs), F32)],
    )
    arrived = exchange(sends, "batch")
    carrived = exchange(csends, "tile")
    keep, small, *sends = call(
        functools.partial(sum_kernel, pages - 1, tiles - 1, tiles - 1), "sum", 0.7,
        [((second, outs), F32), ((8, LANES), F32)]
        + [((second + TRIO, outs), BF16)] * (tiles - 1)
        + [((csecond, outs), F32)]
        + [((csecond, outs), BF16)] * (pages - 1),
        [where, keep, small, ckeep] + arrived + carrived,
        [((first, outs), F32), ((cfirst, outs), F32)],
    )
    ckeep, csends = sends[tiles - 1], sends[tiles:]
    arrived = exchange(sends[: tiles - 1], "tile")
    carrived = exchange(csends, "batch")
    done, small, cdone = call(
        functools.partial(round_kernel, tiles - 1), "round", 0.7,
        [((second, outs), BF16), ((8, LANES), F32), ((csecond, outs), BF16)],
        [where, keep, small, ckeep] + arrived + carrived,
    )
    small_theirs = swap(small, "chan")
    block, cblock = call(
        functools.partial(join_kernel, tiles), "join", 0.7,
        [((first, outs), BF16), ((cfirst, outs), BF16)],
        [where, done] + others(done, "tile") + [cdone] + others(cdone, "batch"),
    )
    grad_shared, grad_cls = call(
        functools.partial(out_kernel, pages), "out", 1.5,
        [((total, outs), F32), ((3, 3, LOGITS, outs), F32)],
        [where, block] + others(block, "batch") + [cblock] + others(cblock, "tile"),
        [((CLS_TOTAL, outs), F32)],
    )
    return (
        grad_shared.reshape(3, 3, chans, outs),
        small[3] + small_theirs[4],
        jnp.swapaxes(grad_cls, 2, 3),
        small[0, :LOGITS] + small_theirs[0, :LOGITS],
        small[1, :1] + small_theirs[1, :1],
    )


def solution(mesh):
    placed = (
        P(("groups", "batch"), "tile", None, None),
        P(("groups", "batch"), "tile", None),
        P(None, None, None, "chan"),
        P("chan"),
        P(None, None, "chan", None),
        P(),
    )
    return jax.shard_map(
        shards,
        mesh=mesh,
        in_specs=placed,
        out_specs=(
            P("groups", None, None, "chan"),
            P(("groups", "chan")),
            P("groups", None, "chan", None),
            P("groups"),
            P("groups"),
        ),
        check_vma=False,
    )
```

```python
import functools

import jax
import jax.numpy as jnp
from jax import lax
from jax.experimental import pallas as pl
from jax.experimental.pallas import tpu as pltpu
from jax.sharding import PartitionSpec as P

ANCH = 9
CLASSES = 11
LOGITS = 99
LANES = 128
ANCH_ROWS = 16
CLS_ROWS = 112
CLS_TOTAL = 1024
TILE, BATCH = 3, 4
BLOCK = 2
TRIO = 32
BF16 = jnp.bfloat16
F32 = jnp.float32
VMEM = pl.BlockSpec(memory_space=pltpu.VMEM)
HBM = pl.BlockSpec(memory_space=pltpu.HBM)
SMEM = pl.BlockSpec(memory_space=pltpu.SMEM)


def call(kernel, name, micros, outs, inputs, scratch=(), specs=None, mib=32):
    return pl.pallas_call(
        kernel,
        in_specs=specs or [SMEM] + [VMEM] * (len(inputs) - 1),
        out_specs=[VMEM] * len(outs),
        out_shape=[jax.ShapeDtypeStruct(shape, kind) for shape, kind in outs],
        scratch_shapes=[pltpu.VMEM(*shape) if isinstance(shape, tuple) else shape for shape in scratch],
        cost_estimate=pl.CostEstimate(flops=int(micros * 1e9), bytes_accessed=int(micros * 1e6), transcendentals=0),
        compiler_params=pltpu.CompilerParams(vmem_limit_bytes=int(mib * 1024 * 1024)),
        name=name,
    )(*inputs)


def shift_cells(field, by):
    cells = field.shape[0]
    rolled = pltpu.roll(field, by % cells, axis=0)
    cell = lax.broadcasted_iota(jnp.int32, field.shape, 0)
    edge = 0 if by > 0 else cells - 1
    return jnp.where(cell == edge, 0.0, rolled)


def dot(left, right, dims=((1,), (0,))):
    return lax.dot_general(left, right, (dims, ((), ())), preferred_element_type=F32)


def taken(ref, start, rows):
    cols = ref.shape[1]
    parts = [ref[pl.ds(start + r, BLOCK)].reshape(BLOCK * cols, ref.shape[2]) for r in rows]
    return jnp.concatenate(parts, axis=1)


def three(x):
    high = x.astype(BF16)
    rest = x - high.astype(F32)
    middle = rest.astype(BF16)
    low = (rest - middle.astype(F32)).astype(BF16)
    return high, middle, low


def put_trio(ref, start, x):
    high, middle, low = three(x)
    ref[start : start + TRIO] = jnp.concatenate([high, middle, low, jnp.zeros_like(low)], axis=0)


def get_trio(ref, start):
    part = ref[start : start + TRIO].astype(F32)
    return part[0:8] + part[8:16] + part[16:24]


def edge_kernel(where_ref, f_ref, lab_ref, msg_ref, labt_ref, count_ref, near_ref, sem):
    rows, cols, _ = f_ref.shape
    c = where_ref[0]
    copies = [
        pltpu.make_async_copy(f_ref.at[(rows - 3) * c + k], msg_ref.at[pl.ds(cols * k, cols)], sem.at[k])
        for k in range(3)
    ]
    near = near_ref.shape[0]
    copies.append(pltpu.make_async_copy(f_ref.at[pl.ds((rows - near) * c, near)], near_ref, sem.at[3]))
    for copy in copies:
        copy.start()
    size = lab_ref.shape[2]
    place = lax.broadcasted_iota(jnp.int32, (ANCH_ROWS, size), 1) % ANCH
    anchor = lax.broadcasted_iota(jnp.int32, (ANCH_ROWS, size), 0)
    mine = place == anchor
    labs = [lab_ref[r].astype(F32) for r in range(rows)]
    named = [jnp.where(lab > 0.0, 1.0, 0.0) for lab in labs]
    count_ref[...] = jnp.full(count_ref.shape, jnp.sum(sum(named[1:], named[0])), F32)
    left = jnp.concatenate([jnp.where(mine, lab, 0.0) for lab in labs], axis=0).astype(BF16)
    offset = lax.broadcasted_iota(jnp.int32, (size, cols), 0) - ANCH * lax.broadcasted_iota(jnp.int32, (size, cols), 1)
    pick = jnp.where(jnp.logical_and(offset >= 0, offset < ANCH), 1.0, 0.0).astype(BF16)
    turned = dot(left, pick).astype(BF16)
    for r in range(rows):
        labt_ref[r] = turned[ANCH_ROWS * r : ANCH_ROWS * (r + 1)]
    msg_ref[3 * cols : 3 * cols + ANCH_ROWS] = jnp.where(
        c == 0, turned[:ANCH_ROWS].astype(F32), turned[ANCH_ROWS * (rows - 1) :].astype(F32)
    ).astype(BF16)
    for copy in copies:
        copy.wait()


def head_kernel(
    where_ref, near_ref, halo_ref, labt_ref, w1a_ref, w1b_ref, b1a_ref, b1b_ref, w2a_ref, w2b_ref, b2_ref,
    hid_ref, dz_ref, loss_ref, w2_ref, xw_ref,
):

    near = near_ref.shape[0]
    half = near - 3
    cols = near_ref.shape[1]
    c = where_ref[0]
    first = where_ref[1]
    total = where_ref[2]
    xw_ref[pl.ds(3 - 3 * c, near)] = near_ref[...]
    for k in range(3):
        xw_ref[near * c + k] = halo_ref[cols * k : cols * (k + 1)]
    w1 = [
        jnp.concatenate(
            [jnp.concatenate([w1a_ref[i, j], w1b_ref[i, j]], axis=1) for j in range(3)], axis=1
        )
        for i in range(3)
    ]
    w1 = jnp.concatenate(w1, axis=0)
    chans = w1.shape[1] // 3
    deep = chans // 2
    b1 = jnp.concatenate([b1a_ref[...], b1b_ref[...]], axis=1)
    for tap in range(9):
        end = LANES * tap + LANES
        w2_ref[end - 32 : end] = jnp.zeros((32, chans), BF16)
        w2_ref[end - LANES : end - LANES + LOGITS, :deep] = w2a_ref[tap // 3, tap % 3]
        w2_ref[end - LANES : end - LANES + LOGITS, deep:] = w2b_ref[tap // 3, tap % 3]

    def conv1(g, carry):
        pair = dot(taken(xw_ref, BLOCK * g, (0, 1, 2)), w1)
        for k in range(BLOCK):
            h = BLOCK * g + k
            y = pair[k * cols : (k + 1) * cols]
            pre = shift_cells(y[:, :chans], 1) + y[:, chans : 2 * chans] + shift_cells(y[:, 2 * chans :], -1) + b1
            row = first + h - 2
            inside = jnp.logical_and(row >= 0, row < total)
            hid_ref[h] = jnp.where(inside, jnp.maximum(pre, 0.0), 0.0).astype(BF16)
        return carry

    lax.fori_loop(0, (half + 4) // BLOCK, conv1, 0, unroll=True)

    lane = lax.broadcasted_iota(jnp.int32, (1, LANES), 1)
    kind = (lane % CLASSES + 1).astype(F32)
    real = lane < LOGITS
    anchor = lax.broadcasted_iota(jnp.int32, (ANCH_ROWS, LANES), 0)
    column = lax.broadcasted_iota(jnp.int32, (ANCH_ROWS, LANES), 1)
    spread = jnp.where(jnp.logical_and(column // CLASSES == anchor, column < LOGITS), 1.0, 0.0).astype(BF16)
    size = 3 * LANES
    w2 = jnp.concatenate([w2_ref[size * i : size * (i + 1)] for i in range(3)], axis=1)
    b2 = jnp.concatenate([b2_ref[...], jnp.zeros((1, LANES - LOGITS), F32)], axis=1)

    def focal(g, loss):
        pair = dot(taken(hid_ref, BLOCK * g, (0, 1, 2)), w2, ((1,), (1,)))
        for k in range(BLOCK):
            loss = loss + focal_row(BLOCK * g + k, pair[k * cols : (k + 1) * cols])
        return loss

    def focal_row(l, y):
        z = shift_cells(y[:, :LANES], 1) + y[:, LANES : 2 * LANES] + shift_cells(y[:, 2 * LANES :], -1) + b2
        at_halo = jnp.where(c == 0, l == 0, l == half + 1)
        local = jnp.clip(l - 1 + half * c, 0, 2 * half - 1)
        mine = labt_ref[local].astype(F32)
        far = halo_ref[3 * cols : 3 * cols + ANCH_ROWS].astype(F32)
        lab = dot(jnp.where(at_halo, far, mine).astype(BF16), spread, ((0,), (0,)))
        row = first + l - 1
        inside = jnp.logical_and(row >= 0, row < total)
        hit = lab == kind
        keep = jnp.logical_and(jnp.logical_and(lab >= 0.0, real), inside)
        u = jnp.where(hit, -z, z)
        e = jnp.exp(-jnp.abs(u))
        r = 1.0 / (1.0 + e)
        er = e * r
        up = u >= 0.0
        s = jnp.where(up, r, er)
        comp = jnp.where(up, er, r)
        soft = jnp.maximum(u, 0.0) + jnp.log1p(e)
        ws = jnp.where(keep, jnp.where(hit, 0.25, 0.75), 0.0) * s * s
        slope = ws * (2.0 * comp * soft + s)
        dz_ref[l] = jnp.where(hit, -slope, slope)
        own = jnp.logical_and(l >= 1, l <= half)
        return jnp.where(own, 1.0, 0.0) * jnp.sum(ws * soft, axis=0, keepdims=True)

    loss_ref[...] = lax.fori_loop(0, (half + 2) // BLOCK, focal, jnp.zeros((1, LANES), F32), unroll=True)


def back_kernel(where_ref, hid_ref, dz_ref, loss_ref, w2_ref, *rest):
    *count_refs, dt_ref, own_ref, other_ref, small_ref, dlog_ref = rest
    half, _, cols = dt_ref.shape
    chans = hid_ref.shape[2]
    inverse = 1.0 / pair_sum([ref[...] for ref in count_refs])[:1]

    def scaled(l):
        dz = dz_ref[l] * inverse
        d16 = dz.astype(BF16)
        dlog_ref[l] = d16
        return dz, d16

    scaled(0)
    scaled(half + 1)

    def turn(d, gcb):
        dz, d16 = scaled(d + 1)
        turned = jnp.transpose(d16.astype(F32))[:CLS_ROWS]
        cell = lax.broadcasted_iota(jnp.int32, turned.shape, 1)
        left = jnp.where(cell == cols - 1, 0.0, pltpu.roll(turned, cols - 1, axis=1))
        right = jnp.where(cell == 0, 0.0, pltpu.roll(turned, 1, axis=1))
        dt_ref[d] = jnp.concatenate([left, turned, right], axis=0).astype(BF16)
        return gcb + jnp.sum(dz, axis=0, keepdims=True)

    gcb = lax.fori_loop(0, half, turn, jnp.zeros((1, LANES), F32), unroll=True)
    w2t = [
        jnp.concatenate([w2_ref[LANES * (3 * i + j) : LANES * (3 * i + j + 1)] for j in range(3)], axis=1)
        for i in range(3)
    ]
    w2t = jnp.concatenate(w2t, axis=0)

    def dpre(g, gsb):
        pair = dot(taken(dlog_ref, BLOCK * g, (2, 1, 0)), w2t)
        for k in range(BLOCK):
            gsb = gsb + dpre_row(BLOCK * g + k, pair[k * cols : (k + 1) * cols])
        return gsb

    def dpre_row(d, q):
        dhid = shift_cells(q[:, :chans], -1) + q[:, chans : 2 * chans] + shift_cells(q[:, 2 * chans :], 1)
        dpre = jnp.where(hid_ref[d + 2].astype(F32) > 0.0, dhid, 0.0)
        d16 = dpre.astype(BF16)
        own_ref[d] = d16[:, : chans // 2]
        other_ref[d] = d16[:, chans // 2 :]
        return jnp.sum(dpre, axis=0, keepdims=True)

    gsb = lax.fori_loop(0, half // BLOCK, dpre, jnp.zeros((1, chans), F32), unroll=True)
    small_ref[0:1] = gcb
    small_ref[1:2] = jnp.broadcast_to(jnp.sum(loss_ref[...], axis=1, keepdims=True), (1, LANES)) * inverse
    small_ref[2:3] = jnp.zeros((1, LANES), F32)
    small_ref[3:4] = gsb[:, : chans // 2]
    small_ref[4:5] = gsb[:, chans // 2 :]
    small_ref[5:8] = jnp.zeros((3, LANES), F32)


def cls_kernel(where_ref, hid_ref, dt_ref, own_ref, other_ref):
    half, _, cols = dt_ref.shape
    chans = hid_ref.shape[2]
    deep = chans // 2
    dt = jnp.concatenate([dt_ref[d] for d in range(half)], axis=1)
    size = 3 * CLS_ROWS
    for i in range(3):
        g = dot(dt, hid_ref[i + 1 : i + 1 + half].reshape(half * cols, chans))
        own_ref[size * i : size * (i + 1)] = g[:, :deep]
        other_ref[size * i : size * (i + 1)] = g[:, deep:]
    blank = jnp.zeros((CLS_TOTAL - 3 * size, deep), F32)
    own_ref[3 * size :] = blank
    other_ref[3 * size :] = blank


def split(total, me, keep_ref, send_refs):
    rows = keep_ref.shape[0]
    keep_ref[...] = total[pl.ds(pl.multiple_of(me * rows, 8), rows)]
    for k, ref in enumerate(send_refs):
        ref[0:rows] = total[pl.ds(pl.multiple_of((me ^ (k + 1)) * rows, 8), rows)].astype(BF16)


def shared_kernel(
    where_ref, f_ref, halo_ref, far_ref, own_ref, other_ref, small_ref, keep_ref, *rest
):
    *send_refs, x_ref, d_ref, g_ref = rest
    rows, cols, chans = f_ref.shape
    half = rows // 2
    c = where_ref[0]
    near = halo_ref[pl.ds(pl.multiple_of(2 * cols * (1 - c), 16), cols)]
    far = far_ref[pl.ds(pl.multiple_of(2 * cols * c, 16), cols)]
    x_ref[pl.ds((rows + 1) * c, 1)] = near.reshape(1, cols, chans)
    x_ref[pl.ds((rows + 1) * (1 - c), 1)] = far.reshape(1, cols, chans)
    x_ref[1 : rows + 1] = f_ref[...]

    def place(ref, start):
        def body(d, carry):
            mid = ref[d].astype(F32)
            d_ref[start + d] = jnp.concatenate(
                [shift_cells(mid, -1).astype(BF16), ref[d], shift_cells(mid, 1).astype(BF16)], axis=1
            )
            return carry

        lax.fori_loop(0, half, body, 0, unroll=True)

    place(own_ref, half * c)
    place(other_ref, half * (1 - c))
    rhs = d_ref[...].reshape(rows * cols, d_ref.shape[2])
    outs = rhs.shape[1] // 3
    for i in range(3):
        lhs = x_ref[i : i + rows].reshape(rows * cols, chans)
        g = dot(lhs, rhs, ((0,), (0,)))
        for j in range(3):
            start = (3 * i + j) * chans
            g_ref[start : start + chans] = g[:, j * outs : (j + 1) * outs]
    split(g_ref, where_ref[BATCH], keep_ref, send_refs)
    for ref in send_refs:
        put_trio(ref, keep_ref.shape[0], small_ref[...])


def cls_split_kernel(where_ref, cls_ref, theirs_ref, keep_ref, *rest):
    *send_refs, total_ref = rest
    total_ref[...] = cls_ref[...] + theirs_ref[...]
    split(total_ref, where_ref[TILE], keep_ref, send_refs)


def pair_sum(parts):
    while len(parts) > 1:
        parts = [parts[k] + parts[k + 1] for k in range(0, len(parts), 2)]
    return parts[0]


def sum_kernel(n_in, n_cls, n_send, where_ref, base_ref, small_ref, cls_ref, *refs):
    in_refs, refs = refs[:n_in], refs[n_in:]
    cls_in_refs, refs = refs[:n_cls], refs[n_cls:]
    keep_ref, sum_ref, *refs, total_ref, cls_total_ref = refs
    send_refs, cls_keep_ref, cls_send_refs = refs[:n_send], refs[n_send], refs[n_send + 1 :]
    rows = base_ref.shape[0]
    total = base_ref[...]
    for ref in in_refs:
        total = total + ref[0:rows].astype(F32)
    total_ref[...] = total
    split(total_ref, where_ref[TILE], keep_ref, send_refs)
    sums = pair_sum([small_ref[...]] + [get_trio(ref, rows) for ref in in_refs])
    sum_ref[...] = sums
    for ref in send_refs:
        put_trio(ref, keep_ref.shape[0], sums)
    total = cls_ref[...]
    for ref in cls_in_refs:
        total = total + ref[...].astype(F32)
    cls_total_ref[...] = total
    split(cls_total_ref, where_ref[BATCH], cls_keep_ref, cls_send_refs)


def round_kernel(n_in, where_ref, base_ref, small_ref, cls_ref, *refs):
    in_refs, cls_in_refs = refs[:n_in], refs[n_in:-3]
    out_ref, sum_ref, cls_out_ref = refs[-3:]
    rows = base_ref.shape[0]
    total = base_ref[...]
    for ref in in_refs:
        total = total + ref[0:rows].astype(F32)
    out_ref[...] = total.astype(BF16)
    sum_ref[...] = pair_sum([small_ref[...]] + [get_trio(ref, rows) for ref in in_refs])
    total = cls_ref[...]
    for ref in cls_in_refs:
        total = total + ref[...].astype(F32)
    cls_out_ref[...] = total.astype(BF16)


def join(me, in_refs, out_ref):
    rows = in_refs[0].shape[0]
    for k, ref in enumerate(in_refs):
        out_ref[pl.ds(pl.multiple_of((me ^ k) * rows, 8), rows)] = ref[...].astype(out_ref.dtype)


def join_kernel(n_in, where_ref, *refs):
    join(where_ref[TILE], refs[:n_in], refs[-2])
    join(where_ref[BATCH], refs[n_in:-2], refs[-1])


def out_kernel(n_in, where_ref, *refs):
    out_ref, cls_out_ref, whole_ref = refs[-3:]
    join(where_ref[BATCH], refs[:n_in], out_ref)
    join(where_ref[TILE], refs[n_in:-3], whole_ref)
    for tap in range(9):
        cls_out_ref[tap // 3, tap % 3] = whole_ref[CLS_ROWS * tap : CLS_ROWS * tap + LOGITS]


def swap(x, axis, bit=1):
    size = lax.axis_size(axis)
    return lax.ppermute(x, axis, [(i, i ^ bit) for i in range(size)])


def others(x, axis):
    return [swap(x, axis, bit) for bit in range(1, lax.axis_size(axis))]


def exchange(sends, axis):
    return [swap(x, axis, k + 1) for k, x in enumerate(sends)]


def shards(features, labels, w_shared, b_shared, w_cls, b_cls):
    _, rows, cols, chans = features.shape
    half = rows // 2
    outs = w_shared.shape[3]
    tiles = lax.axis_size("tile")
    pages = lax.axis_size("batch")
    c = lax.axis_index("chan")
    t = lax.axis_index("tile")
    f = features[0]
    where = jnp.stack([c, t * rows + half * c, jnp.int32(tiles * rows), t, lax.axis_index("batch")]).astype(jnp.int32)
    lab = labels.reshape(rows, 1, labels.shape[2])
    msg, labt, count, near = call(
        edge_kernel, "edge", 2,
        [
            ((3 * cols + ANCH_ROWS, chans), BF16),
            ((rows, ANCH_ROWS, cols), BF16),
            ((8, LANES), F32),
            ((half + 3, cols, chans), BF16),
        ],
        [where, f, lab],
        [pltpu.SemaphoreType.DMA((4,))],
        [SMEM, HBM, VMEM],
        51,
    )
    pairs = []
    for i in range(tiles - 1):
        pairs += [(2 * i + 1, 2 * i + 2), (2 * i + 2, 2 * i + 1)]
    halo = lax.ppermute(msg, ("tile", "chan"), pairs)
    w1b = swap(w_shared, "chan")
    w2b = swap(w_cls, "chan")
    b1b = swap(b_shared, "chan")
    count = pair_sum([count] + others(count, "batch"))
    counts = [count] + others(count, "tile")

    hid, dz, loss, w2 = call(
        head_kernel, "head", 11,
        [((half + 4, cols, chans), BF16), ((half + 2, cols, LANES), F32), ((1, LANES), F32)]
        + [((9 * LANES, chans), BF16)],
        [where, near, halo, labt, w_shared, w1b, b_shared.reshape(1, outs), b1b.reshape(1, outs)]
        + [jnp.swapaxes(w_cls, 2, 3), jnp.swapaxes(w2b, 2, 3), b_cls.reshape(1, LOGITS)],
        [((half + 6, cols, chans), BF16)],
    )
    dt, own, other, small = call(
        back_kernel, "back", 4,
        [
            ((half, 3 * CLS_ROWS, cols), BF16),
            ((half, cols, outs), BF16),
            ((half, cols, outs), BF16),
            ((8, LANES), F32),
        ],
        [where, hid, dz, loss, w2] + counts,
        [((half + 2, cols, LANES), BF16)],
    )
    theirs = swap(other, "chan")
    far = swap(halo, "chan")
    gcls, gcls_other = call(
        cls_kernel, "cls", 1.5, [((CLS_TOTAL, outs), F32)] * 2, [where, hid, dt]
    )
    gcls_theirs = swap(gcls_other, "chan")

    total = 9 * chans
    first, second = total // pages, total // (pages * tiles)
    cfirst, csecond = CLS_TOTAL // tiles, CLS_TOTAL // (pages * tiles)
    keep, *sends = call(
        shared_kernel, "shared", 4,
        [((first, outs), F32)] + [((first + TRIO, outs), BF16)] * (pages - 1),
        [where, f, halo, far, own, theirs, small],
        [((rows + 2, cols, chans), BF16), ((rows, cols, 3 * outs), BF16), ((total, outs), F32)],
    )
    ckeep, *csends = call(
        cls_split_kernel, "cls_split", 0.6,
        [((cfirst, outs), F32)] + [((cfirst, outs), BF16)] * (tiles - 1),
        [where, gcls, gcls_theirs],
        [((CLS_TOTAL, outs), F32)],
    )
    arrived = exchange(sends, "batch")
    carrived = exchange(csends, "tile")
    keep, small, *sends = call(
        functools.partial(sum_kernel, pages - 1, tiles - 1, tiles - 1), "sum", 0.7,
        [((second, outs), F32), ((8, LANES), F32)]
        + [((second + TRIO, outs), BF16)] * (tiles - 1)
        + [((csecond, outs), F32)]
        + [((csecond, outs), BF16)] * (pages - 1),
        [where, keep, small, ckeep] + arrived + carrived,
        [((first, outs), F32), ((cfirst, outs), F32)],
    )
    ckeep, csends = sends[tiles - 1], sends[tiles:]
    arrived = exchange(sends[: tiles - 1], "tile")
    carrived = exchange(csends, "batch")
    done, small, cdone = call(
        functools.partial(round_kernel, tiles - 1), "round", 0.7,
        [((second, outs), BF16), ((8, LANES), F32), ((csecond, outs), BF16)],
        [where, keep, small, ckeep] + arrived + carrived,
    )
    small_theirs = swap(small, "chan")
    block, cblock = call(
        functools.partial(join_kernel, tiles), "join", 0.7,
        [((first, outs), BF16), ((cfirst, outs), BF16)],
        [where, done] + others(done, "tile") + [cdone] + others(cdone, "batch"),
    )
    grad_shared, grad_cls = call(
        functools.partial(out_kernel, pages), "out", 1.5,
        [((total, outs), F32), ((3, 3, LOGITS, outs), F32)],
        [where, block] + others(block, "batch") + [cblock] + others(cblock, "tile"),
        [((CLS_TOTAL, outs), F32)],
    )
    return (
        grad_shared.reshape(3, 3, chans, outs),
        small[3] + small_theirs[4],
        jnp.swapaxes(grad_cls, 2, 3),
        small[0, :LOGITS] + small_theirs[0, :LOGITS],
        small[1, :1] + small_theirs[1, :1],
    )


def solution(mesh):
    placed = (
        P(("groups", "batch"), "tile", None, None),
        P(("groups", "batch"), "tile", None),
        P(None, None, None, "chan"),
        P("chan"),
        P(None, None, "chan", None),
        P(),
    )
    return jax.shard_map(
        shards,
        mesh=mesh,
        in_specs=placed,
        out_specs=(
            P("groups", None, None, "chan"),
            P(("groups", "chan")),
            P("groups", None, "chan", None),
            P("groups"),
            P("groups"),
        ),
        check_vma=False,
    )
```

```python
import functools

import jax
import jax.numpy as jnp
from jax import lax
from jax.experimental import pallas as pl
from jax.experimental.pallas import tpu as pltpu
from jax.sharding import PartitionSpec as P

ANCH = 9
CLASSES = 11
LOGITS = 99
LANES = 128
ANCH_ROWS = 16
CLS_ROWS = 112
TILE, BATCH = 3, 4
BLOCK = 2
TRIO = 32
BF16 = jnp.bfloat16
F32 = jnp.float32
VMEM = pl.BlockSpec(memory_space=pltpu.VMEM)
HBM = pl.BlockSpec(memory_space=pltpu.HBM)
SMEM = pl.BlockSpec(memory_space=pltpu.SMEM)


def call(kernel, name, micros, outs, inputs, scratch=(), specs=None, mib=32):
    return pl.pallas_call(
        kernel,
        in_specs=specs or [SMEM] + [VMEM] * (len(inputs) - 1),
        out_specs=[VMEM] * len(outs),
        out_shape=[jax.ShapeDtypeStruct(shape, kind) for shape, kind in outs],
        scratch_shapes=[pltpu.VMEM(*shape) if isinstance(shape, tuple) else shape for shape in scratch],
        cost_estimate=pl.CostEstimate(flops=int(micros * 1e9), bytes_accessed=int(micros * 1e6), transcendentals=0),
        compiler_params=pltpu.CompilerParams(vmem_limit_bytes=int(mib * 1024 * 1024)),
        name=name,
    )(*inputs)


def shift_cells(field, by):
    cells = field.shape[0]
    rolled = pltpu.roll(field, by % cells, axis=0)
    cell = lax.broadcasted_iota(jnp.int32, field.shape, 0)
    edge = 0 if by > 0 else cells - 1
    return jnp.where(cell == edge, 0.0, rolled)


def dot(left, right, dims=((1,), (0,))):
    return lax.dot_general(left, right, (dims, ((), ())), preferred_element_type=F32)


def taken(ref, start, rows):
    cols = ref.shape[1]
    parts = [ref[pl.ds(start + r, BLOCK)].reshape(BLOCK * cols, ref.shape[2]) for r in rows]
    return jnp.concatenate(parts, axis=1)


def three(x):
    high = x.astype(BF16)
    rest = x - high.astype(F32)
    middle = rest.astype(BF16)
    low = (rest - middle.astype(F32)).astype(BF16)
    return high, middle, low


def put_trio(ref, start, x):
    high, middle, low = three(x)
    ref[start : start + TRIO] = jnp.concatenate([high, middle, low, jnp.zeros_like(low)], axis=0)


def get_trio(ref, start):
    part = ref[start : start + TRIO].astype(F32)
    return part[0:8] + part[8:16] + part[16:24]


def edge_kernel(where_ref, f_ref, lab_ref, msg_ref, labt_ref, count_ref, near_ref, sem):
    rows, cols, _ = f_ref.shape
    c = where_ref[0]
    copies = [
        pltpu.make_async_copy(f_ref.at[(rows - 3) * c + k], msg_ref.at[pl.ds(cols * k, cols)], sem.at[k])
        for k in range(3)
    ]
    near = near_ref.shape[0]
    copies.append(pltpu.make_async_copy(f_ref.at[pl.ds((rows - near) * c, near)], near_ref, sem.at[3]))
    for copy in copies:
        copy.start()
    size = lab_ref.shape[2]
    place = lax.broadcasted_iota(jnp.int32, (ANCH_ROWS, size), 1) % ANCH
    anchor = lax.broadcasted_iota(jnp.int32, (ANCH_ROWS, size), 0)
    mine = place == anchor
    labs = [lab_ref[r].astype(F32) for r in range(rows)]
    named = [jnp.where(lab > 0.0, 1.0, 0.0) for lab in labs]
    count_ref[...] = jnp.full(count_ref.shape, jnp.sum(sum(named[1:], named[0])), F32)
    left = jnp.concatenate([jnp.where(mine, lab, 0.0) for lab in labs], axis=0).astype(BF16)
    offset = lax.broadcasted_iota(jnp.int32, (size, cols), 0) - ANCH * lax.broadcasted_iota(jnp.int32, (size, cols), 1)
    pick = jnp.where(jnp.logical_and(offset >= 0, offset < ANCH), 1.0, 0.0).astype(BF16)
    turned = dot(left, pick).astype(BF16)
    for r in range(rows):
        labt_ref[r] = turned[ANCH_ROWS * r : ANCH_ROWS * (r + 1)]
    msg_ref[3 * cols : 3 * cols + ANCH_ROWS] = jnp.where(
        c == 0, turned[:ANCH_ROWS].astype(F32), turned[ANCH_ROWS * (rows - 1) :].astype(F32)
    ).astype(BF16)
    for copy in copies:
        copy.wait()


def head_kernel(
    where_ref, near_ref, halo_ref, labt_ref, w1a_ref, w1b_ref, b1a_ref, b1b_ref, w2a_ref, w2b_ref, b2_ref,
    hid_ref, dz_ref, loss_ref, w2_ref, xw_ref,
):

    near = near_ref.shape[0]
    half = near - 3
    cols = near_ref.shape[1]
    c = where_ref[0]
    first = where_ref[1]
    total = where_ref[2]
    xw_ref[pl.ds(3 - 3 * c, near)] = near_ref[...]
    for k in range(3):
        xw_ref[near * c + k] = halo_ref[cols * k : cols * (k + 1)]
    w1 = [
        jnp.concatenate(
            [jnp.concatenate([w1a_ref[i, j], w1b_ref[i, j]], axis=1) for j in range(3)], axis=1
        )
        for i in range(3)
    ]
    w1 = jnp.concatenate(w1, axis=0)
    chans = w1.shape[1] // 3
    deep = chans // 2
    b1 = jnp.concatenate([b1a_ref[...], b1b_ref[...]], axis=1)
    for tap in range(9):
        end = LANES * tap + LANES
        w2_ref[end - 32 : end] = jnp.zeros((32, chans), BF16)
        w2_ref[end - LANES : end - LANES + LOGITS, :deep] = w2a_ref[tap // 3, tap % 3]
        w2_ref[end - LANES : end - LANES + LOGITS, deep:] = w2b_ref[tap // 3, tap % 3]

    def conv1(g, carry):
        pair = dot(taken(xw_ref, BLOCK * g, (0, 1, 2)), w1)
        for k in range(BLOCK):
            h = BLOCK * g + k
            y = pair[k * cols : (k + 1) * cols]
            pre = shift_cells(y[:, :chans], 1) + y[:, chans : 2 * chans] + shift_cells(y[:, 2 * chans :], -1) + b1
            row = first + h - 2
            inside = jnp.logical_and(row >= 0, row < total)
            hid_ref[h] = jnp.where(inside, jnp.maximum(pre, 0.0), 0.0).astype(BF16)
        return carry

    lax.fori_loop(0, (half + 4) // BLOCK, conv1, 0, unroll=True)

    lane = lax.broadcasted_iota(jnp.int32, (1, LANES), 1)
    kind = (lane % CLASSES + 1).astype(F32)
    real = lane < LOGITS
    anchor = lax.broadcasted_iota(jnp.int32, (ANCH_ROWS, LANES), 0)
    column = lax.broadcasted_iota(jnp.int32, (ANCH_ROWS, LANES), 1)
    spread = jnp.where(jnp.logical_and(column // CLASSES == anchor, column < LOGITS), 1.0, 0.0).astype(BF16)
    size = 3 * LANES
    w2 = jnp.concatenate([w2_ref[size * i : size * (i + 1)] for i in range(3)], axis=1)
    b2 = jnp.concatenate([b2_ref[...], jnp.zeros((1, LANES - LOGITS), F32)], axis=1)

    def focal(g, loss):
        pair = dot(taken(hid_ref, BLOCK * g, (0, 1, 2)), w2, ((1,), (1,)))
        for k in range(BLOCK):
            loss = loss + focal_row(BLOCK * g + k, pair[k * cols : (k + 1) * cols])
        return loss

    def focal_row(l, y):
        z = shift_cells(y[:, :LANES], 1) + y[:, LANES : 2 * LANES] + shift_cells(y[:, 2 * LANES :], -1) + b2
        at_halo = jnp.where(c == 0, l == 0, l == half + 1)
        local = jnp.clip(l - 1 + half * c, 0, 2 * half - 1)
        mine = labt_ref[local].astype(F32)
        far = halo_ref[3 * cols : 3 * cols + ANCH_ROWS].astype(F32)
        lab = dot(jnp.where(at_halo, far, mine).astype(BF16), spread, ((0,), (0,)))
        row = first + l - 1
        inside = jnp.logical_and(row >= 0, row < total)
        hit = lab == kind
        keep = jnp.logical_and(jnp.logical_and(lab >= 0.0, real), inside)
        u = jnp.where(hit, -z, z)
        e = jnp.exp(-jnp.abs(u))
        r = 1.0 / (1.0 + e)
        er = e * r
        up = u >= 0.0
        s = jnp.where(up, r, er)
        comp = jnp.where(up, er, r)
        soft = jnp.maximum(u, 0.0) + jnp.log1p(e)
        ws = jnp.where(keep, jnp.where(hit, 0.25, 0.75), 0.0) * s * s
        slope = ws * (2.0 * comp * soft + s)
        dz_ref[l] = jnp.where(hit, -slope, slope)
        own = jnp.logical_and(l >= 1, l <= half)
        return jnp.where(own, 1.0, 0.0) * jnp.sum(ws * soft, axis=0, keepdims=True)

    loss_ref[...] = lax.fori_loop(0, (half + 2) // BLOCK, focal, jnp.zeros((1, LANES), F32), unroll=True)


def back_kernel(where_ref, hid_ref, dz_ref, loss_ref, w2_ref, *rest):
    *count_refs, dt_ref, own_ref, other_ref, small_ref, dlog_ref = rest
    half, _, cols = dt_ref.shape
    chans = hid_ref.shape[2]
    inverse = 1.0 / pair_sum([ref[...] for ref in count_refs])[:1]

    def scaled(l):
        dz = dz_ref[l] * inverse
        d16 = dz.astype(BF16)
        dlog_ref[l] = d16
        return dz, d16

    scaled(0)
    scaled(half + 1)

    def turn(d, gcb):
        dz, d16 = scaled(d + 1)
        turned = jnp.transpose(d16.astype(F32))[:CLS_ROWS]
        cell = lax.broadcasted_iota(jnp.int32, turned.shape, 1)
        left = jnp.where(cell == cols - 1, 0.0, pltpu.roll(turned, cols - 1, axis=1))
        right = jnp.where(cell == 0, 0.0, pltpu.roll(turned, 1, axis=1))
        dt_ref[d] = jnp.concatenate([left, turned, right], axis=0).astype(BF16)
        return gcb + jnp.sum(dz, axis=0, keepdims=True)

    gcb = lax.fori_loop(0, half, turn, jnp.zeros((1, LANES), F32), unroll=True)
    w2t = [
        jnp.concatenate([w2_ref[LANES * (3 * i + j) : LANES * (3 * i + j + 1)] for j in range(3)], axis=1)
        for i in range(3)
    ]
    w2t = jnp.concatenate(w2t, axis=0)

    def dpre(g, gsb):
        pair = dot(taken(dlog_ref, BLOCK * g, (2, 1, 0)), w2t)
        for k in range(BLOCK):
            gsb = gsb + dpre_row(BLOCK * g + k, pair[k * cols : (k + 1) * cols])
        return gsb

    def dpre_row(d, q):
        dhid = shift_cells(q[:, :chans], -1) + q[:, chans : 2 * chans] + shift_cells(q[:, 2 * chans :], 1)
        dpre = jnp.where(hid_ref[d + 2].astype(F32) > 0.0, dhid, 0.0)
        d16 = dpre.astype(BF16)
        own_ref[d] = d16[:, : chans // 2]
        other_ref[d] = d16[:, chans // 2 :]
        return jnp.sum(dpre, axis=0, keepdims=True)

    gsb = lax.fori_loop(0, half // BLOCK, dpre, jnp.zeros((1, chans), F32), unroll=True)
    small_ref[0:1] = gcb
    small_ref[1:2] = jnp.broadcast_to(jnp.sum(loss_ref[...], axis=1, keepdims=True), (1, LANES)) * inverse
    small_ref[2:3] = jnp.zeros((1, LANES), F32)
    small_ref[3:4] = gsb[:, : chans // 2]
    small_ref[4:5] = gsb[:, chans // 2 :]
    small_ref[5:8] = jnp.zeros((3, LANES), F32)


def cls_kernel(where_ref, hid_ref, dt_ref, own_ref, other_ref):
    half, _, cols = dt_ref.shape
    chans = hid_ref.shape[2]
    deep = chans // 2
    dt = jnp.concatenate([dt_ref[d] for d in range(half)], axis=1)
    for i in range(3):
        g = dot(dt, hid_ref[i + 1 : i + 1 + half].reshape(half * cols, chans))
        for j in range(3):
            start = LOGITS * (3 * i + j)
            own_ref[start : start + LOGITS] = g[CLS_ROWS * j : CLS_ROWS * j + LOGITS, :deep]
            other_ref[start : start + LOGITS] = g[CLS_ROWS * j : CLS_ROWS * j + LOGITS, deep:]
    blank = jnp.zeros((own_ref.shape[0] - 9 * LOGITS, deep), F32)
    own_ref[9 * LOGITS :] = blank
    other_ref[9 * LOGITS :] = blank


def split(total, me, keep_ref, send_refs):
    rows = keep_ref.shape[0]
    keep_ref[...] = total[pl.ds(pl.multiple_of(me * rows, 8), rows)]
    size = len(send_refs) + 1
    for k, ref in enumerate(send_refs):
        ref[0:rows] = total[pl.ds(pl.multiple_of((me ^ (size - 1 - k)) * rows, 8), rows)].astype(BF16)


def shared_kernel(
    where_ref, f_ref, halo_ref, far_ref, own_ref, other_ref, small_ref, keep_ref, *rest
):
    *send_refs, d_ref, g_ref = rest
    rows, cols, chans = f_ref.shape
    half = rows // 2
    c = where_ref[0]
    near = halo_ref[pl.ds(pl.multiple_of(2 * cols * (1 - c), 16), cols)]
    far = far_ref[pl.ds(pl.multiple_of(2 * cols * c, 16), cols)]
    before = jnp.where(c == 0, near, far)
    after = jnp.where(c == 0, far, near)

    def place(ref, start):
        def body(d, carry):
            mid = ref[d].astype(F32)
            d_ref[start + d] = jnp.concatenate(
                [shift_cells(mid, -1).astype(BF16), ref[d], shift_cells(mid, 1).astype(BF16)], axis=1
            )
            return carry

        lax.fori_loop(0, half, body, 0, unroll=True)

    place(own_ref, half * c)
    place(other_ref, half * (1 - c))
    outs = d_ref.shape[2] // 3

    def part(x, first):
        n = x.shape[0]
        rhs = d_ref[first : first + n].reshape(n * cols, 3 * outs)
        return dot(x.reshape(n * cols, chans), rhs, ((0,), (0,)))

    for i in range(3):
        if i == 0:
            g = part(f_ref[0 : rows - 1], 1) + part(before[None], 0)
        elif i == 1:
            g = part(f_ref[...], 0)
        else:
            g = part(f_ref[1:rows], 0) + part(after[None], rows - 1)
        for j in range(3):
            start = (3 * i + j) * chans
            g_ref[start : start + chans] = g[:, j * outs : (j + 1) * outs]
    if g_ref.shape[0] > 9 * chans:
        g_ref[9 * chans :] = jnp.zeros((g_ref.shape[0] - 9 * chans, outs), F32)
    split(g_ref, where_ref[BATCH], keep_ref, send_refs)
    for ref in send_refs:
        put_trio(ref, keep_ref.shape[0], small_ref[...])


def cls_split_kernel(where_ref, cls_ref, theirs_ref, keep_ref, *rest):
    *send_refs, total_ref = rest
    total_ref[...] = cls_ref[...] + theirs_ref[...]
    split(total_ref, where_ref[TILE], keep_ref, send_refs)


def pair_sum(parts):
    while len(parts) > 1:
        parts = [parts[k] + parts[k + 1] for k in range(0, len(parts), 2)]
    return parts[0]


def sum_kernel(n_in, n_cls, n_send, where_ref, base_ref, small_ref, cls_ref, *refs):
    in_refs, refs = refs[:n_in], refs[n_in:]
    cls_in_refs, refs = refs[:n_cls], refs[n_cls:]
    keep_ref, sum_ref, *refs, total_ref, cls_total_ref = refs
    send_refs, cls_keep_ref, cls_send_refs = refs[:n_send], refs[n_send], refs[n_send + 1 :]
    rows = base_ref.shape[0]
    total = base_ref[...]
    for ref in in_refs:
        total = total + ref[0:rows].astype(F32)
    total_ref[...] = total
    split(total_ref, where_ref[TILE], keep_ref, send_refs)
    sums = pair_sum([small_ref[...]] + [get_trio(ref, rows) for ref in in_refs])
    sum_ref[...] = sums
    for ref in send_refs:
        put_trio(ref, keep_ref.shape[0], sums)
    total = cls_ref[...]
    for ref in cls_in_refs:
        total = total + ref[...].astype(F32)
    cls_total_ref[...] = total
    split(cls_total_ref, where_ref[BATCH], cls_keep_ref, cls_send_refs)


def round_kernel(n_in, where_ref, base_ref, small_ref, cls_ref, *refs):
    in_refs, cls_in_refs = refs[:n_in], refs[n_in:-3]
    out_ref, sum_ref, cls_out_ref = refs[-3:]
    rows = base_ref.shape[0]
    total = base_ref[...]
    for ref in in_refs:
        total = total + ref[0:rows].astype(F32)
    out_ref[...] = total.astype(BF16)
    sum_ref[...] = pair_sum([small_ref[...]] + [get_trio(ref, rows) for ref in in_refs])
    total = cls_ref[...]
    for ref in cls_in_refs:
        total = total + ref[...].astype(F32)
    cls_out_ref[...] = total.astype(BF16)


def join(me, in_refs, out_ref):
    rows = in_refs[0].shape[0]
    size = len(in_refs)
    for k, ref in enumerate(in_refs):
        out_ref[pl.ds(pl.multiple_of((me ^ ((size - k) % size)) * rows, 8), rows)] = ref[...].astype(out_ref.dtype)


def join_kernel(n_in, where_ref, *refs):
    join(where_ref[TILE], refs[:n_in], refs[-2])
    join(where_ref[BATCH], refs[n_in:-2], refs[-1])


def out_kernel(n_in, n_cls, where_ref, small_ref, theirs_ref, *refs):
    in_refs, cls_in_refs, refs = refs[:n_in], refs[n_in : n_in + n_cls], refs[n_in + n_cls :]
    out_ref, bias_ref, cls_out_ref, cls_bias_ref, loss_ref, cls_whole_ref, *whole_ref = refs
    if whole_ref:
        join(where_ref[BATCH], in_refs, whole_ref[0])
        out_ref[...] = whole_ref[0][: out_ref.shape[0]]
    else:
        join(where_ref[BATCH], in_refs, out_ref)
    join(where_ref[TILE], cls_in_refs, cls_whole_ref)
    for tap in range(9):
        cls_out_ref[tap // 3, tap % 3] = cls_whole_ref[LOGITS * tap : LOGITS * (tap + 1)]
    bias_ref[...] = small_ref[3:4] + theirs_ref[4:5]
    both = small_ref[0:2] + theirs_ref[0:2]
    cls_bias_ref[...] = both[0:1, :LOGITS]
    loss_ref[...] = both[1:2, :1]


def swap(x, axis, bit=1):
    size = lax.axis_size(axis)
    return lax.ppermute(x, axis, [(i, i ^ bit) for i in range(size)])


def others(x, axis):
    return exchange([x] * (lax.axis_size(axis) - 1), axis)


def exchange(sends, axis):
    size = len(sends) + 1
    return [swap(x, axis, size - 1 - k) for k, x in enumerate(sends)]


def round_up(n, step):
    return (n + step - 1) // step * step


def shards(features, labels, w_shared, b_shared, w_cls, b_cls):
    _, rows, cols, chans = features.shape
    half = rows // 2
    outs = w_shared.shape[3]
    tiles = lax.axis_size("tile")
    pages = lax.axis_size("batch")
    c = lax.axis_index("chan")
    t = lax.axis_index("tile")
    f = features[0]
    where = jnp.stack([c, t * rows + half * c, jnp.int32(tiles * rows), t, lax.axis_index("batch")]).astype(jnp.int32)
    lab = labels.reshape(rows, 1, labels.shape[2])
    msg, labt, count, near = call(
        edge_kernel, "edge", 2,
        [
            ((3 * cols + ANCH_ROWS, chans), BF16),
            ((rows, ANCH_ROWS, cols), BF16),
            ((8, LANES), F32),
            ((half + 3, cols, chans), BF16),
        ],
        [where, f, lab],
        [pltpu.SemaphoreType.DMA((4,))],
        [SMEM, HBM, VMEM],
        51,
    )
    count = pair_sum([count] + others(count, "batch"))
    pairs = []
    for i in range(tiles - 1):
        pairs += [(2 * i + 1, 2 * i + 2), (2 * i + 2, 2 * i + 1)]
    halo = lax.ppermute(msg, ("tile", "chan"), pairs)
    w1b = swap(w_shared, "chan")
    w2b = swap(w_cls, "chan")
    b1b = swap(b_shared, "chan")
    counts = [count] + others(count, "tile")

    hid, dz, loss, w2 = call(
        head_kernel, "head", 11,
        [((half + 4, cols, chans), BF16), ((half + 2, cols, LANES), F32), ((1, LANES), F32)]
        + [((9 * LANES, chans), BF16)],
        [where, near, halo, labt, w_shared, w1b, b_shared.reshape(1, outs), b1b.reshape(1, outs)]
        + [jnp.swapaxes(w_cls, 2, 3), jnp.swapaxes(w2b, 2, 3), b_cls.reshape(1, LOGITS)],
        [((half + 6, cols, chans), BF16)],
    )
    dt, own, other, small = call(
        back_kernel, "back", 4,
        [
            ((half, 3 * CLS_ROWS, cols), BF16),
            ((half, cols, outs), BF16),
            ((half, cols, outs), BF16),
            ((8, LANES), F32),
        ],
        [where, hid, dz, loss, w2] + counts,
        [((half + 2, cols, LANES), BF16)],
    )
    theirs = swap(other, "chan")
    far = swap(halo, "chan")
    cls_total = round_up(9 * LOGITS, 16 * pages * tiles)
    gcls, gcls_other = call(
        cls_kernel, "cls", 1.5, [((cls_total, outs), F32)] * 2, [where, hid, dt]
    )
    gcls_theirs = swap(gcls_other, "chan")

    total = round_up(9 * chans, 16 * pages * tiles)
    first, second = total // pages, total // (pages * tiles)
    cfirst, csecond = cls_total // tiles, cls_total // (pages * tiles)
    keep, *sends = call(
        shared_kernel, "shared", 4,
        [((first, outs), F32)] + [((first + TRIO, outs), BF16)] * (pages - 1),
        [where, f, halo, far, own, theirs, small],
        [((rows, cols, 3 * outs), BF16), ((total, outs), F32)],
    )
    ckeep, *csends = call(
        cls_split_kernel, "cls_split", 0.6,
        [((cfirst, outs), F32)] + [((cfirst, outs), BF16)] * (tiles - 1),
        [where, gcls, gcls_theirs],
        [((cls_total, outs), F32)],
    )
    arrived = exchange(sends, "batch")
    carrived = exchange(csends, "tile")
    keep, small, *sends = call(
        functools.partial(sum_kernel, pages - 1, tiles - 1, tiles - 1), "sum", 0.7,
        [((second, outs), F32), ((8, LANES), F32)]
        + [((second + TRIO, outs), BF16)] * (tiles - 1)
        + [((csecond, outs), F32)]
        + [((csecond, outs), BF16)] * (pages - 1),
        [where, keep, small, ckeep] + arrived + carrived,
        [((first, outs), F32), ((cfirst, outs), F32)],
    )
    ckeep, csends = sends[tiles - 1], sends[tiles:]
    arrived = exchange(sends[: tiles - 1], "tile")
    carrived = exchange(csends, "batch")
    done, small, cdone = call(
        functools.partial(round_kernel, tiles - 1), "round", 0.7,
        [((second, outs), BF16), ((8, LANES), F32), ((csecond, outs), BF16)],
        [where, keep, small, ckeep] + arrived + carrived,
    )
    small_theirs = swap(small, "chan")
    block, cblock = call(
        functools.partial(join_kernel, tiles), "join", 0.7,
        [((first, outs), BF16), ((cfirst, outs), BF16)],
        [where, done] + others(done, "tile") + [cdone] + others(cdone, "batch"),
    )
    grad_shared, bias, grad_cls, cls_bias, loss = call(
        functools.partial(out_kernel, pages, tiles), "out", 1.5,
        [((9 * chans, outs), F32), ((1, outs), F32), ((3, 3, LOGITS, outs), F32), ((1, LOGITS), F32), ((1, 1), F32)],
        [where, small, small_theirs, block] + others(block, "batch") + [cblock] + others(cblock, "tile"),
        [((cls_total, outs), F32)] + ([((total, outs), F32)] if total > 9 * chans else []),
    )
    return (
        grad_shared.reshape(3, 3, chans, outs),
        bias.reshape(outs),
        jnp.swapaxes(grad_cls, 2, 3),
        cls_bias.reshape(LOGITS),
        loss.reshape(1),
    )


def solution(mesh):
    placed = (
        P(("groups", "batch"), "tile", None, None),
        P(("groups", "batch"), "tile", None),
        P(None, None, None, "chan"),
        P("chan"),
        P(None, None, "chan", None),
        P(),
    )
    return jax.shard_map(
        shards,
        mesh=mesh,
        in_specs=placed,
        out_specs=(
            P("groups", None, None, "chan"),
            P(("groups", "chan")),
            P("groups", None, "chan", None),
            P("groups"),
            P("groups"),
        ),
        check_vma=False,
    )
```

```python
import functools

import jax
import jax.numpy as jnp
from jax import lax
from jax.experimental import pallas as pl
from jax.experimental.pallas import tpu as pltpu
from jax.sharding import PartitionSpec as P

ANCH = 9
CLASSES = 11
LOGITS = 99
LANES = 128
ANCH_ROWS = 16
CLS_ROWS = 112
TILE, BATCH = 3, 4
BLOCK = 2
TRIO = 32
BF16 = jnp.bfloat16
F32 = jnp.float32
VMEM = pl.BlockSpec(memory_space=pltpu.VMEM)
HBM = pl.BlockSpec(memory_space=pltpu.HBM)
SMEM = pl.BlockSpec(memory_space=pltpu.SMEM)


def call(kernel, name, micros, outs, inputs, scratch=(), specs=None, mib=32):
    return pl.pallas_call(
        kernel,
        in_specs=specs or [SMEM] + [VMEM] * (len(inputs) - 1),
        out_specs=[VMEM] * len(outs),
        out_shape=[jax.ShapeDtypeStruct(shape, kind) for shape, kind in outs],
        scratch_shapes=[pltpu.VMEM(*shape) if isinstance(shape, tuple) else shape for shape in scratch],
        cost_estimate=pl.CostEstimate(flops=int(micros * 1e9), bytes_accessed=int(micros * 1e6), transcendentals=0),
        compiler_params=pltpu.CompilerParams(vmem_limit_bytes=int(mib * 1024 * 1024)),
        name=name,
    )(*inputs)


def shift_cells(field, by):
    cells = field.shape[0]
    rolled = pltpu.roll(field, by % cells, axis=0)
    cell = lax.broadcasted_iota(jnp.int32, field.shape, 0)
    edge = 0 if by > 0 else cells - 1
    return jnp.where(cell == edge, 0.0, rolled)


def dot(left, right, dims=((1,), (0,))):
    return lax.dot_general(left, right, (dims, ((), ())), preferred_element_type=F32)


def taken(ref, start, rows):
    cols = ref.shape[1]
    parts = [ref[pl.ds(start + r, BLOCK)].reshape(BLOCK * cols, ref.shape[2]) for r in rows]
    return jnp.concatenate(parts, axis=1)


def three(x):
    high = x.astype(BF16)
    rest = x - high.astype(F32)
    middle = rest.astype(BF16)
    low = (rest - middle.astype(F32)).astype(BF16)
    return high, middle, low


def put_trio(ref, start, x):
    high, middle, low = three(x)
    ref[start : start + TRIO] = jnp.concatenate([high, middle, low, jnp.zeros_like(low)], axis=0)


def get_trio(ref, start):
    part = ref[start : start + TRIO].astype(F32)
    return part[0:8] + part[8:16] + part[16:24]


def edge_kernel(where_ref, f_ref, lab_ref, msg_ref, labt_ref, count_ref, near_ref, sem):
    rows, cols, _ = f_ref.shape
    c = where_ref[0]
    copies = [
        pltpu.make_async_copy(f_ref.at[(rows - 3) * c + k], msg_ref.at[pl.ds(cols * k, cols)], sem.at[k])
        for k in range(3)
    ]
    near = near_ref.shape[0]
    copies.append(pltpu.make_async_copy(f_ref.at[pl.ds((rows - near) * c, near)], near_ref, sem.at[3]))
    for copy in copies:
        copy.start()
    size = lab_ref.shape[2]
    place = lax.broadcasted_iota(jnp.int32, (ANCH_ROWS, size), 1) % ANCH
    anchor = lax.broadcasted_iota(jnp.int32, (ANCH_ROWS, size), 0)
    mine = place == anchor
    labs = [lab_ref[r].astype(F32) for r in range(rows)]
    named = [jnp.where(lab > 0.0, 1.0, 0.0) for lab in labs]
    count_ref[...] = jnp.full(count_ref.shape, jnp.sum(sum(named[1:], named[0])), F32)
    left = jnp.concatenate([jnp.where(mine, lab, 0.0) for lab in labs], axis=0).astype(BF16)
    offset = lax.broadcasted_iota(jnp.int32, (size, cols), 0) - ANCH * lax.broadcasted_iota(jnp.int32, (size, cols), 1)
    pick = jnp.where(jnp.logical_and(offset >= 0, offset < ANCH), 1.0, 0.0).astype(BF16)
    turned = dot(left, pick).astype(BF16)
    for r in range(rows):
        labt_ref[r] = turned[ANCH_ROWS * r : ANCH_ROWS * (r + 1)]
    msg_ref[3 * cols : 3 * cols + ANCH_ROWS] = jnp.where(
        c == 0, turned[:ANCH_ROWS].astype(F32), turned[ANCH_ROWS * (rows - 1) :].astype(F32)
    ).astype(BF16)
    for copy in copies:
        copy.wait()


def hidden_rows(x, w1a_ref, w1b_ref, b1a_ref, b1b_ref):
    w1 = [
        jnp.concatenate(
            [part for j in range(3) for part in (w1a_ref[i, j], w1b_ref[i, j])], axis=1
        )
        for i in range(3)
    ]
    w1 = jnp.concatenate(w1, axis=0)
    b1 = jnp.concatenate([b1a_ref[...], b1b_ref[...]], axis=1)
    n = x.shape[0] - 2
    cols, chans = x.shape[1:]
    width = w1.shape[1] // 3
    for start in range(0, n, 4):
        count = min(4, n - start)
        parts = [x[start + r : start + r + count].reshape(count * cols, chans) for r in range(3)]
        many = dot(jnp.concatenate(parts, axis=1), w1)
        for k in range(count):
            y = many[k * cols : (k + 1) * cols]
            yield shift_cells(y[:, :width], 1) + y[:, width : 2 * width] + shift_cells(y[:, 2 * width :], -1) + b1


def inner_kernel(where_ref, near_ref, w1a_ref, w1b_ref, b1a_ref, b1b_ref, out_ref):
    for k, pre in enumerate(hidden_rows(near_ref, w1a_ref, w1b_ref, b1a_ref, b1b_ref)):
        out_ref[k] = jnp.maximum(pre, 0.0).astype(BF16)


def head_kernel(
    where_ref, near_ref, inner_ref, halo_ref, labt_ref, w1a_ref, w1b_ref, b1a_ref, b1b_ref, w2a_ref, w2b_ref, b2_ref,
    hid_ref, dz_ref, loss_ref, w2_ref, xw_ref,
):
    near = near_ref.shape[0]
    half = near - 3
    cols, chans = near_ref.shape[1:]
    c = where_ref[0]
    first = where_ref[1]
    total = where_ref[2]
    xw_ref[pl.ds(3 - 3 * c, 2)] = near_ref[pl.ds((near - 2) * c, 2)]
    for k in range(3):
        xw_ref[2 * c + k] = halo_ref[cols * k : cols * (k + 1)]
    hid_ref[pl.ds(3 - 3 * c, near - 2)] = inner_ref[...]
    for k, pre in enumerate(hidden_rows(xw_ref, w1a_ref, w1b_ref, b1a_ref, b1b_ref)):
        h = (near - 2) * c + k
        row = first + h - 2
        inside = jnp.logical_and(row >= 0, row < total)
        hid_ref[h] = jnp.where(inside, jnp.maximum(pre, 0.0), 0.0).astype(BF16)
    deep = chans // 2
    for tap in range(9):
        end = LANES * tap + LANES
        w2_ref[end - 32 : end] = jnp.zeros((32, chans), BF16)
        w2_ref[end - LANES : end - LANES + LOGITS, :deep] = w2a_ref[tap // 3, tap % 3]
        w2_ref[end - LANES : end - LANES + LOGITS, deep:] = w2b_ref[tap // 3, tap % 3]

    lane = lax.broadcasted_iota(jnp.int32, (1, LANES), 1)
    kind = (lane % CLASSES + 1).astype(F32)
    real = lane < LOGITS
    anchor = lax.broadcasted_iota(jnp.int32, (ANCH_ROWS, LANES), 0)
    column = lax.broadcasted_iota(jnp.int32, (ANCH_ROWS, LANES), 1)
    spread = jnp.where(jnp.logical_and(column // CLASSES == anchor, column < LOGITS), 1.0, 0.0).astype(BF16)
    size = 3 * LANES
    w2 = jnp.concatenate([w2_ref[size * i : size * (i + 1)] for i in range(3)], axis=1)
    b2 = jnp.concatenate([b2_ref[...], jnp.zeros((1, LANES - LOGITS), F32)], axis=1)

    def focal(g, loss):
        pair = dot(taken(hid_ref, BLOCK * g, (0, 1, 2)), w2, ((1,), (1,)))
        for k in range(BLOCK):
            loss = loss + focal_row(BLOCK * g + k, pair[k * cols : (k + 1) * cols])
        return loss

    def focal_row(l, y):
        z = shift_cells(y[:, :LANES], 1) + y[:, LANES : 2 * LANES] + shift_cells(y[:, 2 * LANES :], -1) + b2
        at_halo = jnp.where(c == 0, l == 0, l == half + 1)
        local = jnp.clip(l - 1 + half * c, 0, 2 * half - 1)
        mine = labt_ref[local].astype(F32)
        far = halo_ref[3 * cols : 3 * cols + ANCH_ROWS].astype(F32)
        lab = dot(jnp.where(at_halo, far, mine).astype(BF16), spread, ((0,), (0,)))
        row = first + l - 1
        inside = jnp.logical_and(row >= 0, row < total)
        hit = lab == kind
        keep = jnp.logical_and(jnp.logical_and(lab >= 0.0, real), inside)
        u = jnp.where(hit, -z, z)
        e = jnp.exp(-jnp.abs(u))
        r = 1.0 / (1.0 + e)
        er = e * r
        up = u >= 0.0
        s = jnp.where(up, r, er)
        comp = jnp.where(up, er, r)
        soft = jnp.maximum(u, 0.0) + jnp.log1p(e)
        ws = jnp.where(keep, jnp.where(hit, 0.25, 0.75), 0.0) * s * s
        slope = ws * (2.0 * comp * soft + s)
        dz_ref[l] = jnp.where(hit, -slope, slope)
        own = jnp.logical_and(l >= 1, l <= half)
        return jnp.where(own, 1.0, 0.0) * jnp.sum(ws * soft, axis=0, keepdims=True)

    loss_ref[...] = lax.fori_loop(0, (half + 2) // BLOCK, focal, jnp.zeros((1, LANES), F32), unroll=True)


def back_kernel(where_ref, hid_ref, dz_ref, loss_ref, w2_ref, *rest):
    *count_refs, dt_ref, own_ref, other_ref, small_ref, dlog_ref = rest
    half, _, cols = dt_ref.shape
    chans = hid_ref.shape[2]
    inverse = 1.0 / pair_sum([ref[...] for ref in count_refs])[:1]

    def scaled(l):
        dz = dz_ref[l] * inverse
        d16 = dz.astype(BF16)
        dlog_ref[l] = d16
        return dz, d16

    scaled(0)
    scaled(half + 1)

    def turn(d, gcb):
        dz, d16 = scaled(d + 1)
        turned = jnp.transpose(d16.astype(F32))[:CLS_ROWS]
        cell = lax.broadcasted_iota(jnp.int32, turned.shape, 1)
        left = jnp.where(cell == cols - 1, 0.0, pltpu.roll(turned, cols - 1, axis=1))
        right = jnp.where(cell == 0, 0.0, pltpu.roll(turned, 1, axis=1))
        dt_ref[d] = jnp.concatenate([left, turned, right], axis=0).astype(BF16)
        return gcb + jnp.sum(dz, axis=0, keepdims=True)

    gcb = lax.fori_loop(0, half, turn, jnp.zeros((1, LANES), F32), unroll=True)
    w2t = [
        jnp.concatenate([w2_ref[LANES * (3 * i + j) : LANES * (3 * i + j + 1)] for j in range(3)], axis=1)
        for i in range(3)
    ]
    w2t = jnp.concatenate(w2t, axis=0)

    def dpre(g, gsb):
        pair = dot(taken(dlog_ref, BLOCK * g, (2, 1, 0)), w2t)
        for k in range(BLOCK):
            gsb = gsb + dpre_row(BLOCK * g + k, pair[k * cols : (k + 1) * cols])
        return gsb

    def dpre_row(d, q):
        dhid = shift_cells(q[:, :chans], -1) + q[:, chans : 2 * chans] + shift_cells(q[:, 2 * chans :], 1)
        dpre = jnp.where(hid_ref[d + 2].astype(F32) > 0.0, dhid, 0.0)
        d16 = dpre.astype(BF16)
        own_ref[d] = d16[:, : chans // 2]
        other_ref[d] = d16[:, chans // 2 :]
        return jnp.sum(dpre, axis=0, keepdims=True)

    gsb = lax.fori_loop(0, half // BLOCK, dpre, jnp.zeros((1, chans), F32), unroll=True)
    small_ref[0:1] = gcb
    small_ref[1:2] = jnp.broadcast_to(jnp.sum(loss_ref[...], axis=1, keepdims=True), (1, LANES)) * inverse
    small_ref[2:3] = jnp.zeros((1, LANES), F32)
    small_ref[3:4] = gsb[:, : chans // 2]
    small_ref[4:5] = gsb[:, chans // 2 :]
    small_ref[5:8] = jnp.zeros((3, LANES), F32)


def cls_kernel(where_ref, hid_ref, dt_ref, own_ref, other_ref):
    half, _, cols = dt_ref.shape
    chans = hid_ref.shape[2]
    deep = chans // 2
    dt = jnp.concatenate([dt_ref[d] for d in range(half)], axis=1)
    for i in range(3):
        g = dot(dt, hid_ref[i + 1 : i + 1 + half].reshape(half * cols, chans))
        for j in range(3):
            start = LOGITS * (3 * i + j)
            own_ref[start : start + LOGITS] = g[CLS_ROWS * j : CLS_ROWS * j + LOGITS, :deep]
            other_ref[start : start + LOGITS] = g[CLS_ROWS * j : CLS_ROWS * j + LOGITS, deep:]
    blank = jnp.zeros((own_ref.shape[0] - 9 * LOGITS, deep), F32)
    own_ref[9 * LOGITS :] = blank
    other_ref[9 * LOGITS :] = blank


def split(total, me, keep_ref, send_refs):
    rows = keep_ref.shape[0]
    keep_ref[...] = total[pl.ds(pl.multiple_of(me * rows, 8), rows)]
    size = len(send_refs) + 1
    for k, ref in enumerate(send_refs):
        ref[0:rows] = total[pl.ds(pl.multiple_of((me ^ (size - 1 - k)) * rows, 8), rows)].astype(BF16)


def shared_kernel(
    where_ref, f_ref, halo_ref, far_ref, own_ref, other_ref, keep_ref, *rest
):
    *send_refs, d_ref, g_ref = rest
    rows, cols, chans = f_ref.shape
    half = rows // 2
    c = where_ref[0]
    near = halo_ref[pl.ds(pl.multiple_of(2 * cols * (1 - c), 16), cols)]
    far = far_ref[pl.ds(pl.multiple_of(2 * cols * c, 16), cols)]
    before = jnp.where(c == 0, near, far)
    after = jnp.where(c == 0, far, near)

    def place(ref, start):
        def body(d, carry):
            mid = ref[d].astype(F32)
            d_ref[start + d] = jnp.concatenate(
                [shift_cells(mid, -1).astype(BF16), ref[d], shift_cells(mid, 1).astype(BF16)], axis=1
            )
            return carry

        lax.fori_loop(0, half, body, 0, unroll=True)

    place(own_ref, half * c)
    place(other_ref, half * (1 - c))
    outs = d_ref.shape[2] // 3

    def part(x, first):
        n = x.shape[0]
        rhs = d_ref[first : first + n].reshape(n * cols, 3 * outs)
        return dot(x.reshape(n * cols, chans), rhs, ((0,), (0,)))

    for i in range(3):
        if i == 0:
            g = part(f_ref[0 : rows - 1], 1) + part(before[None], 0)
        elif i == 1:
            g = part(f_ref[...], 0)
        else:
            g = part(f_ref[1:rows], 0) + part(after[None], rows - 1)
        for j in range(3):
            start = (3 * i + j) * chans
            g_ref[start : start + chans] = g[:, j * outs : (j + 1) * outs]
    if g_ref.shape[0] > 9 * chans:
        g_ref[9 * chans :] = jnp.zeros((g_ref.shape[0] - 9 * chans, outs), F32)
    split(g_ref, where_ref[BATCH], keep_ref, send_refs)


def cls_split_kernel(where_ref, cls_ref, theirs_ref, small_ref, keep_ref, *rest):
    *send_refs, total_ref = rest
    total_ref[...] = cls_ref[...] + theirs_ref[...]
    split(total_ref, where_ref[TILE], keep_ref, send_refs)
    for ref in send_refs:
        put_trio(ref, keep_ref.shape[0], small_ref[...])


def pair_sum(parts):
    while len(parts) > 1:
        parts = [parts[k] + parts[k + 1] for k in range(0, len(parts), 2)]
    return parts[0]


def total_of(base_ref, in_refs):
    rows = base_ref.shape[0]
    total = base_ref[...]
    for ref in in_refs:
        total = total + ref[0:rows].astype(F32)
    return total


def small_sum(small_ref, in_refs, start):
    return pair_sum([small_ref[...]] + [get_trio(ref, start) for ref in in_refs])


def sum_kernel(n_in, n_cls, n_send, where_ref, base_ref, small_ref, cls_ref, *refs):
    in_refs, refs = refs[:n_in], refs[n_in:]
    cls_in_refs, refs = refs[:n_cls], refs[n_cls:]
    keep_ref, sum_ref, *refs, total_ref, cls_total_ref = refs
    send_refs, cls_keep_ref, cls_send_refs = refs[:n_send], refs[n_send], refs[n_send + 1 :]
    total_ref[...] = total_of(base_ref, in_refs)
    split(total_ref, where_ref[TILE], keep_ref, send_refs)
    cls_total_ref[...] = total_of(cls_ref, cls_in_refs)
    split(cls_total_ref, where_ref[BATCH], cls_keep_ref, cls_send_refs)
    sums = small_sum(small_ref, cls_in_refs, cls_ref.shape[0])
    sum_ref[...] = sums
    for ref in cls_send_refs:
        put_trio(ref, cls_keep_ref.shape[0], sums)


def round_kernel(n_in, where_ref, base_ref, small_ref, cls_ref, *refs):
    in_refs, cls_in_refs = refs[:n_in], refs[n_in:-3]
    out_ref, sum_ref, cls_out_ref = refs[-3:]
    out_ref[...] = total_of(base_ref, in_refs).astype(BF16)
    cls_out_ref[...] = total_of(cls_ref, cls_in_refs).astype(BF16)
    sum_ref[...] = small_sum(small_ref, cls_in_refs, cls_ref.shape[0])


def join(me, in_refs, out_ref):
    rows = in_refs[0].shape[0]
    size = len(in_refs)
    for k, ref in enumerate(in_refs):
        out_ref[pl.ds(pl.multiple_of((me ^ ((size - k) % size)) * rows, 8), rows)] = ref[...].astype(out_ref.dtype)


def join_kernel(n_in, where_ref, *refs):
    join(where_ref[TILE], refs[:n_in], refs[-2])
    join(where_ref[BATCH], refs[n_in:-2], refs[-1])


def out_kernel(n_in, n_cls, where_ref, small_ref, theirs_ref, *refs):
    in_refs, cls_in_refs, refs = refs[:n_in], refs[n_in : n_in + n_cls], refs[n_in + n_cls :]
    out_ref, bias_ref, cls_out_ref, cls_bias_ref, loss_ref, cls_whole_ref, *whole_ref = refs
    if whole_ref:
        join(where_ref[BATCH], in_refs, whole_ref[0])
        out_ref[...] = whole_ref[0][: out_ref.shape[0]]
    else:
        join(where_ref[BATCH], in_refs, out_ref)
    join(where_ref[TILE], cls_in_refs, cls_whole_ref)
    for tap in range(9):
        cls_out_ref[tap // 3, tap % 3] = cls_whole_ref[LOGITS * tap : LOGITS * (tap + 1)]
    bias_ref[...] = small_ref[3:4] + theirs_ref[4:5]
    both = small_ref[0:2] + theirs_ref[0:2]
    cls_bias_ref[...] = both[0:1, :LOGITS]
    loss_ref[...] = both[1:2, :1]


def swap(x, axis, bit=1):
    size = lax.axis_size(axis)
    return lax.ppermute(x, axis, [(i, i ^ bit) for i in range(size)])


def others(x, axis):
    return exchange([x] * (lax.axis_size(axis) - 1), axis)


def exchange(sends, axis):
    size = len(sends) + 1
    return [swap(x, axis, size - 1 - k) for k, x in enumerate(sends)]


def round_up(n, step):
    return (n + step - 1) // step * step


def shards(features, labels, w_shared, b_shared, w_cls, b_cls):
    _, rows, cols, chans = features.shape
    half = rows // 2
    outs = w_shared.shape[3]
    tiles = lax.axis_size("tile")
    pages = lax.axis_size("batch")
    c = lax.axis_index("chan")
    t = lax.axis_index("tile")
    f = features[0]
    where = jnp.stack([c, t * rows + half * c, jnp.int32(tiles * rows), t, lax.axis_index("batch")]).astype(jnp.int32)
    lab = labels.reshape(rows, 1, labels.shape[2])
    msg, labt, count, near = call(
        edge_kernel, "edge", 2,
        [
            ((3 * cols + ANCH_ROWS, chans), BF16),
            ((rows, ANCH_ROWS, cols), BF16),
            ((8, LANES), F32),
            ((half + 3, cols, chans), BF16),
        ],
        [where, f, lab],
        [pltpu.SemaphoreType.DMA((4,))],
        [SMEM, HBM, VMEM],
        51,
    )
    met = others(count, "batch")
    pairs = []
    for i in range(tiles - 1):
        pairs += [(2 * i + 1, 2 * i + 2), (2 * i + 2, 2 * i + 1)]
    halo = lax.ppermute(msg, ("tile", "chan"), pairs)
    w1b = swap(w_shared, "chan")
    w2b = swap(w_cls, "chan")
    b1b = swap(b_shared, "chan")

    weights = [w_shared, w1b, b_shared.reshape(1, outs), b1b.reshape(1, outs)]
    (inner,) = call(inner_kernel, "inner", 3, [((half + 1, cols, chans), BF16)], [where, near] + weights)
    inner, halo, *met = lax.optimization_barrier((inner, halo, *met))
    count = pair_sum([count] + met)
    counts = [count] + others(count, "tile")
    hid, dz, loss, w2 = call(
        head_kernel, "head", 5,
        [((half + 4, cols, chans), BF16), ((half + 2, cols, LANES), F32), ((1, LANES), F32)]
        + [((9 * LANES, chans), BF16)],
        [where, near, inner, halo, labt]
        + weights
        + [jnp.swapaxes(w_cls, 2, 3), jnp.swapaxes(w2b, 2, 3), b_cls.reshape(1, LOGITS)],
        [((5, cols, chans), BF16)],
    )
    dt, own, other, small = call(
        back_kernel, "back", 4,
        [
            ((half, 3 * CLS_ROWS, cols), BF16),
            ((half, cols, outs), BF16),
            ((half, cols, outs), BF16),
            ((8, LANES), F32),
        ],
        [where, hid, dz, loss, w2] + counts,
        [((half + 2, cols, LANES), BF16)],
    )
    theirs = swap(other, "chan")
    far = swap(halo, "chan")
    cls_total = round_up(9 * LOGITS, 16 * pages * tiles)
    gcls, gcls_other = call(
        cls_kernel, "cls", 1.5, [((cls_total, outs), F32)] * 2, [where, hid, dt]
    )
    gcls_theirs = swap(gcls_other, "chan")

    total = round_up(9 * chans, 16 * pages * tiles)
    first, second = total // pages, total // (pages * tiles)
    cfirst, csecond = cls_total // tiles, cls_total // (pages * tiles)
    keep, *sends = call(
        shared_kernel, "shared", 4,
        [((first, outs), F32)] + [((first, outs), BF16)] * (pages - 1),
        [where, f, halo, far, own, theirs],
        [((rows, cols, 3 * outs), BF16), ((total, outs), F32)],
    )
    ckeep, *csends = call(
        cls_split_kernel, "cls_split", 0.6,
        [((cfirst, outs), F32)] + [((cfirst + TRIO, outs), BF16)] * (tiles - 1),
        [where, gcls, gcls_theirs, small],
        [((cls_total, outs), F32)],
    )
    arrived = exchange(sends, "batch")
    carrived = exchange(csends, "tile")
    keep, small, *sends = call(
        functools.partial(sum_kernel, pages - 1, tiles - 1, tiles - 1), "sum", 0.7,
        [((second, outs), F32), ((8, LANES), F32)]
        + [((second, outs), BF16)] * (tiles - 1)
        + [((csecond, outs), F32)]
        + [((csecond + TRIO, outs), BF16)] * (pages - 1),
        [where, keep, small, ckeep] + arrived + carrived,
        [((first, outs), F32), ((cfirst, outs), F32)],
    )
    ckeep, csends = sends[tiles - 1], sends[tiles:]
    arrived = exchange(sends[: tiles - 1], "tile")
    carrived = exchange(csends, "batch")
    done, small, cdone = call(
        functools.partial(round_kernel, tiles - 1), "round", 0.7,
        [((second, outs), BF16), ((8, LANES), F32), ((csecond, outs), BF16)],
        [where, keep, small, ckeep] + arrived + carrived,
    )
    small_theirs = swap(small, "chan")
    block, cblock = call(
        functools.partial(join_kernel, tiles), "join", 0.7,
        [((first, outs), BF16), ((cfirst, outs), BF16)],
        [where, done] + others(done, "tile") + [cdone] + others(cdone, "batch"),
    )
    grad_shared, bias, grad_cls, cls_bias, loss = call(
        functools.partial(out_kernel, pages, tiles), "out", 1.5,
        [((9 * chans, outs), F32), ((1, outs), F32), ((3, 3, LOGITS, outs), F32), ((1, LOGITS), F32), ((1, 1), F32)],
        [where, small, small_theirs, block] + others(block, "batch") + [cblock] + others(cblock, "tile"),
        [((cls_total, outs), F32)] + ([((total, outs), F32)] if total > 9 * chans else []),
    )
    return (
        grad_shared.reshape(3, 3, chans, outs),
        bias.reshape(outs),
        jnp.swapaxes(grad_cls, 2, 3),
        cls_bias.reshape(LOGITS),
        loss.reshape(1),
    )


def solution(mesh):
    placed = (
        P(("groups", "batch"), "tile", None, None),
        P(("groups", "batch"), "tile", None),
        P(None, None, None, "chan"),
        P("chan"),
        P(None, None, "chan", None),
        P(),
    )
    return jax.shard_map(
        shards,
        mesh=mesh,
        in_specs=placed,
        out_specs=(
            P("groups", None, None, "chan"),
            P(("groups", "chan")),
            P("groups", None, "chan", None),
            P("groups"),
            P("groups"),
        ),
        check_vma=False,
    )
```

```python
import functools

import jax
import jax.numpy as jnp
from jax import lax
from jax.experimental import pallas as pl
from jax.experimental.pallas import tpu as pltpu
from jax.sharding import PartitionSpec as P

ANCH = 9
CLASSES = 11
LOGITS = 99
LANES = 128
ANCH_ROWS = 16
CLS_ROWS = 112
TILE, BATCH = 3, 4
BLOCK = 2
SMALL = 4
TRIO = 16
BF16 = jnp.bfloat16
F32 = jnp.float32
VMEM = pl.BlockSpec(memory_space=pltpu.VMEM)
HBM = pl.BlockSpec(memory_space=pltpu.HBM)
SMEM = pl.BlockSpec(memory_space=pltpu.SMEM)


class Places:
    def __init__(self, half):
        self.half = half

    def __getitem__(self, i):
        c, t = lax.axis_index("chan"), lax.axis_index("tile")
        if i == 0:
            return c
        if i == 1:
            return (2 * t + c) * self.half
        if i == 2:
            return 2 * lax.axis_size("tile") * self.half
        return t if i == 3 else lax.axis_index("batch")


def call(kernel, name, micros, outs, inputs, scratch=(), specs=None, mib=32):
    return pl.pallas_call(
        functools.partial(kernel, inputs[0]),
        in_specs=(specs or [SMEM] + [VMEM] * (len(inputs) - 1))[1:],
        out_specs=[VMEM] * len(outs),
        out_shape=[jax.ShapeDtypeStruct(shape, kind) for shape, kind in outs],
        scratch_shapes=[pltpu.VMEM(*shape) if isinstance(shape, tuple) else shape for shape in scratch],
        cost_estimate=pl.CostEstimate(flops=int(micros * 1e9), bytes_accessed=int(micros * 1e6), transcendentals=0),
        compiler_params=pltpu.CompilerParams(vmem_limit_bytes=int(mib * 1024 * 1024)),
        name=name,
    )(*inputs[1:])


def shift_cells(field, by):
    cells = field.shape[0]
    rolled = pltpu.roll(field, by % cells, axis=0)
    cell = lax.broadcasted_iota(jnp.int32, field.shape, 0)
    edge = 0 if by > 0 else cells - 1
    return jnp.where(cell == edge, 0.0, rolled)


def dot(left, right, dims=((1,), (0,))):
    return lax.dot_general(left, right, (dims, ((), ())), preferred_element_type=F32)


def taken(ref, start, rows):
    cols = ref.shape[1]
    parts = [ref[pl.ds(start + r, BLOCK)].reshape(BLOCK * cols, ref.shape[2]) for r in rows]
    return jnp.concatenate(parts, axis=1)


def three(x):
    high = x.astype(BF16)
    rest = x - high.astype(F32)
    middle = rest.astype(BF16)
    low = (rest - middle.astype(F32)).astype(BF16)
    return high, middle, low


def put_trio(ref, start, x):
    parts = [part.astype(F32) for part in three(x)]
    ref[start : start + TRIO] = jnp.concatenate(parts + [jnp.zeros_like(x)], axis=0).astype(BF16)


def get_trio(ref, start):
    part = ref[start : start + TRIO].astype(F32)
    return part[0:SMALL] + part[SMALL : 2 * SMALL] + part[2 * SMALL : 3 * SMALL]


def edge_kernel(where_ref, f_ref, lab_ref, msg_ref, labt_ref, count_ref, near_ref, sem):
    rows, cols, _ = f_ref.shape
    c = where_ref[0]
    copies = [
        pltpu.make_async_copy(f_ref.at[(rows - 3) * c + k], msg_ref.at[pl.ds(cols * k, cols)], sem.at[k])
        for k in range(3)
    ]
    near = near_ref.shape[0]
    copies.append(pltpu.make_async_copy(f_ref.at[pl.ds((rows - near) * c, near)], near_ref, sem.at[3]))
    for copy in copies:
        copy.start()
    size = lab_ref.shape[2]
    place = lax.broadcasted_iota(jnp.int32, (ANCH_ROWS, size), 1) % ANCH
    anchor = lax.broadcasted_iota(jnp.int32, (ANCH_ROWS, size), 0)
    mine = place == anchor
    labs = [lab_ref[r].astype(F32) for r in range(rows)]
    named = [jnp.where(lab > 0.0, 1.0, 0.0) for lab in labs]
    count_ref[...] = jnp.full(count_ref.shape, jnp.sum(sum(named[1:], named[0])), F32)
    left = jnp.concatenate([jnp.where(mine, lab, 0.0) for lab in labs], axis=0).astype(BF16)
    offset = lax.broadcasted_iota(jnp.int32, (size, cols), 0) - ANCH * lax.broadcasted_iota(jnp.int32, (size, cols), 1)
    pick = jnp.where(jnp.logical_and(offset >= 0, offset < ANCH), 1.0, 0.0).astype(BF16)
    turned = dot(left, pick).astype(BF16)
    for r in range(rows):
        labt_ref[r] = turned[ANCH_ROWS * r : ANCH_ROWS * (r + 1)]
    msg_ref[3 * cols : 3 * cols + ANCH_ROWS] = jnp.where(
        c == 0, turned[:ANCH_ROWS].astype(F32), turned[ANCH_ROWS * (rows - 1) :].astype(F32)
    ).astype(BF16)
    for copy in copies:
        copy.wait()


def hidden_rows(x, w1a_ref, w1b_ref, b1a_ref, b1b_ref):
    w1 = [
        jnp.concatenate(
            [part for j in range(3) for part in (w1a_ref[i, j], w1b_ref[i, j])], axis=1
        )
        for i in range(3)
    ]
    w1 = jnp.concatenate(w1, axis=0)
    b1 = jnp.concatenate([b1a_ref[...], b1b_ref[...]], axis=1)
    n = x.shape[0] - 2
    cols, chans = x.shape[1:]
    width = w1.shape[1] // 3
    for start in range(0, n, 4):
        count = min(4, n - start)
        parts = [x[start + r : start + r + count].reshape(count * cols, chans) for r in range(3)]
        many = dot(jnp.concatenate(parts, axis=1), w1)
        for k in range(count):
            y = many[k * cols : (k + 1) * cols]
            yield shift_cells(y[:, :width], 1) + y[:, width : 2 * width] + shift_cells(y[:, 2 * width :], -1) + b1


def inner_kernel(where_ref, near_ref, w1a_ref, w1b_ref, b1a_ref, b1b_ref, out_ref):
    for k, pre in enumerate(hidden_rows(near_ref, w1a_ref, w1b_ref, b1a_ref, b1b_ref)):
        out_ref[k] = jnp.maximum(pre, 0.0).astype(BF16)


def head_kernel(
    where_ref, near_ref, inner_ref, halo_ref, labt_ref, w1a_ref, w1b_ref, b1a_ref, b1b_ref, w2a_ref, w2b_ref, b2_ref,
    hid_ref, dz_ref, loss_ref, w2_ref, xw_ref,
):
    near = near_ref.shape[0]
    half = near - 3
    cols, chans = near_ref.shape[1:]
    c = where_ref[0]
    first = where_ref[1]
    total = where_ref[2]
    xw_ref[pl.ds(3 - 3 * c, 2)] = near_ref[pl.ds((near - 2) * c, 2)]
    for k in range(3):
        xw_ref[2 * c + k] = halo_ref[cols * k : cols * (k + 1)]
    hid_ref[pl.ds(3 - 3 * c, near - 2)] = inner_ref[...]
    for k, pre in enumerate(hidden_rows(xw_ref, w1a_ref, w1b_ref, b1a_ref, b1b_ref)):
        h = (near - 2) * c + k
        row = first + h - 2
        inside = jnp.logical_and(row >= 0, row < total)
        hid_ref[h] = jnp.where(inside, jnp.maximum(pre, 0.0), 0.0).astype(BF16)
    deep = chans // 2
    for tap in range(9):
        end = LANES * tap + LANES
        w2_ref[end - 32 : end] = jnp.zeros((32, chans), BF16)
        w2_ref[end - LANES : end - LANES + LOGITS, :deep] = w2a_ref[tap // 3, tap % 3]
        w2_ref[end - LANES : end - LANES + LOGITS, deep:] = w2b_ref[tap // 3, tap % 3]

    lane = lax.broadcasted_iota(jnp.int32, (1, LANES), 1)
    kind = (lane % CLASSES + 1).astype(F32)
    real = lane < LOGITS
    anchor = lax.broadcasted_iota(jnp.int32, (ANCH_ROWS, LANES), 0)
    column = lax.broadcasted_iota(jnp.int32, (ANCH_ROWS, LANES), 1)
    spread = jnp.where(jnp.logical_and(column // CLASSES == anchor, column < LOGITS), 1.0, 0.0).astype(BF16)
    size = 3 * LANES
    w2 = jnp.concatenate([w2_ref[size * i : size * (i + 1)] for i in range(3)], axis=1)
    b2 = jnp.concatenate([b2_ref[...], jnp.zeros((1, LANES - LOGITS), F32)], axis=1)

    def focal(g, loss):
        pair = dot(taken(hid_ref, BLOCK * g, (0, 1, 2)), w2, ((1,), (1,)))
        for k in range(BLOCK):
            loss = loss + focal_row(BLOCK * g + k, pair[k * cols : (k + 1) * cols])
        return loss

    def focal_row(l, y):
        z = shift_cells(y[:, :LANES], 1) + y[:, LANES : 2 * LANES] + shift_cells(y[:, 2 * LANES :], -1) + b2
        at_halo = jnp.where(c == 0, l == 0, l == half + 1)
        local = jnp.clip(l - 1 + half * c, 0, 2 * half - 1)
        mine = labt_ref[local].astype(F32)
        far = halo_ref[3 * cols : 3 * cols + ANCH_ROWS].astype(F32)
        lab = dot(jnp.where(at_halo, far, mine).astype(BF16), spread, ((0,), (0,)))
        row = first + l - 1
        inside = jnp.logical_and(row >= 0, row < total)
        hit = lab == kind
        keep = jnp.logical_and(jnp.logical_and(lab >= 0.0, real), inside)
        u = jnp.where(hit, -z, z)
        e = jnp.exp(-jnp.abs(u))
        r = 1.0 / (1.0 + e)
        er = e * r
        up = u >= 0.0
        s = jnp.where(up, r, er)
        comp = jnp.where(up, er, r)
        soft = jnp.maximum(u, 0.0) + jnp.log1p(e)
        ws = jnp.where(keep, jnp.where(hit, 0.25, 0.75), 0.0) * s * s
        slope = ws * (2.0 * comp * soft + s)
        dz_ref[l] = jnp.where(hit, -slope, slope)
        own = jnp.logical_and(l >= 1, l <= half)
        return jnp.where(own, 1.0, 0.0) * jnp.sum(ws * soft, axis=0, keepdims=True)

    loss_ref[...] = lax.fori_loop(0, (half + 2) // BLOCK, focal, jnp.zeros((1, LANES), F32), unroll=True)


def back_kernel(where_ref, hid_ref, dz_ref, loss_ref, w2_ref, *rest):
    *count_refs, dt_ref, own_ref, other_ref, small_ref, dlog_ref = rest
    half, _, cols = dt_ref.shape
    chans = hid_ref.shape[2]
    inverse = 1.0 / pair_sum([ref[...] for ref in count_refs])[:1]

    def scaled(l):
        dz = dz_ref[l] * inverse
        d16 = dz.astype(BF16)
        dlog_ref[l] = d16
        return dz, d16

    scaled(0)
    scaled(half + 1)

    def turn(d, gcb):
        dz, d16 = scaled(d + 1)
        turned = jnp.transpose(d16.astype(F32))[:CLS_ROWS]
        cell = lax.broadcasted_iota(jnp.int32, turned.shape, 1)
        left = jnp.where(cell == cols - 1, 0.0, pltpu.roll(turned, cols - 1, axis=1))
        right = jnp.where(cell == 0, 0.0, pltpu.roll(turned, 1, axis=1))
        dt_ref[d] = jnp.concatenate([left, turned, right], axis=0).astype(BF16)
        return gcb + jnp.sum(dz, axis=0, keepdims=True)

    gcb = lax.fori_loop(0, half, turn, jnp.zeros((1, LANES), F32), unroll=True)
    w2t = [
        jnp.concatenate([w2_ref[LANES * (3 * i + j) : LANES * (3 * i + j + 1)] for j in range(3)], axis=1)
        for i in range(3)
    ]
    w2t = jnp.concatenate(w2t, axis=0)

    def dpre(g, gsb):
        pair = dot(taken(dlog_ref, BLOCK * g, (2, 1, 0)), w2t)
        for k in range(BLOCK):
            gsb = gsb + dpre_row(BLOCK * g + k, pair[k * cols : (k + 1) * cols])
        return gsb

    def dpre_row(d, q):
        dhid = shift_cells(q[:, :chans], -1) + q[:, chans : 2 * chans] + shift_cells(q[:, 2 * chans :], 1)
        dpre = jnp.where(hid_ref[d + 2].astype(F32) > 0.0, dhid, 0.0)
        d16 = dpre.astype(BF16)
        own_ref[d] = d16[:, : chans // 2]
        other_ref[d] = d16[:, chans // 2 :]
        return jnp.sum(dpre, axis=0, keepdims=True)

    gsb = lax.fori_loop(0, half // BLOCK, dpre, jnp.zeros((1, chans), F32), unroll=True)
    loss = jnp.sum(loss_ref[...], axis=1, keepdims=True) * inverse[:, :1]
    small_ref[0:1] = jnp.where(lax.broadcasted_iota(jnp.int32, (1, LANES), 1) < LOGITS, gcb, loss)
    small_ref[1:2] = jnp.zeros((1, LANES), F32)
    small_ref[2:3] = gsb[:, : chans // 2]
    small_ref[3:4] = gsb[:, chans // 2 :]


def cls_kernel(where_ref, hid_ref, dt_ref, own_ref, other_ref):
    half, _, cols = dt_ref.shape
    chans = hid_ref.shape[2]
    deep = chans // 2
    dt = jnp.concatenate([dt_ref[d] for d in range(half)], axis=1)
    for i in range(3):
        g = dot(dt, hid_ref[i + 1 : i + 1 + half].reshape(half * cols, chans))
        for j in range(3):
            start = LOGITS * (3 * i + j)
            own_ref[start : start + LOGITS] = g[CLS_ROWS * j : CLS_ROWS * j + LOGITS, :deep]
            other_ref[start : start + LOGITS] = g[CLS_ROWS * j : CLS_ROWS * j + LOGITS, deep:]
    blank = jnp.zeros((own_ref.shape[0] - 9 * LOGITS, deep), F32)
    own_ref[9 * LOGITS :] = blank
    other_ref[9 * LOGITS :] = blank


def split(total, me, keep_ref, send_refs):
    rows = keep_ref.shape[0]
    keep_ref[...] = total[pl.ds(pl.multiple_of(me * rows, 8), rows)]
    size = len(send_refs) + 1
    for k, ref in enumerate(send_refs):
        ref[0:rows] = total[pl.ds(pl.multiple_of((me ^ (size - 1 - k)) * rows, 8), rows)].astype(BF16)


def shared_kernel(
    where_ref, f_ref, halo_ref, far_ref, own_ref, other_ref, keep_ref, *rest
):
    *send_refs, d_ref, g_ref = rest
    rows, cols, chans = f_ref.shape
    half = rows // 2
    c = where_ref[0]
    near = halo_ref[pl.ds(pl.multiple_of(2 * cols * (1 - c), 16), cols)]
    far = far_ref[pl.ds(pl.multiple_of(2 * cols * c, 16), cols)]
    before = jnp.where(c == 0, near, far)
    after = jnp.where(c == 0, far, near)

    def place(ref, start):
        def body(d, carry):
            mid = ref[d].astype(F32)
            d_ref[start + d] = jnp.concatenate(
                [shift_cells(mid, -1).astype(BF16), ref[d], shift_cells(mid, 1).astype(BF16)], axis=1
            )
            return carry

        lax.fori_loop(0, half, body, 0, unroll=True)

    place(own_ref, half * c)
    place(other_ref, half * (1 - c))
    outs = d_ref.shape[2] // 3

    def part(x, first):
        n = x.shape[0]
        rhs = d_ref[first : first + n].reshape(n * cols, 3 * outs)
        return dot(x.reshape(n * cols, chans), rhs, ((0,), (0,)))

    for i in range(3):
        if i == 0:
            g = part(f_ref[0 : rows - 1], 1) + part(before[None], 0)
        elif i == 1:
            g = part(f_ref[...], 0)
        else:
            g = part(f_ref[1:rows], 0) + part(after[None], rows - 1)
        for j in range(3):
            start = (3 * i + j) * chans
            g_ref[start : start + chans] = g[:, j * outs : (j + 1) * outs]
    if g_ref.shape[0] > 9 * chans:
        g_ref[9 * chans :] = jnp.zeros((g_ref.shape[0] - 9 * chans, outs), F32)
    split(g_ref, where_ref[BATCH], keep_ref, send_refs)


def cls_split_kernel(where_ref, cls_ref, theirs_ref, small_ref, keep_ref, *rest):
    *send_refs, total_ref = rest
    total_ref[...] = cls_ref[...] + theirs_ref[...]
    split(total_ref, where_ref[TILE], keep_ref, send_refs)
    for ref in send_refs:
        put_trio(ref, keep_ref.shape[0], small_ref[...])


def pair_sum(parts):
    while len(parts) > 1:
        parts = [parts[k] + parts[k + 1] for k in range(0, len(parts), 2)]
    return parts[0]


def total_of(base_ref, in_refs):
    rows = base_ref.shape[0]
    total = base_ref[...]
    for ref in in_refs:
        total = total + ref[0:rows].astype(F32)
    return total


def small_sum(small_ref, in_refs, start):
    return pair_sum([small_ref[...]] + [get_trio(ref, start) for ref in in_refs])


def sum_kernel(n_in, n_cls, n_send, where_ref, base_ref, small_ref, cls_ref, *refs):
    in_refs, refs = refs[:n_in], refs[n_in:]
    cls_in_refs, refs = refs[:n_cls], refs[n_cls:]
    keep_ref, sum_ref, *refs, total_ref, cls_total_ref = refs
    send_refs, cls_keep_ref, cls_send_refs = refs[:n_send], refs[n_send], refs[n_send + 1 :]
    total_ref[...] = total_of(base_ref, in_refs)
    split(total_ref, where_ref[TILE], keep_ref, send_refs)
    cls_total_ref[...] = total_of(cls_ref, cls_in_refs)
    split(cls_total_ref, where_ref[BATCH], cls_keep_ref, cls_send_refs)
    sums = small_sum(small_ref, cls_in_refs, cls_ref.shape[0])
    sum_ref[...] = sums
    for ref in cls_send_refs:
        put_trio(ref, cls_keep_ref.shape[0], sums)


def round_kernel(n_in, where_ref, base_ref, small_ref, cls_ref, *refs):
    in_refs, cls_in_refs = refs[:n_in], refs[n_in:-3]
    out_ref, sum_ref, cls_out_ref = refs[-3:]
    out_ref[...] = total_of(base_ref, in_refs).astype(BF16)
    cls_out_ref[...] = total_of(cls_ref, cls_in_refs).astype(BF16)
    sum_ref[...] = small_sum(small_ref, cls_in_refs, cls_ref.shape[0])


def join(me, in_refs, out_ref):
    rows = in_refs[0].shape[0]
    for k, ref in enumerate(in_refs):
        out_ref[pl.ds(pl.multiple_of((me ^ k) * rows, 8), rows)] = ref[...].astype(out_ref.dtype)


def join_kernel(n_in, where_ref, *refs):
    join(where_ref[TILE], refs[:n_in], refs[-2])
    join(where_ref[BATCH], refs[n_in:-2], refs[-1])


def out_kernel(n_in, n_cls, where_ref, small_ref, theirs_ref, *refs):
    in_refs, cls_in_refs, refs = refs[:n_in], refs[n_in : n_in + n_cls], refs[n_in + n_cls :]
    out_ref, bias_ref, cls_out_ref, cls_bias_ref, loss_ref, cls_whole_ref, *whole_ref = refs
    if whole_ref:
        join(where_ref[BATCH], in_refs, whole_ref[0])
        out_ref[...] = whole_ref[0][: out_ref.shape[0]]
    else:
        join(where_ref[BATCH], in_refs, out_ref)
    join(where_ref[TILE], cls_in_refs, cls_whole_ref)
    for tap in range(9):
        cls_out_ref[tap // 3, tap % 3] = cls_whole_ref[LOGITS * tap : LOGITS * (tap + 1)]
    bias_ref[...] = small_ref[2:3] + theirs_ref[3:4]
    both = small_ref[0:1] + theirs_ref[0:1]
    cls_bias_ref[...] = both[:, :LOGITS]
    loss_ref[...] = both[:, LOGITS : LOGITS + 1]


def swap(x, axis, bit=1):
    size = lax.axis_size(axis)
    return lax.ppermute(x, axis, [(i, i ^ bit) for i in range(size)])


def others(x, axis):
    return [swap(x, axis, bit) for bit in range(1, lax.axis_size(axis))]


def exchange(sends, axis):
    size = len(sends) + 1
    return [swap(x, axis, size - 1 - k) for k, x in enumerate(sends)]


def round_up(n, step):
    return (n + step - 1) // step * step


def shards(features, labels, w_shared, b_shared, w_cls, b_cls):
    _, rows, cols, chans = features.shape
    half = rows // 2
    outs = w_shared.shape[3]
    tiles = lax.axis_size("tile")
    pages = lax.axis_size("batch")
    c = lax.axis_index("chan")
    t = lax.axis_index("tile")
    f = features[0]
    where = Places(half)
    lab = labels.reshape(rows, 1, labels.shape[2])
    msg, labt, count, near = call(
        edge_kernel, "edge", 2,
        [
            ((3 * cols + ANCH_ROWS, chans), BF16),
            ((rows, ANCH_ROWS, cols), BF16),
            ((8, LANES), F32),
            ((half + 3, cols, chans), BF16),
        ],
        [where, f, lab],
        [pltpu.SemaphoreType.DMA((4,))],
        [SMEM, HBM, VMEM],
        51,
    )
    met = others(count, "batch")
    pairs = []
    for i in range(tiles - 1):
        pairs += [(2 * i + 1, 2 * i + 2), (2 * i + 2, 2 * i + 1)]
    halo = lax.ppermute(msg, ("tile", "chan"), pairs)
    w1b = swap(w_shared, "chan")
    w2b = swap(w_cls, "chan")
    b1b = swap(b_shared, "chan")

    weights = [w_shared, w1b, b_shared.reshape(1, outs), b1b.reshape(1, outs)]
    (inner,) = call(inner_kernel, "inner", 3, [((half + 1, cols, chans), BF16)], [where, near] + weights)
    inner, *met = lax.optimization_barrier((inner, *met))
    count = pair_sum([count] + met)
    halo, _ = lax.optimization_barrier((halo, count))
    counts = [count] + others(count, "tile")
    hid, dz, loss, w2 = call(
        head_kernel, "head", 5,
        [((half + 4, cols, chans), BF16), ((half + 2, cols, LANES), F32), ((1, LANES), F32)]
        + [((9 * LANES, chans), BF16)],
        [where, near, inner, halo, labt]
        + weights
        + [jnp.swapaxes(w_cls, 2, 3), jnp.swapaxes(w2b, 2, 3), b_cls.reshape(1, LOGITS)],
        [((5, cols, chans), BF16)],
    )
    dt, own, other, small = call(
        back_kernel, "back", 4,
        [
            ((half, 3 * CLS_ROWS, cols), BF16),
            ((half, cols, outs), BF16),
            ((half, cols, outs), BF16),
            ((SMALL, LANES), F32),
        ],
        [where, hid, dz, loss, w2] + counts,
        [((half + 2, cols, LANES), BF16)],
    )
    theirs = swap(other, "chan")
    far = swap(halo, "chan")
    cls_total = round_up(9 * LOGITS, 16 * pages * tiles)
    gcls, gcls_other = call(
        cls_kernel, "cls", 1.5, [((cls_total, outs), F32)] * 2, [where, hid, dt]
    )
    gcls_theirs = swap(gcls_other, "chan")

    total = round_up(9 * chans, 16 * pages * tiles)
    first, second = total // pages, total // (pages * tiles)
    cfirst, csecond = cls_total // tiles, cls_total // (pages * tiles)
    keep, *sends = call(
        shared_kernel, "shared", 4,
        [((first, outs), F32)] + [((first, outs), BF16)] * (pages - 1),
        [where, f, halo, far, own, theirs],
        [((rows, cols, 3 * outs), BF16), ((total, outs), F32)],
    )
    ckeep, *csends = call(
        cls_split_kernel, "cls_split", 0.6,
        [((cfirst, outs), F32)] + [((cfirst + TRIO, outs), BF16)] * (tiles - 1),
        [where, gcls, gcls_theirs, small],
        [((cls_total, outs), F32)],
    )
    arrived = exchange(sends, "batch")
    carrived = exchange(csends, "tile")
    keep, small, *sends = call(
        functools.partial(sum_kernel, pages - 1, tiles - 1, tiles - 1), "sum", 0.7,
        [((second, outs), F32), ((SMALL, LANES), F32)]
        + [((second, outs), BF16)] * (tiles - 1)
        + [((csecond, outs), F32)]
        + [((csecond + TRIO, outs), BF16)] * (pages - 1),
        [where, keep, small, ckeep] + arrived + carrived,
        [((first, outs), F32), ((cfirst, outs), F32)],
    )
    ckeep, csends = sends[tiles - 1], sends[tiles:]
    arrived = exchange(sends[: tiles - 1], "tile")
    carrived = exchange(csends, "batch")
    done, small, cdone = call(
        functools.partial(round_kernel, tiles - 1), "round", 0.7,
        [((second, outs), BF16), ((SMALL, LANES), F32), ((csecond, outs), BF16)],
        [where, keep, small, ckeep] + arrived + carrived,
    )
    small_theirs = swap(small, "chan")
    block, cblock = call(
        functools.partial(join_kernel, tiles), "join", 0.7,
        [((first, outs), BF16), ((cfirst, outs), BF16)],
        [where, done] + others(done, "tile") + [cdone] + others(cdone, "batch"),
    )
    grad_shared, bias, grad_cls, cls_bias, loss = call(
        functools.partial(out_kernel, pages, tiles), "out", 1.5,
        [((9 * chans, outs), F32), ((1, outs), F32), ((3, 3, LOGITS, outs), F32), ((1, LOGITS), F32), ((1, 1), F32)],
        [where, small, small_theirs, block] + others(block, "batch") + [cblock] + others(cblock, "tile"),
        [((cls_total, outs), F32)] + ([((total, outs), F32)] if total > 9 * chans else []),
    )
    return (
        grad_shared.reshape(3, 3, chans, outs),
        bias.reshape(outs),
        jnp.swapaxes(grad_cls, 2, 3),
        cls_bias.reshape(LOGITS),
        loss.reshape(1),
    )


def solution(mesh):
    placed = (
        P(("groups", "batch"), "tile", None, None),
        P(("groups", "batch"), "tile", None),
        P(None, None, None, "chan"),
        P("chan"),
        P(None, None, "chan", None),
        P(),
    )
    return jax.shard_map(
        shards,
        mesh=mesh,
        in_specs=placed,
        out_specs=(
            P("groups", None, None, "chan"),
            P(("groups", "chan")),
            P("groups", None, "chan", None),
            P("groups"),
            P("groups"),
        ),
        check_vma=False,
    )
```

```python
import functools

import jax
import jax.numpy as jnp
from jax import lax
from jax.experimental import pallas as pl
from jax.experimental.pallas import tpu as pltpu
from jax.sharding import PartitionSpec as P

ANCH = 9
CLASSES = 11
LOGITS = 99
LANES = 128
ANCH_ROWS = 16
CLS_ROWS = 112
TILE, BATCH = 3, 4
BLOCK = 2
SMALL = 4
TRIO = 16
BF16 = jnp.bfloat16
F32 = jnp.float32
VMEM = pl.BlockSpec(memory_space=pltpu.VMEM)
HBM = pl.BlockSpec(memory_space=pltpu.HBM)
SMEM = pl.BlockSpec(memory_space=pltpu.SMEM)


class Places:
    def __init__(self, half):
        self.half = half

    def __getitem__(self, i):
        c, t = lax.axis_index("chan"), lax.axis_index("tile")
        if i == 0:
            return c
        if i == 1:
            return (2 * t + c) * self.half
        if i == 2:
            return 2 * lax.axis_size("tile") * self.half
        return t if i == 3 else lax.axis_index("batch")


def call(kernel, name, micros, outs, inputs, scratch=(), specs=None, mib=32):
    return pl.pallas_call(
        functools.partial(kernel, inputs[0]),
        in_specs=(specs or [SMEM] + [VMEM] * (len(inputs) - 1))[1:],
        out_specs=[VMEM] * len(outs),
        out_shape=[jax.ShapeDtypeStruct(shape, kind) for shape, kind in outs],
        scratch_shapes=[pltpu.VMEM(*shape) if isinstance(shape, tuple) else shape for shape in scratch],
        cost_estimate=pl.CostEstimate(flops=int(micros * 1e9), bytes_accessed=int(micros * 1e6), transcendentals=0),
        compiler_params=pltpu.CompilerParams(vmem_limit_bytes=int(mib * 1024 * 1024)),
        name=name,
    )(*inputs[1:])


def shift_cells(field, by):
    cells = field.shape[0]
    rolled = pltpu.roll(field, by % cells, axis=0)
    cell = lax.broadcasted_iota(jnp.int32, field.shape, 0)
    edge = 0 if by > 0 else cells - 1
    return jnp.where(cell == edge, 0.0, rolled)


def dot(left, right, dims=((1,), (0,))):
    return lax.dot_general(left, right, (dims, ((), ())), preferred_element_type=F32)


def taken(ref, start, rows):
    cols = ref.shape[1]
    parts = [ref[pl.ds(start + r, BLOCK)].reshape(BLOCK * cols, ref.shape[2]) for r in rows]
    return jnp.concatenate(parts, axis=1)


def three(x):
    high = x.astype(BF16)
    rest = x - high.astype(F32)
    middle = rest.astype(BF16)
    low = (rest - middle.astype(F32)).astype(BF16)
    return high, middle, low


def put_trio(ref, start, x):
    parts = [part.astype(F32) for part in three(x)]
    ref[start : start + TRIO] = jnp.concatenate(parts + [jnp.zeros_like(x)], axis=0).astype(BF16)


def get_trio(ref, start):
    part = ref[start : start + TRIO].astype(F32)
    return part[0:SMALL] + part[SMALL : 2 * SMALL] + part[2 * SMALL : 3 * SMALL]


def edge_kernel(where_ref, f_ref, lab_ref, msg_ref, labt_ref, count_ref, near_ref, sem):
    rows, cols, _ = f_ref.shape
    c = where_ref[0]
    copies = [
        pltpu.make_async_copy(f_ref.at[(rows - 3) * c + k], msg_ref.at[pl.ds(cols * k, cols)], sem.at[k])
        for k in range(3)
    ]
    near = near_ref.shape[0]
    copies.append(pltpu.make_async_copy(f_ref.at[pl.ds((rows - near) * c, near)], near_ref, sem.at[3]))
    for copy in copies:
        copy.start()
    size = lab_ref.shape[2]
    place = lax.broadcasted_iota(jnp.int32, (ANCH_ROWS, size), 1) % ANCH
    anchor = lax.broadcasted_iota(jnp.int32, (ANCH_ROWS, size), 0)
    mine = place == anchor
    labs = [lab_ref[r].astype(F32) for r in range(rows)]
    named = [jnp.where(lab > 0.0, 1.0, 0.0) for lab in labs]
    count_ref[...] = jnp.full(count_ref.shape, jnp.sum(sum(named[1:], named[0])), F32)
    left = jnp.concatenate([jnp.where(mine, lab, 0.0) for lab in labs], axis=0).astype(BF16)
    offset = lax.broadcasted_iota(jnp.int32, (size, cols), 0) - ANCH * lax.broadcasted_iota(jnp.int32, (size, cols), 1)
    pick = jnp.where(jnp.logical_and(offset >= 0, offset < ANCH), 1.0, 0.0).astype(BF16)
    turned = dot(left, pick).astype(BF16)
    for r in range(rows):
        labt_ref[r] = turned[ANCH_ROWS * r : ANCH_ROWS * (r + 1)]
    msg_ref[3 * cols : 3 * cols + ANCH_ROWS] = jnp.where(
        c == 0, turned[:ANCH_ROWS].astype(F32), turned[ANCH_ROWS * (rows - 1) :].astype(F32)
    ).astype(BF16)
    for copy in copies:
        copy.wait()


def hidden_rows(x, w1a_ref, w1b_ref, b1a_ref, b1b_ref):
    w1 = [
        jnp.concatenate(
            [part for j in range(3) for part in (w1a_ref[i, j], w1b_ref[i, j])], axis=1
        )
        for i in range(3)
    ]
    w1 = jnp.concatenate(w1, axis=0)
    b1 = jnp.concatenate([b1a_ref[...], b1b_ref[...]], axis=1)
    n = x.shape[0] - 2
    cols, chans = x.shape[1:]
    width = w1.shape[1] // 3
    for start in range(0, n, 4):
        count = min(4, n - start)
        parts = [x[start + r : start + r + count].reshape(count * cols, chans) for r in range(3)]
        many = dot(jnp.concatenate(parts, axis=1), w1)
        for k in range(count):
            y = many[k * cols : (k + 1) * cols]
            yield shift_cells(y[:, :width], 1) + y[:, width : 2 * width] + shift_cells(y[:, 2 * width :], -1) + b1


def inner_kernel(start, where_ref, near_ref, w1a_ref, w1b_ref, b1a_ref, b1b_ref, out_ref):
    some = near_ref.at[start : start + out_ref.shape[0] + 2]
    for k, pre in enumerate(hidden_rows(some, w1a_ref, w1b_ref, b1a_ref, b1b_ref)):
        out_ref[k] = jnp.maximum(pre, 0.0).astype(BF16)


def head_kernel(
    where_ref, near_ref, inner_ref, later_ref, halo_ref, labt_ref, w1a_ref, w1b_ref, b1a_ref, b1b_ref, w2a_ref, w2b_ref, b2_ref,
    hid_ref, dz_ref, loss_ref, w2_ref, xw_ref,
):
    near = near_ref.shape[0]
    half = near - 3
    cols, chans = near_ref.shape[1:]
    c = where_ref[0]
    first = where_ref[1]
    total = where_ref[2]
    xw_ref[pl.ds(3 - 3 * c, 2)] = near_ref[pl.ds((near - 2) * c, 2)]
    for k in range(3):
        xw_ref[2 * c + k] = halo_ref[cols * k : cols * (k + 1)]
    early = inner_ref.shape[0]
    hid_ref[pl.ds(3 - 3 * c, early)] = inner_ref[...]
    hid_ref[pl.ds(3 - 3 * c + early, later_ref.shape[0])] = later_ref[...]
    for k, pre in enumerate(hidden_rows(xw_ref, w1a_ref, w1b_ref, b1a_ref, b1b_ref)):
        h = (near - 2) * c + k
        row = first + h - 2
        inside = jnp.logical_and(row >= 0, row < total)
        hid_ref[h] = jnp.where(inside, jnp.maximum(pre, 0.0), 0.0).astype(BF16)
    deep = chans // 2
    for tap in range(9):
        end = LANES * tap + LANES
        w2_ref[end - 32 : end] = jnp.zeros((32, chans), BF16)
        w2_ref[end - LANES : end - LANES + LOGITS, :deep] = w2a_ref[tap // 3, tap % 3]
        w2_ref[end - LANES : end - LANES + LOGITS, deep:] = w2b_ref[tap // 3, tap % 3]

    lane = lax.broadcasted_iota(jnp.int32, (1, LANES), 1)
    kind = (lane % CLASSES + 1).astype(F32)
    real = lane < LOGITS
    anchor = lax.broadcasted_iota(jnp.int32, (ANCH_ROWS, LANES), 0)
    column = lax.broadcasted_iota(jnp.int32, (ANCH_ROWS, LANES), 1)
    spread = jnp.where(jnp.logical_and(column // CLASSES == anchor, column < LOGITS), 1.0, 0.0).astype(BF16)
    size = 3 * LANES
    w2 = jnp.concatenate([w2_ref[size * i : size * (i + 1)] for i in range(3)], axis=1)
    b2 = jnp.concatenate([b2_ref[...], jnp.zeros((1, LANES - LOGITS), F32)], axis=1)

    def focal(g, loss):
        pair = dot(taken(hid_ref, BLOCK * g, (0, 1, 2)), w2, ((1,), (1,)))
        for k in range(BLOCK):
            loss = loss + focal_row(BLOCK * g + k, pair[k * cols : (k + 1) * cols])
        return loss

    def focal_row(l, y):
        z = shift_cells(y[:, :LANES], 1) + y[:, LANES : 2 * LANES] + shift_cells(y[:, 2 * LANES :], -1) + b2
        at_halo = jnp.where(c == 0, l == 0, l == half + 1)
        local = jnp.clip(l - 1 + half * c, 0, 2 * half - 1)
        mine = labt_ref[local].astype(F32)
        far = halo_ref[3 * cols : 3 * cols + ANCH_ROWS].astype(F32)
        lab = dot(jnp.where(at_halo, far, mine).astype(BF16), spread, ((0,), (0,)))
        row = first + l - 1
        inside = jnp.logical_and(row >= 0, row < total)
        hit = lab == kind
        keep = jnp.logical_and(jnp.logical_and(lab >= 0.0, real), inside)
        u = jnp.where(hit, -z, z)
        e = jnp.exp(-jnp.abs(u))
        r = 1.0 / (1.0 + e)
        er = e * r
        up = u >= 0.0
        s = jnp.where(up, r, er)
        comp = jnp.where(up, er, r)
        soft = jnp.maximum(u, 0.0) + jnp.log1p(e)
        ws = jnp.where(keep, jnp.where(hit, 0.25, 0.75), 0.0) * s * s
        slope = ws * (2.0 * comp * soft + s)
        dz_ref[l] = jnp.where(hit, -slope, slope)
        own = jnp.logical_and(l >= 1, l <= half)
        return jnp.where(own, 1.0, 0.0) * jnp.sum(ws * soft, axis=0, keepdims=True)

    loss_ref[...] = lax.fori_loop(0, (half + 2) // BLOCK, focal, jnp.zeros((1, LANES), F32), unroll=True)


def back_kernel(where_ref, hid_ref, dz_ref, loss_ref, w2_ref, *rest):
    *count_refs, dt_ref, own_ref, other_ref, small_ref, dlog_ref = rest
    half, _, cols = dt_ref.shape
    chans = hid_ref.shape[2]
    inverse = 1.0 / pair_sum([ref[...] for ref in count_refs])[:1]

    def scaled(l):
        dz = dz_ref[l] * inverse
        d16 = dz.astype(BF16)
        dlog_ref[l] = d16
        return dz, d16

    scaled(0)
    scaled(half + 1)

    def turn(d, gcb):
        dz, d16 = scaled(d + 1)
        turned = jnp.transpose(d16.astype(F32))[:CLS_ROWS]
        cell = lax.broadcasted_iota(jnp.int32, turned.shape, 1)
        left = jnp.where(cell == cols - 1, 0.0, pltpu.roll(turned, cols - 1, axis=1))
        right = jnp.where(cell == 0, 0.0, pltpu.roll(turned, 1, axis=1))
        dt_ref[d] = jnp.concatenate([left, turned, right], axis=0).astype(BF16)
        return gcb + jnp.sum(dz, axis=0, keepdims=True)

    gcb = lax.fori_loop(0, half, turn, jnp.zeros((1, LANES), F32), unroll=True)
    w2t = [
        jnp.concatenate([w2_ref[LANES * (3 * i + j) : LANES * (3 * i + j + 1)] for j in range(3)], axis=1)
        for i in range(3)
    ]
    w2t = jnp.concatenate(w2t, axis=0)

    def dpre(g, gsb):
        pair = dot(taken(dlog_ref, BLOCK * g, (2, 1, 0)), w2t)
        for k in range(BLOCK):
            gsb = gsb + dpre_row(BLOCK * g + k, pair[k * cols : (k + 1) * cols])
        return gsb

    def dpre_row(d, q):
        dhid = shift_cells(q[:, :chans], -1) + q[:, chans : 2 * chans] + shift_cells(q[:, 2 * chans :], 1)
        dpre = jnp.where(hid_ref[d + 2].astype(F32) > 0.0, dhid, 0.0)
        d16 = dpre.astype(BF16)
        own_ref[d] = d16[:, : chans // 2]
        other_ref[d] = d16[:, chans // 2 :]
        return jnp.sum(dpre, axis=0, keepdims=True)

    gsb = lax.fori_loop(0, half // BLOCK, dpre, jnp.zeros((1, chans), F32), unroll=True)
    loss = jnp.sum(loss_ref[...], axis=1, keepdims=True) * inverse[:, :1]
    small_ref[0:1] = jnp.where(lax.broadcasted_iota(jnp.int32, (1, LANES), 1) < LOGITS, gcb, loss)
    small_ref[1:2] = jnp.zeros((1, LANES), F32)
    small_ref[2:3] = gsb[:, : chans // 2]
    small_ref[3:4] = gsb[:, chans // 2 :]


def cls_kernel(where_ref, hid_ref, dt_ref, own_ref, other_ref):
    half, _, cols = dt_ref.shape
    chans = hid_ref.shape[2]
    deep = chans // 2
    dt = jnp.concatenate([dt_ref[d] for d in range(half)], axis=1)
    for i in range(3):
        g = dot(dt, hid_ref[i + 1 : i + 1 + half].reshape(half * cols, chans))
        for j in range(3):
            start = LOGITS * (3 * i + j)
            own_ref[start : start + LOGITS] = g[CLS_ROWS * j : CLS_ROWS * j + LOGITS, :deep]
            other_ref[start : start + LOGITS] = g[CLS_ROWS * j : CLS_ROWS * j + LOGITS, deep:]
    blank = jnp.zeros((own_ref.shape[0] - 9 * LOGITS, deep), F32)
    own_ref[9 * LOGITS :] = blank
    other_ref[9 * LOGITS :] = blank


def split(total, me, keep_ref, send_refs):
    rows = keep_ref.shape[0]
    keep_ref[...] = total[pl.ds(pl.multiple_of(me * rows, 8), rows)]
    size = len(send_refs) + 1
    for k, ref in enumerate(send_refs):
        ref[0:rows] = total[pl.ds(pl.multiple_of((me ^ (size - 1 - k)) * rows, 8), rows)].astype(BF16)


def shared_kernel(
    where_ref, f_ref, halo_ref, far_ref, own_ref, other_ref, keep_ref, *rest
):
    *send_refs, d_ref, g_ref = rest
    rows, cols, chans = f_ref.shape
    half = rows // 2
    c = where_ref[0]
    near = halo_ref[pl.ds(pl.multiple_of(2 * cols * (1 - c), 16), cols)]
    far = far_ref[pl.ds(pl.multiple_of(2 * cols * c, 16), cols)]
    before = jnp.where(c == 0, near, far)
    after = jnp.where(c == 0, far, near)

    for r in range(rows):
        mine, theirs = own_ref[r % half].astype(F32), other_ref[r % half].astype(F32)
        mid = jnp.where(c == (0 if r < half else 1), mine, theirs)
        d_ref[r] = jnp.concatenate([shift_cells(mid, -1), mid, shift_cells(mid, 1)], axis=1).astype(BF16)
    outs = d_ref.shape[2] // 3

    def part(x, first):
        n = x.shape[0]
        rhs = d_ref[first : first + n].reshape(n * cols, 3 * outs)
        return dot(x.reshape(n * cols, chans), rhs, ((0,), (0,)))

    for i in range(3):
        if i == 0:
            g = part(f_ref[0 : rows - 1], 1) + part(before[None], 0)
        elif i == 1:
            g = part(f_ref[...], 0)
        else:
            g = part(f_ref[1:rows], 0) + part(after[None], rows - 1)
        for j in range(3):
            start = (3 * i + j) * chans
            g_ref[start : start + chans] = g[:, j * outs : (j + 1) * outs]
    if g_ref.shape[0] > 9 * chans:
        g_ref[9 * chans :] = jnp.zeros((g_ref.shape[0] - 9 * chans, outs), F32)
    split(g_ref, where_ref[BATCH], keep_ref, send_refs)


def cls_split_kernel(where_ref, cls_ref, theirs_ref, small_ref, keep_ref, *rest):
    *send_refs, total_ref = rest
    total_ref[...] = cls_ref[...] + theirs_ref[...]
    split(total_ref, where_ref[TILE], keep_ref, send_refs)
    for ref in send_refs:
        put_trio(ref, keep_ref.shape[0], small_ref[...])


def pair_sum(parts):
    while len(parts) > 1:
        parts = [parts[k] + parts[k + 1] for k in range(0, len(parts), 2)]
    return parts[0]


def total_of(base_ref, in_refs):
    rows = base_ref.shape[0]
    total = base_ref[...]
    for ref in in_refs:
        total = total + ref[0:rows].astype(F32)
    return total


def small_sum(small_ref, in_refs, start):
    return pair_sum([small_ref[...]] + [get_trio(ref, start) for ref in in_refs])


def sum_kernel(n_in, n_cls, n_send, where_ref, base_ref, small_ref, cls_ref, *refs):
    in_refs, refs = refs[:n_in], refs[n_in:]
    cls_in_refs, refs = refs[:n_cls], refs[n_cls:]
    keep_ref, sum_ref, *refs, total_ref, cls_total_ref = refs
    send_refs, cls_keep_ref, cls_send_refs = refs[:n_send], refs[n_send], refs[n_send + 1 :]
    total_ref[...] = total_of(base_ref, in_refs)
    split(total_ref, where_ref[TILE], keep_ref, send_refs)
    cls_total_ref[...] = total_of(cls_ref, cls_in_refs)
    split(cls_total_ref, where_ref[BATCH], cls_keep_ref, cls_send_refs)
    sums = small_sum(small_ref, cls_in_refs, cls_ref.shape[0])
    sum_ref[...] = sums
    for ref in cls_send_refs:
        put_trio(ref, cls_keep_ref.shape[0], sums)


def round_kernel(n_in, where_ref, base_ref, small_ref, cls_ref, *refs):
    in_refs, cls_in_refs = refs[:n_in], refs[n_in:-3]
    out_ref, sum_ref, cls_out_ref = refs[-3:]
    out_ref[...] = total_of(base_ref, in_refs).astype(BF16)
    cls_out_ref[...] = total_of(cls_ref, cls_in_refs).astype(BF16)
    sum_ref[...] = small_sum(small_ref, cls_in_refs, cls_ref.shape[0])


def join(me, in_refs, out_ref):
    rows = in_refs[0].shape[0]
    for k, ref in enumerate(in_refs):
        out_ref[pl.ds(pl.multiple_of((me ^ k) * rows, 8), rows)] = ref[...].astype(out_ref.dtype)


def join_kernel(n_in, where_ref, *refs):
    join(where_ref[TILE], refs[:n_in], refs[-2])
    join(where_ref[BATCH], refs[n_in:-2], refs[-1])


def out_kernel(n_in, n_cls, where_ref, small_ref, theirs_ref, *refs):
    in_refs, cls_in_refs, refs = refs[:n_in], refs[n_in : n_in + n_cls], refs[n_in + n_cls :]
    out_ref, bias_ref, cls_out_ref, cls_bias_ref, loss_ref, cls_whole_ref, *whole_ref = refs
    if whole_ref:
        join(where_ref[BATCH], in_refs, whole_ref[0])
        out_ref[...] = whole_ref[0][: out_ref.shape[0]]
    else:
        join(where_ref[BATCH], in_refs, out_ref)
    join(where_ref[TILE], cls_in_refs, cls_whole_ref)
    for tap in range(9):
        cls_out_ref[tap // 3, tap % 3] = cls_whole_ref[LOGITS * tap : LOGITS * (tap + 1)]
    bias_ref[...] = small_ref[2:3] + theirs_ref[3:4]
    both = small_ref[0:1] + theirs_ref[0:1]
    cls_bias_ref[...] = both[:, :LOGITS]
    loss_ref[...] = both[:, LOGITS : LOGITS + 1]


def swap(x, axis, bit=1):
    size = lax.axis_size(axis)
    return lax.ppermute(x, axis, [(i, i ^ bit) for i in range(size)])


def others(x, axis):
    return [swap(x, axis, bit) for bit in range(1, lax.axis_size(axis))]


def exchange(sends, axis):
    size = len(sends) + 1
    return [swap(x, axis, size - 1 - k) for k, x in enumerate(sends)]


def round_up(n, step):
    return (n + step - 1) // step * step


def shards(features, labels, w_shared, b_shared, w_cls, b_cls):
    _, rows, cols, chans = features.shape
    half = rows // 2
    outs = w_shared.shape[3]
    tiles = lax.axis_size("tile")
    pages = lax.axis_size("batch")
    c = lax.axis_index("chan")
    t = lax.axis_index("tile")
    f = features[0]
    where = Places(half)
    lab = labels.reshape(rows, 1, labels.shape[2])
    msg, labt, count, near = call(
        edge_kernel, "edge", 2,
        [
            ((3 * cols + ANCH_ROWS, chans), BF16),
            ((rows, ANCH_ROWS, cols), BF16),
            ((8, LANES), F32),
            ((half + 3, cols, chans), BF16),
        ],
        [where, f, lab],
        [pltpu.SemaphoreType.DMA((4,))],
        [SMEM, HBM, VMEM],
        51,
    )
    met = others(count, "batch")
    pairs = []
    for i in range(tiles - 1):
        pairs += [(2 * i + 1, 2 * i + 2), (2 * i + 2, 2 * i + 1)]
    halo = lax.ppermute(msg, ("tile", "chan"), pairs)
    w1b = swap(w_shared, "chan")
    w2b = swap(w_cls, "chan")
    b1b = swap(b_shared, "chan")

    weights = [w_shared, w1b, b_shared.reshape(1, outs), b1b.reshape(1, outs)]
    early = (half + 2) // 2

    def rows_of(start, n, name):
        kernel = functools.partial(inner_kernel, start)
        return call(kernel, name, 1.3, [((n, cols, chans), BF16)], [where, near] + weights)[0]

    inner = rows_of(0, early, "inner")
    inner, *met = lax.optimization_barrier((inner, *met))
    count = pair_sum([count] + met)
    later = rows_of(early, half + 1 - early, "later")
    bit = 1
    while 2 * bit < tiles:
        met = swap(count, "tile", bit)
        later, met = lax.optimization_barrier((later, met))
        count = count + met
        bit *= 2
    halo, _ = lax.optimization_barrier((halo, count))
    counts = [count, swap(count, "tile", bit)]
    hid, dz, loss, w2 = call(
        head_kernel, "head", 5,
        [((half + 4, cols, chans), BF16), ((half + 2, cols, LANES), F32), ((1, LANES), F32)]
        + [((9 * LANES, chans), BF16)],
        [where, near, inner, later, halo, labt]
        + weights
        + [jnp.swapaxes(w_cls, 2, 3), jnp.swapaxes(w2b, 2, 3), b_cls.reshape(1, LOGITS)],
        [((5, cols, chans), BF16)],
    )
    dt, own, other, small = call(
        back_kernel, "back", 4,
        [
            ((half, 3 * CLS_ROWS, cols), BF16),
            ((half, cols, outs), BF16),
            ((half, cols, outs), BF16),
            ((SMALL, LANES), F32),
        ],
        [where, hid, dz, loss, w2] + counts,
        [((half + 2, cols, LANES), BF16)],
    )
    theirs = swap(other, "chan")
    far = swap(halo, "chan")
    cls_total = round_up(9 * LOGITS, 16 * pages * tiles)
    gcls, gcls_other = call(
        cls_kernel, "cls", 1.5, [((cls_total, outs), F32)] * 2, [where, hid, dt]
    )
    gcls_theirs = swap(gcls_other, "chan")

    total = round_up(9 * chans, 16 * pages * tiles)
    first, second = total // pages, total // (pages * tiles)
    cfirst, csecond = cls_total // tiles, cls_total // (pages * tiles)
    keep, *sends = call(
        shared_kernel, "shared", 4,
        [((first, outs), F32)] + [((first, outs), BF16)] * (pages - 1),
        [where, f, halo, far, own, theirs],
        [((rows, cols, 3 * outs), BF16), ((total, outs), F32)],
    )
    ckeep, *csends = call(
        cls_split_kernel, "cls_split", 0.6,
        [((cfirst, outs), F32)] + [((cfirst + TRIO, outs), BF16)] * (tiles - 1),
        [where, gcls, gcls_theirs, small],
        [((cls_total, outs), F32)],
    )
    arrived = exchange(sends, "batch")
    carrived = exchange(csends, "tile")
    keep, small, *sends = call(
        functools.partial(sum_kernel, pages - 1, tiles - 1, tiles - 1), "sum", 0.7,
        [((second, outs), F32), ((SMALL, LANES), F32)]
        + [((second, outs), BF16)] * (tiles - 1)
        + [((csecond, outs), F32)]
        + [((csecond + TRIO, outs), BF16)] * (pages - 1),
        [where, keep, small, ckeep] + arrived + carrived,
        [((first, outs), F32), ((cfirst, outs), F32)],
    )
    ckeep, csends = sends[tiles - 1], sends[tiles:]
    arrived = exchange(sends[: tiles - 1], "tile")
    carrived = exchange(csends, "batch")
    done, small, cdone = call(
        functools.partial(round_kernel, tiles - 1), "round", 0.7,
        [((second, outs), BF16), ((SMALL, LANES), F32), ((csecond, outs), BF16)],
        [where, keep, small, ckeep] + arrived + carrived,
    )
    small_theirs = swap(small, "chan")
    block, cblock = call(
        functools.partial(join_kernel, tiles), "join", 0.7,
        [((first, outs), BF16), ((cfirst, outs), BF16)],
        [where, done] + others(done, "tile") + [cdone] + others(cdone, "batch"),
    )
    grad_shared, bias, grad_cls, cls_bias, loss = call(
        functools.partial(out_kernel, pages, tiles), "out", 1.5,
        [((9 * chans, outs), F32), ((1, outs), F32), ((3, 3, LOGITS, outs), F32), ((1, LOGITS), F32), ((1, 1), F32)],
        [where, small, small_theirs, block] + others(block, "batch") + [cblock] + others(cblock, "tile"),
        [((cls_total, outs), F32)] + ([((total, outs), F32)] if total > 9 * chans else []),
    )
    return (
        grad_shared.reshape(3, 3, chans, outs),
        bias.reshape(outs),
        jnp.swapaxes(grad_cls, 2, 3),
        cls_bias.reshape(LOGITS),
        loss.reshape(1),
    )


def solution(mesh):
    placed = (
        P(("groups", "batch"), "tile", None, None),
        P(("groups", "batch"), "tile", None),
        P(None, None, None, "chan"),
        P("chan"),
        P(None, None, "chan", None),
        P(),
    )
    return jax.shard_map(
        shards,
        mesh=mesh,
        in_specs=placed,
        out_specs=(
            P("groups", None, None, "chan"),
            P(("groups", "chan")),
            P("groups", None, "chan", None),
            P("groups"),
            P("groups"),
        ),
        check_vma=False,
    )
```

```python
import functools

import jax
import jax.numpy as jnp
from jax import lax
from jax.experimental import pallas as pl
from jax.experimental.pallas import tpu as pltpu
from jax.sharding import PartitionSpec as P

ANCH = 9
CLASSES = 11
LOGITS = 99
LANES = 128
ANCH_ROWS = 16
CLS_ROWS = 112
TILE, BATCH = 3, 4
BLOCK = 2
SMALL = 4
TRIO = 16
BF16 = jnp.bfloat16
F32 = jnp.float32
VMEM = pl.BlockSpec(memory_space=pltpu.VMEM)
HBM = pl.BlockSpec(memory_space=pltpu.HBM)
SMEM = pl.BlockSpec(memory_space=pltpu.SMEM)


class Places:
    def __init__(self, half):
        self.half = half

    def __getitem__(self, i):
        c, t = lax.axis_index("chan"), lax.axis_index("tile")
        if i == 0:
            return c
        if i == 1:
            return (2 * t + c) * self.half
        if i == 2:
            return 2 * lax.axis_size("tile") * self.half
        return t if i == 3 else lax.axis_index("batch")


def call(kernel, name, micros, outs, inputs, scratch=(), specs=None, mib=32):
    return pl.pallas_call(
        functools.partial(kernel, inputs[0]),
        in_specs=(specs or [SMEM] + [VMEM] * (len(inputs) - 1))[1:],
        out_specs=[VMEM] * len(outs),
        out_shape=[jax.ShapeDtypeStruct(shape, kind) for shape, kind in outs],
        scratch_shapes=[pltpu.VMEM(*shape) if isinstance(shape, tuple) else shape for shape in scratch],
        cost_estimate=pl.CostEstimate(flops=int(micros * 1e9), bytes_accessed=int(micros * 1e6), transcendentals=0),
        compiler_params=pltpu.CompilerParams(vmem_limit_bytes=int(mib * 1024 * 1024)),
        name=name,
    )(*inputs[1:])


def shift_cells(field, by):
    cells = field.shape[0]
    rolled = pltpu.roll(field, by % cells, axis=0)
    cell = lax.broadcasted_iota(jnp.int32, field.shape, 0)
    edge = 0 if by > 0 else cells - 1
    return jnp.where(cell == edge, 0.0, rolled)


def dot(left, right, dims=((1,), (0,))):
    return lax.dot_general(left, right, (dims, ((), ())), preferred_element_type=F32)


def taken(ref, start, rows):
    cols = ref.shape[1]
    parts = [ref[pl.ds(start + r, BLOCK)].reshape(BLOCK * cols, ref.shape[2]) for r in rows]
    return jnp.concatenate(parts, axis=1)


def three(x):
    high = x.astype(BF16)
    rest = x - high.astype(F32)
    middle = rest.astype(BF16)
    low = (rest - middle.astype(F32)).astype(BF16)
    return high, middle, low


def put_trio(ref, start, x):
    parts = [part.astype(F32) for part in three(x)]
    ref[start : start + TRIO] = jnp.concatenate(parts + [jnp.zeros_like(x)], axis=0).astype(BF16)


def get_trio(ref, start):
    part = ref[start : start + TRIO].astype(F32)
    return part[0:SMALL] + part[SMALL : 2 * SMALL] + part[2 * SMALL : 3 * SMALL]


def edge_kernel(where_ref, f_ref, lab_ref, msg_ref, labt_ref, count_ref, near_ref, sem):
    rows, cols, _ = f_ref.shape
    c = where_ref[0]
    copies = [
        pltpu.make_async_copy(f_ref.at[(rows - 3) * c + k], msg_ref.at[pl.ds(cols * k, cols)], sem.at[k])
        for k in range(3)
    ]
    near = near_ref.shape[0]
    copies.append(pltpu.make_async_copy(f_ref.at[pl.ds((rows - near) * c, near)], near_ref, sem.at[3]))
    for copy in copies:
        copy.start()
    size = lab_ref.shape[2]
    place = lax.broadcasted_iota(jnp.int32, (ANCH_ROWS, size), 1) % ANCH
    anchor = lax.broadcasted_iota(jnp.int32, (ANCH_ROWS, size), 0)
    mine = place == anchor
    labs = [lab_ref[r].astype(F32) for r in range(rows)]
    named = [jnp.where(lab > 0.0, 1.0, 0.0) for lab in labs]
    count_ref[...] = jnp.full(count_ref.shape, jnp.sum(sum(named[1:], named[0])), F32)
    left = jnp.concatenate([jnp.where(mine, lab, 0.0) for lab in labs], axis=0).astype(BF16)
    offset = lax.broadcasted_iota(jnp.int32, (size, cols), 0) - ANCH * lax.broadcasted_iota(jnp.int32, (size, cols), 1)
    pick = jnp.where(jnp.logical_and(offset >= 0, offset < ANCH), 1.0, 0.0).astype(BF16)
    turned = dot(left, pick).astype(BF16)
    for r in range(rows):
        labt_ref[r] = turned[ANCH_ROWS * r : ANCH_ROWS * (r + 1)]
    msg_ref[3 * cols : 3 * cols + ANCH_ROWS] = jnp.where(
        c == 0, turned[:ANCH_ROWS].astype(F32), turned[ANCH_ROWS * (rows - 1) :].astype(F32)
    ).astype(BF16)
    for copy in copies:
        copy.wait()


def hidden_rows(x, w1a_ref, w1b_ref, b1a_ref, b1b_ref):
    w1 = [
        jnp.concatenate(
            [part for j in range(3) for part in (w1a_ref[i, j], w1b_ref[i, j])], axis=1
        )
        for i in range(3)
    ]
    w1 = jnp.concatenate(w1, axis=0)
    b1 = jnp.concatenate([b1a_ref[...], b1b_ref[...]], axis=1)
    n = x.shape[0] - 2
    cols, chans = x.shape[1:]
    width = w1.shape[1] // 3
    for start in range(0, n, 4):
        count = min(4, n - start)
        parts = [x[start + r : start + r + count].reshape(count * cols, chans) for r in range(3)]
        many = dot(jnp.concatenate(parts, axis=1), w1)
        for k in range(count):
            y = many[k * cols : (k + 1) * cols]
            yield shift_cells(y[:, :width], 1) + y[:, width : 2 * width] + shift_cells(y[:, 2 * width :], -1) + b1


def inner_kernel(where_ref, near_ref, w1a_ref, w1b_ref, b1a_ref, b1b_ref, out_ref):
    for k, pre in enumerate(hidden_rows(near_ref, w1a_ref, w1b_ref, b1a_ref, b1b_ref)):
        out_ref[k] = jnp.maximum(pre, 0.0).astype(BF16)


def head_kernel(
    where_ref, near_ref, inner_ref, halo_ref, labt_ref, w1a_ref, w1b_ref, b1a_ref, b1b_ref, w2a_ref, w2b_ref, b2_ref,
    hid_ref, dz_ref, loss_ref, w2_ref, xw_ref,
):
    near = near_ref.shape[0]
    half = near - 3
    cols, chans = near_ref.shape[1:]
    c = where_ref[0]
    first = where_ref[1]
    total = where_ref[2]
    xw_ref[pl.ds(3 - 3 * c, 2)] = near_ref[pl.ds((near - 2) * c, 2)]
    for k in range(3):
        xw_ref[2 * c + k] = halo_ref[cols * k : cols * (k + 1)]
    hid_ref[pl.ds(3 - 3 * c, near - 2)] = inner_ref[...]
    for k, pre in enumerate(hidden_rows(xw_ref, w1a_ref, w1b_ref, b1a_ref, b1b_ref)):
        h = (near - 2) * c + k
        row = first + h - 2
        inside = jnp.logical_and(row >= 0, row < total)
        hid_ref[h] = jnp.where(inside, jnp.maximum(pre, 0.0), 0.0).astype(BF16)
    deep = chans // 2
    for tap in range(9):
        end = LANES * tap + LANES
        w2_ref[end - 32 : end] = jnp.zeros((32, chans), BF16)
        w2_ref[end - LANES : end - LANES + LOGITS, :deep] = w2a_ref[tap // 3, tap % 3]
        w2_ref[end - LANES : end - LANES + LOGITS, deep:] = w2b_ref[tap // 3, tap % 3]

    lane = lax.broadcasted_iota(jnp.int32, (1, LANES), 1)
    kind = (lane % CLASSES + 1).astype(F32)
    real = lane < LOGITS
    anchor = lax.broadcasted_iota(jnp.int32, (ANCH_ROWS, LANES), 0)
    column = lax.broadcasted_iota(jnp.int32, (ANCH_ROWS, LANES), 1)
    spread = jnp.where(jnp.logical_and(column // CLASSES == anchor, column < LOGITS), 1.0, 0.0).astype(BF16)
    size = 3 * LANES
    w2 = jnp.concatenate([w2_ref[size * i : size * (i + 1)] for i in range(3)], axis=1)
    b2 = jnp.concatenate([b2_ref[...], jnp.zeros((1, LANES - LOGITS), F32)], axis=1)

    def focal(g, loss):
        pair = dot(taken(hid_ref, BLOCK * g, (0, 1, 2)), w2, ((1,), (1,)))
        for k in range(BLOCK):
            loss = loss + focal_row(BLOCK * g + k, pair[k * cols : (k + 1) * cols])
        return loss

    def focal_row(l, y):
        z = shift_cells(y[:, :LANES], 1) + y[:, LANES : 2 * LANES] + shift_cells(y[:, 2 * LANES :], -1) + b2
        at_halo = jnp.where(c == 0, l == 0, l == half + 1)
        local = jnp.clip(l - 1 + half * c, 0, 2 * half - 1)
        mine = labt_ref[local].astype(F32)
        far = halo_ref[3 * cols : 3 * cols + ANCH_ROWS].astype(F32)
        lab = dot(jnp.where(at_halo, far, mine).astype(BF16), spread, ((0,), (0,)))
        row = first + l - 1
        inside = jnp.logical_and(row >= 0, row < total)
        hit = lab == kind
        keep = jnp.logical_and(jnp.logical_and(lab >= 0.0, real), inside)
        u = jnp.where(hit, -z, z)
        e = jnp.exp(-jnp.abs(u))
        r = 1.0 / (1.0 + e)
        er = e * r
        up = u >= 0.0
        s = jnp.where(up, r, er)
        comp = jnp.where(up, er, r)
        soft = jnp.maximum(u, 0.0) + jnp.log1p(e)
        ws = jnp.where(keep, jnp.where(hit, 0.25, 0.75), 0.0) * s * s
        slope = ws * (2.0 * comp * soft + s)
        dz_ref[l] = jnp.where(hit, -slope, slope)
        own = jnp.logical_and(l >= 1, l <= half)
        return jnp.where(own, 1.0, 0.0) * jnp.sum(ws * soft, axis=0, keepdims=True)

    loss_ref[...] = lax.fori_loop(0, (half + 2) // BLOCK, focal, jnp.zeros((1, LANES), F32), unroll=True)


def back_kernel(where_ref, hid_ref, dz_ref, loss_ref, w2_ref, *rest):
    *count_refs, dt_ref, own_ref, other_ref, small_ref, dlog_ref = rest
    half, _, cols = dt_ref.shape
    chans = hid_ref.shape[2]
    inverse = 1.0 / pair_sum([ref[...] for ref in count_refs])[:1]

    def scaled(l):
        dz = dz_ref[l] * inverse
        d16 = dz.astype(BF16)
        dlog_ref[l] = d16
        return dz, d16

    scaled(0)
    scaled(half + 1)

    def turn(d, gcb):
        dz, d16 = scaled(d + 1)
        turned = jnp.transpose(d16.astype(F32))[:CLS_ROWS]
        cell = lax.broadcasted_iota(jnp.int32, turned.shape, 1)
        left = jnp.where(cell == cols - 1, 0.0, pltpu.roll(turned, cols - 1, axis=1))
        right = jnp.where(cell == 0, 0.0, pltpu.roll(turned, 1, axis=1))
        dt_ref[d] = jnp.concatenate([left, turned, right], axis=0).astype(BF16)
        return gcb + jnp.sum(dz, axis=0, keepdims=True)

    gcb = lax.fori_loop(0, half, turn, jnp.zeros((1, LANES), F32), unroll=True)
    w2t = [
        jnp.concatenate([w2_ref[LANES * (3 * i + j) : LANES * (3 * i + j + 1)] for j in range(3)], axis=1)
        for i in range(3)
    ]
    w2t = jnp.concatenate(w2t, axis=0)

    def dpre(g, gsb):
        pair = dot(taken(dlog_ref, BLOCK * g, (2, 1, 0)), w2t)
        for k in range(BLOCK):
            gsb = gsb + dpre_row(BLOCK * g + k, pair[k * cols : (k + 1) * cols])
        return gsb

    def dpre_row(d, q):
        dhid = shift_cells(q[:, :chans], -1) + q[:, chans : 2 * chans] + shift_cells(q[:, 2 * chans :], 1)
        dpre = jnp.where(hid_ref[d + 2].astype(F32) > 0.0, dhid, 0.0)
        d16 = dpre.astype(BF16)
        own_ref[d] = d16[:, : chans // 2]
        other_ref[d] = d16[:, chans // 2 :]
        return jnp.sum(dpre, axis=0, keepdims=True)

    gsb = lax.fori_loop(0, half // BLOCK, dpre, jnp.zeros((1, chans), F32), unroll=True)
    loss = jnp.sum(loss_ref[...], axis=1, keepdims=True) * inverse[:, :1]
    small_ref[0:1] = jnp.where(lax.broadcasted_iota(jnp.int32, (1, LANES), 1) < LOGITS, gcb, loss)
    small_ref[1:2] = jnp.zeros((1, LANES), F32)
    small_ref[2:3] = gsb[:, : chans // 2]
    small_ref[3:4] = gsb[:, chans // 2 :]


def cls_kernel(where_ref, hid_ref, dt_ref, own_ref, other_ref):
    half, _, cols = dt_ref.shape
    chans = hid_ref.shape[2]
    deep = chans // 2
    dt = jnp.concatenate([dt_ref[d] for d in range(half)], axis=1)
    for i in range(3):
        g = dot(dt, hid_ref[i + 1 : i + 1 + half].reshape(half * cols, chans))
        for j in range(3):
            start = LOGITS * (3 * i + j)
            own_ref[start : start + LOGITS] = g[CLS_ROWS * j : CLS_ROWS * j + LOGITS, :deep]
            other_ref[start : start + LOGITS] = g[CLS_ROWS * j : CLS_ROWS * j + LOGITS, deep:]
    blank = jnp.zeros((own_ref.shape[0] - 9 * LOGITS, deep), F32)
    own_ref[9 * LOGITS :] = blank
    other_ref[9 * LOGITS :] = blank


def split(total, me, keep_ref, send_refs):
    rows = keep_ref.shape[0]
    keep_ref[...] = total[pl.ds(pl.multiple_of(me * rows, 8), rows)]
    size = len(send_refs) + 1
    for k, ref in enumerate(send_refs):
        ref[0:rows] = total[pl.ds(pl.multiple_of((me ^ (size - 1 - k)) * rows, 8), rows)].astype(BF16)


def shared_kernel(
    where_ref, f_ref, halo_ref, far_ref, own_ref, other_ref, keep_ref, *rest
):
    *send_refs, d_ref, g_ref = rest
    rows, cols, chans = f_ref.shape
    half = rows // 2
    c = where_ref[0]
    near = halo_ref[pl.ds(pl.multiple_of(2 * cols * (1 - c), 16), cols)]
    far = far_ref[pl.ds(pl.multiple_of(2 * cols * c, 16), cols)]
    before = jnp.where(c == 0, near, far)
    after = jnp.where(c == 0, far, near)

    for r in range(rows):
        mine, theirs = own_ref[r % half].astype(F32), other_ref[r % half].astype(F32)
        mid = jnp.where(c == (0 if r < half else 1), mine, theirs)
        d_ref[r] = jnp.concatenate([shift_cells(mid, -1), mid, shift_cells(mid, 1)], axis=1).astype(BF16)
    outs = d_ref.shape[2] // 3

    def part(x, first):
        n = x.shape[0]
        rhs = d_ref[first : first + n].reshape(n * cols, 3 * outs)
        return dot(x.reshape(n * cols, chans), rhs, ((0,), (0,)))

    for i in range(3):
        if i == 0:
            g = part(f_ref[0 : rows - 1], 1) + part(before[None], 0)
        elif i == 1:
            g = part(f_ref[...], 0)
        else:
            g = part(f_ref[1:rows], 0) + part(after[None], rows - 1)
        for j in range(3):
            start = (3 * i + j) * chans
            g_ref[start : start + chans] = g[:, j * outs : (j + 1) * outs]
    if g_ref.shape[0] > 9 * chans:
        g_ref[9 * chans :] = jnp.zeros((g_ref.shape[0] - 9 * chans, outs), F32)
    split(g_ref, where_ref[BATCH], keep_ref, send_refs)


def cls_split_kernel(where_ref, cls_ref, theirs_ref, small_ref, keep_ref, *rest):
    *send_refs, total_ref = rest
    total_ref[...] = cls_ref[...] + theirs_ref[...]
    split(total_ref, where_ref[TILE], keep_ref, send_refs)
    for ref in send_refs:
        put_trio(ref, keep_ref.shape[0], small_ref[...])


def pair_sum(parts):
    while len(parts) > 1:
        parts = [parts[k] + parts[k + 1] for k in range(0, len(parts), 2)]
    return parts[0]


def total_of(base_ref, in_refs):
    rows = base_ref.shape[0]
    total = base_ref[...]
    for ref in in_refs:
        total = total + ref[0:rows].astype(F32)
    return total


def small_sum(small_ref, in_refs, start):
    return pair_sum([small_ref[...]] + [get_trio(ref, start) for ref in in_refs])


def sum_kernel(n_in, n_cls, n_send, where_ref, base_ref, small_ref, cls_ref, *refs):
    in_refs, refs = refs[:n_in], refs[n_in:]
    cls_in_refs, refs = refs[:n_cls], refs[n_cls:]
    keep_ref, sum_ref, *refs, total_ref, cls_total_ref = refs
    send_refs, cls_keep_ref, cls_send_refs = refs[:n_send], refs[n_send], refs[n_send + 1 :]
    total_ref[...] = total_of(base_ref, in_refs)
    split(total_ref, where_ref[TILE], keep_ref, send_refs)
    cls_total_ref[...] = total_of(cls_ref, cls_in_refs)
    split(cls_total_ref, where_ref[BATCH], cls_keep_ref, cls_send_refs)
    sums = small_sum(small_ref, cls_in_refs, cls_ref.shape[0])
    sum_ref[...] = sums
    for ref in cls_send_refs:
        put_trio(ref, cls_keep_ref.shape[0], sums)


def round_kernel(n_in, where_ref, base_ref, small_ref, cls_ref, *refs):
    in_refs, cls_in_refs = refs[:n_in], refs[n_in:-3]
    out_ref, sum_ref, cls_out_ref = refs[-3:]
    out_ref[...] = total_of(base_ref, in_refs).astype(BF16)
    cls_out_ref[...] = total_of(cls_ref, cls_in_refs).astype(BF16)
    sum_ref[...] = small_sum(small_ref, cls_in_refs, cls_ref.shape[0])


def join(me, in_refs, out_ref):
    rows = in_refs[0].shape[0]
    for k, ref in enumerate(in_refs):
        out_ref[pl.ds(pl.multiple_of((me ^ k) * rows, 8), rows)] = ref[...].astype(out_ref.dtype)


def join_kernel(n_in, where_ref, *refs):
    join(where_ref[TILE], refs[:n_in], refs[-2])
    join(where_ref[BATCH], refs[n_in:-2], refs[-1])


def out_kernel(n_in, n_cls, where_ref, small_ref, theirs_ref, *refs):
    in_refs, cls_in_refs, refs = refs[:n_in], refs[n_in : n_in + n_cls], refs[n_in + n_cls :]
    out_ref, bias_ref, cls_out_ref, cls_bias_ref, loss_ref, cls_whole_ref, *whole_ref = refs
    if whole_ref:
        join(where_ref[BATCH], in_refs, whole_ref[0])
        out_ref[...] = whole_ref[0][: out_ref.shape[0]]
    else:
        join(where_ref[BATCH], in_refs, out_ref)
    join(where_ref[TILE], cls_in_refs, cls_whole_ref)
    for tap in range(9):
        cls_out_ref[tap // 3, tap % 3] = cls_whole_ref[LOGITS * tap : LOGITS * (tap + 1)]
    bias_ref[...] = small_ref[2:3] + theirs_ref[3:4]
    both = small_ref[0:1] + theirs_ref[0:1]
    cls_bias_ref[...] = both[:, :LOGITS]
    loss_ref[...] = both[:, LOGITS : LOGITS + 1]


def swap(x, axis, bit=1):
    size = lax.axis_size(axis)
    return lax.ppermute(x, axis, [(i, i ^ bit) for i in range(size)])


def others(x, axis):
    return [swap(x, axis, bit) for bit in range(1, lax.axis_size(axis))]


def exchange(sends, axis):
    size = len(sends) + 1
    return [swap(x, axis, size - 1 - k) for k, x in enumerate(sends)]


def round_up(n, step):
    return (n + step - 1) // step * step


def shards(features, labels, w_shared, b_shared, w_cls, b_cls):
    _, rows, cols, chans = features.shape
    half = rows // 2
    outs = w_shared.shape[3]
    tiles = lax.axis_size("tile")
    pages = lax.axis_size("batch")
    c = lax.axis_index("chan")
    t = lax.axis_index("tile")
    f = features[0]
    where = Places(half)
    lab = labels.reshape(rows, 1, labels.shape[2])
    msg, labt, count, near = call(
        edge_kernel, "edge", 2,
        [
            ((3 * cols + ANCH_ROWS, chans), BF16),
            ((rows, ANCH_ROWS, cols), BF16),
            ((8, LANES), F32),
            ((half + 3, cols, chans), BF16),
        ],
        [where, f, lab],
        [pltpu.SemaphoreType.DMA((4,))],
        [SMEM, HBM, VMEM],
        51,
    )
    met = others(count, "batch")
    pairs = []
    for i in range(tiles - 1):
        pairs += [(2 * i + 1, 2 * i + 2), (2 * i + 2, 2 * i + 1)]
    halo = lax.ppermute(msg, ("tile", "chan"), pairs)
    w1b = swap(w_shared, "chan")
    w2b = swap(w_cls, "chan")
    b1b = swap(b_shared, "chan")

    weights = [w_shared, w1b, b_shared.reshape(1, outs), b1b.reshape(1, outs)]
    (inner,) = call(inner_kernel, "inner", 3, [((half + 1, cols, chans), BF16)], [where, near] + weights)
    inner, *met = lax.optimization_barrier((inner, *met))
    count = pair_sum([count] + met)
    halo, _ = lax.optimization_barrier((halo, count))
    counts = [count] + others(count, "tile")
    hid, dz, loss, w2 = call(
        head_kernel, "head", 5,
        [((half + 4, cols, chans), BF16), ((half + 2, cols, LANES), F32), ((1, LANES), F32)]
        + [((9 * LANES, chans), BF16)],
        [where, near, inner, halo, labt]
        + weights
        + [jnp.swapaxes(w_cls, 2, 3), jnp.swapaxes(w2b, 2, 3), b_cls.reshape(1, LOGITS)],
        [((5, cols, chans), BF16)],
    )
    dt, own, other, small = call(
        back_kernel, "back", 4,
        [
            ((half, 3 * CLS_ROWS, cols), BF16),
            ((half, cols, outs), BF16),
            ((half, cols, outs), BF16),
            ((SMALL, LANES), F32),
        ],
        [where, hid, dz, loss, w2] + counts,
        [((half + 2, cols, LANES), BF16)],
    )
    theirs = swap(other, "chan")
    far = swap(halo, "chan")
    cls_total = round_up(9 * LOGITS, 16 * pages * tiles)
    gcls, gcls_other = call(
        cls_kernel, "cls", 1.5, [((cls_total, outs), F32)] * 2, [where, hid, dt]
    )
    gcls_theirs = swap(gcls_other, "chan")

    total = round_up(9 * chans, 16 * pages * tiles)
    first, second = total // pages, total // (pages * tiles)
    cfirst, csecond = cls_total // tiles, cls_total // (pages * tiles)
    keep, *sends = call(
        shared_kernel, "shared", 4,
        [((first, outs), F32)] + [((first, outs), BF16)] * (pages - 1),
        [where, f, halo, far, own, theirs],
        [((rows, cols, 3 * outs), BF16), ((total, outs), F32)],
    )
    ckeep, *csends = call(
        cls_split_kernel, "cls_split", 0.6,
        [((cfirst, outs), F32)] + [((cfirst + TRIO, outs), BF16)] * (tiles - 1),
        [where, gcls, gcls_theirs, small],
        [((cls_total, outs), F32)],
    )
    arrived = exchange(sends, "batch")
    carrived = exchange(csends, "tile")
    keep, small, *sends = call(
        functools.partial(sum_kernel, pages - 1, tiles - 1, tiles - 1), "sum", 0.7,
        [((second, outs), F32), ((SMALL, LANES), F32)]
        + [((second, outs), BF16)] * (tiles - 1)
        + [((csecond, outs), F32)]
        + [((csecond + TRIO, outs), BF16)] * (pages - 1),
        [where, keep, small, ckeep] + arrived + carrived,
        [((first, outs), F32), ((cfirst, outs), F32)],
    )
    ckeep, csends = sends[tiles - 1], sends[tiles:]
    arrived = exchange(sends[: tiles - 1], "tile")
    carrived = exchange(csends, "batch")
    done, small, cdone = call(
        functools.partial(round_kernel, tiles - 1), "round", 0.7,
        [((second, outs), BF16), ((SMALL, LANES), F32), ((csecond, outs), BF16)],
        [where, keep, small, ckeep] + arrived + carrived,
    )
    small_theirs = swap(small, "chan")
    block, cblock = call(
        functools.partial(join_kernel, tiles), "join", 0.7,
        [((first, outs), BF16), ((cfirst, outs), BF16)],
        [where, done] + others(done, "tile") + [cdone] + others(cdone, "batch"),
    )
    grad_shared, bias, grad_cls, cls_bias, loss = call(
        functools.partial(out_kernel, pages, tiles), "out", 1.5,
        [((9 * chans, outs), F32), ((1, outs), F32), ((3, 3, LOGITS, outs), F32), ((1, LOGITS), F32), ((1, 1), F32)],
        [where, small, small_theirs, block] + others(block, "batch") + [cblock] + others(cblock, "tile"),
        [((cls_total, outs), F32)] + ([((total, outs), F32)] if total > 9 * chans else []),
    )
    return (
        grad_shared.reshape(3, 3, chans, outs),
        bias.reshape(outs),
        jnp.swapaxes(grad_cls, 2, 3),
        cls_bias.reshape(LOGITS),
        loss.reshape(1),
    )


def solution(mesh):
    placed = (
        P(("groups", "batch"), "tile", None, None),
        P(("groups", "batch"), "tile", None),
        P(None, None, None, "chan"),
        P("chan"),
        P(None, None, "chan", None),
        P(),
    )
    return jax.shard_map(
        shards,
        mesh=mesh,
        in_specs=placed,
        out_specs=(
            P("groups", None, None, "chan"),
            P(("groups", "chan")),
            P("groups", None, "chan", None),
            P("groups"),
            P("groups"),
        ),
        check_vma=False,
    )
```

```python
import functools

import jax
import jax.numpy as jnp
from jax import lax
from jax.experimental import pallas as pl
from jax.experimental.pallas import tpu as pltpu
from jax.sharding import PartitionSpec as P

ANCH = 9
CLASSES = 11
LOGITS = 99
LANES = 128
ANCH_ROWS = 16
CLS_ROWS = 112
TILE, BATCH = 3, 4
BLOCK = 2
SMALL = 4
TRIO = 16
BF16 = jnp.bfloat16
F32 = jnp.float32
VMEM = pl.BlockSpec(memory_space=pltpu.VMEM)
HBM = pl.BlockSpec(memory_space=pltpu.HBM)
SMEM = pl.BlockSpec(memory_space=pltpu.SMEM)


class Places:
    def __init__(self, half):
        self.half = half

    def __getitem__(self, i):
        c, t = lax.axis_index("chan"), lax.axis_index("tile")
        if i == 0:
            return c
        if i == 1:
            return (2 * t + c) * self.half
        if i == 2:
            return 2 * lax.axis_size("tile") * self.half
        return t if i == 3 else lax.axis_index("batch")


def call(kernel, name, micros, outs, inputs, scratch=(), specs=None, mib=32):
    return pl.pallas_call(
        functools.partial(kernel, inputs[0]),
        in_specs=(specs or [SMEM] + [VMEM] * (len(inputs) - 1))[1:],
        out_specs=[VMEM] * len(outs),
        out_shape=[jax.ShapeDtypeStruct(shape, kind) for shape, kind in outs],
        scratch_shapes=[pltpu.VMEM(*shape) if isinstance(shape, tuple) else shape for shape in scratch],
        cost_estimate=pl.CostEstimate(flops=int(micros * 1e9), bytes_accessed=int(micros * 1e6), transcendentals=0),
        compiler_params=pltpu.CompilerParams(vmem_limit_bytes=int(mib * 1024 * 1024)),
        name=name,
    )(*inputs[1:])


def shift_cells(field, by):
    cells = field.shape[0]
    rolled = pltpu.roll(field, by % cells, axis=0)
    cell = lax.broadcasted_iota(jnp.int32, field.shape, 0)
    edge = 0 if by > 0 else cells - 1
    return jnp.where(cell == edge, 0.0, rolled)


def dot(left, right, dims=((1,), (0,))):
    return lax.dot_general(left, right, (dims, ((), ())), preferred_element_type=F32)


def taken(ref, start, rows):
    cols = ref.shape[1]
    parts = [ref[pl.ds(start + r, BLOCK)].reshape(BLOCK * cols, ref.shape[2]) for r in rows]
    return jnp.concatenate(parts, axis=1)


def three(x):
    high = x.astype(BF16)
    rest = x - high.astype(F32)
    middle = rest.astype(BF16)
    low = (rest - middle.astype(F32)).astype(BF16)
    return high, middle, low


def put_trio(ref, start, x):
    parts = [part.astype(F32) for part in three(x)]
    ref[start : start + TRIO] = jnp.concatenate(parts + [jnp.zeros_like(x)], axis=0).astype(BF16)


def get_trio(ref, start):
    part = ref[start : start + TRIO].astype(F32)
    return part[0:SMALL] + part[SMALL : 2 * SMALL] + part[2 * SMALL : 3 * SMALL]


def edge_kernel(where_ref, f_ref, lab_ref, msg_ref, labt_ref, count_ref, near_ref, sem):
    rows, cols, _ = f_ref.shape
    c = where_ref[0]
    copies = [
        pltpu.make_async_copy(f_ref.at[(rows - 3) * c + k], msg_ref.at[pl.ds(cols * k, cols)], sem.at[k])
        for k in range(3)
    ]
    near = near_ref.shape[0]
    copies.append(pltpu.make_async_copy(f_ref.at[pl.ds((rows - near) * c, near)], near_ref, sem.at[3]))
    for copy in copies:
        copy.start()
    size = lab_ref.shape[2]
    place = lax.broadcasted_iota(jnp.int32, (ANCH_ROWS, size), 1) % ANCH
    anchor = lax.broadcasted_iota(jnp.int32, (ANCH_ROWS, size), 0)
    mine = place == anchor
    labs = [lab_ref[r].astype(F32) for r in range(rows)]
    named = [jnp.where(lab > 0.0, 1.0, 0.0) for lab in labs]
    count_ref[...] = jnp.full(count_ref.shape, jnp.sum(sum(named[1:], named[0])), F32)
    left = jnp.concatenate([jnp.where(mine, lab, 0.0) for lab in labs], axis=0).astype(BF16)
    offset = lax.broadcasted_iota(jnp.int32, (size, cols), 0) - ANCH * lax.broadcasted_iota(jnp.int32, (size, cols), 1)
    pick = jnp.where(jnp.logical_and(offset >= 0, offset < ANCH), 1.0, 0.0).astype(BF16)
    turned = dot(left, pick).astype(BF16)
    for r in range(rows):
        labt_ref[r] = turned[ANCH_ROWS * r : ANCH_ROWS * (r + 1)]
    msg_ref[3 * cols : 3 * cols + ANCH_ROWS] = jnp.where(
        c == 0, turned[:ANCH_ROWS].astype(F32), turned[ANCH_ROWS * (rows - 1) :].astype(F32)
    ).astype(BF16)
    for copy in copies:
        copy.wait()


def hidden_rows(x, w1a_ref, w1b_ref, b1a_ref, b1b_ref):
    w1 = [
        jnp.concatenate(
            [part for j in range(3) for part in (w1a_ref[i, j], w1b_ref[i, j])], axis=1
        )
        for i in range(3)
    ]
    w1 = jnp.concatenate(w1, axis=0)
    b1 = jnp.concatenate([b1a_ref[...], b1b_ref[...]], axis=1)
    n = x.shape[0] - 2
    cols, chans = x.shape[1:]
    width = w1.shape[1] // 3
    for start in range(0, n, 4):
        count = min(4, n - start)
        parts = [x[start + r : start + r + count].reshape(count * cols, chans) for r in range(3)]
        many = dot(jnp.concatenate(parts, axis=1), w1)
        for k in range(count):
            y = many[k * cols : (k + 1) * cols]
            yield shift_cells(y[:, :width], 1) + y[:, width : 2 * width] + shift_cells(y[:, 2 * width :], -1) + b1


def inner_kernel(where_ref, near_ref, w1a_ref, w1b_ref, b1a_ref, b1b_ref, out_ref):
    for k, pre in enumerate(hidden_rows(near_ref, w1a_ref, w1b_ref, b1a_ref, b1b_ref)):
        out_ref[k] = jnp.maximum(pre, 0.0).astype(BF16)


def head_kernel(
    where_ref, near_ref, inner_ref, halo_ref, labt_ref, w1a_ref, w1b_ref, b1a_ref, b1b_ref, w2a_ref, w2b_ref, b2_ref,
    hid_ref, dz_ref, loss_ref, w2_ref, xw_ref,
):
    near = near_ref.shape[0]
    half = near - 3
    cols, chans = near_ref.shape[1:]
    c = where_ref[0]
    first = where_ref[1]
    total = where_ref[2]
    xw_ref[pl.ds(3 - 3 * c, 2)] = near_ref[pl.ds((near - 2) * c, 2)]
    for k in range(3):
        xw_ref[2 * c + k] = halo_ref[cols * k : cols * (k + 1)]
    hid_ref[pl.ds(3 - 3 * c, near - 2)] = inner_ref[...]
    for k, pre in enumerate(hidden_rows(xw_ref, w1a_ref, w1b_ref, b1a_ref, b1b_ref)):
        h = (near - 2) * c + k
        row = first + h - 2
        inside = jnp.logical_and(row >= 0, row < total)
        hid_ref[h] = jnp.where(inside, jnp.maximum(pre, 0.0), 0.0).astype(BF16)
    deep = chans // 2
    for tap in range(9):
        end = LANES * tap + LANES
        w2_ref[end - 32 : end] = jnp.zeros((32, chans), BF16)
        w2_ref[end - LANES : end - LANES + LOGITS, :deep] = w2a_ref[tap // 3, tap % 3]
        w2_ref[end - LANES : end - LANES + LOGITS, deep:] = w2b_ref[tap // 3, tap % 3]

    lane = lax.broadcasted_iota(jnp.int32, (1, LANES), 1)
    kind = (lane % CLASSES + 1).astype(F32)
    real = lane < LOGITS
    anchor = lax.broadcasted_iota(jnp.int32, (ANCH_ROWS, LANES), 0)
    column = lax.broadcasted_iota(jnp.int32, (ANCH_ROWS, LANES), 1)
    spread = jnp.where(jnp.logical_and(column // CLASSES == anchor, column < LOGITS), 1.0, 0.0).astype(BF16)
    size = 3 * LANES
    w2 = jnp.concatenate([w2_ref[size * i : size * (i + 1)] for i in range(3)], axis=1)
    b2 = jnp.concatenate([b2_ref[...], jnp.zeros((1, LANES - LOGITS), F32)], axis=1)

    def focal(g, loss):
        pair = dot(taken(hid_ref, BLOCK * g, (0, 1, 2)), w2, ((1,), (1,)))
        for k in range(BLOCK):
            loss = loss + focal_row(BLOCK * g + k, pair[k * cols : (k + 1) * cols])
        return loss

    def focal_row(l, y):
        z = shift_cells(y[:, :LANES], 1) + y[:, LANES : 2 * LANES] + shift_cells(y[:, 2 * LANES :], -1) + b2
        at_halo = jnp.where(c == 0, l == 0, l == half + 1)
        local = jnp.clip(l - 1 + half * c, 0, 2 * half - 1)
        mine = labt_ref[local].astype(F32)
        far = halo_ref[3 * cols : 3 * cols + ANCH_ROWS].astype(F32)
        lab = dot(jnp.where(at_halo, far, mine).astype(BF16), spread, ((0,), (0,)))
        row = first + l - 1
        inside = jnp.logical_and(row >= 0, row < total)
        hit = lab == kind
        keep = jnp.logical_and(jnp.logical_and(lab >= 0.0, real), inside)
        u = jnp.where(hit, -z, z)
        e = jnp.exp(-jnp.abs(u))
        r = 1.0 / (1.0 + e)
        er = e * r
        up = u >= 0.0
        s = jnp.where(up, r, er)
        comp = jnp.where(up, er, r)
        soft = jnp.maximum(u, 0.0) + jnp.log1p(e)
        ws = jnp.where(keep, jnp.where(hit, 0.25, 0.75), 0.0) * s * s
        slope = ws * (2.0 * comp * soft + s)
        dz_ref[l] = jnp.where(hit, -slope, slope)
        own = jnp.logical_and(l >= 1, l <= half)
        return jnp.where(own, 1.0, 0.0) * jnp.sum(ws * soft, axis=0, keepdims=True)

    loss_ref[...] = lax.fori_loop(0, (half + 2) // BLOCK, focal, jnp.zeros((1, LANES), F32), unroll=True)


def back_kernel(where_ref, hid_ref, dz_ref, loss_ref, w2_ref, *rest):
    *count_refs, dt_ref, own_ref, other_ref, small_ref, dlog_ref = rest
    half, _, cols = dt_ref.shape
    chans = hid_ref.shape[2]
    inverse = 1.0 / pair_sum([ref[...] for ref in count_refs])[:1]

    def scaled(l):
        dz = dz_ref[l] * inverse
        d16 = dz.astype(BF16)
        dlog_ref[l] = d16
        return dz, d16

    scaled(0)
    scaled(half + 1)

    def turn(d, gcb):
        dz, d16 = scaled(d + 1)
        turned = jnp.transpose(d16.astype(F32))[:CLS_ROWS]
        cell = lax.broadcasted_iota(jnp.int32, turned.shape, 1)
        left = jnp.where(cell == cols - 1, 0.0, pltpu.roll(turned, cols - 1, axis=1))
        right = jnp.where(cell == 0, 0.0, pltpu.roll(turned, 1, axis=1))
        dt_ref[d] = jnp.concatenate([left, turned, right], axis=0).astype(BF16)
        return gcb + jnp.sum(dz, axis=0, keepdims=True)

    gcb = lax.fori_loop(0, half, turn, jnp.zeros((1, LANES), F32), unroll=True)
    w2t = [
        jnp.concatenate([w2_ref[LANES * (3 * i + j) : LANES * (3 * i + j + 1)] for j in range(3)], axis=1)
        for i in range(3)
    ]
    w2t = jnp.concatenate(w2t, axis=0)

    def dpre(g, gsb):
        pair = dot(taken(dlog_ref, BLOCK * g, (2, 1, 0)), w2t)
        for k in range(BLOCK):
            gsb = gsb + dpre_row(BLOCK * g + k, pair[k * cols : (k + 1) * cols])
        return gsb

    def dpre_row(d, q):
        dhid = shift_cells(q[:, :chans], -1) + q[:, chans : 2 * chans] + shift_cells(q[:, 2 * chans :], 1)
        dpre = jnp.where(hid_ref[d + 2].astype(F32) > 0.0, dhid, 0.0)
        d16 = dpre.astype(BF16)
        own_ref[d] = d16[:, : chans // 2]
        other_ref[d] = d16[:, chans // 2 :]
        return jnp.sum(dpre, axis=0, keepdims=True)

    gsb = lax.fori_loop(0, half // BLOCK, dpre, jnp.zeros((1, chans), F32), unroll=True)
    loss = jnp.sum(loss_ref[...], axis=1, keepdims=True) * inverse[:, :1]
    small_ref[0:1] = jnp.where(lax.broadcasted_iota(jnp.int32, (1, LANES), 1) < LOGITS, gcb, loss)
    small_ref[1:2] = jnp.zeros((1, LANES), F32)
    small_ref[2:3] = gsb[:, : chans // 2]
    small_ref[3:4] = gsb[:, chans // 2 :]


def cls_kernel(where_ref, hid_ref, dt_ref, own_ref, other_ref):
    half, _, cols = dt_ref.shape
    chans = hid_ref.shape[2]
    deep = chans // 2
    dt = jnp.concatenate([dt_ref[d] for d in range(half)], axis=1)
    for i in range(3):
        g = dot(dt, hid_ref[i + 1 : i + 1 + half].reshape(half * cols, chans))
        for j in range(3):
            start = LOGITS * (3 * i + j)
            own_ref[start : start + LOGITS] = g[CLS_ROWS * j : CLS_ROWS * j + LOGITS, :deep]
            other_ref[start : start + LOGITS] = g[CLS_ROWS * j : CLS_ROWS * j + LOGITS, deep:]
    blank = jnp.zeros((own_ref.shape[0] - 9 * LOGITS, deep), F32)
    own_ref[9 * LOGITS :] = blank
    other_ref[9 * LOGITS :] = blank


def split(total, me, keep_ref, send_refs):
    rows = keep_ref.shape[0]
    keep_ref[...] = total[pl.ds(pl.multiple_of(me * rows, 8), rows)]
    size = len(send_refs) + 1
    for k, ref in enumerate(send_refs):
        ref[0:rows] = total[pl.ds(pl.multiple_of((me ^ (size - 1 - k)) * rows, 8), rows)].astype(BF16)


def shared_kernel(
    where_ref, f_ref, halo_ref, far_ref, own_ref, other_ref, keep_ref, *rest
):
    *send_refs, d_ref, g_ref = rest
    rows, cols, chans = f_ref.shape
    half = rows // 2
    c = where_ref[0]
    near = halo_ref[pl.ds(pl.multiple_of(2 * cols * (1 - c), 16), cols)]
    far = far_ref[pl.ds(pl.multiple_of(2 * cols * c, 16), cols)]
    before = jnp.where(c == 0, near, far)
    after = jnp.where(c == 0, far, near)

    for r in range(rows):
        mine, theirs = own_ref[r % half].astype(F32), other_ref[r % half].astype(F32)
        mid = jnp.where(c == (0 if r < half else 1), mine, theirs)
        d_ref[r] = jnp.concatenate([shift_cells(mid, -1), mid, shift_cells(mid, 1)], axis=1).astype(BF16)
    outs = d_ref.shape[2] // 3

    def part(x, first):
        n = x.shape[0]
        rhs = d_ref[first : first + n].reshape(n * cols, 3 * outs)
        return dot(x.reshape(n * cols, chans), rhs, ((0,), (0,)))

    for i in range(3):
        if i == 0:
            g = part(f_ref[0 : rows - 1], 1) + part(before[None], 0)
        elif i == 1:
            g = part(f_ref[...], 0)
        else:
            g = part(f_ref[1:rows], 0) + part(after[None], rows - 1)
        for j in range(3):
            start = (3 * i + j) * chans
            g_ref[start : start + chans] = g[:, j * outs : (j + 1) * outs]
    if g_ref.shape[0] > 9 * chans:
        g_ref[9 * chans :] = jnp.zeros((g_ref.shape[0] - 9 * chans, outs), F32)
    split(g_ref, where_ref[BATCH], keep_ref, send_refs)


def lane_half(shape):
    return lax.broadcasted_iota(jnp.int32, shape, len(shape) - 1) < LANES // 2


def low_pair(a, b):
    return jnp.where(lane_half(a.shape), a, pltpu.roll(b, LANES // 2, axis=1))


def high_pair(a, b):
    return jnp.where(lane_half(a.shape), pltpu.roll(a, LANES // 2, axis=1), b)


def half_kernel(flip, where_ref, f_ref, halo_ref, far_ref, own_ref, other_ref, out_ref, d_ref):
    rows, cols, chans = f_ref.shape
    half = rows // 2
    c = where_ref[0]
    upper = (where_ref[BATCH] ^ flip) == 1
    near = halo_ref[pl.ds(pl.multiple_of(2 * cols * (1 - c), 16), cols)]
    far = far_ref[pl.ds(pl.multiple_of(2 * cols * c, 16), cols)]
    before = jnp.where(c == 0, near, far)
    after = jnp.where(c == 0, far, near)
    for r in range(rows):
        mine, theirs = own_ref[r % half].astype(F32), other_ref[r % half].astype(F32)
        mid = jnp.where(c == (0 if r < half else 1), mine, theirs)
        mid = jnp.where(upper, pltpu.roll(mid, LANES // 2, axis=1), mid)
        pair = low_pair(shift_cells(mid, -1), mid)
        d_ref[r] = jnp.concatenate([pair, shift_cells(mid, 1)], axis=1).astype(BF16)

    def part(x, first):
        n = x.shape[0]
        rhs = d_ref[first : first + n].reshape(n * cols, 2 * LANES)
        return dot(x.reshape(n * cols, chans), rhs, ((0,), (0,)))

    taps = [
        part(f_ref[0 : rows - 1], 1) + part(before[None], 0),
        part(f_ref[...], 0),
        part(f_ref[1:rows], 0) + part(after[None], rows - 1),
    ]
    last = [g[:, LANES:] for g in taps]
    for i in range(3):
        out_ref[chans * i : chans * (i + 1)] = taps[i][:, :LANES].astype(out_ref.dtype)
    out_ref[3 * chans : 4 * chans] = low_pair(last[0], last[1]).astype(out_ref.dtype)
    out_ref[4 * chans :] = low_pair(last[2][: chans // 2], last[2][chans // 2 :]).astype(out_ref.dtype)


def unpack(place, own_ref, other_ref, out_ref):
    rows = own_ref.shape[0]
    chans = out_ref.shape[0] // 9
    own, other = own_ref[...].astype(F32), other_ref[...].astype(F32)
    low = jnp.where(place == 0, own, other)
    high = jnp.where(place == 0, other, own)
    first, second = low_pair(low, high), high_pair(low, high)
    for i in range(3):
        out_ref[chans * 3 * i : chans * (3 * i + 1)] = first[chans * i : chans * (i + 1)]
        out_ref[chans * (3 * i + 1) : chans * (3 * i + 2)] = second[chans * i : chans * (i + 1)]
    out_ref[chans * 2 : chans * 3] = first[3 * chans : 4 * chans]
    out_ref[chans * 5 : chans * 6] = second[3 * chans : 4 * chans]
    out_ref[chans * 8 : chans * 8 + chans // 2] = first[4 * chans : rows]
    out_ref[chans * 8 + chans // 2 : chans * 9] = second[4 * chans : rows]


def cls_split_kernel(where_ref, cls_ref, theirs_ref, small_ref, keep_ref, *rest):
    *send_refs, total_ref = rest
    total_ref[...] = cls_ref[...] + theirs_ref[...]
    split(total_ref, where_ref[TILE], keep_ref, send_refs)
    for ref in send_refs:
        put_trio(ref, keep_ref.shape[0], small_ref[...])


def pair_sum(parts):
    while len(parts) > 1:
        parts = [parts[k] + parts[k + 1] for k in range(0, len(parts), 2)]
    return parts[0]


def total_of(base_ref, in_refs):
    rows = base_ref.shape[0]
    total = base_ref[...]
    for ref in in_refs:
        total = total + ref[0:rows].astype(F32)
    return total


def small_sum(small_ref, in_refs, start):
    return pair_sum([small_ref[...]] + [get_trio(ref, start) for ref in in_refs])


def sum_kernel(n_in, n_cls, n_send, where_ref, base_ref, small_ref, cls_ref, *refs):
    in_refs, refs = refs[:n_in], refs[n_in:]
    cls_in_refs, refs = refs[:n_cls], refs[n_cls:]
    keep_ref, sum_ref, *refs, total_ref, cls_total_ref = refs
    send_refs, cls_keep_ref, cls_send_refs = refs[:n_send], refs[n_send], refs[n_send + 1 :]
    total_ref[...] = total_of(base_ref, in_refs)
    split(total_ref, where_ref[TILE], keep_ref, send_refs)
    cls_total_ref[...] = total_of(cls_ref, cls_in_refs)
    split(cls_total_ref, where_ref[BATCH], cls_keep_ref, cls_send_refs)
    sums = small_sum(small_ref, cls_in_refs, cls_ref.shape[0])
    sum_ref[...] = sums
    for ref in cls_send_refs:
        put_trio(ref, cls_keep_ref.shape[0], sums)


def round_kernel(n_in, where_ref, base_ref, small_ref, cls_ref, *refs):
    in_refs, cls_in_refs = refs[:n_in], refs[n_in:-3]
    out_ref, sum_ref, cls_out_ref = refs[-3:]
    out_ref[...] = total_of(base_ref, in_refs).astype(BF16)
    cls_out_ref[...] = total_of(cls_ref, cls_in_refs).astype(BF16)
    sum_ref[...] = small_sum(small_ref, cls_in_refs, cls_ref.shape[0])


def join(me, in_refs, out_ref):
    rows = in_refs[0].shape[0]
    for k, ref in enumerate(in_refs):
        out_ref[pl.ds(pl.multiple_of((me ^ k) * rows, 8), rows)] = ref[...].astype(out_ref.dtype)


def join_kernel(n_in, where_ref, *refs):
    join(where_ref[TILE], refs[:n_in], refs[-2])
    join(where_ref[BATCH], refs[n_in:-2], refs[-1])


def out_kernel(n_in, n_cls, halves, where_ref, small_ref, theirs_ref, *refs):
    in_refs, cls_in_refs, refs = refs[:n_in], refs[n_in : n_in + n_cls], refs[n_in + n_cls :]
    out_ref, bias_ref, cls_out_ref, cls_bias_ref, loss_ref, cls_whole_ref, *whole_ref = refs
    if halves:
        unpack(where_ref[BATCH], in_refs[0], in_refs[1], out_ref)
    elif whole_ref:
        join(where_ref[BATCH], in_refs, whole_ref[0])
        out_ref[...] = whole_ref[0][: out_ref.shape[0]]
    else:
        join(where_ref[BATCH], in_refs, out_ref)
    join(where_ref[TILE], cls_in_refs, cls_whole_ref)
    for tap in range(9):
        cls_out_ref[tap // 3, tap % 3] = cls_whole_ref[LOGITS * tap : LOGITS * (tap + 1)]
    bias_ref[...] = small_ref[2:3] + theirs_ref[3:4]
    both = small_ref[0:1] + theirs_ref[0:1]
    cls_bias_ref[...] = both[:, :LOGITS]
    loss_ref[...] = both[:, LOGITS : LOGITS + 1]


def swap(x, axis, bit=1):
    size = lax.axis_size(axis)
    return lax.ppermute(x, axis, [(i, i ^ bit) for i in range(size)])


def others(x, axis):
    return [swap(x, axis, bit) for bit in range(1, lax.axis_size(axis))]


def exchange(sends, axis):
    size = len(sends) + 1
    return [swap(x, axis, size - 1 - k) for k, x in enumerate(sends)]


def round_up(n, step):
    return (n + step - 1) // step * step


def shards(features, labels, w_shared, b_shared, w_cls, b_cls):
    _, rows, cols, chans = features.shape
    half = rows // 2
    outs = w_shared.shape[3]
    tiles = lax.axis_size("tile")
    pages = lax.axis_size("batch")
    c = lax.axis_index("chan")
    t = lax.axis_index("tile")
    f = features[0]
    where = Places(half)
    lab = labels.reshape(rows, 1, labels.shape[2])
    msg, labt, count, near = call(
        edge_kernel, "edge", 2,
        [
            ((3 * cols + ANCH_ROWS, chans), BF16),
            ((rows, ANCH_ROWS, cols), BF16),
            ((8, LANES), F32),
            ((half + 3, cols, chans), BF16),
        ],
        [where, f, lab],
        [pltpu.SemaphoreType.DMA((4,))],
        [SMEM, HBM, VMEM],
        51,
    )
    met = others(count, "batch")
    pairs = []
    for i in range(tiles - 1):
        pairs += [(2 * i + 1, 2 * i + 2), (2 * i + 2, 2 * i + 1)]
    halo = lax.ppermute(msg, ("tile", "chan"), pairs)
    w1b = swap(w_shared, "chan")
    w2b = swap(w_cls, "chan")
    b1b = swap(b_shared, "chan")

    weights = [w_shared, w1b, b_shared.reshape(1, outs), b1b.reshape(1, outs)]
    (inner,) = call(inner_kernel, "inner", 3, [((half + 1, cols, chans), BF16)], [where, near] + weights)
    inner, *met = lax.optimization_barrier((inner, *met))
    count = pair_sum([count] + met)
    halo, _ = lax.optimization_barrier((halo, count))
    counts = [count] + others(count, "tile")
    hid, dz, loss, w2 = call(
        head_kernel, "head", 5,
        [((half + 4, cols, chans), BF16), ((half + 2, cols, LANES), F32), ((1, LANES), F32)]
        + [((9 * LANES, chans), BF16)],
        [where, near, inner, halo, labt]
        + weights
        + [jnp.swapaxes(w_cls, 2, 3), jnp.swapaxes(w2b, 2, 3), b_cls.reshape(1, LOGITS)],
        [((5, cols, chans), BF16)],
    )
    dt, own, other, small = call(
        back_kernel, "back", 4,
        [
            ((half, 3 * CLS_ROWS, cols), BF16),
            ((half, cols, outs), BF16),
            ((half, cols, outs), BF16),
            ((SMALL, LANES), F32),
        ],
        [where, hid, dz, loss, w2] + counts,
        [((half + 2, cols, LANES), BF16)],
    )
    theirs = swap(other, "chan")
    later, _ = lax.optimization_barrier((halo, loss))
    far = swap(later, "chan")
    cls_total = round_up(9 * LOGITS, 16 * pages * tiles)
    gcls, gcls_other = call(
        cls_kernel, "cls", 1.5, [((cls_total, outs), F32)] * 2, [where, hid, dt]
    )
    gcls_theirs = swap(gcls_other, "chan")

    total = round_up(9 * chans, 16 * pages * tiles)
    first, second = total // pages, total // (pages * tiles)
    cfirst, csecond = cls_total // tiles, cls_total // (pages * tiles)
    halves = pages == 2 and outs == LANES and first % (16 * tiles) == 0 and total == 9 * chans
    shared_inputs = [where, f, halo, far, own, theirs]
    if halves:
        scratch = [((rows, cols, 2 * LANES), BF16)]
        sends = call(
            functools.partial(half_kernel, 1), "shared_sent", 2, [((first, outs), BF16)], shared_inputs, scratch
        )
        (keep,) = call(
            functools.partial(half_kernel, 0), "shared_kept", 2, [((first, outs), F32)], shared_inputs, scratch
        )
    else:
        keep, *sends = call(
            shared_kernel, "shared", 4,
            [((first, outs), F32)] + [((first, outs), BF16)] * (pages - 1),
            shared_inputs,
            [((rows, cols, 3 * outs), BF16), ((total, outs), F32)],
        )
    ckeep, *csends = call(
        cls_split_kernel, "cls_split", 0.6,
        [((cfirst, outs), F32)] + [((cfirst + TRIO, outs), BF16)] * (tiles - 1),
        [where, gcls, gcls_theirs, small],
        [((cls_total, outs), F32)],
    )
    arrived = exchange(sends, "batch")
    carrived = exchange(csends, "tile")
    keep, small, *sends = call(
        functools.partial(sum_kernel, pages - 1, tiles - 1, tiles - 1), "sum", 0.7,
        [((second, outs), F32), ((SMALL, LANES), F32)]
        + [((second, outs), BF16)] * (tiles - 1)
        + [((csecond, outs), F32)]
        + [((csecond + TRIO, outs), BF16)] * (pages - 1),
        [where, keep, small, ckeep] + arrived + carrived,
        [((first, outs), F32), ((cfirst, outs), F32)],
    )
    ckeep, csends = sends[tiles - 1], sends[tiles:]
    arrived = exchange(sends[: tiles - 1], "tile")
    carrived = exchange(csends, "batch")
    done, small, cdone = call(
        functools.partial(round_kernel, tiles - 1), "round", 0.7,
        [((second, outs), BF16), ((SMALL, LANES), F32), ((csecond, outs), BF16)],
        [where, keep, small, ckeep] + arrived + carrived,
    )
    small_theirs = swap(small, "chan")
    block, cblock = call(
        functools.partial(join_kernel, tiles), "join", 0.7,
        [((first, outs), BF16), ((cfirst, outs), BF16)],
        [where, done] + others(done, "tile") + [cdone] + others(cdone, "batch"),
    )
    grad_shared, bias, grad_cls, cls_bias, loss = call(
        functools.partial(out_kernel, pages, tiles, halves), "out", 1.5,
        [((9 * chans, outs), F32), ((1, outs), F32), ((3, 3, LOGITS, outs), F32), ((1, LOGITS), F32), ((1, 1), F32)],
        [where, small, small_theirs, block] + others(block, "batch") + [cblock] + others(cblock, "tile"),
        [((cls_total, outs), F32)] + ([((total, outs), F32)] if total > 9 * chans else []),
    )
    return (
        grad_shared.reshape(3, 3, chans, outs),
        bias.reshape(outs),
        jnp.swapaxes(grad_cls, 2, 3),
        cls_bias.reshape(LOGITS),
        loss.reshape(1),
    )


def solution(mesh):
    placed = (
        P(("groups", "batch"), "tile", None, None),
        P(("groups", "batch"), "tile", None),
        P(None, None, None, "chan"),
        P("chan"),
        P(None, None, "chan", None),
        P(),
    )
    return jax.shard_map(
        shards,
        mesh=mesh,
        in_specs=placed,
        out_specs=(
            P("groups", None, None, "chan"),
            P(("groups", "chan")),
            P("groups", None, "chan", None),
            P("groups"),
            P("groups"),
        ),
        check_vma=False,
    )
```

```python
import functools

import jax
import jax.numpy as jnp
from jax import lax
from jax.experimental import pallas as pl
from jax.experimental.pallas import tpu as pltpu
from jax.sharding import PartitionSpec as P

ANCH = 9
CLASSES = 11
LOGITS = 99
LANES = 128
ANCH_ROWS = 16
CLS_ROWS = 112
TILE, BATCH = 3, 4
BLOCK = 2
SMALL = 4
TRIO = 16
BF16 = jnp.bfloat16
F32 = jnp.float32
VMEM = pl.BlockSpec(memory_space=pltpu.VMEM)
HBM = pl.BlockSpec(memory_space=pltpu.HBM)
SMEM = pl.BlockSpec(memory_space=pltpu.SMEM)


class Places:
    def __init__(self, half):
        self.half = half

    def __getitem__(self, i):
        c, t = lax.axis_index("chan"), lax.axis_index("tile")
        if i == 0:
            return c
        if i == 1:
            return (2 * t + c) * self.half
        if i == 2:
            return 2 * lax.axis_size("tile") * self.half
        return t if i == 3 else lax.axis_index("batch")


def call(kernel, name, micros, outs, inputs, scratch=(), specs=None, mib=32):
    return pl.pallas_call(
        functools.partial(kernel, inputs[0]),
        in_specs=(specs or [SMEM] + [VMEM] * (len(inputs) - 1))[1:],
        out_specs=[VMEM] * len(outs),
        out_shape=[jax.ShapeDtypeStruct(shape, kind) for shape, kind in outs],
        scratch_shapes=[pltpu.VMEM(*shape) if isinstance(shape, tuple) else shape for shape in scratch],
        cost_estimate=pl.CostEstimate(flops=int(micros * 1e9), bytes_accessed=int(micros * 1e6), transcendentals=0),
        compiler_params=pltpu.CompilerParams(vmem_limit_bytes=int(mib * 1024 * 1024)),
        name=name,
    )(*inputs[1:])


def shift_cells(field, by):
    cells = field.shape[0]
    rolled = pltpu.roll(field, by % cells, axis=0)
    cell = lax.broadcasted_iota(jnp.int32, field.shape, 0)
    edge = 0 if by > 0 else cells - 1
    return jnp.where(cell == edge, 0.0, rolled)


def beside(row):
    return jnp.concatenate([shift_cells(row, -1), row, shift_cells(row, 1)], axis=1).astype(BF16)


def dot(left, right, dims=((1,), (0,))):
    return lax.dot_general(left, right, (dims, ((), ())), preferred_element_type=F32)


def taken(ref, start, rows):
    cols = ref.shape[1]
    parts = [ref[pl.ds(start + r, BLOCK)].reshape(BLOCK * cols, ref.shape[2]) for r in rows]
    return jnp.concatenate(parts, axis=1)


def three(x):
    high = x.astype(BF16)
    rest = x - high.astype(F32)
    middle = rest.astype(BF16)
    low = (rest - middle.astype(F32)).astype(BF16)
    return high, middle, low


def put_trio(ref, start, x):
    parts = [part.astype(F32) for part in three(x)]
    ref[start : start + TRIO] = jnp.concatenate(parts + [jnp.zeros_like(x)], axis=0).astype(BF16)


def get_trio(ref, start):
    part = ref[start : start + TRIO].astype(F32)
    return part[0:SMALL] + part[SMALL : 2 * SMALL] + part[2 * SMALL : 3 * SMALL]


def edge_kernel(where_ref, f_ref, lab_ref, msg_ref, labt_ref, count_ref, near_ref, sem):
    rows, cols, _ = f_ref.shape
    c = where_ref[0]
    copies = [
        pltpu.make_async_copy(f_ref.at[(rows - 3) * c + k], msg_ref.at[pl.ds(cols * k, cols)], sem.at[k])
        for k in range(3)
    ]
    near = near_ref.shape[0]
    copies.append(pltpu.make_async_copy(f_ref.at[pl.ds((rows - near) * c, near)], near_ref, sem.at[3]))
    for copy in copies:
        copy.start()
    size = lab_ref.shape[2]
    place = lax.broadcasted_iota(jnp.int32, (ANCH_ROWS, size), 1) % ANCH
    anchor = lax.broadcasted_iota(jnp.int32, (ANCH_ROWS, size), 0)
    mine = place == anchor
    labs = [lab_ref[r].astype(F32) for r in range(rows)]
    named = [jnp.where(lab > 0.0, 1.0, 0.0) for lab in labs]
    count_ref[...] = jnp.full(count_ref.shape, jnp.sum(sum(named[1:], named[0])), F32)
    left = jnp.concatenate([jnp.where(mine, lab, 0.0) for lab in labs], axis=0).astype(BF16)
    offset = lax.broadcasted_iota(jnp.int32, (size, cols), 0) - ANCH * lax.broadcasted_iota(jnp.int32, (size, cols), 1)
    pick = jnp.where(jnp.logical_and(offset >= 0, offset < ANCH), 1.0, 0.0).astype(BF16)
    turned = dot(left, pick).astype(BF16)
    for r in range(rows):
        labt_ref[r] = turned[ANCH_ROWS * r : ANCH_ROWS * (r + 1)]
    msg_ref[3 * cols : 3 * cols + ANCH_ROWS] = jnp.where(
        c == 0, turned[:ANCH_ROWS].astype(F32), turned[ANCH_ROWS * (rows - 1) :].astype(F32)
    ).astype(BF16)
    for copy in copies:
        copy.wait()


def hidden_rows(x, w1a_ref, w1b_ref, b1a_ref, b1b_ref):
    w1 = [
        jnp.concatenate(
            [part for j in range(3) for part in (w1a_ref[i, j], w1b_ref[i, j])], axis=1
        )
        for i in range(3)
    ]
    w1 = jnp.concatenate(w1, axis=0)
    b1 = jnp.concatenate([b1a_ref[...], b1b_ref[...]], axis=1)
    n = x.shape[0] - 2
    cols, chans = x.shape[1:]
    width = w1.shape[1] // 3
    for start in range(0, n, 4):
        count = min(4, n - start)
        parts = [x[start + r : start + r + count].reshape(count * cols, chans) for r in range(3)]
        many = dot(jnp.concatenate(parts, axis=1), w1)
        for k in range(count):
            y = many[k * cols : (k + 1) * cols]
            yield shift_cells(y[:, :width], 1) + y[:, width : 2 * width] + shift_cells(y[:, 2 * width :], -1) + b1


def inner_kernel(where_ref, near_ref, w1a_ref, w1b_ref, b1a_ref, b1b_ref, out_ref):
    for k, pre in enumerate(hidden_rows(near_ref, w1a_ref, w1b_ref, b1a_ref, b1b_ref)):
        out_ref[k] = jnp.maximum(pre, 0.0).astype(BF16)


def head_kernel(
    where_ref, near_ref, inner_ref, halo_ref, labt_ref, w1a_ref, w1b_ref, b1a_ref, b1b_ref, w2a_ref, w2b_ref, b2_ref,
    hid_ref, dz_ref, loss_ref, w2_ref, xw_ref,
):
    near = near_ref.shape[0]
    half = near - 3
    cols, chans = near_ref.shape[1:]
    c = where_ref[0]
    first = where_ref[1]
    total = where_ref[2]
    xw_ref[pl.ds(3 - 3 * c, 2)] = near_ref[pl.ds((near - 2) * c, 2)]
    for k in range(3):
        xw_ref[2 * c + k] = halo_ref[cols * k : cols * (k + 1)]
    hid_ref[pl.ds(3 - 3 * c, near - 2)] = inner_ref[...]
    for k, pre in enumerate(hidden_rows(xw_ref, w1a_ref, w1b_ref, b1a_ref, b1b_ref)):
        h = (near - 2) * c + k
        row = first + h - 2
        inside = jnp.logical_and(row >= 0, row < total)
        hid_ref[h] = jnp.where(inside, jnp.maximum(pre, 0.0), 0.0).astype(BF16)
    deep = chans // 2
    for tap in range(9):
        end = LANES * tap + LANES
        w2_ref[end - 32 : end] = jnp.zeros((32, chans), BF16)
        w2_ref[end - LANES : end - LANES + LOGITS, :deep] = w2a_ref[tap // 3, tap % 3]
        w2_ref[end - LANES : end - LANES + LOGITS, deep:] = w2b_ref[tap // 3, tap % 3]

    lane = lax.broadcasted_iota(jnp.int32, (1, LANES), 1)
    kind = (lane % CLASSES + 1).astype(F32)
    real = lane < LOGITS
    anchor = lax.broadcasted_iota(jnp.int32, (ANCH_ROWS, LANES), 0)
    column = lax.broadcasted_iota(jnp.int32, (ANCH_ROWS, LANES), 1)
    spread = jnp.where(jnp.logical_and(column // CLASSES == anchor, column < LOGITS), 1.0, 0.0).astype(BF16)
    size = 3 * LANES
    w2 = jnp.concatenate([w2_ref[size * i : size * (i + 1)] for i in range(3)], axis=1)
    b2 = jnp.concatenate([b2_ref[...], jnp.zeros((1, LANES - LOGITS), F32)], axis=1)

    def focal(g, loss):
        pair = dot(taken(hid_ref, BLOCK * g, (0, 1, 2)), w2, ((1,), (1,)))
        for k in range(BLOCK):
            loss = loss + focal_row(BLOCK * g + k, pair[k * cols : (k + 1) * cols])
        return loss

    def focal_row(l, y):
        z = shift_cells(y[:, :LANES], 1) + y[:, LANES : 2 * LANES] + shift_cells(y[:, 2 * LANES :], -1) + b2
        at_halo = jnp.where(c == 0, l == 0, l == half + 1)
        local = jnp.clip(l - 1 + half * c, 0, 2 * half - 1)
        mine = labt_ref[local].astype(F32)
        far = halo_ref[3 * cols : 3 * cols + ANCH_ROWS].astype(F32)
        lab = dot(jnp.where(at_halo, far, mine).astype(BF16), spread, ((0,), (0,)))
        row = first + l - 1
        inside = jnp.logical_and(row >= 0, row < total)
        hit = lab == kind
        keep = jnp.logical_and(jnp.logical_and(lab >= 0.0, real), inside)
        u = jnp.where(hit, -z, z)
        e = jnp.exp(-jnp.abs(u))
        r = 1.0 / (1.0 + e)
        er = e * r
        up = u >= 0.0
        s = jnp.where(up, r, er)
        comp = jnp.where(up, er, r)
        soft = jnp.maximum(u, 0.0) + jnp.log1p(e)
        ws = jnp.where(keep, jnp.where(hit, 0.25, 0.75), 0.0) * s * s
        slope = ws * (2.0 * comp * soft + s)
        dz_ref[l] = jnp.where(hit, -slope, slope)
        own = jnp.logical_and(l >= 1, l <= half)
        return jnp.where(own, 1.0, 0.0) * jnp.sum(ws * soft, axis=0, keepdims=True)

    loss_ref[...] = lax.fori_loop(0, (half + 2) // BLOCK, focal, jnp.zeros((1, LANES), F32), unroll=True)


def back_kernel(where_ref, hid_ref, dz_ref, loss_ref, w2_ref, *rest):
    *count_refs, dt_ref, own_ref, other_ref, small_ref, dlog_ref = rest
    half, _, cols = dt_ref.shape
    chans = hid_ref.shape[2]
    inverse = 1.0 / pair_sum([ref[...] for ref in count_refs])[:1]

    def scaled(l):
        dz = dz_ref[l] * inverse
        d16 = dz.astype(BF16)
        dlog_ref[l] = d16
        return dz, d16

    scaled(0)
    scaled(half + 1)

    def turn(d, gcb):
        dz, d16 = scaled(d + 1)
        turned = jnp.transpose(d16.astype(F32))[:CLS_ROWS]
        cell = lax.broadcasted_iota(jnp.int32, turned.shape, 1)
        left = jnp.where(cell == cols - 1, 0.0, pltpu.roll(turned, cols - 1, axis=1))
        right = jnp.where(cell == 0, 0.0, pltpu.roll(turned, 1, axis=1))
        dt_ref[d] = jnp.concatenate([left, turned, right], axis=0).astype(BF16)
        return gcb + jnp.sum(dz, axis=0, keepdims=True)

    gcb = lax.fori_loop(0, half, turn, jnp.zeros((1, LANES), F32), unroll=True)
    w2t = [
        jnp.concatenate([w2_ref[LANES * (3 * i + j) : LANES * (3 * i + j + 1)] for j in range(3)], axis=1)
        for i in range(3)
    ]
    w2t = jnp.concatenate(w2t, axis=0)

    def dpre(g, gsb):
        pair = dot(taken(dlog_ref, BLOCK * g, (2, 1, 0)), w2t)
        for k in range(BLOCK):
            gsb = gsb + dpre_row(BLOCK * g + k, pair[k * cols : (k + 1) * cols])
        return gsb

    def dpre_row(d, q):
        dhid = shift_cells(q[:, :chans], -1) + q[:, chans : 2 * chans] + shift_cells(q[:, 2 * chans :], 1)
        dpre = jnp.where(hid_ref[d + 2].astype(F32) > 0.0, dhid, 0.0)
        d16 = dpre.astype(BF16)
        own_ref[d] = beside(d16[:, : chans // 2].astype(F32))
        other_ref[d] = d16[:, chans // 2 :]
        return jnp.sum(dpre, axis=0, keepdims=True)

    gsb = lax.fori_loop(0, half // BLOCK, dpre, jnp.zeros((1, chans), F32), unroll=True)
    loss = jnp.sum(loss_ref[...], axis=1, keepdims=True) * inverse[:, :1]
    small_ref[0:1] = jnp.where(lax.broadcasted_iota(jnp.int32, (1, LANES), 1) < LOGITS, gcb, loss)
    small_ref[1:2] = jnp.zeros((1, LANES), F32)
    small_ref[2:3] = gsb[:, : chans // 2]
    small_ref[3:4] = gsb[:, chans // 2 :]


def cls_kernel(where_ref, hid_ref, dt_ref, own_ref, other_ref):
    half, _, cols = dt_ref.shape
    chans = hid_ref.shape[2]
    deep = chans // 2
    dt = jnp.concatenate([dt_ref[d] for d in range(half)], axis=1)
    for i in range(3):
        g = dot(dt, hid_ref[i + 1 : i + 1 + half].reshape(half * cols, chans))
        for j in range(3):
            start = LOGITS * (3 * i + j)
            own_ref[start : start + LOGITS] = g[CLS_ROWS * j : CLS_ROWS * j + LOGITS, :deep]
            other_ref[start : start + LOGITS] = g[CLS_ROWS * j : CLS_ROWS * j + LOGITS, deep:]
    blank = jnp.zeros((own_ref.shape[0] - 9 * LOGITS, deep), F32)
    own_ref[9 * LOGITS :] = blank
    other_ref[9 * LOGITS :] = blank


def split(total, me, keep_ref, send_refs):
    rows = keep_ref.shape[0]
    keep_ref[...] = total[pl.ds(pl.multiple_of(me * rows, 8), rows)]
    size = len(send_refs) + 1
    for k, ref in enumerate(send_refs):
        ref[0:rows] = total[pl.ds(pl.multiple_of((me ^ (size - 1 - k)) * rows, 8), rows)].astype(BF16)


def shared_kernel(
    where_ref, f_ref, halo_ref, far_ref, own_ref, other_ref, keep_ref, *rest
):
    *send_refs, d_ref, g_ref = rest
    rows, cols, chans = f_ref.shape
    half = rows // 2
    c = where_ref[0]
    near = halo_ref[pl.ds(pl.multiple_of(2 * cols * (1 - c), 16), cols)]
    far = far_ref[pl.ds(pl.multiple_of(2 * cols * c, 16), cols)]
    before = jnp.where(c == 0, near, far)
    after = jnp.where(c == 0, far, near)

    d_ref[pl.ds(half * c, half)] = own_ref[...]
    for r in range(half):
        d_ref[half * (1 - c) + r] = beside(other_ref[r].astype(F32))
    outs = d_ref.shape[2] // 3

    def part(x, first):
        n = x.shape[0]
        rhs = d_ref[first : first + n].reshape(n * cols, 3 * outs)
        return dot(x.reshape(n * cols, chans), rhs, ((0,), (0,)))

    for i in range(3):
        if i == 0:
            g = part(f_ref[0 : rows - 1], 1) + part(before[None], 0)
        elif i == 1:
            g = part(f_ref[...], 0)
        else:
            g = part(f_ref[1:rows], 0) + part(after[None], rows - 1)
        for j in range(3):
            start = (3 * i + j) * chans
            g_ref[start : start + chans] = g[:, j * outs : (j + 1) * outs]
    if g_ref.shape[0] > 9 * chans:
        g_ref[9 * chans :] = jnp.zeros((g_ref.shape[0] - 9 * chans, outs), F32)
    split(g_ref, where_ref[BATCH], keep_ref, send_refs)


def cls_split_kernel(where_ref, cls_ref, theirs_ref, small_ref, keep_ref, *rest):
    *send_refs, total_ref = rest
    total_ref[...] = cls_ref[...] + theirs_ref[...]
    split(total_ref, where_ref[TILE], keep_ref, send_refs)
    for ref in send_refs:
        put_trio(ref, keep_ref.shape[0], small_ref[...])


def pair_sum(parts):
    while len(parts) > 1:
        parts = [parts[k] + parts[k + 1] for k in range(0, len(parts), 2)]
    return parts[0]


def total_of(base_ref, in_refs):
    rows = base_ref.shape[0]
    total = base_ref[...]
    for ref in in_refs:
        total = total + ref[0:rows].astype(F32)
    return total


def small_sum(small_ref, in_refs, start):
    return pair_sum([small_ref[...]] + [get_trio(ref, start) for ref in in_refs])


def sum_kernel(n_in, n_cls, n_send, where_ref, base_ref, small_ref, cls_ref, *refs):
    in_refs, refs = refs[:n_in], refs[n_in:]
    cls_in_refs, refs = refs[:n_cls], refs[n_cls:]
    keep_ref, sum_ref, *refs, total_ref, cls_total_ref = refs
    send_refs, cls_keep_ref, cls_send_refs = refs[:n_send], refs[n_send], refs[n_send + 1 :]
    total_ref[...] = total_of(base_ref, in_refs)
    split(total_ref, where_ref[TILE], keep_ref, send_refs)
    cls_total_ref[...] = total_of(cls_ref, cls_in_refs)
    split(cls_total_ref, where_ref[BATCH], cls_keep_ref, cls_send_refs)
    sums = small_sum(small_ref, cls_in_refs, cls_ref.shape[0])
    sum_ref[...] = sums
    for ref in cls_send_refs:
        put_trio(ref, cls_keep_ref.shape[0], sums)


def round_kernel(n_in, where_ref, base_ref, small_ref, cls_ref, *refs):
    in_refs, cls_in_refs = refs[:n_in], refs[n_in:-3]
    out_ref, sum_ref, cls_out_ref = refs[-3:]
    out_ref[...] = total_of(base_ref, in_refs).astype(BF16)
    cls_out_ref[...] = total_of(cls_ref, cls_in_refs).astype(BF16)
    sum_ref[...] = small_sum(small_ref, cls_in_refs, cls_ref.shape[0])


def join(me, in_refs, out_ref):
    rows = in_refs[0].shape[0]
    for k, ref in enumerate(in_refs):
        out_ref[pl.ds(pl.multiple_of((me ^ k) * rows, 8), rows)] = ref[...].astype(out_ref.dtype)


def join_kernel(n_in, where_ref, *refs):
    join(where_ref[TILE], refs[:n_in], refs[-2])
    join(where_ref[BATCH], refs[n_in:-2], refs[-1])


def out_kernel(n_in, n_cls, where_ref, small_ref, theirs_ref, *refs):
    in_refs, cls_in_refs, refs = refs[:n_in], refs[n_in : n_in + n_cls], refs[n_in + n_cls :]
    out_ref, bias_ref, cls_out_ref, cls_bias_ref, loss_ref, cls_whole_ref, *whole_ref = refs
    if whole_ref:
        join(where_ref[BATCH], in_refs, whole_ref[0])
        out_ref[...] = whole_ref[0][: out_ref.shape[0]]
    else:
        join(where_ref[BATCH], in_refs, out_ref)
    join(where_ref[TILE], cls_in_refs, cls_whole_ref)
    for tap in range(9):
        cls_out_ref[tap // 3, tap % 3] = cls_whole_ref[LOGITS * tap : LOGITS * (tap + 1)]
    bias_ref[...] = small_ref[2:3] + theirs_ref[3:4]
    both = small_ref[0:1] + theirs_ref[0:1]
    cls_bias_ref[...] = both[:, :LOGITS]
    loss_ref[...] = both[:, LOGITS : LOGITS + 1]


def swap(x, axis, bit=1):
    size = lax.axis_size(axis)
    return lax.ppermute(x, axis, [(i, i ^ bit) for i in range(size)])


def others(x, axis):
    return [swap(x, axis, bit) for bit in range(1, lax.axis_size(axis))]


def exchange(sends, axis):
    size = len(sends) + 1
    return [swap(x, axis, size - 1 - k) for k, x in enumerate(sends)]


def round_up(n, step):
    return (n + step - 1) // step * step


def shards(features, labels, w_shared, b_shared, w_cls, b_cls):
    _, rows, cols, chans = features.shape
    half = rows // 2
    outs = w_shared.shape[3]
    tiles = lax.axis_size("tile")
    pages = lax.axis_size("batch")
    c = lax.axis_index("chan")
    t = lax.axis_index("tile")
    f = features[0]
    where = Places(half)
    lab = labels.reshape(rows, 1, labels.shape[2])
    msg, labt, count, near = call(
        edge_kernel, "edge", 2,
        [
            ((3 * cols + ANCH_ROWS, chans), BF16),
            ((rows, ANCH_ROWS, cols), BF16),
            ((8, LANES), F32),
            ((half + 3, cols, chans), BF16),
        ],
        [where, f, lab],
        [pltpu.SemaphoreType.DMA((4,))],
        [SMEM, HBM, VMEM],
        51,
    )
    met = others(count, "batch")
    pairs = []
    for i in range(tiles - 1):
        pairs += [(2 * i + 1, 2 * i + 2), (2 * i + 2, 2 * i + 1)]
    halo = lax.ppermute(msg, ("tile", "chan"), pairs)
    later, _ = lax.optimization_barrier((w_shared, msg))
    w1b = swap(later, "chan")
    w2b = swap(w_cls, "chan")
    b1b = swap(b_shared, "chan")

    weights = [w_shared, w1b, b_shared.reshape(1, outs), b1b.reshape(1, outs)]
    (inner,) = call(inner_kernel, "inner", 3, [((half + 1, cols, chans), BF16)], [where, near] + weights)
    inner, *met = lax.optimization_barrier((inner, *met))
    count = pair_sum([count] + met)
    halo, _ = lax.optimization_barrier((halo, count))
    counts = [count] + others(count, "tile")
    hid, dz, loss, w2 = call(
        head_kernel, "head", 5,
        [((half + 4, cols, chans), BF16), ((half + 2, cols, LANES), F32), ((1, LANES), F32)]
        + [((9 * LANES, chans), BF16)],
        [where, near, inner, halo, labt]
        + weights
        + [jnp.swapaxes(w_cls, 2, 3), jnp.swapaxes(w2b, 2, 3), b_cls.reshape(1, LOGITS)],
        [((5, cols, chans), BF16)],
    )
    dt, own, other, small = call(
        back_kernel, "back", 4,
        [
            ((half, 3 * CLS_ROWS, cols), BF16),
            ((half, cols, 3 * outs), BF16),
            ((half, cols, outs), BF16),
            ((SMALL, LANES), F32),
        ],
        [where, hid, dz, loss, w2] + counts,
        [((half + 2, cols, LANES), BF16)],
    )
    theirs = swap(other, "chan")
    later, _ = lax.optimization_barrier((halo, loss))
    far = swap(later, "chan")
    cls_total = round_up(9 * LOGITS, 16 * pages * tiles)
    gcls, gcls_other = call(
        cls_kernel, "cls", 1.5, [((cls_total, outs), F32)] * 2, [where, hid, dt]
    )
    gcls_theirs = swap(gcls_other, "chan")

    total = round_up(9 * chans, 16 * pages * tiles)
    first, second = total // pages, total // (pages * tiles)
    cfirst, csecond = cls_total // tiles, cls_total // (pages * tiles)
    keep, *sends = call(
        shared_kernel, "shared", 4,
        [((first, outs), F32)] + [((first, outs), BF16)] * (pages - 1),
        [where, f, halo, far, own, theirs],
        [((rows, cols, 3 * outs), BF16), ((total, outs), F32)],
    )
    ckeep, *csends = call(
        cls_split_kernel, "cls_split", 0.6,
        [((cfirst, outs), F32)] + [((cfirst + TRIO, outs), BF16)] * (tiles - 1),
        [where, gcls, gcls_theirs, small],
        [((cls_total, outs), F32)],
    )
    arrived = exchange(sends, "batch")
    carrived = exchange(csends, "tile")
    keep, small, *sends = call(
        functools.partial(sum_kernel, pages - 1, tiles - 1, tiles - 1), "sum", 0.7,
        [((second, outs), F32), ((SMALL, LANES), F32)]
        + [((second, outs), BF16)] * (tiles - 1)
        + [((csecond, outs), F32)]
        + [((csecond + TRIO, outs), BF16)] * (pages - 1),
        [where, keep, small, ckeep] + arrived + carrived,
        [((first, outs), F32), ((cfirst, outs), F32)],
    )
    ckeep, csends = sends[tiles - 1], sends[tiles:]
    arrived = exchange(sends[: tiles - 1], "tile")
    carrived = exchange(csends, "batch")
    done, small, cdone = call(
        functools.partial(round_kernel, tiles - 1), "round", 0.7,
        [((second, outs), BF16), ((SMALL, LANES), F32), ((csecond, outs), BF16)],
        [where, keep, small, ckeep] + arrived + carrived,
    )
    small_theirs = swap(small, "chan")
    block, cblock = call(
        functools.partial(join_kernel, tiles), "join", 0.7,
        [((first, outs), BF16), ((cfirst, outs), BF16)],
        [where, done] + others(done, "tile") + [cdone] + others(cdone, "batch"),
    )
    grad_shared, bias, grad_cls, cls_bias, loss = call(
        functools.partial(out_kernel, pages, tiles), "out", 1.5,
        [((9 * chans, outs), F32), ((1, outs), F32), ((3, 3, LOGITS, outs), F32), ((1, LOGITS), F32), ((1, 1), F32)],
        [where, small, small_theirs, block] + others(block, "batch") + [cblock] + others(cblock, "tile"),
        [((cls_total, outs), F32)] + ([((total, outs), F32)] if total > 9 * chans else []),
    )
    return (
        grad_shared.reshape(3, 3, chans, outs),
        bias.reshape(outs),
        jnp.swapaxes(grad_cls, 2, 3),
        cls_bias.reshape(LOGITS),
        loss.reshape(1),
    )


def solution(mesh):
    placed = (
        P(("groups", "batch"), "tile", None, None),
        P(("groups", "batch"), "tile", None),
        P(None, None, None, "chan"),
        P("chan"),
        P(None, None, "chan", None),
        P(),
    )
    return jax.shard_map(
        shards,
        mesh=mesh,
        in_specs=placed,
        out_specs=(
            P("groups", None, None, "chan"),
            P(("groups", "chan")),
            P("groups", None, "chan", None),
            P("groups"),
            P("groups"),
        ),
        check_vma=False,
    )
```

```python
import functools

import jax
import jax.numpy as jnp
from jax import lax
from jax.experimental import pallas as pl
from jax.experimental.pallas import tpu as pltpu
from jax.sharding import PartitionSpec as P

ANCH = 9
CLASSES = 11
LOGITS = 99
LANES = 128
ANCH_ROWS = 16
CLS_ROWS = 112
TILE, BATCH = 3, 4
BLOCK = 2
SMALL = 4
TRIO = 16
BF16 = jnp.bfloat16
F32 = jnp.float32
VMEM = pl.BlockSpec(memory_space=pltpu.VMEM)
HBM = pl.BlockSpec(memory_space=pltpu.HBM)
SMEM = pl.BlockSpec(memory_space=pltpu.SMEM)


class Places:
    def __init__(self, half):
        self.half = half

    def __getitem__(self, i):
        c, t = lax.axis_index("chan"), lax.axis_index("tile")
        if i == 0:
            return c
        if i == 1:
            return (2 * t + c) * self.half
        if i == 2:
            return 2 * lax.axis_size("tile") * self.half
        return t if i == 3 else lax.axis_index("batch")


def call(kernel, name, micros, outs, inputs, scratch=(), specs=None, mib=32):
    return pl.pallas_call(
        functools.partial(kernel, inputs[0]),
        in_specs=(specs or [SMEM] + [VMEM] * (len(inputs) - 1))[1:],
        out_specs=[VMEM] * len(outs),
        out_shape=[jax.ShapeDtypeStruct(shape, kind) for shape, kind in outs],
        scratch_shapes=[pltpu.VMEM(*shape) if isinstance(shape, tuple) else shape for shape in scratch],
        cost_estimate=pl.CostEstimate(flops=int(micros * 1e9), bytes_accessed=int(micros * 1e6), transcendentals=0),
        compiler_params=pltpu.CompilerParams(vmem_limit_bytes=int(mib * 1024 * 1024)),
        name=name,
    )(*inputs[1:])


def shift_cells(field, by):
    cells = field.shape[0]
    rolled = pltpu.roll(field, by % cells, axis=0)
    cell = lax.broadcasted_iota(jnp.int32, field.shape, 0)
    edge = 0 if by > 0 else cells - 1
    return jnp.where(cell == edge, 0.0, rolled)


def dot(left, right, dims=((1,), (0,))):
    return lax.dot_general(left, right, (dims, ((), ())), preferred_element_type=F32)


def taken(ref, start, rows):
    cols = ref.shape[1]
    parts = [ref[pl.ds(start + r, BLOCK)].reshape(BLOCK * cols, ref.shape[2]) for r in rows]
    return jnp.concatenate(parts, axis=1)


def three(x):
    high = x.astype(BF16)
    rest = x - high.astype(F32)
    middle = rest.astype(BF16)
    low = (rest - middle.astype(F32)).astype(BF16)
    return high, middle, low


def put_trio(ref, start, x):
    parts = [part.astype(F32) for part in three(x)]
    ref[start : start + TRIO] = jnp.concatenate(parts + [jnp.zeros_like(x)], axis=0).astype(BF16)


def get_trio(ref, start):
    part = ref[start : start + TRIO].astype(F32)
    return part[0:SMALL] + part[SMALL : 2 * SMALL] + part[2 * SMALL : 3 * SMALL]


def edge_kernel(where_ref, f_ref, lab_ref, msg_ref, labt_ref, count_ref, near_ref, sem):
    rows, cols, _ = f_ref.shape
    c = where_ref[0]
    copies = [
        pltpu.make_async_copy(f_ref.at[(rows - 3) * c + k], msg_ref.at[pl.ds(cols * k, cols)], sem.at[k])
        for k in range(3)
    ]
    near = near_ref.shape[0]
    copies.append(pltpu.make_async_copy(f_ref.at[pl.ds((rows - near) * c, near)], near_ref, sem.at[3]))
    for copy in copies:
        copy.start()
    size = lab_ref.shape[2]
    place = lax.broadcasted_iota(jnp.int32, (ANCH_ROWS, size), 1) % ANCH
    anchor = lax.broadcasted_iota(jnp.int32, (ANCH_ROWS, size), 0)
    mine = place == anchor
    labs = [lab_ref[r].astype(F32) for r in range(rows)]
    named = [jnp.where(lab > 0.0, 1.0, 0.0) for lab in labs]
    count_ref[...] = jnp.full(count_ref.shape, jnp.sum(sum(named[1:], named[0])), F32)
    left = jnp.concatenate([jnp.where(mine, lab, 0.0) for lab in labs], axis=0).astype(BF16)
    offset = lax.broadcasted_iota(jnp.int32, (size, cols), 0) - ANCH * lax.broadcasted_iota(jnp.int32, (size, cols), 1)
    pick = jnp.where(jnp.logical_and(offset >= 0, offset < ANCH), 1.0, 0.0).astype(BF16)
    turned = dot(left, pick).astype(BF16)
    for r in range(rows):
        labt_ref[r] = turned[ANCH_ROWS * r : ANCH_ROWS * (r + 1)]
    msg_ref[3 * cols : 3 * cols + ANCH_ROWS] = jnp.where(
        c == 0, turned[:ANCH_ROWS].astype(F32), turned[ANCH_ROWS * (rows - 1) :].astype(F32)
    ).astype(BF16)
    for copy in copies:
        copy.wait()


def hidden_rows(x, w1a_ref, w1b_ref, b1a_ref, b1b_ref):
    w1 = [
        jnp.concatenate(
            [part for j in range(3) for part in (w1a_ref[i, j], w1b_ref[i, j])], axis=1
        )
        for i in range(3)
    ]
    w1 = jnp.concatenate(w1, axis=0)
    b1 = jnp.concatenate([b1a_ref[...], b1b_ref[...]], axis=1)
    n = x.shape[0] - 2
    cols, chans = x.shape[1:]
    width = w1.shape[1] // 3
    for start in range(0, n, 4):
        count = min(4, n - start)
        parts = [x[start + r : start + r + count].reshape(count * cols, chans) for r in range(3)]
        many = dot(jnp.concatenate(parts, axis=1), w1)
        for k in range(count):
            y = many[k * cols : (k + 1) * cols]
            yield shift_cells(y[:, :width], 1) + y[:, width : 2 * width] + shift_cells(y[:, 2 * width :], -1) + b1


def inner_kernel(where_ref, near_ref, w1a_ref, w1b_ref, b1a_ref, b1b_ref, out_ref):
    for k, pre in enumerate(hidden_rows(near_ref, w1a_ref, w1b_ref, b1a_ref, b1b_ref)):
        out_ref[k] = jnp.maximum(pre, 0.0).astype(BF16)


def head_kernel(
    where_ref, near_ref, inner_ref, halo_ref, labt_ref, w1a_ref, w1b_ref, b1a_ref, b1b_ref, w2a_ref, w2b_ref, b2_ref,
    hid_ref, dz_ref, loss_ref, w2_ref, xw_ref,
):
    near = near_ref.shape[0]
    half = near - 3
    cols, chans = near_ref.shape[1:]
    c = where_ref[0]
    first = where_ref[1]
    total = where_ref[2]
    xw_ref[pl.ds(3 - 3 * c, 2)] = near_ref[pl.ds((near - 2) * c, 2)]
    for k in range(3):
        xw_ref[2 * c + k] = halo_ref[cols * k : cols * (k + 1)]
    hid_ref[pl.ds(3 - 3 * c, near - 2)] = inner_ref[...]
    for k, pre in enumerate(hidden_rows(xw_ref, w1a_ref, w1b_ref, b1a_ref, b1b_ref)):
        h = (near - 2) * c + k
        row = first + h - 2
        inside = jnp.logical_and(row >= 0, row < total)
        hid_ref[h] = jnp.where(inside, jnp.maximum(pre, 0.0), 0.0).astype(BF16)
    deep = chans // 2
    for tap in range(9):
        end = LANES * tap + LANES
        w2_ref[end - 32 : end] = jnp.zeros((32, chans), BF16)
        w2_ref[end - LANES : end - LANES + LOGITS, :deep] = w2a_ref[tap // 3, tap % 3]
        w2_ref[end - LANES : end - LANES + LOGITS, deep:] = w2b_ref[tap // 3, tap % 3]

    lane = lax.broadcasted_iota(jnp.int32, (1, LANES), 1)
    kind = (lane % CLASSES + 1).astype(F32)
    real = lane < LOGITS
    anchor = lax.broadcasted_iota(jnp.int32, (ANCH_ROWS, LANES), 0)
    column = lax.broadcasted_iota(jnp.int32, (ANCH_ROWS, LANES), 1)
    spread = jnp.where(jnp.logical_and(column // CLASSES == anchor, column < LOGITS), 1.0, 0.0).astype(BF16)
    size = 3 * LANES
    w2 = jnp.concatenate([w2_ref[size * i : size * (i + 1)] for i in range(3)], axis=1)
    b2 = jnp.concatenate([b2_ref[...], jnp.zeros((1, LANES - LOGITS), F32)], axis=1)

    def focal(g, loss):
        pair = dot(taken(hid_ref, BLOCK * g, (0, 1, 2)), w2, ((1,), (1,)))
        for k in range(BLOCK):
            loss = loss + focal_row(BLOCK * g + k, pair[k * cols : (k + 1) * cols])
        return loss

    def focal_row(l, y):
        z = shift_cells(y[:, :LANES], 1) + y[:, LANES : 2 * LANES] + shift_cells(y[:, 2 * LANES :], -1) + b2
        at_halo = jnp.where(c == 0, l == 0, l == half + 1)
        local = jnp.clip(l - 1 + half * c, 0, 2 * half - 1)
        mine = labt_ref[local].astype(F32)
        far = halo_ref[3 * cols : 3 * cols + ANCH_ROWS].astype(F32)
        lab = dot(jnp.where(at_halo, far, mine).astype(BF16), spread, ((0,), (0,)))
        row = first + l - 1
        inside = jnp.logical_and(row >= 0, row < total)
        hit = lab == kind
        keep = jnp.logical_and(jnp.logical_and(lab >= 0.0, real), inside)
        u = jnp.where(hit, -z, z)
        e = jnp.exp(-jnp.abs(u))
        r = 1.0 / (1.0 + e)
        er = e * r
        up = u >= 0.0
        s = jnp.where(up, r, er)
        comp = jnp.where(up, er, r)
        soft = jnp.maximum(u, 0.0) + jnp.log1p(e)
        ws = jnp.where(keep, jnp.where(hit, 0.25, 0.75), 0.0) * s * s
        slope = ws * (2.0 * comp * soft + s)
        dz_ref[l] = jnp.where(hit, -slope, slope)
        own = jnp.logical_and(l >= 1, l <= half)
        return jnp.where(own, 1.0, 0.0) * jnp.sum(ws * soft, axis=0, keepdims=True)

    loss_ref[...] = lax.fori_loop(0, (half + 2) // BLOCK, focal, jnp.zeros((1, LANES), F32), unroll=True)


def back_kernel(where_ref, hid_ref, dz_ref, loss_ref, w2_ref, halo_ref, *rest):
    *count_refs, dt_ref, own_ref, other_ref, small_ref, dlog_ref = rest
    half, _, cols = dt_ref.shape
    chans = hid_ref.shape[2]
    inverse = 1.0 / pair_sum([ref[...] for ref in count_refs])[:1]

    def scaled(l):
        dz = dz_ref[l] * inverse
        d16 = dz.astype(BF16)
        dlog_ref[l] = d16
        return dz, d16

    scaled(0)
    scaled(half + 1)

    def turn(d, gcb):
        dz, d16 = scaled(d + 1)
        turned = jnp.transpose(d16.astype(F32))[:CLS_ROWS]
        cell = lax.broadcasted_iota(jnp.int32, turned.shape, 1)
        left = jnp.where(cell == cols - 1, 0.0, pltpu.roll(turned, cols - 1, axis=1))
        right = jnp.where(cell == 0, 0.0, pltpu.roll(turned, 1, axis=1))
        dt_ref[d] = jnp.concatenate([left, turned, right], axis=0).astype(BF16)
        return gcb + jnp.sum(dz, axis=0, keepdims=True)

    gcb = lax.fori_loop(0, half, turn, jnp.zeros((1, LANES), F32), unroll=True)
    w2t = [
        jnp.concatenate([w2_ref[LANES * (3 * i + j) : LANES * (3 * i + j + 1)] for j in range(3)], axis=1)
        for i in range(3)
    ]
    w2t = jnp.concatenate(w2t, axis=0)

    def dpre(g, gsb):
        pair = dot(taken(dlog_ref, BLOCK * g, (2, 1, 0)), w2t)
        for k in range(BLOCK):
            gsb = gsb + dpre_row(BLOCK * g + k, pair[k * cols : (k + 1) * cols])
        return gsb

    def dpre_row(d, q):
        dhid = shift_cells(q[:, :chans], -1) + q[:, chans : 2 * chans] + shift_cells(q[:, 2 * chans :], 1)
        dpre = jnp.where(hid_ref[d + 2].astype(F32) > 0.0, dhid, 0.0)
        d16 = dpre.astype(BF16)
        own_ref[d] = d16[:, : chans // 2]
        other_ref[d] = d16[:, chans // 2 :]
        return jnp.sum(dpre, axis=0, keepdims=True)

    gsb = lax.fori_loop(0, half // BLOCK, dpre, jnp.zeros((1, chans), F32), unroll=True)
    near = halo_ref[pl.ds(pl.multiple_of(2 * cols * (1 - where_ref[0]), 16), cols)]
    other_ref[half] = near[:, : chans // 2]
    other_ref[half + 1] = near[:, chans // 2 :]
    loss = jnp.sum(loss_ref[...], axis=1, keepdims=True) * inverse[:, :1]
    small_ref[0:1] = jnp.where(lax.broadcasted_iota(jnp.int32, (1, LANES), 1) < LOGITS, gcb, loss)
    small_ref[1:2] = jnp.zeros((1, LANES), F32)
    small_ref[2:3] = gsb[:, : chans // 2]
    small_ref[3:4] = gsb[:, chans // 2 :]


def cls_kernel(where_ref, hid_ref, dt_ref, own_ref, other_ref):
    half, _, cols = dt_ref.shape
    chans = hid_ref.shape[2]
    deep = chans // 2
    dt = jnp.concatenate([dt_ref[d] for d in range(half)], axis=1)
    for i in range(3):
        g = dot(dt, hid_ref[i + 1 : i + 1 + half].reshape(half * cols, chans))
        for j in range(3):
            start = LOGITS * (3 * i + j)
            own_ref[start : start + LOGITS] = g[CLS_ROWS * j : CLS_ROWS * j + LOGITS, :deep]
            other_ref[start : start + LOGITS] = g[CLS_ROWS * j : CLS_ROWS * j + LOGITS, deep:]
    blank = jnp.zeros((own_ref.shape[0] - 9 * LOGITS, deep), F32)
    own_ref[9 * LOGITS :] = blank
    other_ref[9 * LOGITS :] = blank


def split(total, me, keep_ref, send_refs):
    rows = keep_ref.shape[0]
    keep_ref[...] = total[pl.ds(pl.multiple_of(me * rows, 8), rows)]
    size = len(send_refs) + 1
    for k, ref in enumerate(send_refs):
        ref[0:rows] = total[pl.ds(pl.multiple_of((me ^ (size - 1 - k)) * rows, 8), rows)].astype(BF16)


def shared_kernel(
    where_ref, f_ref, halo_ref, own_ref, other_ref, keep_ref, *rest
):
    *send_refs, d_ref, g_ref = rest
    rows, cols, chans = f_ref.shape
    half = rows // 2
    c = where_ref[0]
    near = halo_ref[pl.ds(pl.multiple_of(2 * cols * (1 - c), 16), cols)]
    far = jnp.concatenate([other_ref[half], other_ref[half + 1]], axis=1)
    before = jnp.where(c == 0, near, far)
    after = jnp.where(c == 0, far, near)

    for r in range(rows):
        mine, theirs = own_ref[r % half].astype(F32), other_ref[r % half].astype(F32)
        mid = jnp.where(c == (0 if r < half else 1), mine, theirs)
        d_ref[r] = jnp.concatenate([shift_cells(mid, -1), mid, shift_cells(mid, 1)], axis=1).astype(BF16)
    outs = d_ref.shape[2] // 3

    def part(x, first):
        n = x.shape[0]
        rhs = d_ref[first : first + n].reshape(n * cols, 3 * outs)
        return dot(x.reshape(n * cols, chans), rhs, ((0,), (0,)))

    for i in range(3):
        if i == 0:
            g = part(f_ref[0 : rows - 1], 1) + part(before[None], 0)
        elif i == 1:
            g = part(f_ref[...], 0)
        else:
            g = part(f_ref[1:rows], 0) + part(after[None], rows - 1)
        for j in range(3):
            start = (3 * i + j) * chans
            g_ref[start : start + chans] = g[:, j * outs : (j + 1) * outs]
    if g_ref.shape[0] > 9 * chans:
        g_ref[9 * chans :] = jnp.zeros((g_ref.shape[0] - 9 * chans, outs), F32)
    split(g_ref, where_ref[BATCH], keep_ref, send_refs)


def cls_split_kernel(where_ref, cls_ref, theirs_ref, small_ref, keep_ref, *rest):
    *send_refs, total_ref = rest
    total_ref[...] = cls_ref[...] + theirs_ref[...]
    split(total_ref, where_ref[TILE], keep_ref, send_refs)
    for ref in send_refs:
        put_trio(ref, keep_ref.shape[0], small_ref[...])


def pair_sum(parts):
    while len(parts) > 1:
        parts = [parts[k] + parts[k + 1] for k in range(0, len(parts), 2)]
    return parts[0]


def total_of(base_ref, in_refs):
    rows = base_ref.shape[0]
    total = base_ref[...]
    for ref in in_refs:
        total = total + ref[0:rows].astype(F32)
    return total


def small_sum(small_ref, in_refs, start):
    return pair_sum([small_ref[...]] + [get_trio(ref, start) for ref in in_refs])


def sum_kernel(n_in, n_cls, n_send, where_ref, base_ref, small_ref, cls_ref, *refs):
    in_refs, refs = refs[:n_in], refs[n_in:]
    cls_in_refs, refs = refs[:n_cls], refs[n_cls:]
    keep_ref, sum_ref, *refs, total_ref, cls_total_ref = refs
    send_refs, cls_keep_ref, cls_send_refs = refs[:n_send], refs[n_send], refs[n_send + 1 :]
    total_ref[...] = total_of(base_ref, in_refs)
    split(total_ref, where_ref[TILE], keep_ref, send_refs)
    cls_total_ref[...] = total_of(cls_ref, cls_in_refs)
    split(cls_total_ref, where_ref[BATCH], cls_keep_ref, cls_send_refs)
    sums = small_sum(small_ref, cls_in_refs, cls_ref.shape[0])
    sum_ref[...] = sums
    for ref in cls_send_refs:
        put_trio(ref, cls_keep_ref.shape[0], sums)


def round_kernel(n_in, where_ref, base_ref, small_ref, cls_ref, *refs):
    in_refs, cls_in_refs = refs[:n_in], refs[n_in:-3]
    out_ref, sum_ref, cls_out_ref = refs[-3:]
    out_ref[...] = total_of(base_ref, in_refs).astype(BF16)
    cls_out_ref[...] = total_of(cls_ref, cls_in_refs).astype(BF16)
    sum_ref[...] = small_sum(small_ref, cls_in_refs, cls_ref.shape[0])


def join(me, in_refs, out_ref):
    rows = in_refs[0].shape[0]
    for k, ref in enumerate(in_refs):
        out_ref[pl.ds(pl.multiple_of((me ^ k) * rows, 8), rows)] = ref[...].astype(out_ref.dtype)


def join_kernel(n_in, where_ref, *refs):
    join(where_ref[TILE], refs[:n_in], refs[-2])
    join(where_ref[BATCH], refs[n_in:-2], refs[-1])


def out_kernel(n_in, n_cls, where_ref, small_ref, theirs_ref, *refs):
    in_refs, cls_in_refs, refs = refs[:n_in], refs[n_in : n_in + n_cls], refs[n_in + n_cls :]
    out_ref, bias_ref, cls_out_ref, cls_bias_ref, loss_ref, cls_whole_ref, *whole_ref = refs
    if whole_ref:
        join(where_ref[BATCH], in_refs, whole_ref[0])
        out_ref[...] = whole_ref[0][: out_ref.shape[0]]
    else:
        join(where_ref[BATCH], in_refs, out_ref)
    join(where_ref[TILE], cls_in_refs, cls_whole_ref)
    for tap in range(9):
        cls_out_ref[tap // 3, tap % 3] = cls_whole_ref[LOGITS * tap : LOGITS * (tap + 1)]
    bias_ref[...] = small_ref[2:3] + theirs_ref[3:4]
    both = small_ref[0:1] + theirs_ref[0:1]
    cls_bias_ref[...] = both[:, :LOGITS]
    loss_ref[...] = both[:, LOGITS : LOGITS + 1]


def swap(x, axis, bit=1):
    size = lax.axis_size(axis)
    return lax.ppermute(x, axis, [(i, i ^ bit) for i in range(size)])


def others(x, axis):
    return [swap(x, axis, bit) for bit in range(1, lax.axis_size(axis))]


def exchange(sends, axis):
    size = len(sends) + 1
    return [swap(x, axis, size - 1 - k) for k, x in enumerate(sends)]


def round_up(n, step):
    return (n + step - 1) // step * step


def shards(features, labels, w_shared, b_shared, w_cls, b_cls):
    _, rows, cols, chans = features.shape
    half = rows // 2
    outs = w_shared.shape[3]
    tiles = lax.axis_size("tile")
    pages = lax.axis_size("batch")
    c = lax.axis_index("chan")
    t = lax.axis_index("tile")
    f = features[0]
    where = Places(half)
    lab = labels.reshape(rows, 1, labels.shape[2])
    msg, labt, count, near = call(
        edge_kernel, "edge", 2,
        [
            ((3 * cols + ANCH_ROWS, chans), BF16),
            ((rows, ANCH_ROWS, cols), BF16),
            ((8, LANES), F32),
            ((half + 3, cols, chans), BF16),
        ],
        [where, f, lab],
        [pltpu.SemaphoreType.DMA((4,))],
        [SMEM, HBM, VMEM],
        51,
    )
    met = others(count, "batch")
    pairs = []
    for i in range(tiles - 1):
        pairs += [(2 * i + 1, 2 * i + 2), (2 * i + 2, 2 * i + 1)]
    halo = lax.ppermute(msg, ("tile", "chan"), pairs)
    w1b = swap(w_shared, "chan")
    w2b = swap(w_cls, "chan")
    b1b = swap(b_shared, "chan")

    weights = [w_shared, w1b, b_shared.reshape(1, outs), b1b.reshape(1, outs)]
    (inner,) = call(inner_kernel, "inner", 3, [((half + 1, cols, chans), BF16)], [where, near] + weights)
    inner, *met = lax.optimization_barrier((inner, *met))
    count = pair_sum([count] + met)
    halo, _ = lax.optimization_barrier((halo, count))
    counts = [count] + others(count, "tile")
    hid, dz, loss, w2 = call(
        head_kernel, "head", 5,
        [((half + 4, cols, chans), BF16), ((half + 2, cols, LANES), F32), ((1, LANES), F32)]
        + [((9 * LANES, chans), BF16)],
        [where, near, inner, halo, labt]
        + weights
        + [jnp.swapaxes(w_cls, 2, 3), jnp.swapaxes(w2b, 2, 3), b_cls.reshape(1, LOGITS)],
        [((5, cols, chans), BF16)],
    )
    dt, own, other, small = call(
        back_kernel, "back", 4,
        [
            ((half, 3 * CLS_ROWS, cols), BF16),
            ((half, cols, outs), BF16),
            ((half + 2, cols, outs), BF16),
            ((SMALL, LANES), F32),
        ],
        [where, hid, dz, loss, w2, halo] + counts,
        [((half + 2, cols, LANES), BF16)],
    )
    theirs = swap(other, "chan")
    cls_total = round_up(9 * LOGITS, 16 * pages * tiles)
    gcls, gcls_other = call(
        cls_kernel, "cls", 1.5, [((cls_total, outs), F32)] * 2, [where, hid, dt]
    )
    gcls_theirs = swap(gcls_other, "chan")

    total = round_up(9 * chans, 16 * pages * tiles)
    first, second = total // pages, total // (pages * tiles)
    cfirst, csecond = cls_total // tiles, cls_total // (pages * tiles)
    keep, *sends = call(
        shared_kernel, "shared", 4,
        [((first, outs), F32)] + [((first, outs), BF16)] * (pages - 1),
        [where, f, halo, own, theirs],
        [((rows, cols, 3 * outs), BF16), ((total, outs), F32)],
    )
    ckeep, *csends = call(
        cls_split_kernel, "cls_split", 0.6,
        [((cfirst, outs), F32)] + [((cfirst + TRIO, outs), BF16)] * (tiles - 1),
        [where, gcls, gcls_theirs, small],
        [((cls_total, outs), F32)],
    )
    arrived = exchange(sends, "batch")
    carrived = exchange(csends, "tile")
    keep, small, *sends = call(
        functools.partial(sum_kernel, pages - 1, tiles - 1, tiles - 1), "sum", 0.7,
        [((second, outs), F32), ((SMALL, LANES), F32)]
        + [((second, outs), BF16)] * (tiles - 1)
        + [((csecond, outs), F32)]
        + [((csecond + TRIO, outs), BF16)] * (pages - 1),
        [where, keep, small, ckeep] + arrived + carrived,
        [((first, outs), F32), ((cfirst, outs), F32)],
    )
    ckeep, csends = sends[tiles - 1], sends[tiles:]
    arrived = exchange(sends[: tiles - 1], "tile")
    carrived = exchange(csends, "batch")
    done, small, cdone = call(
        functools.partial(round_kernel, tiles - 1), "round", 0.7,
        [((second, outs), BF16), ((SMALL, LANES), F32), ((csecond, outs), BF16)],
        [where, keep, small, ckeep] + arrived + carrived,
    )
    small_theirs = swap(small, "chan")
    block, cblock = call(
        functools.partial(join_kernel, tiles), "join", 0.7,
        [((first, outs), BF16), ((cfirst, outs), BF16)],
        [where, done] + others(done, "tile") + [cdone] + others(cdone, "batch"),
    )
    grad_shared, bias, grad_cls, cls_bias, loss = call(
        functools.partial(out_kernel, pages, tiles), "out", 1.5,
        [((9 * chans, outs), F32), ((1, outs), F32), ((3, 3, LOGITS, outs), F32), ((1, LOGITS), F32), ((1, 1), F32)],
        [where, small, small_theirs, block] + others(block, "batch") + [cblock] + others(cblock, "tile"),
        [((cls_total, outs), F32)] + ([((total, outs), F32)] if total > 9 * chans else []),
    )
    return (
        grad_shared.reshape(3, 3, chans, outs),
        bias.reshape(outs),
        jnp.swapaxes(grad_cls, 2, 3),
        cls_bias.reshape(LOGITS),
        loss.reshape(1),
    )


def solution(mesh):
    placed = (
        P(("groups", "batch"), "tile", None, None),
        P(("groups", "batch"), "tile", None),
        P(None, None, None, "chan"),
        P("chan"),
        P(None, None, "chan", None),
        P(),
    )
    return jax.shard_map(
        shards,
        mesh=mesh,
        in_specs=placed,
        out_specs=(
            P("groups", None, None, "chan"),
            P(("groups", "chan")),
            P("groups", None, "chan", None),
            P("groups"),
            P("groups"),
        ),
        check_vma=False,
    )
```

```python
import functools

import jax
import jax.numpy as jnp
from jax import lax
from jax.experimental import pallas as pl
from jax.experimental.pallas import tpu as pltpu
from jax.sharding import PartitionSpec as P

ANCH = 9
CLASSES = 11
LOGITS = 99
LANES = 128
ANCH_ROWS = 16
CLS_ROWS = 112
TILE, BATCH = 3, 4
BLOCK = 2
SMALL = 4
TRIO = 16
BF16 = jnp.bfloat16
F32 = jnp.float32
VMEM = pl.BlockSpec(memory_space=pltpu.VMEM)
HBM = pl.BlockSpec(memory_space=pltpu.HBM)
SMEM = pl.BlockSpec(memory_space=pltpu.SMEM)


class Places:
    def __init__(self, half):
        self.half = half

    def __getitem__(self, i):
        c, t = lax.axis_index("chan"), lax.axis_index("tile")
        if i == 0:
            return c
        if i == 1:
            return (2 * t + c) * self.half
        if i == 2:
            return 2 * lax.axis_size("tile") * self.half
        return t if i == 3 else lax.axis_index("batch")


def call(kernel, name, micros, outs, inputs, scratch=(), specs=None, mib=32):
    return pl.pallas_call(
        functools.partial(kernel, inputs[0]),
        in_specs=(specs or [SMEM] + [VMEM] * (len(inputs) - 1))[1:],
        out_specs=[VMEM] * len(outs),
        out_shape=[jax.ShapeDtypeStruct(shape, kind) for shape, kind in outs],
        scratch_shapes=[pltpu.VMEM(*shape) if isinstance(shape, tuple) else shape for shape in scratch],
        cost_estimate=pl.CostEstimate(flops=int(micros * 1e9), bytes_accessed=int(micros * 1e6), transcendentals=0),
        compiler_params=pltpu.CompilerParams(vmem_limit_bytes=int(mib * 1024 * 1024)),
        name=name,
    )(*inputs[1:])


def shift_cells(field, by):
    cells = field.shape[0]
    rolled = pltpu.roll(field, by % cells, axis=0)
    cell = lax.broadcasted_iota(jnp.int32, field.shape, 0)
    edge = 0 if by > 0 else cells - 1
    return jnp.where(cell == edge, 0.0, rolled)


def dot(left, right, dims=((1,), (0,))):
    return lax.dot_general(left, right, (dims, ((), ())), preferred_element_type=F32)


def taken(ref, start, rows):
    cols = ref.shape[1]
    parts = [ref[pl.ds(start + r, BLOCK)].reshape(BLOCK * cols, ref.shape[2]) for r in rows]
    return jnp.concatenate(parts, axis=1)


def three(x):
    high = x.astype(BF16)
    rest = x - high.astype(F32)
    middle = rest.astype(BF16)
    low = (rest - middle.astype(F32)).astype(BF16)
    return high, middle, low


def put_trio(ref, start, x):
    parts = [part.astype(F32) for part in three(x)]
    ref[start : start + TRIO] = jnp.concatenate(parts + [jnp.zeros_like(x)], axis=0).astype(BF16)


def get_trio(ref, start):
    part = ref[start : start + TRIO].astype(F32)
    return part[0:SMALL] + part[SMALL : 2 * SMALL] + part[2 * SMALL : 3 * SMALL]


def edge_kernel(where_ref, f_ref, lab_ref, msg_ref, labt_ref, count_ref, near_ref, sem):
    rows, cols, _ = f_ref.shape
    c = where_ref[0]
    copies = [
        pltpu.make_async_copy(f_ref.at[(rows - 3) * c + k], msg_ref.at[pl.ds(cols * k, cols)], sem.at[k])
        for k in range(3)
    ]
    near = near_ref.shape[0]
    copies.append(pltpu.make_async_copy(f_ref.at[pl.ds((rows - near) * c, near)], near_ref, sem.at[3]))
    for copy in copies:
        copy.start()
    size = lab_ref.shape[2]
    place = lax.broadcasted_iota(jnp.int32, (ANCH_ROWS, size), 1) % ANCH
    anchor = lax.broadcasted_iota(jnp.int32, (ANCH_ROWS, size), 0)
    mine = place == anchor
    labs = [lab_ref[r].astype(F32) for r in range(rows)]
    named = [jnp.where(lab > 0.0, 1.0, 0.0) for lab in labs]
    count_ref[...] = jnp.full(count_ref.shape, jnp.sum(sum(named[1:], named[0])), F32)
    left = jnp.concatenate([jnp.where(mine, lab, 0.0) for lab in labs], axis=0).astype(BF16)
    offset = lax.broadcasted_iota(jnp.int32, (size, cols), 0) - ANCH * lax.broadcasted_iota(jnp.int32, (size, cols), 1)
    pick = jnp.where(jnp.logical_and(offset >= 0, offset < ANCH), 1.0, 0.0).astype(BF16)
    turned = dot(left, pick).astype(BF16)
    for r in range(rows):
        labt_ref[r] = turned[ANCH_ROWS * r : ANCH_ROWS * (r + 1)]
    msg_ref[3 * cols : 3 * cols + ANCH_ROWS] = jnp.where(
        c == 0, turned[:ANCH_ROWS].astype(F32), turned[ANCH_ROWS * (rows - 1) :].astype(F32)
    ).astype(BF16)
    for copy in copies:
        copy.wait()


def hidden_rows(x, w1a_ref, w1b_ref, b1a_ref, b1b_ref):
    w1 = [
        jnp.concatenate(
            [part for j in range(3) for part in (w1a_ref[i, j], w1b_ref[i, j])], axis=1
        )
        for i in range(3)
    ]
    w1 = jnp.concatenate(w1, axis=0)
    b1 = jnp.concatenate([b1a_ref[...], b1b_ref[...]], axis=1)
    n = x.shape[0] - 2
    cols, chans = x.shape[1:]
    width = w1.shape[1] // 3
    for start in range(0, n, 4):
        count = min(4, n - start)
        parts = [x[start + r : start + r + count].reshape(count * cols, chans) for r in range(3)]
        many = dot(jnp.concatenate(parts, axis=1), w1)
        for k in range(count):
            y = many[k * cols : (k + 1) * cols]
            yield shift_cells(y[:, :width], 1) + y[:, width : 2 * width] + shift_cells(y[:, 2 * width :], -1) + b1


def inner_kernel(where_ref, near_ref, w1a_ref, w1b_ref, b1a_ref, b1b_ref, out_ref):
    for k, pre in enumerate(hidden_rows(near_ref, w1a_ref, w1b_ref, b1a_ref, b1b_ref)):
        out_ref[k] = jnp.maximum(pre, 0.0).astype(BF16)


def head_kernel(
    where_ref, near_ref, inner_ref, halo_ref, labt_ref, w1a_ref, w1b_ref, b1a_ref, b1b_ref, w2a_ref, w2b_ref, b2_ref,
    hid_ref, dz_ref, loss_ref, w2_ref, xw_ref,
):
    near = near_ref.shape[0]
    half = near - 3
    cols, chans = near_ref.shape[1:]
    c = where_ref[0]
    first = where_ref[1]
    total = where_ref[2]
    xw_ref[pl.ds(3 - 3 * c, 2)] = near_ref[pl.ds((near - 2) * c, 2)]
    for k in range(3):
        xw_ref[2 * c + k] = halo_ref[cols * k : cols * (k + 1)]
    hid_ref[pl.ds(3 - 3 * c, near - 2)] = inner_ref[...]
    for k, pre in enumerate(hidden_rows(xw_ref, w1a_ref, w1b_ref, b1a_ref, b1b_ref)):
        h = (near - 2) * c + k
        row = first + h - 2
        inside = jnp.logical_and(row >= 0, row < total)
        hid_ref[h] = jnp.where(inside, jnp.maximum(pre, 0.0), 0.0).astype(BF16)
    deep = chans // 2
    for tap in range(9):
        end = LANES * tap + LANES
        w2_ref[end - 32 : end] = jnp.zeros((32, chans), BF16)
        w2_ref[end - LANES : end - LANES + LOGITS, :deep] = w2a_ref[tap // 3, tap % 3]
        w2_ref[end - LANES : end - LANES + LOGITS, deep:] = w2b_ref[tap // 3, tap % 3]

    lane = lax.broadcasted_iota(jnp.int32, (1, LANES), 1)
    kind = (lane % CLASSES + 1).astype(F32)
    real = lane < LOGITS
    anchor = lax.broadcasted_iota(jnp.int32, (ANCH_ROWS, LANES), 0)
    column = lax.broadcasted_iota(jnp.int32, (ANCH_ROWS, LANES), 1)
    spread = jnp.where(jnp.logical_and(column // CLASSES == anchor, column < LOGITS), 1.0, 0.0).astype(BF16)
    size = 3 * LANES
    w2 = jnp.concatenate([w2_ref[size * i : size * (i + 1)] for i in range(3)], axis=1)
    b2 = jnp.concatenate([b2_ref[...], jnp.zeros((1, LANES - LOGITS), F32)], axis=1)

    def focal(g, loss):
        pair = dot(taken(hid_ref, BLOCK * g, (0, 1, 2)), w2, ((1,), (1,)))
        for k in range(BLOCK):
            loss = loss + focal_row(BLOCK * g + k, pair[k * cols : (k + 1) * cols])
        return loss

    def focal_row(l, y):
        z = shift_cells(y[:, :LANES], 1) + y[:, LANES : 2 * LANES] + shift_cells(y[:, 2 * LANES :], -1) + b2
        at_halo = jnp.where(c == 0, l == 0, l == half + 1)
        local = jnp.clip(l - 1 + half * c, 0, 2 * half - 1)
        mine = labt_ref[local].astype(F32)
        far = halo_ref[3 * cols : 3 * cols + ANCH_ROWS].astype(F32)
        lab = dot(jnp.where(at_halo, far, mine).astype(BF16), spread, ((0,), (0,)))
        row = first + l - 1
        inside = jnp.logical_and(row >= 0, row < total)
        hit = lab == kind
        keep = jnp.logical_and(jnp.logical_and(lab >= 0.0, real), inside)
        u = jnp.where(hit, -z, z)
        e = jnp.exp(-jnp.abs(u))
        r = 1.0 / (1.0 + e)
        er = e * r
        up = u >= 0.0
        s = jnp.where(up, r, er)
        comp = jnp.where(up, er, r)
        soft = jnp.maximum(u, 0.0) + jnp.log1p(e)
        ws = jnp.where(keep, jnp.where(hit, 0.25, 0.75), 0.0) * s * s
        slope = ws * (2.0 * comp * soft + s)
        dz_ref[l] = jnp.where(hit, -slope, slope)
        own = jnp.logical_and(l >= 1, l <= half)
        return jnp.where(own, 1.0, 0.0) * jnp.sum(ws * soft, axis=0, keepdims=True)

    loss_ref[...] = lax.fori_loop(0, (half + 2) // BLOCK, focal, jnp.zeros((1, LANES), F32), unroll=True)


def back_kernel(where_ref, hid_ref, dz_ref, loss_ref, w2_ref, halo_ref, *rest):
    *count_refs, dt_ref, own_ref, other_ref, small_ref, dlog_ref = rest
    half, _, cols = dt_ref.shape
    chans = hid_ref.shape[2]
    inverse = 1.0 / pair_sum([ref[...] for ref in count_refs])[:1]

    def scaled(l):
        dz = dz_ref[l] * inverse
        d16 = dz.astype(BF16)
        dlog_ref[l] = d16
        return dz, d16

    scaled(0)
    scaled(half + 1)

    def turn(d, gcb):
        dz, d16 = scaled(d + 1)
        turned = jnp.transpose(d16.astype(F32))[:CLS_ROWS]
        cell = lax.broadcasted_iota(jnp.int32, turned.shape, 1)
        left = jnp.where(cell == cols - 1, 0.0, pltpu.roll(turned, cols - 1, axis=1))
        right = jnp.where(cell == 0, 0.0, pltpu.roll(turned, 1, axis=1))
        dt_ref[d] = jnp.concatenate([left, turned, right], axis=0).astype(BF16)
        return gcb + jnp.sum(dz, axis=0, keepdims=True)

    gcb = lax.fori_loop(0, half, turn, jnp.zeros((1, LANES), F32), unroll=True)
    w2t = [
        jnp.concatenate([w2_ref[LANES * (3 * i + j) : LANES * (3 * i + j + 1)] for j in range(3)], axis=1)
        for i in range(3)
    ]
    w2t = jnp.concatenate(w2t, axis=0)

    def dpre(g, gsb):
        pair = dot(taken(dlog_ref, BLOCK * g, (2, 1, 0)), w2t)
        for k in range(BLOCK):
            gsb = gsb + dpre_row(BLOCK * g + k, pair[k * cols : (k + 1) * cols])
        return gsb

    def dpre_row(d, q):
        dhid = shift_cells(q[:, :chans], -1) + q[:, chans : 2 * chans] + shift_cells(q[:, 2 * chans :], 1)
        dpre = jnp.where(hid_ref[d + 2].astype(F32) > 0.0, dhid, 0.0)
        d16 = dpre.astype(BF16)
        own_ref[d] = d16[:, : chans // 2]
        other_ref[d] = d16[:, chans // 2 :]
        return jnp.sum(dpre, axis=0, keepdims=True)

    gsb = lax.fori_loop(0, half // BLOCK, dpre, jnp.zeros((1, chans), F32), unroll=True)
    near = halo_ref[pl.ds(pl.multiple_of(2 * cols * (1 - where_ref[0]), 16), cols)]
    other_ref[half] = near[:, : chans // 2]
    other_ref[half + 1] = near[:, chans // 2 :]
    loss = jnp.sum(loss_ref[...], axis=1, keepdims=True) * inverse[:, :1]
    small_ref[0:1] = jnp.where(lax.broadcasted_iota(jnp.int32, (1, LANES), 1) < LOGITS, gcb, loss)
    small_ref[1:2] = jnp.zeros((1, LANES), F32)
    small_ref[2:3] = gsb[:, : chans // 2]
    small_ref[3:4] = gsb[:, chans // 2 :]


def cls_kernel(where_ref, hid_ref, dt_ref, own_ref, other_ref):
    half, _, cols = dt_ref.shape
    chans = hid_ref.shape[2]
    deep = chans // 2
    dt = jnp.concatenate([dt_ref[d] for d in range(half)], axis=1)
    for i in range(3):
        g = dot(dt, hid_ref[i + 1 : i + 1 + half].reshape(half * cols, chans))
        for j in range(3):
            start = LOGITS * (3 * i + j)
            own_ref[start : start + LOGITS] = g[CLS_ROWS * j : CLS_ROWS * j + LOGITS, :deep]
            other_ref[start : start + LOGITS] = g[CLS_ROWS * j : CLS_ROWS * j + LOGITS, deep:]
    blank = jnp.zeros((own_ref.shape[0] - 9 * LOGITS, deep), F32)
    own_ref[9 * LOGITS :] = blank
    other_ref[9 * LOGITS :] = blank


def partners(size):
    return [2, 3, 1] if size == 4 else list(range(size - 1, 0, -1))


def split(total, me, keep_ref, send_refs):
    rows = keep_ref.shape[0]
    keep_ref[...] = total[pl.ds(pl.multiple_of(me * rows, 8), rows)]
    for bit, ref in zip(partners(len(send_refs) + 1), send_refs):
        ref[0:rows] = total[pl.ds(pl.multiple_of((me ^ bit) * rows, 8), rows)].astype(BF16)


def shared_kernel(
    where_ref, f_ref, halo_ref, own_ref, other_ref, keep_ref, *rest
):
    *send_refs, d_ref, g_ref = rest
    rows, cols, chans = f_ref.shape
    half = rows // 2
    c = where_ref[0]
    near = halo_ref[pl.ds(pl.multiple_of(2 * cols * (1 - c), 16), cols)]
    far = jnp.concatenate([other_ref[half], other_ref[half + 1]], axis=1)
    before = jnp.where(c == 0, near, far)
    after = jnp.where(c == 0, far, near)

    for r in range(rows):
        mine, theirs = own_ref[r % half].astype(F32), other_ref[r % half].astype(F32)
        mid = jnp.where(c == (0 if r < half else 1), mine, theirs)
        d_ref[r] = jnp.concatenate([shift_cells(mid, -1), mid, shift_cells(mid, 1)], axis=1).astype(BF16)
    outs = d_ref.shape[2] // 3

    def part(x, first):
        n = x.shape[0]
        rhs = d_ref[first : first + n].reshape(n * cols, 3 * outs)
        return dot(x.reshape(n * cols, chans), rhs, ((0,), (0,)))

    for i in range(3):
        if i == 0:
            g = part(f_ref[0 : rows - 1], 1) + part(before[None], 0)
        elif i == 1:
            g = part(f_ref[...], 0)
        else:
            g = part(f_ref[1:rows], 0) + part(after[None], rows - 1)
        for j in range(3):
            start = (3 * i + j) * chans
            g_ref[start : start + chans] = g[:, j * outs : (j + 1) * outs]
    if g_ref.shape[0] > 9 * chans:
        g_ref[9 * chans :] = jnp.zeros((g_ref.shape[0] - 9 * chans, outs), F32)
    split(g_ref, where_ref[BATCH], keep_ref, send_refs)


def cls_split_kernel(where_ref, cls_ref, theirs_ref, small_ref, keep_ref, *rest):
    *send_refs, total_ref = rest
    total_ref[...] = cls_ref[...] + theirs_ref[...]
    split(total_ref, where_ref[TILE], keep_ref, send_refs)
    for ref in send_refs:
        put_trio(ref, keep_ref.shape[0], small_ref[...])


def pair_sum(parts):
    while len(parts) > 1:
        parts = [parts[k] + parts[k + 1] for k in range(0, len(parts), 2)]
    return parts[0]


def total_of(base_ref, in_refs):
    rows = base_ref.shape[0]
    total = base_ref[...]
    for ref in in_refs:
        total = total + ref[0:rows].astype(F32)
    return total


def small_sum(small_ref, in_refs, start):
    return pair_sum([small_ref[...]] + [get_trio(ref, start) for ref in in_refs])


def sum_kernel(n_in, n_cls, n_send, where_ref, base_ref, small_ref, cls_ref, *refs):
    in_refs, refs = refs[:n_in], refs[n_in:]
    cls_in_refs, refs = refs[:n_cls], refs[n_cls:]
    keep_ref, sum_ref, *refs, total_ref, cls_total_ref = refs
    send_refs, cls_keep_ref, cls_send_refs = refs[:n_send], refs[n_send], refs[n_send + 1 :]
    total_ref[...] = total_of(base_ref, in_refs)
    split(total_ref, where_ref[TILE], keep_ref, send_refs)
    cls_total_ref[...] = total_of(cls_ref, cls_in_refs)
    split(cls_total_ref, where_ref[BATCH], cls_keep_ref, cls_send_refs)
    sums = small_sum(small_ref, cls_in_refs, cls_ref.shape[0])
    sum_ref[...] = sums
    for ref in cls_send_refs:
        put_trio(ref, cls_keep_ref.shape[0], sums)


def round_kernel(n_in, where_ref, base_ref, small_ref, cls_ref, *refs):
    in_refs, cls_in_refs = refs[:n_in], refs[n_in:-3]
    out_ref, sum_ref, cls_out_ref = refs[-3:]
    out_ref[...] = total_of(base_ref, in_refs).astype(BF16)
    cls_out_ref[...] = total_of(cls_ref, cls_in_refs).astype(BF16)
    sum_ref[...] = small_sum(small_ref, cls_in_refs, cls_ref.shape[0])


def join(me, in_refs, out_ref):
    rows = in_refs[0].shape[0]
    for bit, ref in zip([0] + partners(len(in_refs))[::-1], in_refs):
        out_ref[pl.ds(pl.multiple_of((me ^ bit) * rows, 8), rows)] = ref[...].astype(out_ref.dtype)


def join_kernel(n_in, where_ref, *refs):
    join(where_ref[TILE], refs[:n_in], refs[-2])
    join(where_ref[BATCH], refs[n_in:-2], refs[-1])


def out_kernel(n_in, n_cls, where_ref, small_ref, theirs_ref, *refs):
    in_refs, cls_in_refs, refs = refs[:n_in], refs[n_in : n_in + n_cls], refs[n_in + n_cls :]
    out_ref, bias_ref, cls_out_ref, cls_bias_ref, loss_ref, cls_whole_ref, *whole_ref = refs
    if whole_ref:
        join(where_ref[BATCH], in_refs, whole_ref[0])
        out_ref[...] = whole_ref[0][: out_ref.shape[0]]
    else:
        join(where_ref[BATCH], in_refs, out_ref)
    join(where_ref[TILE], cls_in_refs, cls_whole_ref)
    for tap in range(9):
        cls_out_ref[tap // 3, tap % 3] = cls_whole_ref[LOGITS * tap : LOGITS * (tap + 1)]
    bias_ref[...] = small_ref[2:3] + theirs_ref[3:4]
    both = small_ref[0:1] + theirs_ref[0:1]
    cls_bias_ref[...] = both[:, :LOGITS]
    loss_ref[...] = both[:, LOGITS : LOGITS + 1]


def swap(x, axis, bit=1):
    size = lax.axis_size(axis)
    return lax.ppermute(x, axis, [(i, i ^ bit) for i in range(size)])


def others(x, axis):
    return [swap(x, axis, bit) for bit in partners(lax.axis_size(axis))[::-1]]


def exchange(sends, axis):
    return [swap(x, axis, bit) for bit, x in zip(partners(len(sends) + 1), sends)]


def round_up(n, step):
    return (n + step - 1) // step * step


def shards(features, labels, w_shared, b_shared, w_cls, b_cls):
    _, rows, cols, chans = features.shape
    half = rows // 2
    outs = w_shared.shape[3]
    tiles = lax.axis_size("tile")
    pages = lax.axis_size("batch")
    c = lax.axis_index("chan")
    t = lax.axis_index("tile")
    f = features[0]
    where = Places(half)
    lab = labels.reshape(rows, 1, labels.shape[2])
    msg, labt, count, near = call(
        edge_kernel, "edge", 2,
        [
            ((3 * cols + ANCH_ROWS, chans), BF16),
            ((rows, ANCH_ROWS, cols), BF16),
            ((8, LANES), F32),
            ((half + 3, cols, chans), BF16),
        ],
        [where, f, lab],
        [pltpu.SemaphoreType.DMA((4,))],
        [SMEM, HBM, VMEM],
        51,
    )
    met = others(count, "batch")
    pairs = []
    for i in range(tiles - 1):
        pairs += [(2 * i + 1, 2 * i + 2), (2 * i + 2, 2 * i + 1)]
    halo = lax.ppermute(msg, ("tile", "chan"), pairs)
    w1b = swap(w_shared, "chan")
    w2b = swap(w_cls, "chan")
    b1b = swap(b_shared, "chan")

    weights = [w_shared, w1b, b_shared.reshape(1, outs), b1b.reshape(1, outs)]
    (inner,) = call(inner_kernel, "inner", 3, [((half + 1, cols, chans), BF16)], [where, near] + weights)
    inner, *met = lax.optimization_barrier((inner, *met))
    count = pair_sum([count] + met)
    halo, _ = lax.optimization_barrier((halo, count))
    counts = [count] + others(count, "tile")
    hid, dz, loss, w2 = call(
        head_kernel, "head", 5,
        [((half + 4, cols, chans), BF16), ((half + 2, cols, LANES), F32), ((1, LANES), F32)]
        + [((9 * LANES, chans), BF16)],
        [where, near, inner, halo, labt]
        + weights
        + [jnp.swapaxes(w_cls, 2, 3), jnp.swapaxes(w2b, 2, 3), b_cls.reshape(1, LOGITS)],
        [((5, cols, chans), BF16)],
    )
    dt, own, other, small = call(
        back_kernel, "back", 4,
        [
            ((half, 3 * CLS_ROWS, cols), BF16),
            ((half, cols, outs), BF16),
            ((half + 2, cols, outs), BF16),
            ((SMALL, LANES), F32),
        ],
        [where, hid, dz, loss, w2, halo] + counts,
        [((half + 2, cols, LANES), BF16)],
    )
    theirs = swap(other, "chan")
    cls_total = round_up(9 * LOGITS, 16 * pages * tiles)
    gcls, gcls_other = call(
        cls_kernel, "cls", 1.5, [((cls_total, outs), F32)] * 2, [where, hid, dt]
    )
    gcls_theirs = swap(gcls_other, "chan")

    total = round_up(9 * chans, 16 * pages * tiles)
    first, second = total // pages, total // (pages * tiles)
    cfirst, csecond = cls_total // tiles, cls_total // (pages * tiles)
    keep, *sends = call(
        shared_kernel, "shared", 4,
        [((first, outs), F32)] + [((first, outs), BF16)] * (pages - 1),
        [where, f, halo, own, theirs],
        [((rows, cols, 3 * outs), BF16), ((total, outs), F32)],
    )
    ckeep, *csends = call(
        cls_split_kernel, "cls_split", 0.6,
        [((cfirst, outs), F32)] + [((cfirst + TRIO, outs), BF16)] * (tiles - 1),
        [where, gcls, gcls_theirs, small],
        [((cls_total, outs), F32)],
    )
    arrived = exchange(sends, "batch")
    carrived = exchange(csends, "tile")
    keep, small, *sends = call(
        functools.partial(sum_kernel, pages - 1, tiles - 1, tiles - 1), "sum", 0.7,
        [((second, outs), F32), ((SMALL, LANES), F32)]
        + [((second, outs), BF16)] * (tiles - 1)
        + [((csecond, outs), F32)]
        + [((csecond + TRIO, outs), BF16)] * (pages - 1),
        [where, keep, small, ckeep] + arrived + carrived,
        [((first, outs), F32), ((cfirst, outs), F32)],
    )
    ckeep, csends = sends[tiles - 1], sends[tiles:]
    arrived = exchange(sends[: tiles - 1], "tile")
    carrived = exchange(csends, "batch")
    done, small, cdone = call(
        functools.partial(round_kernel, tiles - 1), "round", 0.7,
        [((second, outs), BF16), ((SMALL, LANES), F32), ((csecond, outs), BF16)],
        [where, keep, small, ckeep] + arrived + carrived,
    )
    small_theirs = swap(small, "chan")
    block, cblock = call(
        functools.partial(join_kernel, tiles), "join", 0.7,
        [((first, outs), BF16), ((cfirst, outs), BF16)],
        [where, done] + others(done, "tile") + [cdone] + others(cdone, "batch"),
    )
    grad_shared, bias, grad_cls, cls_bias, loss = call(
        functools.partial(out_kernel, pages, tiles), "out", 1.5,
        [((9 * chans, outs), F32), ((1, outs), F32), ((3, 3, LOGITS, outs), F32), ((1, LOGITS), F32), ((1, 1), F32)],
        [where, small, small_theirs, block] + others(block, "batch") + [cblock] + others(cblock, "tile"),
        [((cls_total, outs), F32)] + ([((total, outs), F32)] if total > 9 * chans else []),
    )
    return (
        grad_shared.reshape(3, 3, chans, outs),
        bias.reshape(outs),
        jnp.swapaxes(grad_cls, 2, 3),
        cls_bias.reshape(LOGITS),
        loss.reshape(1),
    )


def solution(mesh):
    placed = (
        P(("groups", "batch"), "tile", None, None),
        P(("groups", "batch"), "tile", None),
        P(None, None, None, "chan"),
        P("chan"),
        P(None, None, "chan", None),
        P(),
    )
    return jax.shard_map(
        shards,
        mesh=mesh,
        in_specs=placed,
        out_specs=(
            P("groups", None, None, "chan"),
            P(("groups", "chan")),
            P("groups", None, "chan", None),
            P("groups"),
            P("groups"),
        ),
        check_vma=False,
    )
```

```python
import functools

import jax
import jax.numpy as jnp
from jax import lax
from jax.experimental import pallas as pl
from jax.experimental.pallas import tpu as pltpu
from jax.sharding import PartitionSpec as P

ANCH = 9
CLASSES = 11
LOGITS = 99
LANES = 128
ANCH_ROWS = 16
CLS_ROWS = 112
TILE, BATCH = 3, 4
BLOCK = 2
SMALL = 4
TRIO = 16
BF16 = jnp.bfloat16
F32 = jnp.float32
VMEM = pl.BlockSpec(memory_space=pltpu.VMEM)
HBM = pl.BlockSpec(memory_space=pltpu.HBM)
SMEM = pl.BlockSpec(memory_space=pltpu.SMEM)


class Places:
    def __init__(self, half):
        self.half = half

    def __getitem__(self, i):
        c, t = lax.axis_index("chan"), lax.axis_index("tile")
        if i == 0:
            return c
        if i == 1:
            return (2 * t + c) * self.half
        if i == 2:
            return 2 * lax.axis_size("tile") * self.half
        return t if i == 3 else lax.axis_index("batch")


def call(kernel, name, micros, outs, inputs, scratch=(), specs=None, mib=32):
    return pl.pallas_call(
        functools.partial(kernel, inputs[0]),
        in_specs=(specs or [SMEM] + [VMEM] * (len(inputs) - 1))[1:],
        out_specs=[VMEM] * len(outs),
        out_shape=[jax.ShapeDtypeStruct(shape, kind) for shape, kind in outs],
        scratch_shapes=[pltpu.VMEM(*shape) if isinstance(shape, tuple) else shape for shape in scratch],
        cost_estimate=pl.CostEstimate(flops=int(micros * 1e9), bytes_accessed=int(micros * 1e6), transcendentals=0),
        compiler_params=pltpu.CompilerParams(vmem_limit_bytes=int(mib * 1024 * 1024)),
        name=name,
    )(*inputs[1:])


def shift_cells(field, by):
    cells = field.shape[0]
    rolled = pltpu.roll(field, by % cells, axis=0)
    cell = lax.broadcasted_iota(jnp.int32, field.shape, 0)
    edge = 0 if by > 0 else cells - 1
    return jnp.where(cell == edge, 0.0, rolled)


def dot(left, right, dims=((1,), (0,))):
    return lax.dot_general(left, right, (dims, ((), ())), preferred_element_type=F32)


def taken(ref, start, rows):
    cols = ref.shape[1]
    parts = [ref[pl.ds(start + r, BLOCK)].reshape(BLOCK * cols, ref.shape[2]) for r in rows]
    return jnp.concatenate(parts, axis=1)


def three(x):
    high = x.astype(BF16)
    rest = x - high.astype(F32)
    middle = rest.astype(BF16)
    low = (rest - middle.astype(F32)).astype(BF16)
    return high, middle, low


def put_trio(ref, start, x):
    parts = [part.astype(F32) for part in three(x)]
    ref[start : start + TRIO] = jnp.concatenate(parts + [jnp.zeros_like(x)], axis=0).astype(BF16)


def get_trio(ref, start):
    part = ref[start : start + TRIO].astype(F32)
    return part[0:SMALL] + part[SMALL : 2 * SMALL] + part[2 * SMALL : 3 * SMALL]


def edge_kernel(where_ref, f_ref, lab_ref, msg_ref, labt_ref, count_ref, near_ref, sem):
    rows, cols, _ = f_ref.shape
    c = where_ref[0]
    copies = [
        pltpu.make_async_copy(f_ref.at[(rows - 3) * c + k], msg_ref.at[pl.ds(cols * k, cols)], sem.at[k])
        for k in range(3)
    ]
    near = near_ref.shape[0]
    copies.append(pltpu.make_async_copy(f_ref.at[pl.ds((rows - near) * c, near)], near_ref, sem.at[3]))
    for copy in copies:
        copy.start()
    size = lab_ref.shape[2]
    place = lax.broadcasted_iota(jnp.int32, (ANCH_ROWS, size), 1) % ANCH
    anchor = lax.broadcasted_iota(jnp.int32, (ANCH_ROWS, size), 0)
    mine = place == anchor
    labs = [lab_ref[r].astype(F32) for r in range(rows)]
    named = [jnp.where(lab > 0.0, 1.0, 0.0) for lab in labs]
    count_ref[...] = jnp.full(count_ref.shape, jnp.sum(sum(named[1:], named[0])), F32)
    left = jnp.concatenate([jnp.where(mine, lab, 0.0) for lab in labs], axis=0).astype(BF16)
    offset = lax.broadcasted_iota(jnp.int32, (size, cols), 0) - ANCH * lax.broadcasted_iota(jnp.int32, (size, cols), 1)
    pick = jnp.where(jnp.logical_and(offset >= 0, offset < ANCH), 1.0, 0.0).astype(BF16)
    turned = dot(left, pick).astype(BF16)
    for r in range(rows):
        labt_ref[r] = turned[ANCH_ROWS * r : ANCH_ROWS * (r + 1)]
    msg_ref[3 * cols : 3 * cols + ANCH_ROWS] = jnp.where(
        c == 0, turned[:ANCH_ROWS].astype(F32), turned[ANCH_ROWS * (rows - 1) :].astype(F32)
    ).astype(BF16)
    for copy in copies:
        copy.wait()


def hidden_rows(x, w1a_ref, w1b_ref, b1a_ref, b1b_ref):
    w1 = [
        jnp.concatenate(
            [part for j in range(3) for part in (w1a_ref[i, j], w1b_ref[i, j])], axis=1
        )
        for i in range(3)
    ]
    w1 = jnp.concatenate(w1, axis=0)
    b1 = jnp.concatenate([b1a_ref[...], b1b_ref[...]], axis=1)
    n = x.shape[0] - 2
    cols, chans = x.shape[1:]
    width = w1.shape[1] // 3
    for start in range(0, n, 4):
        count = min(4, n - start)
        parts = [x[start + r : start + r + count].reshape(count * cols, chans) for r in range(3)]
        many = dot(jnp.concatenate(parts, axis=1), w1)
        for k in range(count):
            y = many[k * cols : (k + 1) * cols]
            yield shift_cells(y[:, :width], 1) + y[:, width : 2 * width] + shift_cells(y[:, 2 * width :], -1) + b1


def inner_kernel(where_ref, near_ref, w1a_ref, w1b_ref, b1a_ref, b1b_ref, out_ref):
    for k, pre in enumerate(hidden_rows(near_ref, w1a_ref, w1b_ref, b1a_ref, b1b_ref)):
        out_ref[k] = jnp.maximum(pre, 0.0).astype(BF16)


def head_kernel(
    where_ref, near_ref, inner_ref, halo_ref, labt_ref, w1a_ref, w1b_ref, b1a_ref, b1b_ref, w2a_ref, w2b_ref, b2_ref,
    hid_ref, dz_ref, loss_ref, w2_ref, xw_ref,
):
    near = near_ref.shape[0]
    half = near - 3
    cols, chans = near_ref.shape[1:]
    c = where_ref[0]
    first = where_ref[1]
    total = where_ref[2]
    xw_ref[pl.ds(3 - 3 * c, 2)] = near_ref[pl.ds((near - 2) * c, 2)]
    for k in range(3):
        xw_ref[2 * c + k] = halo_ref[cols * k : cols * (k + 1)]
    hid_ref[pl.ds(3 - 3 * c, near - 2)] = inner_ref[...]
    for k, pre in enumerate(hidden_rows(xw_ref, w1a_ref, w1b_ref, b1a_ref, b1b_ref)):
        h = (near - 2) * c + k
        row = first + h - 2
        inside = jnp.logical_and(row >= 0, row < total)
        hid_ref[h] = jnp.where(inside, jnp.maximum(pre, 0.0), 0.0).astype(BF16)
    deep = chans // 2
    for tap in range(9):
        end = LANES * tap + LANES
        w2_ref[end - 32 : end] = jnp.zeros((32, chans), BF16)
        w2_ref[end - LANES : end - LANES + LOGITS, :deep] = w2a_ref[tap // 3, tap % 3]
        w2_ref[end - LANES : end - LANES + LOGITS, deep:] = w2b_ref[tap // 3, tap % 3]

    lane = lax.broadcasted_iota(jnp.int32, (1, LANES), 1)
    kind = (lane % CLASSES + 1).astype(F32)
    real = lane < LOGITS
    anchor = lax.broadcasted_iota(jnp.int32, (ANCH_ROWS, LANES), 0)
    column = lax.broadcasted_iota(jnp.int32, (ANCH_ROWS, LANES), 1)
    spread = jnp.where(jnp.logical_and(column // CLASSES == anchor, column < LOGITS), 1.0, 0.0).astype(BF16)
    size = 3 * LANES
    w2 = jnp.concatenate([w2_ref[size * i : size * (i + 1)] for i in range(3)], axis=1)
    b2 = jnp.concatenate([b2_ref[...], jnp.zeros((1, LANES - LOGITS), F32)], axis=1)

    def focal(g, loss):
        pair = dot(taken(hid_ref, BLOCK * g, (0, 1, 2)), w2, ((1,), (1,)))
        for k in range(BLOCK):
            loss = loss + focal_row(BLOCK * g + k, pair[k * cols : (k + 1) * cols])
        return loss

    def focal_row(l, y):
        z = shift_cells(y[:, :LANES], 1) + y[:, LANES : 2 * LANES] + shift_cells(y[:, 2 * LANES :], -1) + b2
        at_halo = jnp.where(c == 0, l == 0, l == half + 1)
        local = jnp.clip(l - 1 + half * c, 0, 2 * half - 1)
        mine = labt_ref[local].astype(F32)
        far = halo_ref[3 * cols : 3 * cols + ANCH_ROWS].astype(F32)
        lab = dot(jnp.where(at_halo, far, mine).astype(BF16), spread, ((0,), (0,)))
        row = first + l - 1
        inside = jnp.logical_and(row >= 0, row < total)
        hit = lab == kind
        keep = jnp.logical_and(jnp.logical_and(lab >= 0.0, real), inside)
        u = jnp.where(hit, -z, z)
        e = jnp.exp(-jnp.abs(u))
        r = 1.0 / (1.0 + e)
        er = e * r
        up = u >= 0.0
        s = jnp.where(up, r, er)
        comp = jnp.where(up, er, r)
        soft = jnp.maximum(u, 0.0) + jnp.log1p(e)
        ws = jnp.where(keep, jnp.where(hit, 0.25, 0.75), 0.0) * s * s
        slope = ws * (2.0 * comp * soft + s)
        dz_ref[l] = jnp.where(hit, -slope, slope)
        own = jnp.logical_and(l >= 1, l <= half)
        return jnp.where(own, 1.0, 0.0) * jnp.sum(ws * soft, axis=0, keepdims=True)

    loss_ref[...] = lax.fori_loop(0, (half + 2) // BLOCK, focal, jnp.zeros((1, LANES), F32), unroll=True)


def back_kernel(where_ref, hid_ref, dz_ref, loss_ref, w2_ref, halo_ref, *rest):
    *count_refs, dt_ref, own_ref, other_ref, small_ref, dlog_ref = rest
    half, _, cols = dt_ref.shape
    chans = hid_ref.shape[2]
    inverse = 1.0 / pair_sum([ref[...] for ref in count_refs])[:1]

    def scaled(l):
        dz = dz_ref[l] * inverse
        d16 = dz.astype(BF16)
        dlog_ref[l] = d16
        return dz, d16

    scaled(0)
    scaled(half + 1)

    def turn(d, gcb):
        dz, d16 = scaled(d + 1)
        turned = jnp.transpose(d16.astype(F32))[:CLS_ROWS]
        cell = lax.broadcasted_iota(jnp.int32, turned.shape, 1)
        left = jnp.where(cell == cols - 1, 0.0, pltpu.roll(turned, cols - 1, axis=1))
        right = jnp.where(cell == 0, 0.0, pltpu.roll(turned, 1, axis=1))
        dt_ref[d] = jnp.concatenate([left, turned, right], axis=0).astype(BF16)
        return gcb + jnp.sum(dz, axis=0, keepdims=True)

    gcb = lax.fori_loop(0, half, turn, jnp.zeros((1, LANES), F32), unroll=True)
    w2t = [
        jnp.concatenate([w2_ref[LANES * (3 * i + j) : LANES * (3 * i + j + 1)] for j in range(3)], axis=1)
        for i in range(3)
    ]
    w2t = jnp.concatenate(w2t, axis=0)

    def dpre(g, gsb):
        pair = dot(taken(dlog_ref, BLOCK * g, (2, 1, 0)), w2t)
        for k in range(BLOCK):
            gsb = gsb + dpre_row(BLOCK * g + k, pair[k * cols : (k + 1) * cols])
        return gsb

    def dpre_row(d, q):
        dhid = shift_cells(q[:, :chans], -1) + q[:, chans : 2 * chans] + shift_cells(q[:, 2 * chans :], 1)
        dpre = jnp.where(hid_ref[d + 2].astype(F32) > 0.0, dhid, 0.0)
        d16 = dpre.astype(BF16)
        own_ref[d] = d16[:, : chans // 2]
        other_ref[d] = d16[:, chans // 2 :]
        return jnp.sum(dpre, axis=0, keepdims=True)

    gsb = lax.fori_loop(0, half // BLOCK, dpre, jnp.zeros((1, chans), F32), unroll=True)
    near = halo_ref[pl.ds(pl.multiple_of(2 * cols * (1 - where_ref[0]), 16), cols)]
    other_ref[half] = near[:, : chans // 2]
    other_ref[half + 1] = near[:, chans // 2 :]
    loss = jnp.sum(loss_ref[...], axis=1, keepdims=True) * inverse[:, :1]
    small_ref[0:1] = jnp.where(lax.broadcasted_iota(jnp.int32, (1, LANES), 1) < LOGITS, gcb, loss)
    small_ref[1:2] = jnp.zeros((1, LANES), F32)
    small_ref[2:3] = gsb[:, : chans // 2]
    small_ref[3:4] = gsb[:, chans // 2 :]


def cls_kernel(where_ref, hid_ref, dt_ref, own_ref, other_ref):
    half, _, cols = dt_ref.shape
    chans = hid_ref.shape[2]
    deep = chans // 2
    dt = jnp.concatenate([dt_ref[d] for d in range(half)], axis=1)
    for i in range(3):
        g = dot(dt, hid_ref[i + 1 : i + 1 + half].reshape(half * cols, chans))
        for j in range(3):
            start = LOGITS * (3 * i + j)
            own_ref[start : start + LOGITS] = g[CLS_ROWS * j : CLS_ROWS * j + LOGITS, :deep]
            other_ref[start : start + LOGITS] = g[CLS_ROWS * j : CLS_ROWS * j + LOGITS, deep:]
    blank = jnp.zeros((own_ref.shape[0] - 9 * LOGITS, deep), F32)
    own_ref[9 * LOGITS :] = blank
    other_ref[9 * LOGITS :] = blank


def partners(size, core=0):
    if size == 4:
        return [3, 2, 1] if core else [2, 3, 1]
    return list(range(size - 1, 0, -1))


def partner_of(size, k, where_ref):
    even, odd = partners(size)[k], partners(size, 1)[k]
    return even if even == odd else jnp.where(where_ref[0] == 0, even, odd)


def split(total, where_ref, slot, keep_ref, send_refs):
    rows = keep_ref.shape[0]
    me = where_ref[slot]
    keep_ref[...] = total[pl.ds(pl.multiple_of(me * rows, 8), rows)]
    for k, ref in enumerate(send_refs):
        bit = partner_of(len(send_refs) + 1, k, where_ref)
        ref[0:rows] = total[pl.ds(pl.multiple_of((me ^ bit) * rows, 8), rows)].astype(BF16)


def shared_kernel(
    where_ref, f_ref, halo_ref, own_ref, other_ref, keep_ref, *rest
):
    *send_refs, d_ref, g_ref = rest
    rows, cols, chans = f_ref.shape
    half = rows // 2
    c = where_ref[0]
    near = halo_ref[pl.ds(pl.multiple_of(2 * cols * (1 - c), 16), cols)]
    far = jnp.concatenate([other_ref[half], other_ref[half + 1]], axis=1)
    before = jnp.where(c == 0, near, far)
    after = jnp.where(c == 0, far, near)

    for r in range(rows):
        mine, theirs = own_ref[r % half].astype(F32), other_ref[r % half].astype(F32)
        mid = jnp.where(c == (0 if r < half else 1), mine, theirs)
        d_ref[r] = jnp.concatenate([shift_cells(mid, -1), mid, shift_cells(mid, 1)], axis=1).astype(BF16)
    outs = d_ref.shape[2] // 3

    def part(x, first):
        n = x.shape[0]
        rhs = d_ref[first : first + n].reshape(n * cols, 3 * outs)
        return dot(x.reshape(n * cols, chans), rhs, ((0,), (0,)))

    for i in range(3):
        if i == 0:
            g = part(f_ref[0 : rows - 1], 1) + part(before[None], 0)
        elif i == 1:
            g = part(f_ref[...], 0)
        else:
            g = part(f_ref[1:rows], 0) + part(after[None], rows - 1)
        for j in range(3):
            start = (3 * i + j) * chans
            g_ref[start : start + chans] = g[:, j * outs : (j + 1) * outs]
    if g_ref.shape[0] > 9 * chans:
        g_ref[9 * chans :] = jnp.zeros((g_ref.shape[0] - 9 * chans, outs), F32)
    split(g_ref, where_ref, BATCH, keep_ref, send_refs)


def cls_split_kernel(where_ref, cls_ref, theirs_ref, small_ref, keep_ref, *rest):
    *send_refs, total_ref = rest
    total_ref[...] = cls_ref[...] + theirs_ref[...]
    split(total_ref, where_ref, TILE, keep_ref, send_refs)
    for ref in send_refs:
        put_trio(ref, keep_ref.shape[0], small_ref[...])


def pair_sum(parts):
    while len(parts) > 1:
        parts = [parts[k] + parts[k + 1] for k in range(0, len(parts), 2)]
    return parts[0]


def total_of(base_ref, in_refs):
    rows = base_ref.shape[0]
    total = base_ref[...]
    for ref in in_refs:
        total = total + ref[0:rows].astype(F32)
    return total


def small_sum(small_ref, in_refs, start):
    return pair_sum([small_ref[...]] + [get_trio(ref, start) for ref in in_refs])


def sum_kernel(n_in, n_cls, n_send, where_ref, base_ref, small_ref, cls_ref, *refs):
    in_refs, refs = refs[:n_in], refs[n_in:]
    cls_in_refs, refs = refs[:n_cls], refs[n_cls:]
    keep_ref, sum_ref, *refs, total_ref, cls_total_ref = refs
    send_refs, cls_keep_ref, cls_send_refs = refs[:n_send], refs[n_send], refs[n_send + 1 :]
    total_ref[...] = total_of(base_ref, in_refs)
    split(total_ref, where_ref, TILE, keep_ref, send_refs)
    cls_total_ref[...] = total_of(cls_ref, cls_in_refs)
    split(cls_total_ref, where_ref, BATCH, cls_keep_ref, cls_send_refs)
    sums = small_sum(small_ref, cls_in_refs, cls_ref.shape[0])
    sum_ref[...] = sums
    for ref in cls_send_refs:
        put_trio(ref, cls_keep_ref.shape[0], sums)


def round_kernel(n_in, where_ref, base_ref, small_ref, cls_ref, *refs):
    in_refs, cls_in_refs = refs[:n_in], refs[n_in:-3]
    out_ref, sum_ref, cls_out_ref = refs[-3:]
    out_ref[...] = total_of(base_ref, in_refs).astype(BF16)
    cls_out_ref[...] = total_of(cls_ref, cls_in_refs).astype(BF16)
    sum_ref[...] = small_sum(small_ref, cls_in_refs, cls_ref.shape[0])


def join(where_ref, slot, in_refs, out_ref):
    rows = in_refs[0].shape[0]
    me = where_ref[slot]
    size = len(in_refs)
    for k, ref in enumerate(in_refs):
        bit = partner_of(size, size - 1 - k, where_ref) if k else 0
        out_ref[pl.ds(pl.multiple_of((me ^ bit) * rows, 8), rows)] = ref[...].astype(out_ref.dtype)


def join_kernel(n_in, where_ref, *refs):
    join(where_ref, TILE, refs[:n_in], refs[-2])
    join(where_ref, BATCH, refs[n_in:-2], refs[-1])


def out_kernel(n_in, n_cls, where_ref, small_ref, theirs_ref, *refs):
    in_refs, cls_in_refs, refs = refs[:n_in], refs[n_in : n_in + n_cls], refs[n_in + n_cls :]
    out_ref, bias_ref, cls_out_ref, cls_bias_ref, loss_ref, cls_whole_ref, *whole_ref = refs
    if whole_ref:
        join(where_ref, BATCH, in_refs, whole_ref[0])
        out_ref[...] = whole_ref[0][: out_ref.shape[0]]
    else:
        join(where_ref, BATCH, in_refs, out_ref)
    join(where_ref, TILE, cls_in_refs, cls_whole_ref)
    for tap in range(9):
        cls_out_ref[tap // 3, tap % 3] = cls_whole_ref[LOGITS * tap : LOGITS * (tap + 1)]
    bias_ref[...] = small_ref[2:3] + theirs_ref[3:4]
    both = small_ref[0:1] + theirs_ref[0:1]
    cls_bias_ref[...] = both[:, :LOGITS]
    loss_ref[...] = both[:, LOGITS : LOGITS + 1]


def swap(x, axis, bit=1):
    size = lax.axis_size(axis)
    return lax.ppermute(x, axis, [(i, i ^ bit) for i in range(size)])


def send(x, axis, k):
    size, cores = lax.axis_size(axis), lax.axis_size("chan")
    pairs = [
        (i * cores + core, (i ^ partners(size, core % 2)[k]) * cores + core) for i in range(size) for core in range(cores)
    ]
    return lax.ppermute(x, (axis, "chan"), pairs)


def others(x, axis):
    return [send(x, axis, k) for k in reversed(range(lax.axis_size(axis) - 1))]


def exchange(sends, axis):
    return [send(x, axis, k) for k, x in enumerate(sends)]


def round_up(n, step):
    return (n + step - 1) // step * step


def shards(features, labels, w_shared, b_shared, w_cls, b_cls):
    _, rows, cols, chans = features.shape
    half = rows // 2
    outs = w_shared.shape[3]
    tiles = lax.axis_size("tile")
    pages = lax.axis_size("batch")
    c = lax.axis_index("chan")
    t = lax.axis_index("tile")
    f = features[0]
    where = Places(half)
    lab = labels.reshape(rows, 1, labels.shape[2])
    msg, labt, count, near = call(
        edge_kernel, "edge", 2,
        [
            ((3 * cols + ANCH_ROWS, chans), BF16),
            ((rows, ANCH_ROWS, cols), BF16),
            ((8, LANES), F32),
            ((half + 3, cols, chans), BF16),
        ],
        [where, f, lab],
        [pltpu.SemaphoreType.DMA((4,))],
        [SMEM, HBM, VMEM],
        51,
    )
    met = others(count, "batch")
    pairs = []
    for i in range(tiles - 1):
        pairs += [(2 * i + 1, 2 * i + 2), (2 * i + 2, 2 * i + 1)]
    halo = lax.ppermute(msg, ("tile", "chan"), pairs)
    w1b = swap(w_shared, "chan")
    w2b = swap(w_cls, "chan")
    b1b = swap(b_shared, "chan")

    weights = [w_shared, w1b, b_shared.reshape(1, outs), b1b.reshape(1, outs)]
    (inner,) = call(inner_kernel, "inner", 3, [((half + 1, cols, chans), BF16)], [where, near] + weights)
    inner, *met = lax.optimization_barrier((inner, *met))
    count = pair_sum([count] + met)
    halo, _ = lax.optimization_barrier((halo, count))
    counts = [count] + others(count, "tile")
    hid, dz, loss, w2 = call(
        head_kernel, "head", 5,
        [((half + 4, cols, chans), BF16), ((half + 2, cols, LANES), F32), ((1, LANES), F32)]
        + [((9 * LANES, chans), BF16)],
        [where, near, inner, halo, labt]
        + weights
        + [jnp.swapaxes(w_cls, 2, 3), jnp.swapaxes(w2b, 2, 3), b_cls.reshape(1, LOGITS)],
        [((5, cols, chans), BF16)],
    )
    dt, own, other, small = call(
        back_kernel, "back", 4,
        [
            ((half, 3 * CLS_ROWS, cols), BF16),
            ((half, cols, outs), BF16),
            ((half + 2, cols, outs), BF16),
            ((SMALL, LANES), F32),
        ],
        [where, hid, dz, loss, w2, halo] + counts,
        [((half + 2, cols, LANES), BF16)],
    )
    theirs = swap(other, "chan")
    cls_total = round_up(9 * LOGITS, 16 * pages * tiles)
    gcls, gcls_other = call(
        cls_kernel, "cls", 1.5, [((cls_total, outs), F32)] * 2, [where, hid, dt]
    )
    gcls_theirs = swap(gcls_other, "chan")

    total = round_up(9 * chans, 16 * pages * tiles)
    first, second = total // pages, total // (pages * tiles)
    cfirst, csecond = cls_total // tiles, cls_total // (pages * tiles)
    keep, *sends = call(
        shared_kernel, "shared", 4,
        [((first, outs), F32)] + [((first, outs), BF16)] * (pages - 1),
        [where, f, halo, own, theirs],
        [((rows, cols, 3 * outs), BF16), ((total, outs), F32)],
    )
    ckeep, *csends = call(
        cls_split_kernel, "cls_split", 0.6,
        [((cfirst, outs), F32)] + [((cfirst + TRIO, outs), BF16)] * (tiles - 1),
        [where, gcls, gcls_theirs, small],
        [((cls_total, outs), F32)],
    )
    arrived = exchange(sends, "batch")
    carrived = exchange(csends, "tile")
    keep, small, *sends = call(
        functools.partial(sum_kernel, pages - 1, tiles - 1, tiles - 1), "sum", 0.7,
        [((second, outs), F32), ((SMALL, LANES), F32)]
        + [((second, outs), BF16)] * (tiles - 1)
        + [((csecond, outs), F32)]
        + [((csecond + TRIO, outs), BF16)] * (pages - 1),
        [where, keep, small, ckeep] + arrived + carrived,
        [((first, outs), F32), ((cfirst, outs), F32)],
    )
    ckeep, csends = sends[tiles - 1], sends[tiles:]
    arrived = exchange(sends[: tiles - 1], "tile")
    carrived = exchange(csends, "batch")
    done, small, cdone = call(
        functools.partial(round_kernel, tiles - 1), "round", 0.7,
        [((second, outs), BF16), ((SMALL, LANES), F32), ((csecond, outs), BF16)],
        [where, keep, small, ckeep] + arrived + carrived,
    )
    small_theirs = swap(small, "chan")
    block, cblock = call(
        functools.partial(join_kernel, tiles), "join", 0.7,
        [((first, outs), BF16), ((cfirst, outs), BF16)],
        [where, done] + others(done, "tile") + [cdone] + others(cdone, "batch"),
    )
    grad_shared, bias, grad_cls, cls_bias, loss = call(
        functools.partial(out_kernel, pages, tiles), "out", 1.5,
        [((9 * chans, outs), F32), ((1, outs), F32), ((3, 3, LOGITS, outs), F32), ((1, LOGITS), F32), ((1, 1), F32)],
        [where, small, small_theirs, block] + others(block, "batch") + [cblock] + others(cblock, "tile"),
        [((cls_total, outs), F32)] + ([((total, outs), F32)] if total > 9 * chans else []),
    )
    return (
        grad_shared.reshape(3, 3, chans, outs),
        bias.reshape(outs),
        jnp.swapaxes(grad_cls, 2, 3),
        cls_bias.reshape(LOGITS),
        loss.reshape(1),
    )


def solution(mesh):
    placed = (
        P(("groups", "batch"), "tile", None, None),
        P(("groups", "batch"), "tile", None),
        P(None, None, None, "chan"),
        P("chan"),
        P(None, None, "chan", None),
        P(),
    )
    return jax.shard_map(
        shards,
        mesh=mesh,
        in_specs=placed,
        out_specs=(
            P("groups", None, None, "chan"),
            P(("groups", "chan")),
            P("groups", None, "chan", None),
            P("groups"),
            P("groups"),
        ),
        check_vma=False,
    )
```
